32 devices in a mesh: event: 2 (over x), phi: 16 (over z, y, core).
Axes of the slice: x: 2, y: 2, z: 4, core: 2. Of those that a mesh axis runs over, the one named last changes fastest.
Arguments:
- hit_feats: bfloat16 [12, 131072], P(None, ('event', 'phi')), parts along dimension 1, may hold values from -6 to 6
- layer_ids: int32 [131072], P(('event', 'phi')), parts along dimension 0, may hold values from 0 to 15
- edge_tiles: bfloat16 [1024, 8, 128, 128], P(('event', 'phi')), parts along dimension 0
- src_blocks: int32 [1024, 8], P(('event', 'phi')), parts along dimension 0, may hold values from 0 to 159
- live_slots: int32 [1024], P(('event', 'phi')), parts along dimension 0, may hold values from 1 to 8, as said below
- anchor_hits: int32 [32768], P(('event', 'phi')), parts along dimension 0, may hold values from 0 to 4095
- positive_hits: int32 [32768], P(('event', 'phi')), parts along dimension 0, may hold values from 0 to 20479
- negative_hits: int32 [32768], P(('event', 'phi')), parts along dimension 0, may hold values from 0 to 20479
- w_enc: bfloat16 [12, 128], replicated, may hold values from -1.75 to 1.75
- layer_table: bfloat16 [16, 128], replicated, may hold values from -3 to 3
- w_self: bfloat16 [2, 128, 128], replicated, may hold values from -0.5 to 0.5
- w_agg: bfloat16 [2, 128, 128], replicated, may hold values from -0.5 to 0.5
- w_out: bfloat16 [2, 128, 128], replicated, may hold values from -0.5 to 0.5
Outputs:
- loss: float32 [2], P('event'), parts along dimension 0
- grad_enc: float32 [24, 128], P('event'), parts along dimension 0
- grad_table: float32 [32, 128], P('event'), parts along dimension 0
- grad_self: float32 [4, 128, 128], P('event'), parts along dimension 0
- grad_agg: float32 [4, 128, 128], P('event'), parts along dimension 0
- grad_out: float32 [4, 128, 128], P('event'), parts along dimension 0
The draws below stay inside these ranges and needn't reach their ends.
There are 2 independent parts, one for each index of `event`. The reference program is written for one: setup_inputs(seed, part) draws one part's arguments, and reference() takes and returns one part's arrays. A program takes and returns all parts, laid end to end along the dimension named above; an argument that names none is the same for every part. Nothing has to cross between parts.
Inputs may be any that keep to these rules, and one draw needn't show every extreme that they name: `live_slots`: in every draw some node block has all 8 slots live.
All inputs are finite; a program needn't handle non-finite values.
Results may differ from the reference program's by a relative error of at most 0.0022.
Values may be sent and summed in bfloat16 or wider, within the bound.
A program may use at most 128 MiB of HBM per device.

```python
import math
import jax
import jax.numpy as jnp
from jax import lax

WIDTH = 128
FEAT = 12
NLAY = 16
LAYERS = 2
BLK = 128
SLOTS = 8
REACH = 2
NB = 32
CON = 1024
NB_ALL = 512
HITS = 65536
CON_ALL = 16384
N_PHI = 16


def draw_edge_tiles(key, part):
    first_key, second_key = jax.random.split(key)
    shape = (NB_ALL, SLOTS, BLK, BLK)
    present = jax.random.uniform(first_key, shape, jnp.float32) < 0.25
    weights = jax.random.uniform(second_key, shape, jnp.float32, minval=0.05, maxval=0.25)
    return jnp.where(present, weights, 0.0).astype(jnp.bfloat16)


def draw_live_slots(key, part):
    sector_count = NB_ALL // NB
    first_key, second_key, third_key = jax.random.split(key, 3)
    order = jax.random.permutation(first_key, sector_count).astype(jnp.int32)
    level = 1 + order * SLOTS // sector_count
    level_rows = jnp.repeat(level, NB)
    dropped = jax.random.randint(second_key, (NB_ALL,), 0, level_rows // 2 + 1, dtype=jnp.int32)
    counts = level_rows - dropped
    chosen_block = jax.random.randint(third_key, (sector_count,), 0, NB, dtype=jnp.int32)
    filled = jnp.arange(NB_ALL, dtype=jnp.int32) % NB == jnp.repeat(chosen_block, NB)
    return jnp.where(filled, level_rows, counts).astype(jnp.int32)


def set_ends(result, own_key, smallest, top_value):
    spot = [jax.random.randint(jax.random.fold_in(own_key, axis), (), 0, length) for axis, length in enumerate(result.shape)]
    main_axis = result.shape.index(max(result.shape))
    next_to = spot[:main_axis] + [(spot[main_axis] + 1) % result.shape[main_axis]] + spot[main_axis + 1:]
    return result.at[tuple(spot)].set(smallest).at[tuple(next_to)].set(top_value)


def level_of(key, extent, cuts, low, largest):
    level, own = 1.0, jax.random.fold_in(key, 6)
    for position, parts in cuts:
        draws = jnp.exp(jax.random.uniform(jax.random.fold_in(own, position), (parts,), jnp.float32, low / len(cuts), largest / len(cuts)))
        level = level * jnp.repeat(draws, extent[position] // parts).reshape([-1 if axis == position else 1 for axis in range(len(extent))])
    return level


def normal_values(key, dims, width, most, cuts=(), kind=jnp.bfloat16):
    values = jax.random.normal(key, dims, jnp.float32) * width
    if len(cuts) > 0:
        values = level_of(key, dims, cuts, -0.22, 0.18) * values
    return jnp.clip(values, min=-most, max=most).astype(kind)


def setup_inputs(seed: int = 0, part: int = 0) -> dict:
    splits = jax.random.split(jax.random.key(seed), 14)
    part_splits = jax.random.split(jax.random.fold_in(splits[13], part), 14)
    hit_feats = normal_values(part_splits[0], (FEAT, HITS), 1.0, 6.0, ((1, 16),))
    layer_ids = set_ends(jax.random.randint(part_splits[1], (HITS,), 0, NLAY), jax.random.fold_in(part_splits[1], 1), 0, NLAY - 1).astype(jnp.int32)
    edge_tiles = draw_edge_tiles(jax.random.fold_in(jax.random.fold_in(splits[13], part), 71), part)
    src_blocks = set_ends(jax.random.randint(part_splits[3], (NB_ALL, SLOTS), 0, (2 * REACH + 1) * NB), jax.random.fold_in(part_splits[3], 1), 0, ((2 * REACH + 1) * NB) - 1).astype(jnp.int32)
    live_slots = draw_live_slots(jax.random.fold_in(jax.random.fold_in(splits[13], part), 71), part)
    anchor_hits = set_ends(jax.random.randint(part_splits[5], (CON_ALL,), 0, NB * BLK), jax.random.fold_in(part_splits[5], 1), 0, (NB * BLK) - 1).astype(jnp.int32)
    positive_hits = set_ends(jax.random.randint(part_splits[6], (CON_ALL,), 0, (2 * REACH + 1) * NB * BLK), jax.random.fold_in(part_splits[6], 1), 0, ((2 * REACH + 1) * NB * BLK) - 1).astype(jnp.int32)
    negative_hits = set_ends(jax.random.randint(part_splits[7], (CON_ALL,), 0, (2 * REACH + 1) * NB * BLK), jax.random.fold_in(part_splits[7], 1), 0, ((2 * REACH + 1) * NB * BLK) - 1).astype(jnp.int32)
    w_enc = normal_values(splits[8], (FEAT, WIDTH), FEAT ** -0.5, 1.75)
    layer_table = normal_values(splits[9], (NLAY, WIDTH), 0.5, 3.0)
    w_self = normal_values(splits[10], (LAYERS, WIDTH, WIDTH), WIDTH ** -0.5, 0.5)
    w_agg = normal_values(splits[11], (LAYERS, WIDTH, WIDTH), WIDTH ** -0.5, 0.5)
    w_out = normal_values(splits[12], (LAYERS, WIDTH, WIDTH), WIDTH ** -0.5, 0.5)
    return {"hit_feats": hit_feats, "layer_ids": layer_ids, "edge_tiles": edge_tiles, "src_blocks": src_blocks, "live_slots": live_slots, "anchor_hits": anchor_hits, "positive_hits": positive_hits, "negative_hits": negative_hits, "w_enc": w_enc, "layer_table": layer_table, "w_self": w_self, "w_agg": w_agg, "w_out": w_out}


loss_divisor = 64.0

def contract_rows(left_side, right_side):
    return lax.dot_general(left_side, right_side, (((0,), (0,)), ((), ())), preferred_element_type=jnp.float32)

def contract_cols(left_side, right_side):
    return lax.dot_general(left_side, right_side, (((1,), (1,)), ((), ())), preferred_element_type=jnp.float32)

def contract_inner(left_side, right_side):
    return lax.dot_general(left_side, right_side, (((1,), (0,)), ((), ())), preferred_element_type=jnp.float32)

def contrast_terms(window, anchor_here, positive_here, negative_here, centre, latent_width):
    anchor = window[centre + anchor_here].astype(jnp.float32)
    positive = window[positive_here].astype(jnp.float32)
    negative = window[negative_here].astype(jnp.float32)
    inv_root = 1.0 / math.sqrt(latent_width)
    score_gap = (lax.optimization_barrier(jnp.sum(anchor * negative, axis=1)) - lax.optimization_barrier(jnp.sum(anchor * positive, axis=1))) * inv_root
    return (score_gap, anchor, positive, negative)

def contrast_grad(window, anchor_here, positive_here, negative_here, centre, latent_width):
    score_gap, anchor, positive, negative = contrast_terms(window, anchor_here, positive_here, negative_here, centre, latent_width)
    weight_coef = (jax.nn.sigmoid(score_gap) * (1.0 / (loss_divisor * math.sqrt(latent_width))))[:, None]
    gradient = jnp.zeros(window.shape, jnp.float32)
    gradient = gradient.at[centre + anchor_here].add(weight_coef * (negative - positive))
    gradient = gradient.at[positive_here].add(-weight_coef * anchor)
    gradient = gradient.at[negative_here].add(weight_coef * anchor)
    return gradient

def reference(hit_feats, layer_ids, edge_tiles, src_blocks, live_slots, anchor_hits, positive_hits, negative_hits, w_enc, layer_table, w_self, w_agg, w_out):
    hit_count = NB * BLK
    span_count = 2 * REACH + 1
    sectors = jnp.arange(N_PHI, dtype=jnp.int32)
    offsets = jnp.arange(-REACH, REACH + 1, dtype=jnp.int32)
    onehot = (jnp.arange(NLAY, dtype=jnp.int32)[:, None] == layer_ids[None, :]).astype(jnp.bfloat16)
    encoded = contract_rows(hit_feats, w_enc) + contract_rows(onehot, layer_table)
    squashed = jnp.tanh(encoded)
    latents = squashed.astype(jnp.bfloat16)
    tiles = edge_tiles.reshape(N_PHI, NB, SLOTS, BLK, BLK)
    sources = src_blocks.reshape(N_PHI, NB, SLOTS)
    live_mask = jnp.arange(SLOTS, dtype=jnp.int32)[None, None, :] < live_slots.reshape(N_PHI, NB)[:, :, None]

    def window_of(grid, sector):
        return jnp.take(grid, (sector + offsets) % N_PHI, axis=0).reshape(span_count * hit_count, WIDTH)

    def aggregate(current):
        grid = current.reshape(N_PHI, hit_count, WIDTH)

        def one_sector(sector_items):
            sector, tiles_here, sources_here, live_here = sector_items
            blocks = window_of(grid, sector).reshape(span_count * NB, BLK, WIDTH)
            chosen = jnp.where(live_here[:, :, None, None], blocks[sources_here], jnp.zeros((), blocks.dtype))
            return jnp.einsum('bsij,bsjw->biw', tiles_here.astype(jnp.float32), chosen.astype(jnp.float32))
        return lax.map(one_sector, (sectors, tiles, sources, live_mask)).reshape(N_PHI * hit_count, WIDTH)

    def give_back(piece_fn, sector_items):

        def advance(running, item_now):
            pieces = piece_fn(item_now).reshape(span_count, hit_count, WIDTH)
            for slot_index in range(span_count):
                portion = pieces[slot_index]
                if slot_index != REACH:
                    portion = lax.optimization_barrier(portion.astype(jnp.bfloat16)).astype(jnp.float32)
                target = (item_now[0] + slot_index - REACH) % N_PHI
                current = lax.dynamic_index_in_dim(running, target, 0, keepdims=False)
                running = lax.dynamic_update_index_in_dim(running, current + portion, target, 0)
            return (running, None)
        running, _ = lax.scan(advance, jnp.zeros((N_PHI, hit_count, WIDTH), jnp.float32), sector_items)
        return running.reshape(N_PHI * hit_count, WIDTH)
    stored = []
    for layer_index in range(LAYERS):
        aggregated = aggregate(latents).astype(jnp.bfloat16)
        activation = jnp.dot(latents, w_self[layer_index], preferred_element_type=jnp.float32) + jnp.dot(aggregated, w_agg[layer_index], preferred_element_type=jnp.float32)
        hidden = jax.nn.relu(activation).astype(jnp.bfloat16)
        updated = (latents.astype(jnp.float32) + jnp.dot(hidden, w_out[layer_index], preferred_element_type=jnp.float32)).astype(jnp.bfloat16)
        stored.append((latents, aggregated, activation, hidden))
        latents = updated
    final_grid = latents.reshape(N_PHI, hit_count, WIDTH)
    centre = REACH * hit_count
    triplets = (sectors, anchor_hits.reshape(N_PHI, CON), positive_hits.reshape(N_PHI, CON), negative_hits.reshape(N_PHI, CON))

    def sector_loss(sector_items):
        sector, anchor_here, positive_here, negative_here = sector_items
        score_gap = contrast_terms(window_of(final_grid, sector), anchor_here, positive_here, negative_here, centre, WIDTH)[0]
        return jnp.sum(jax.nn.softplus(score_gap))
    loss = (jnp.sum(lax.map(sector_loss, triplets)) / CON_ALL).reshape(1)

    def contrast_piece(sector_items):
        sector, anchor_here, positive_here, negative_here = sector_items
        return contrast_grad(window_of(final_grid, sector), anchor_here, positive_here, negative_here, centre, WIDTH)
    gradient = give_back(contrast_piece, triplets)
    self_grads = [None] * LAYERS
    agg_grads = [None] * LAYERS
    out_grads = [None] * LAYERS
    for layer_index in range(LAYERS - 1, -1, -1):
        before, aggregated, activation, hidden = stored[layer_index]
        upstream = gradient.astype(jnp.bfloat16)
        out_grads[layer_index] = contract_rows(hidden, upstream)
        hidden_grad = contract_cols(upstream, w_out[layer_index])
        act_grad = jnp.where(activation > 0, hidden_grad, 0.0).astype(jnp.bfloat16)
        self_grads[layer_index] = contract_rows(before, act_grad)
        agg_grads[layer_index] = contract_rows(aggregated, act_grad)
        agg_grad = contract_cols(act_grad, w_agg[layer_index]).astype(jnp.bfloat16)
        direct = gradient + contract_cols(act_grad, w_self[layer_index])
        agg_grid = agg_grad.reshape(N_PHI, NB, BLK, WIDTH)

        def adjacency_piece(sector_items):
            sector, tiles_here, sources_here, live_here, grad_here = sector_items
            contrib = jnp.einsum('bsij,biw->bsjw', tiles_here.astype(jnp.float32), grad_here.astype(jnp.float32))
            contrib = jnp.where(live_here[:, :, None, None], contrib, 0.0)
            return jax.ops.segment_sum(contrib.reshape(NB * SLOTS, BLK, WIDTH), sources_here.reshape(NB * SLOTS), num_segments=span_count * NB)
        gradient = direct + give_back(adjacency_piece, (sectors, tiles, sources, live_mask, agg_grid))
    encoded_grad = (gradient * (1.0 - squashed * squashed)).astype(jnp.bfloat16)
    grad_enc = contract_inner(hit_feats, encoded_grad)
    grad_table = contract_inner(onehot, encoded_grad)
    return (loss, grad_enc, grad_table, jnp.stack(self_grads), jnp.stack(agg_grads), jnp.stack(out_grads))
```

```python
import functools
import math

import jax
import jax.numpy as jnp
from jax import lax
from jax.experimental import pallas as pl
from jax.experimental.pallas import tpu as pltpu
from jax.sharding import PartitionSpec as P

loss_divisor = 64.0
F32 = jnp.float32
BF16 = jnp.bfloat16
VMEM_BYTES = 60 * 1024 * 1024


def dot(left, right, left_dim, right_dim):
    return lax.dot_general(
        left, right, (((left_dim,), (right_dim,)), ((), ())), preferred_element_type=F32
    )


def full(shape):
    return pl.BlockSpec(shape, lambda *_: (0,) * len(shape))


def params():
    return pltpu.CompilerParams(
        dimension_semantics=("arbitrary",), vmem_limit_bytes=VMEM_BYTES
    )


CHUNKS = 8


def permute(value, target_of):
    count = lax.axis_size("phi")
    return lax.ppermute(value, "phi", [(s, target_of(s) % count) for s in range(count)])


def direct_target(s):
    return s ^ 2


def relayed_target(s):
    return s + 2 if (s // 2) % 2 else s - 2


def sibling_target(s):
    return s ^ 1


def cross_target(s):
    return s + 1 if s % 2 else s - 1


def peers():
    count = lax.axis_size("phi")
    me = lax.axis_index("phi")
    odd_pair = (me // 2) % 2
    odd_core = me % 2
    direct = me + 2 - 4 * odd_pair
    sibling = me + 1 - 2 * odd_core
    stride = 4 - 8 * odd_pair
    onward = (me + stride + count) % count
    source = (me - stride + count) % count
    return direct, sibling, onward, source, odd_pair == odd_core


def remote(src, dst, send, recv, target):
    return pltpu.make_async_remote_copy(
        src_ref=src,
        dst_ref=dst,
        send_sem=send,
        recv_sem=recv,
        device_id={"phi": target},
        device_id_type=pl.DeviceIdType.MESH,
    )


def greet(targets):
    barrier = pltpu.get_barrier_semaphore()
    for target in targets:
        pl.semaphore_signal(
            barrier, inc=1, device_id={"phi": target}, device_id_type=pl.DeviceIdType.MESH
        )
    pl.semaphore_wait(barrier, len(targets))


def role_targets():
    count = lax.axis_size("phi")
    me = lax.axis_index("phi")
    odd_pair = (me // 2) % 2
    odd_core = me % 2
    sibling = me + 1 - 2 * odd_core
    across = (me - 1 + 2 * odd_core + count) % count
    direct = me + 2 - 4 * odd_pair
    far = (me - 2 + 4 * odd_pair + count) % count
    return sibling, across, direct, far


def exchange_kernel(own, keys, direct_out, relay_out, sib_out, cross_out, lists_out, *sems):
    ys, yr, zs, zr, cs, cr, ss, sr, ls, lr = sems
    direct, sibling, onward, source, direct_crosses = peers()
    size = own.shape[0] // CHUNKS
    roles = role_targets()
    greet((direct, sibling, source, roles[1], roles[3]))
    lists = [
        remote(keys, lists_out.at[j], ls.at[j], lr.at[j], target)
        for j, target in enumerate(roles)
    ]
    for copy in lists:
        copy.start()

    def part(ref, i):
        return ref.at[pl.ds(i * size, size)]

    first = [
        remote(part(own, i), part(direct_out, i), ys.at[i], yr.at[i], direct) for i in range(CHUNKS)
    ]
    second = [
        remote(part(direct_out, i), part(relay_out, i), zs.at[i], zr.at[i], onward)
        for i in range(CHUNKS)
    ]
    cross_a = [
        remote(part(direct_out, i), part(cross_out, i), cs.at[i], cr.at[i], sibling)
        for i in range(CHUNKS)
    ]
    cross_b = [
        remote(part(relay_out, i), part(cross_out, i), cs.at[i], cr.at[i], sibling)
        for i in range(CHUNKS)
    ]
    near = remote(own, sib_out, ss.at[0], sr.at[0], sibling)
    for copy in first:
        copy.start()
    near.start()
    for i in range(CHUNKS):
        first[i].wait_recv()
        second[i].start()

        @pl.when(direct_crosses)
        def _():
            cross_a[i].start()

    for i in range(CHUNKS):
        second[i].wait_recv()

        @pl.when(jnp.logical_not(direct_crosses))
        def _():
            cross_b[i].start()

    near.wait()
    for i in range(CHUNKS):
        first[i].wait_send()
        second[i].wait_send()
        cross_a[i].wait()
    for copy in lists:
        copy.wait()


def window_pieces(latents, keys):
    hits, width = latents.shape
    any_spec = pl.BlockSpec(memory_space=pl.ANY)
    direct, relayed, sibling, cross, lists = pl.pallas_call(
        exchange_kernel,
        in_specs=[any_spec] * 2,
        out_specs=[any_spec] * 5,
        out_shape=[jax.ShapeDtypeStruct((hits, width), BF16)] * 4
        + [jax.ShapeDtypeStruct((4,) + keys.shape, keys.dtype)],
        scratch_shapes=[pltpu.SemaphoreType.DMA((CHUNKS,))] * 6
        + [pltpu.SemaphoreType.DMA((1,))] * 2
        + [pltpu.SemaphoreType.DMA((4,))] * 2,
        compiler_params=pltpu.CompilerParams(collective_id=1, has_side_effects=True),
        name="exchange",
    )(latents, keys)
    return (direct, latents, relayed, sibling, cross), lists


def return_kernel(
    direct_ref,
    relay_ref,
    sib_ref,
    cross_ref,
    total_out,
    sib_out,
    cross_in,
    relay_send,
    relay_in,
    direct_send,
    *sems,
):
    ys, yr, zs, zr, cs, cr, ss, sr = sems
    direct, sibling, onward, source, to_direct = peers()
    size = direct_ref.shape[0] // CHUNKS
    greet((direct, sibling, onward))

    def rows(i):
        return pl.ds(i * size, size)

    crosses = [
        remote(cross_ref.at[rows(i)], cross_in.at[rows(i)], cs.at[i], cr.at[i], sibling)
        for i in range(CHUNKS)
    ]
    first = [
        remote(relay_send.at[rows(i)], relay_in.at[rows(i)], zs.at[i], zr.at[i], source)
        for i in range(CHUNKS)
    ]
    second = [
        remote(direct_send.at[rows(i)], total_out.at[rows(i)], ys.at[i], yr.at[i], direct)
        for i in range(CHUNKS)
    ]
    near = remote(sib_ref, sib_out, ss.at[0], sr.at[0], sibling)
    for copy in crosses:
        copy.start()
    near.start()
    for i in range(CHUNKS):
        crosses[i].wait_recv()
        extra = jnp.where(to_direct, 0.0, cross_in[rows(i), :].astype(F32))
        relay_send[rows(i), :] = (relay_ref[rows(i), :] + extra).astype(BF16)
        first[i].start()
    for i in range(CHUNKS):
        first[i].wait_recv()
        extra = jnp.where(to_direct, cross_in[rows(i), :].astype(F32), 0.0)
        direct_send[rows(i), :] = (
            direct_ref[rows(i), :] + extra + relay_in[rows(i), :].astype(F32)
        ).astype(BF16)
        second[i].start()
    near.wait()
    for i in range(CHUNKS):
        crosses[i].wait_send()
        first[i].wait_send()
        second[i].wait()


def return_pieces(direct, relayed, sibling, cross):
    shape = sibling.shape
    hits, width = math.prod(shape[:-1]), shape[-1]
    vmem = pl.BlockSpec(memory_space=pltpu.VMEM)
    half = jax.ShapeDtypeStruct((hits, width), BF16)
    total, sib = pl.pallas_call(
        return_kernel,
        in_specs=[vmem] * 4,
        out_specs=[vmem] * 2,
        out_shape=[half] * 2,
        scratch_shapes=[pltpu.VMEM((hits, width), BF16)] * 4
        + [pltpu.SemaphoreType.DMA((CHUNKS,))] * 6
        + [pltpu.SemaphoreType.DMA((1,))] * 2,
        compiler_params=pltpu.CompilerParams(
            collective_id=2, has_side_effects=True, vmem_limit_bytes=VMEM_BYTES
        ),
        name="give_back",
    )(*[piece.reshape(hits, width) for piece in (direct, relayed, sibling, cross)])
    return total.reshape(shape), sib.reshape(shape)


def sum_kernel(
    pairs, x_ref, out_ref, half_in, acc_ref, slots_in, all_ref, s0, r0, s1, r1, s2, r2, s3, r3
):
    me = lax.axis_index("phi")
    pair, core = me // 2, me % 2
    sibling = me + 1 - 2 * core
    half = x_ref.shape[0] // 2
    chunk = half // pairs
    others = [((pair + d) % pairs) * 2 + core for d in range(1, pairs)]
    greet([sibling] + others)

    def span(start, size):
        return pl.ds(pl.multiple_of(start, 8), size)

    swap = remote(x_ref.at[span((1 - core) * half, half)], half_in, s0.at[0], r0.at[0], sibling)
    swap.start()
    swap.wait()
    acc_ref[...] = x_ref[span(core * half, half), :] + half_in[...]
    scatter = [
        remote(
            acc_ref.at[span(((pair + d) % pairs) * chunk, chunk)],
            slots_in.at[d - 1],
            s1.at[d - 1],
            r1.at[d - 1],
            others[d - 1],
        )
        for d in range(1, pairs)
    ]
    for copy in scatter:
        copy.start()
    total = acc_ref[span(pair * chunk, chunk), :]
    for d in range(1, pairs):
        scatter[d - 1].wait_recv()
        total = total + slots_in[d - 1]
    mine = span(core * half + pair * chunk, chunk)
    all_ref[mine, :] = total
    gather = [
        remote(all_ref.at[mine], all_ref.at[mine], s2.at[d - 1], r2.at[d - 1], others[d - 1])
        for d in range(1, pairs)
    ]
    for copy in gather:
        copy.start()
    for copy in gather:
        copy.wait()
    for copy in scatter:
        copy.wait_send()
    whole = span(core * half, half)
    last = remote(all_ref.at[whole], all_ref.at[whole], s3.at[0], r3.at[0], sibling)
    last.start()
    last.wait()
    out_ref[...] = all_ref[...]


def sum_all(value):
    pairs = lax.axis_size("phi") // 2
    rows, width = value.shape
    chunk = -(-rows // (16 * pairs)) * 8
    total = 2 * pairs * chunk
    value = jnp.concatenate([value, jnp.zeros((total - rows, width), F32)], axis=0)
    vmem = pl.BlockSpec(memory_space=pltpu.VMEM)
    one = pltpu.SemaphoreType.DMA((1,))
    many = pltpu.SemaphoreType.DMA((pairs - 1,))
    return pl.pallas_call(
        functools.partial(sum_kernel, pairs),
        in_specs=[vmem],
        out_specs=vmem,
        out_shape=jax.ShapeDtypeStruct((total, width), F32),
        scratch_shapes=[
            pltpu.VMEM((total // 2, width), F32),
            pltpu.VMEM((total // 2, width), F32),
            pltpu.VMEM((pairs - 1, chunk, width), F32),
            pltpu.VMEM((total, width), F32),
            one, one, many, many, many, many, one, one,
        ],
        compiler_params=pltpu.CompilerParams(
            collective_id=3, has_side_effects=True, vmem_limit_bytes=VMEM_BYTES
        ),
        name="sum_all",
    )(value)


def aggregate_group(index_ref, tiles_ref, window_ref, step, group, slots, rows):
    results = []
    for g in range(group):
        tile = jnp.concatenate([tiles_ref[g, s] for s in range(slots)], axis=1)
        source = jnp.concatenate(
            [
                window_ref[
                    pl.ds(
                        pl.multiple_of(index_ref[(step * group + g) * slots + s] * rows, rows),
                        rows,
                    ),
                    :,
                ]
                for s in range(slots)
            ],
            axis=0,
        )
        results.append(dot(tile, source, 1, 0).astype(BF16))
    return jnp.concatenate(results, axis=0)


def node_update(own, aggregated, w_self, w_agg, w_out):
    activation = dot(own, w_self, 1, 0) + dot(aggregated, w_agg, 1, 0)
    hidden = jnp.maximum(activation, 0.0).astype(BF16)
    updated = (own.astype(F32) + dot(hidden, w_out, 1, 0)).astype(BF16)
    return hidden, updated


def first_forward(
    group,
    index_ref,
    tiles_ref,
    feats_ref,
    wcat_ref,
    w_self_ref,
    w_agg_ref,
    w_out_ref,
    before_ref,
    agg_ref,
    hidden_ref,
    updated_ref,
    window_ref,
):
    step = pl.program_id(0)
    slots, rows = tiles_ref.shape[1], tiles_ref.shape[2]
    span = group * rows
    total = feats_ref.shape[1]

    @pl.when(step == 0)
    def _():
        def encode(i, carry):
            at = pl.multiple_of(i * 512, 512)
            encoded = dot(feats_ref[:, pl.ds(at, 512)], wcat_ref[...], 0, 0)
            window_ref[pl.ds(at, 512), :] = jnp.tanh(encoded).astype(BF16)
            return carry

        lax.fori_loop(0, total // 512, encode, 0)
        window_ref[pl.ds(total, rows), :] = jnp.zeros((rows, window_ref.shape[1]), BF16)

    aggregated = aggregate_group(index_ref, tiles_ref, window_ref, step, group, slots, rows)
    own = window_ref[pl.ds(pl.multiple_of(total // 5 + step * span, span), span), :]
    hidden, updated = node_update(own, aggregated, w_self_ref[...], w_agg_ref[...], w_out_ref[...])
    before_ref[...] = own
    agg_ref[...] = aggregated
    hidden_ref[...] = hidden
    updated_ref[...] = updated


def later_forward(
    group,
    index_ref,
    tiles_ref,
    below_ref,
    own_ref,
    above_ref,
    sibling_ref,
    cross_ref,
    w_self_ref,
    w_agg_ref,
    w_out_ref,
    agg_ref,
    hidden_ref,
    updated_ref,
    window_ref,
    sems,
):
    step = pl.program_id(0)
    slots, rows = tiles_ref.shape[1], tiles_ref.shape[2]
    span = group * rows
    hits = own_ref.shape[0]

    @pl.when(step == 0)
    def _():
        copies = [
            pltpu.make_async_copy(piece, window_ref.at[pl.ds(k * hits, hits)], sems.at[k])
            for k, piece in enumerate((below_ref, own_ref, above_ref, sibling_ref, cross_ref))
        ]
        for copy in copies:
            copy.start()
        window_ref[pl.ds(5 * hits, rows), :] = jnp.zeros((rows, window_ref.shape[1]), BF16)
        for copy in copies:
            copy.wait()

    aggregated = aggregate_group(index_ref, tiles_ref, window_ref, step, group, slots, rows)
    own = window_ref[pl.ds(pl.multiple_of(hits + step * span, span), span), :]
    hidden, updated = node_update(own, aggregated, w_self_ref[...], w_agg_ref[...], w_out_ref[...])
    agg_ref[...] = aggregated
    hidden_ref[...] = hidden
    updated_ref[...] = updated.astype(F32)


def gather_kernel(list_ref, bound_ref, anchor_ref, z_ref, *refs):
    outs, (anchor_out, buf_ref) = refs[:5], refs[5:]
    triplets, width = anchor_out.shape
    hits = z_ref.shape[0]
    stride = list_ref.shape[0] // 5

    def anchors(i, carry):
        at = pl.multiple_of(i * 8, 8)
        anchor_out[pl.ds(at, 8), :] = jnp.concatenate(
            [z_ref[pl.ds(anchor_ref[i * 8 + u], 1), :] for u in range(8)], axis=0
        )
        return carry

    lax.fori_loop(0, triplets // 8, anchors, 0)
    zeros = jnp.zeros((64, width), F32)

    def clear(i, carry):
        buf_ref[pl.ds(pl.multiple_of(i * 64, 64), 64), :] = zeros
        return carry

    for j in range(5):
        lax.fori_loop(0, 2 * triplets // 64, clear, 0)
        start, end = bound_ref[2 * j], bound_ref[2 * j + 1]

        def fetch(i, carry, j=j, start=start, end=end):
            for u in range(8):
                key = list_ref[j * stride + jnp.minimum(start + i * 8 + u, end - 1)]
                row = lax.rem(lax.div(key, 2 * triplets), hits)
                buf_ref[pl.ds(lax.rem(key, 2 * triplets), 1), :] = z_ref[pl.ds(row, 1), :]
            return carry

        lax.fori_loop(0, lax.div(end - start + 7, 8), fetch, 0)

        def subtract(i, carry, j=j):
            at = pl.multiple_of(i * 64, 64)
            value = buf_ref[pl.ds(triplets + at, 64), :] - buf_ref[pl.ds(at, 64), :]
            outs[j][pl.ds(at, 64), :] = value.astype(BF16)
            return carry

        lax.fori_loop(0, triplets // 64, subtract, 0)


PARTS = 4


def contrast_kernel(
    inv_root,
    self_ref,
    sib_ref,
    cross_ref,
    near_ref,
    far_ref,
    anchor_ref,
    loss_ref,
    ganchor_ref,
    mown_ref,
    msib_ref,
    mcross_ref,
    mdirect_ref,
    mfar_ref,
    sib_in,
    cross_in,
    far_send,
    far_in,
    near_send,
    near_in,
    *sems,
):
    s = [sems[2 * i : 2 * i + 2] for i in range(8)]
    direct, sibling, onward, source, near_adds = peers()
    size = anchor_ref.shape[0] // PARTS
    greet((direct, sibling, onward, source))

    def rows(i):
        return pl.ds(i * size, size)

    def copies(k, src, dst, target):
        return [
            remote(src.at[rows(i)], dst.at[rows(i)], s[k][0].at[i], s[k][1].at[i], target)
            for i in range(PARTS)
        ]

    crosses = copies(0, cross_ref, cross_in, sibling)
    sibs = copies(1, sib_ref, sib_in, sibling)
    hops = copies(2, far_send, far_in, source)
    nears = copies(3, near_send, near_in, direct)
    to_direct = copies(4, mown_ref, mdirect_ref, direct)
    to_sibling = copies(5, mown_ref, msib_ref, sibling)
    relays = copies(6, mdirect_ref, mfar_ref, onward)
    cross_a = copies(7, mdirect_ref, mcross_ref, sibling)
    cross_b = copies(7, mfar_ref, mcross_ref, sibling)
    for copy in crosses:
        copy.start()
    for copy in sibs:
        copy.start()
    for i in range(PARTS):
        crosses[i].wait_recv()
        extra = jnp.where(near_adds, 0.0, cross_in[rows(i), :].astype(F32))
        far_send[rows(i), :] = (far_ref[rows(i), :].astype(F32) + extra).astype(BF16)
        hops[i].start()
    for i in range(PARTS):
        hops[i].wait_recv()
        extra = jnp.where(near_adds, cross_in[rows(i), :].astype(F32), 0.0)
        near_send[rows(i), :] = (
            near_ref[rows(i), :].astype(F32) + extra + far_in[rows(i), :].astype(F32)
        ).astype(BF16)
        nears[i].start()
    total = jnp.zeros((1, 1), F32)
    for i in range(PARTS):
        sibs[i].wait_recv()
        nears[i].wait_recv()
        change = (
            near_in[rows(i), :].astype(F32)
            + self_ref[rows(i), :].astype(F32)
            + sib_in[rows(i), :].astype(F32)
        )
        anchor = anchor_ref[rows(i), :]
        gap = jnp.sum(anchor * change, axis=1, keepdims=True) * inv_root
        soft = jnp.maximum(gap, 0.0) + jnp.log1p(jnp.exp(-jnp.abs(gap)))
        coef = jax.nn.sigmoid(gap) * (inv_root / loss_divisor)
        mown_ref[rows(i), :] = (coef * anchor).astype(BF16)
        to_direct[i].start()
        to_sibling[i].start()
        ganchor_ref[rows(i), :] = coef * change
        total = total + jnp.sum(soft, axis=0, keepdims=True)
    loss_ref[...] = jnp.broadcast_to(total, loss_ref.shape)
    for i in range(PARTS):
        to_direct[i].wait_recv()
        relays[i].start()

        @pl.when(near_adds)
        def _():
            cross_a[i].start()

    for i in range(PARTS):
        relays[i].wait_recv()

        @pl.when(jnp.logical_not(near_adds))
        def _():
            cross_b[i].start()

    for i in range(PARTS):
        crosses[i].wait_send()
        sibs[i].wait_send()
        hops[i].wait_send()
        nears[i].wait_send()
        to_direct[i].wait_send()
        to_sibling[i].wait()
        relays[i].wait_send()
        cross_a[i].wait()


def node_backward(
    gradient, hidden_ref, before_ref, agg_ref, w_out, gout_ref, gself_ref, gagg_ref, step
):
    upstream = gradient.astype(BF16)
    hidden = hidden_ref[...]
    hidden_grad = dot(upstream, w_out, 1, 1)
    act_grad = jnp.where(hidden.astype(F32) > 0, hidden_grad, 0.0).astype(BF16)

    @pl.when(step == 0)
    def _():
        gout_ref[...] = jnp.zeros(gout_ref.shape, F32)
        gself_ref[...] = jnp.zeros(gself_ref.shape, F32)
        gagg_ref[...] = jnp.zeros(gagg_ref.shape, F32)

    gout_ref[...] += dot(hidden, upstream, 0, 0)
    gself_ref[...] += dot(before_ref[...], act_grad, 0, 0)
    gagg_ref[...] += dot(agg_ref[...], act_grad, 0, 0)
    return act_grad


def spread_group(index_ref, tiles_ref, adj_ref, agg_grad_t, step, group, slots, rows):
    for g in range(group):
        tile = jnp.concatenate([tiles_ref[g, s] for s in range(slots)], axis=1)
        contrib = dot(agg_grad_t[:, g * rows : (g + 1) * rows], tile, 1, 0)
        for s in range(slots):
            at = index_ref[(step * group + g) * slots + s]
            adj_ref[at] = adj_ref[at] + contrib[:, s * rows : (s + 1) * rows]


def clear_blocks(adj_ref):
    def clear(i, carry):
        adj_ref[i] = jnp.zeros(adj_ref.shape[1:], F32)
        return carry

    lax.fori_loop(0, adj_ref.shape[0], clear, 0)


def scatter_rows(list_ref, bound_ref, anchor_ref, ganchor_ref, moves, moved_ref, sums):
    triplets, width = ganchor_ref.shape
    hits = sums[0].shape[0] - 8
    stride = list_ref.shape[0] // 5
    zeros = jnp.zeros((64, width), F32)

    def clear(i, carry):
        for target in sums:
            target[pl.ds(pl.multiple_of(i * 64, 64), 64), :] = zeros
        return carry

    lax.fori_loop(0, hits // 64, clear, 0)
    for j, source in enumerate(moves):

        def widen(i, carry, j=j, source=source):
            at = pl.multiple_of(i * 64, 64)
            value = source[pl.ds(at, 64), :].astype(F32)
            moved_ref[pl.ds(2 * j * triplets + at, 64), :] = -value
            moved_ref[pl.ds((2 * j + 1) * triplets + at, 64), :] = value
            return carry

        lax.fori_loop(0, triplets // 64, widen, 0)

    def anchors(i, carry):
        for u in range(8):
            t = i * 8 + u
            here = pl.ds(anchor_ref[t], 1)
            target = sums[u % 4]
            target[here, :] = target[here, :] + ganchor_ref[pl.ds(t, 1), :]
        return carry

    lax.fori_loop(0, triplets // 8, anchors, 0)
    for j in range(5):
        start, end = bound_ref[2 * j], bound_ref[2 * j + 1]

        def add(i, carry, j=j, start=start, end=end):
            for u in range(8):
                at = start + i * 8 + u
                key = list_ref[j * stride + jnp.minimum(at, end - 1)]
                row = lax.rem(lax.div(key, 2 * triplets), hits)
                here = pl.ds(jnp.where(at < end, row, hits), 1)
                target = sums[u % 4]
                moved = moved_ref[pl.ds(2 * j * triplets + lax.rem(key, 2 * triplets), 1), :]
                target[here, :] = target[here, :] + moved
            return carry

        lax.fori_loop(0, lax.div(end - start + 7, 8), add, 0)


def last_backward(
    group,
    steps,
    index_ref,
    list_ref,
    bound_ref,
    anchor_ref,
    tiles_ref,
    ganchor_ref,
    mself_ref,
    msib_ref,
    mcross_ref,
    mdirect_ref,
    mfar_ref,
    hidden_ref,
    before_ref,
    agg_ref,
    w_self_ref,
    w_agg_ref,
    w_out_ref,
    gout_ref,
    gself_ref,
    gagg_ref,
    direct_ref,
    obelow_ref,
    oown_ref,
    oabove_ref,
    osibling_ref,
    ocross_ref,
    adj_ref,
    moved_ref,
    *sums,
):
    step = pl.program_id(0)
    slots, rows = tiles_ref.shape[1], tiles_ref.shape[2]
    span = group * rows

    @pl.when(step == 0)
    def _():
        clear_blocks(adj_ref)
        scatter_rows(
            list_ref, bound_ref, anchor_ref, ganchor_ref,
            (mself_ref, msib_ref, mcross_ref, mdirect_ref, mfar_ref), moved_ref, sums,
        )

    here = pl.ds(pl.multiple_of(step * span, span), span)
    gradient = (sums[0][here, :] + sums[1][here, :]) + (sums[2][here, :] + sums[3][here, :])
    act_grad = node_backward(
        gradient, hidden_ref, before_ref, agg_ref, w_out_ref[...], gout_ref, gself_ref, gagg_ref, step
    )
    direct_ref[...] = gradient + dot(act_grad, w_self_ref[...], 1, 1)
    agg_grad_t = dot(w_agg_ref[...], act_grad, 1, 1).astype(BF16)
    spread_group(index_ref, tiles_ref, adj_ref, agg_grad_t, step, group, slots, rows)

    @pl.when(step == steps - 1)
    def _():
        blocks = oown_ref.shape[0]
        for k, target in enumerate((obelow_ref, oown_ref, oabove_ref, osibling_ref, ocross_ref)):

            def store(i, carry, k=k, target=target):
                target[i] = adj_ref[k * blocks + i].astype(target.dtype)
                return carry

            lax.fori_loop(0, blocks, store, 0)


def first_backward(
    group,
    steps,
    index_ref,
    tiles_ref,
    direct_ref,
    own_ref,
    total_ref,
    sib_ref,
    hidden_ref,
    before_ref,
    agg_ref,
    w_self_ref,
    w_agg_ref,
    w_out_ref,
    feats_ref,
    wcat_ref,
    wcat_t_ref,
    gout_ref,
    gself_ref,
    gagg_ref,
    genc_ref,
    adj_ref,
):
    step = pl.program_id(0)
    slots, rows = tiles_ref.shape[1], tiles_ref.shape[2]
    span = group * rows
    total = feats_ref.shape[1]

    @pl.when(step == 0)
    def _():
        clear_blocks(adj_ref)
        genc_ref[...] = jnp.zeros(genc_ref.shape, F32)

    pieces = []
    for g in range(group):
        returned = own_ref[g] + (
            total_ref[g].astype(F32) + sib_ref[g].astype(F32)
        )
        pieces.append(returned.T)
    gradient = direct_ref[...] + jnp.concatenate(pieces, axis=0)
    act_grad = node_backward(
        gradient, hidden_ref, before_ref, agg_ref, w_out_ref[...], gout_ref, gself_ref, gagg_ref, step
    )
    direct = gradient + dot(act_grad, w_self_ref[...], 1, 1)
    here = feats_ref[:, pl.ds(pl.multiple_of(total // 5 + step * span, span), span)]
    squashed = jnp.tanh(dot(here, wcat_ref[...], 0, 0))
    genc_ref[...] += dot(here, (direct * (1.0 - squashed * squashed)).astype(BF16), 1, 0)
    agg_grad_t = dot(w_agg_ref[...], act_grad, 1, 1).astype(BF16)
    spread_group(index_ref, tiles_ref, adj_ref, agg_grad_t, step, group, slots, rows)

    @pl.when(step == steps - 1)
    def _():
        per = 4

        def encode(i, carry):
            at = pl.multiple_of(i * (per * rows), per * rows)
            feats = feats_ref[:, pl.ds(at, per * rows)]
            squashed_t = jnp.tanh(dot(wcat_t_ref[...], feats, 1, 0))
            grad_t = jnp.concatenate([adj_ref[i * per + u] for u in range(per)], axis=1)
            grad_t = (grad_t * (1.0 - squashed_t * squashed_t)).astype(BF16)
            return carry + dot(feats, grad_t, 1, 1)

        genc_ref[...] += lax.fori_loop(
            0, total // (per * rows), encode, jnp.zeros(genc_ref.shape, F32)
        )


def body(
    hit_feats,
    layer_ids,
    edge_tiles,
    src_blocks,
    live_slots,
    anchor_hits,
    positive_hits,
    negative_hits,
    w_enc,
    layer_table,
    w_self,
    w_agg,
    w_out,
):
    blocks, slots, rows, _ = edge_tiles.shape
    width = w_enc.shape[1]
    features = hit_feats.shape[0]
    kinds = layer_table.shape[0]
    hits = blocks * rows
    layer_total = w_self.shape[0]
    triplets = anchor_hits.shape[0]
    group = 4
    steps = blocks // group
    span = group * rows
    me = lax.axis_index("phi")
    is_even = me % 2 == 0
    even_pair = (me // 2) % 2 == 0

    def place(part):
        spots = (
            jnp.where(even_pair, 2, 0),
            jnp.where(is_even, 4, 3),
            1,
            jnp.where(is_even, 3, 4),
            jnp.where(even_pair, 0, 2),
        )
        return sum(jnp.where(part == k, spot, 0) for k, spot in enumerate(spots))

    live = jnp.arange(slots, dtype=jnp.int32)[None, :] < live_slots[:, None]
    index = jnp.where(
        live, place(src_blocks // blocks) * blocks + src_blocks % blocks, 5 * blocks
    ).reshape(blocks * slots)
    order = jnp.arange(triplets, dtype=jnp.int32)
    keys = jnp.concatenate(
        [positive_hits * (2 * triplets) + order, negative_hits * (2 * triplets) + triplets + order]
    )
    ranks = jnp.sum((keys[None, :] < keys[:, None]).astype(jnp.int32), axis=1)
    places = jnp.arange(2 * triplets, dtype=jnp.int32)
    ordered = jnp.sum(jnp.where(ranks[None, :] == places[:, None], keys[None, :], 0), axis=1)
    edges = jnp.arange(128, dtype=jnp.int32) * (hits * 2 * triplets)
    starts = jnp.sum((keys[None, :] < edges[:8, None]).astype(jnp.int32), axis=1)
    listed = 2 * triplets // 128
    starts = jnp.pad(starts.reshape(1, 8), ((0, 7), (0, 120)))
    keys = jnp.concatenate([ordered.reshape(listed, 128), starts], axis=0)

    pad = -(features + 1) % 16
    packed = jnp.concatenate(
        [hit_feats, layer_ids.astype(BF16)[None, :], jnp.zeros((pad, hits), BF16)], axis=0
    )
    packed = jnp.concatenate(
        [
            permute(packed, direct_target),
            packed,
            permute(packed, relayed_target),
            permute(packed, sibling_target),
            permute(packed, cross_target),
        ],
        axis=1,
    )
    feature_pad = -features % 16
    onehot = (
        jnp.arange(kinds, dtype=jnp.int32)[:, None].astype(BF16) == packed[features][None, :]
    ).astype(BF16)
    feats = jnp.concatenate(
        [packed[:features], jnp.zeros((feature_pad, 5 * hits), BF16), onehot], axis=0
    )
    wcat = jnp.concatenate([w_enc, jnp.zeros((feature_pad, width), BF16), layer_table], axis=0)
    depth = wcat.shape[0]

    tile_spec = pl.BlockSpec((group, slots, rows, rows), lambda i, *_: (i, 0, 0, 0))
    row_spec = pl.BlockSpec((span, width), lambda i, *_: (i, 0))
    block_spec = pl.BlockSpec((group, width, rows), lambda i, *_: (i, 0, 0))
    weight_spec = full((width, width))
    any_spec = pl.BlockSpec(memory_space=pl.ANY)
    row_shape = jax.ShapeDtypeStruct((hits, width), BF16)
    weight_shape = jax.ShapeDtypeStruct((width, width), F32)

    before0, agg0, hidden0, latents = pl.pallas_call(
        functools.partial(first_forward, group),
        grid_spec=pltpu.PrefetchScalarGridSpec(
            num_scalar_prefetch=1,
            grid=(steps,),
            in_specs=[tile_spec, full((depth, 5 * hits)), full((depth, width))] + [weight_spec] * 3,
            out_specs=[row_spec] * 4,
            scratch_shapes=[pltpu.VMEM((5 * hits + rows, width), BF16)],
        ),
        out_shape=[row_shape] * 4,
        compiler_params=params(),
        name="first_forward",
    )(index, edge_tiles, feats, wcat, w_self[0], w_agg[0], w_out[0])
    wide_shape = jax.ShapeDtypeStruct((hits, width), F32)
    pieces, lists = window_pieces(latents, keys)
    latents1 = latents
    agg1, hidden1, latents2 = pl.pallas_call(
        functools.partial(later_forward, group),
        grid_spec=pltpu.PrefetchScalarGridSpec(
            num_scalar_prefetch=1,
            grid=(steps,),
            in_specs=[tile_spec] + [any_spec] * 5 + [weight_spec] * 3,
            out_specs=[row_spec] * 3,
            scratch_shapes=[
                pltpu.VMEM((5 * hits + rows, width), BF16),
                pltpu.SemaphoreType.DMA((5,)),
            ],
        ),
        out_shape=[row_shape] * 2 + [wide_shape],
        compiler_params=params(),
        name="later_forward",
    )(index, edge_tiles, *pieces, w_self[1], w_agg[1], w_out[1])

    lists = jnp.concatenate([keys[None], lists], axis=0)
    odd_core, odd_pair = me % 2, (me // 2) % 2
    bounds = []
    for j, k in enumerate(
        (2, 1 + 2 * odd_core, 3 - 2 * odd_core, 4 * odd_pair, 4 - 4 * odd_pair)
    ):
        bounds.append(lax.dynamic_slice(lists[j, listed], (k,), (2,)))
    bounds = jnp.concatenate(bounds)
    lists = lists[:, :listed].reshape(-1)
    move_shape = jax.ShapeDtypeStruct((triplets, width), BF16)
    wide_move = jax.ShapeDtypeStruct((triplets, width), F32)
    move_spec = full((triplets, width))
    *found, anchors = pl.pallas_call(
        gather_kernel,
        grid_spec=pltpu.PrefetchScalarGridSpec(
            num_scalar_prefetch=3,
            grid=(1,),
            in_specs=[full((hits, width))],
            out_specs=[move_spec] * 6,
            scratch_shapes=[pltpu.VMEM((2 * triplets, width), F32)],
        ),
        out_shape=[move_shape] * 5 + [wide_move],
        compiler_params=params(),
        name="gather",
    )(lists, bounds, anchor_hits, latents2)
    vmem = pl.BlockSpec(memory_space=pltpu.VMEM)
    loss_part, ganchor, *moves = pl.pallas_call(
        functools.partial(contrast_kernel, 1.0 / math.sqrt(width)),
        in_specs=[vmem] * 6,
        out_specs=[vmem] * 7,
        out_shape=[jax.ShapeDtypeStruct((8, width), F32), wide_move] + [move_shape] * 5,
        scratch_shapes=[pltpu.VMEM((triplets, width), BF16)] * 6
        + [pltpu.SemaphoreType.DMA((PARTS,))] * 16,
        compiler_params=pltpu.CompilerParams(
            collective_id=4, has_side_effects=True, vmem_limit_bytes=VMEM_BYTES
        ),
        name="contrast",
    )(*found, anchors)

    t_shape = jax.ShapeDtypeStruct((blocks, width, rows), F32)
    t_half = jax.ShapeDtypeStruct((blocks, width, rows), BF16)
    t_full = pl.BlockSpec(
        (blocks, width, rows), lambda *_: (0, 0, 0), pipeline_mode=pl.Buffered(1)
    )
    adj_shape = pltpu.VMEM((5 * blocks + 1, width, rows), F32)
    gout1, gself1, gagg1, direct, obelow, own, oabove, osibling, ocross = pl.pallas_call(
        functools.partial(last_backward, group, steps),
        grid_spec=pltpu.PrefetchScalarGridSpec(
            num_scalar_prefetch=4,
            grid=(steps,),
            in_specs=[tile_spec] + [move_spec] * 6 + [row_spec] * 3 + [weight_spec] * 3,
            out_specs=[weight_spec] * 3 + [row_spec] + [t_full] * 5,
            scratch_shapes=[adj_shape, pltpu.VMEM((10 * triplets, width), F32)]
            + [pltpu.VMEM((hits + 8, width), F32)] * 4,
        ),
        out_shape=[weight_shape] * 3 + [wide_shape] + [t_shape] * 3 + [t_half] * 2,
        compiler_params=params(),
        name="last_backward",
    )(
        index, lists, bounds, anchor_hits, edge_tiles, ganchor, *moves, hidden1, latents1, agg1,
        w_self[1], w_agg[1], w_out[1],
    )
    total, sib = return_pieces(obelow, oabove, osibling, ocross)
    gout0, gself0, gagg0, genc = pl.pallas_call(
        functools.partial(first_backward, group, steps),
        grid_spec=pltpu.PrefetchScalarGridSpec(
            num_scalar_prefetch=1,
            grid=(steps,),
            in_specs=[tile_spec, row_spec]
            + [block_spec] * 3
            + [row_spec] * 3
            + [weight_spec] * 3
            + [full((depth, 5 * hits)), full((depth, width)), full((width, depth))],
            out_specs=[weight_spec] * 3 + [full((depth, width))],
            scratch_shapes=[adj_shape],
        ),
        out_shape=[weight_shape] * 3 + [jax.ShapeDtypeStruct((depth, width), F32)],
        compiler_params=params(),
        name="first_backward",
    )(
        index, edge_tiles, direct, own, total, sib, hidden0, before0, agg0,
        w_self[0], w_agg[0], w_out[0], feats, wcat, wcat.T,
    )
    late = sum_all(
        jnp.concatenate([gout0, gout1, gself0, gself1, gagg0, gagg1, genc, loss_part], axis=0)
    )

    triplet_total = triplets * lax.axis_size("phi")
    base = 6 * width
    loss = (late[base + depth, 0] / triplet_total).reshape(1)
    grad_enc = late[base : base + features]
    grad_table = late[base + depth - kinds : base + depth]

    def pair(k):
        return late[2 * k * width : 2 * (k + 1) * width].reshape(layer_total, width, width)

    return (loss, grad_enc, grad_table, pair(1), pair(2), pair(0))


def solution(mesh):
    both = ("event", "phi")
    in_specs = (
        P(None, both),
        P(both),
        P(both, None, None, None),
        P(both, None),
        P(both),
        P(both),
        P(both),
        P(both),
        P(),
        P(),
        P(),
        P(),
        P(),
    )
    out_specs = (
        P("event"),
        P("event", None),
        P("event", None),
        P("event", None, None),
        P("event", None, None),
        P("event", None, None),
    )
    return jax.shard_map(body, mesh=mesh, in_specs=in_specs, out_specs=out_specs, check_vma=False)
```

```python
import functools
import math

import jax
import jax.numpy as jnp
from jax import lax
from jax.experimental import pallas as pl
from jax.experimental.pallas import tpu as pltpu
from jax.sharding import PartitionSpec as P

loss_divisor = 64.0
F32 = jnp.float32
BF16 = jnp.bfloat16
VMEM_BYTES = 60 * 1024 * 1024


def dot(left, right, left_dim, right_dim):
    return lax.dot_general(
        left, right, (((left_dim,), (right_dim,)), ((), ())), preferred_element_type=F32
    )


def full(shape):
    return pl.BlockSpec(shape, lambda *_: (0,) * len(shape))


def params():
    return pltpu.CompilerParams(
        dimension_semantics=("arbitrary",), vmem_limit_bytes=VMEM_BYTES
    )


CHUNKS = 8


def permute(value, target_of):
    count = lax.axis_size("phi")
    return lax.ppermute(value, "phi", [(s, target_of(s) % count) for s in range(count)])


def direct_target(s):
    return s ^ 2


def relayed_target(s):
    return s + 2 if (s // 2) % 2 else s - 2


def sibling_target(s):
    return s ^ 1


def cross_target(s):
    return s + 1 if s % 2 else s - 1


def peers():
    count = lax.axis_size("phi")
    me = lax.axis_index("phi")
    odd_pair = (me // 2) % 2
    odd_core = me % 2
    direct = me + 2 - 4 * odd_pair
    sibling = me + 1 - 2 * odd_core
    stride = 4 - 8 * odd_pair
    onward = (me + stride + count) % count
    source = (me - stride + count) % count
    return direct, sibling, onward, source, odd_pair == odd_core


def remote(src, dst, send, recv, target):
    return pltpu.make_async_remote_copy(
        src_ref=src,
        dst_ref=dst,
        send_sem=send,
        recv_sem=recv,
        device_id={"phi": target},
        device_id_type=pl.DeviceIdType.MESH,
    )


def greet(targets):
    barrier = pltpu.get_barrier_semaphore()
    for target in targets:
        pl.semaphore_signal(
            barrier, inc=1, device_id={"phi": target}, device_id_type=pl.DeviceIdType.MESH
        )
    pl.semaphore_wait(barrier, len(targets))


def role_targets():
    count = lax.axis_size("phi")
    me = lax.axis_index("phi")
    odd_pair = (me // 2) % 2
    odd_core = me % 2
    sibling = me + 1 - 2 * odd_core
    across = (me - 1 + 2 * odd_core + count) % count
    direct = me + 2 - 4 * odd_pair
    far = (me - 2 + 4 * odd_pair + count) % count
    return sibling, across, direct, far


def exchange_kernel(own, keys, direct_out, relay_out, sib_out, cross_out, lists_out, *sems):
    ys, yr, zs, zr, cs, cr, ss, sr, ls, lr = sems
    direct, sibling, onward, source, direct_crosses = peers()
    size = own.shape[0] // CHUNKS
    roles = role_targets()
    greet((direct, sibling, source, roles[1], roles[3]))
    lists = [
        remote(keys, lists_out.at[j], ls.at[j], lr.at[j], target)
        for j, target in enumerate(roles)
    ]
    for copy in lists:
        copy.start()

    def part(ref, i):
        return ref.at[pl.ds(i * size, size)]

    first = [
        remote(part(own, i), part(direct_out, i), ys.at[i], yr.at[i], direct) for i in range(CHUNKS)
    ]
    second = [
        remote(part(direct_out, i), part(relay_out, i), zs.at[i], zr.at[i], onward)
        for i in range(CHUNKS)
    ]
    cross_a = [
        remote(part(direct_out, i), part(cross_out, i), cs.at[i], cr.at[i], sibling)
        for i in range(CHUNKS)
    ]
    cross_b = [
        remote(part(relay_out, i), part(cross_out, i), cs.at[i], cr.at[i], sibling)
        for i in range(CHUNKS)
    ]
    near = remote(own, sib_out, ss.at[0], sr.at[0], sibling)
    for copy in first:
        copy.start()
    near.start()
    for i in range(CHUNKS):
        first[i].wait_recv()
        second[i].start()

        @pl.when(direct_crosses)
        def _():
            cross_a[i].start()

    for i in range(CHUNKS):
        second[i].wait_recv()

        @pl.when(jnp.logical_not(direct_crosses))
        def _():
            cross_b[i].start()

    near.wait()
    for i in range(CHUNKS):
        first[i].wait_send()
        second[i].wait_send()
        cross_a[i].wait()
    for copy in lists:
        copy.wait()


def window_pieces(latents, keys):
    hits, width = latents.shape
    any_spec = pl.BlockSpec(memory_space=pl.ANY)
    direct, relayed, sibling, cross, lists = pl.pallas_call(
        exchange_kernel,
        in_specs=[any_spec] * 2,
        out_specs=[any_spec] * 5,
        out_shape=[jax.ShapeDtypeStruct((hits, width), BF16)] * 4
        + [jax.ShapeDtypeStruct((4,) + keys.shape, keys.dtype)],
        scratch_shapes=[pltpu.SemaphoreType.DMA((CHUNKS,))] * 6
        + [pltpu.SemaphoreType.DMA((1,))] * 2
        + [pltpu.SemaphoreType.DMA((4,))] * 2,
        compiler_params=pltpu.CompilerParams(collective_id=1, has_side_effects=True),
        name="exchange",
    )(latents, keys)
    return (direct, latents, relayed, sibling, cross), lists


def return_kernel(
    direct_ref,
    relay_ref,
    sib_ref,
    cross_ref,
    total_out,
    sib_out,
    cross_in,
    relay_send,
    relay_in,
    direct_send,
    *sems,
):
    ys, yr, zs, zr, cs, cr, ss, sr = sems
    direct, sibling, onward, source, to_direct = peers()
    size = direct_ref.shape[0] // CHUNKS
    greet((direct, sibling, onward))

    def rows(i):
        return pl.ds(i * size, size)

    crosses = [
        remote(cross_ref.at[rows(i)], cross_in.at[rows(i)], cs.at[i], cr.at[i], sibling)
        for i in range(CHUNKS)
    ]
    first = [
        remote(relay_send.at[rows(i)], relay_in.at[rows(i)], zs.at[i], zr.at[i], source)
        for i in range(CHUNKS)
    ]
    second = [
        remote(direct_send.at[rows(i)], total_out.at[rows(i)], ys.at[i], yr.at[i], direct)
        for i in range(CHUNKS)
    ]
    near = remote(sib_ref, sib_out, ss.at[0], sr.at[0], sibling)
    for copy in crosses:
        copy.start()
    near.start()
    for i in range(CHUNKS):
        crosses[i].wait_recv()
        extra = jnp.where(to_direct, 0.0, cross_in[rows(i), :].astype(F32))
        relay_send[rows(i), :] = (relay_ref[rows(i), :] + extra).astype(BF16)
        first[i].start()
    for i in range(CHUNKS):
        first[i].wait_recv()
        extra = jnp.where(to_direct, cross_in[rows(i), :].astype(F32), 0.0)
        direct_send[rows(i), :] = (
            direct_ref[rows(i), :] + extra + relay_in[rows(i), :].astype(F32)
        ).astype(BF16)
        second[i].start()
    near.wait()
    for i in range(CHUNKS):
        crosses[i].wait_send()
        first[i].wait_send()
        second[i].wait()


def return_pieces(direct, relayed, sibling, cross):
    shape = sibling.shape
    hits, width = math.prod(shape[:-1]), shape[-1]
    vmem = pl.BlockSpec(memory_space=pltpu.VMEM)
    half = jax.ShapeDtypeStruct((hits, width), BF16)
    total, sib = pl.pallas_call(
        return_kernel,
        in_specs=[vmem] * 4,
        out_specs=[vmem] * 2,
        out_shape=[half] * 2,
        scratch_shapes=[pltpu.VMEM((hits, width), BF16)] * 4
        + [pltpu.SemaphoreType.DMA((CHUNKS,))] * 6
        + [pltpu.SemaphoreType.DMA((1,))] * 2,
        compiler_params=pltpu.CompilerParams(
            collective_id=2, has_side_effects=True, vmem_limit_bytes=VMEM_BYTES
        ),
        name="give_back",
    )(*[piece.reshape(hits, width) for piece in (direct, relayed, sibling, cross)])
    return total.reshape(shape), sib.reshape(shape)


def sum_kernel(
    pairs, x_ref, out_ref, half_in, acc_ref, slots_in, all_ref, s0, r0, s1, r1, s2, r2, s3, r3
):
    me = lax.axis_index("phi")
    pair, core = me // 2, me % 2
    sibling = me + 1 - 2 * core
    half = x_ref.shape[0] // 2
    chunk = half // pairs
    others = [((pair + d) % pairs) * 2 + core for d in range(1, pairs)]
    greet([sibling] + others)

    def span(start, size):
        return pl.ds(pl.multiple_of(start, 8), size)

    swap = remote(x_ref.at[span((1 - core) * half, half)], half_in, s0.at[0], r0.at[0], sibling)
    swap.start()
    swap.wait()
    acc_ref[...] = x_ref[span(core * half, half), :] + half_in[...]
    scatter = [
        remote(
            acc_ref.at[span(((pair + d) % pairs) * chunk, chunk)],
            slots_in.at[d - 1],
            s1.at[d - 1],
            r1.at[d - 1],
            others[d - 1],
        )
        for d in range(1, pairs)
    ]
    for copy in scatter:
        copy.start()
    total = acc_ref[span(pair * chunk, chunk), :]
    for d in range(1, pairs):
        scatter[d - 1].wait_recv()
        total = total + slots_in[d - 1]
    mine = span(core * half + pair * chunk, chunk)
    all_ref[mine, :] = total
    gather = [
        remote(all_ref.at[mine], all_ref.at[mine], s2.at[d - 1], r2.at[d - 1], others[d - 1])
        for d in range(1, pairs)
    ]
    for copy in gather:
        copy.start()
    for copy in gather:
        copy.wait()
    for copy in scatter:
        copy.wait_send()
    whole = span(core * half, half)
    last = remote(all_ref.at[whole], all_ref.at[whole], s3.at[0], r3.at[0], sibling)
    last.start()
    last.wait()
    out_ref[...] = all_ref[...]


def sum_all(value):
    pairs = lax.axis_size("phi") // 2
    rows, width = value.shape
    chunk = -(-rows // (16 * pairs)) * 8
    total = 2 * pairs * chunk
    value = jnp.concatenate([value, jnp.zeros((total - rows, width), F32)], axis=0)
    vmem = pl.BlockSpec(memory_space=pltpu.VMEM)
    one = pltpu.SemaphoreType.DMA((1,))
    many = pltpu.SemaphoreType.DMA((pairs - 1,))
    return pl.pallas_call(
        functools.partial(sum_kernel, pairs),
        in_specs=[vmem],
        out_specs=vmem,
        out_shape=jax.ShapeDtypeStruct((total, width), F32),
        scratch_shapes=[
            pltpu.VMEM((total // 2, width), F32),
            pltpu.VMEM((total // 2, width), F32),
            pltpu.VMEM((pairs - 1, chunk, width), F32),
            pltpu.VMEM((total, width), F32),
            one, one, many, many, many, many, one, one,
        ],
        compiler_params=pltpu.CompilerParams(
            collective_id=3, has_side_effects=True, vmem_limit_bytes=VMEM_BYTES
        ),
        name="sum_all",
    )(value)


def aggregate_group(index_ref, tiles_ref, window_ref, step, group, slots, rows):
    results = []
    for g in range(group):
        tile = jnp.concatenate([tiles_ref[g, s] for s in range(slots)], axis=1)
        source = jnp.concatenate(
            [
                window_ref[
                    pl.ds(
                        pl.multiple_of(index_ref[(step * group + g) * slots + s] * rows, rows),
                        rows,
                    ),
                    :,
                ]
                for s in range(slots)
            ],
            axis=0,
        )
        results.append(dot(tile, source, 1, 0).astype(BF16))
    return jnp.concatenate(results, axis=0)


def node_update(own, aggregated, w_self, w_agg, w_out):
    activation = dot(own, w_self, 1, 0) + dot(aggregated, w_agg, 1, 0)
    hidden = jnp.maximum(activation, 0.0).astype(BF16)
    updated = (own.astype(F32) + dot(hidden, w_out, 1, 0)).astype(BF16)
    return hidden, updated


def first_forward(
    group,
    index_ref,
    tiles_ref,
    feats_ref,
    wcat_ref,
    w_self_ref,
    w_agg_ref,
    w_out_ref,
    before_ref,
    agg_ref,
    hidden_ref,
    updated_ref,
    window_ref,
):
    step = pl.program_id(0)
    slots, rows = tiles_ref.shape[1], tiles_ref.shape[2]
    span = group * rows
    total = feats_ref.shape[1]

    @pl.when(step == 0)
    def _():
        def encode(i, carry):
            at = pl.multiple_of(i * 512, 512)
            encoded = dot(feats_ref[:, pl.ds(at, 512)], wcat_ref[...], 0, 0)
            window_ref[pl.ds(at, 512), :] = jnp.tanh(encoded).astype(BF16)
            return carry

        lax.fori_loop(0, total // 512, encode, 0)
        window_ref[pl.ds(total, rows), :] = jnp.zeros((rows, window_ref.shape[1]), BF16)

    aggregated = aggregate_group(index_ref, tiles_ref, window_ref, step, group, slots, rows)
    own = window_ref[pl.ds(pl.multiple_of(total // 5 + step * span, span), span), :]
    hidden, updated = node_update(own, aggregated, w_self_ref[...], w_agg_ref[...], w_out_ref[...])
    before_ref[...] = own
    agg_ref[...] = aggregated
    hidden_ref[...] = hidden
    updated_ref[...] = updated


def later_forward(
    group,
    index_ref,
    tiles_ref,
    below_ref,
    own_ref,
    above_ref,
    sibling_ref,
    cross_ref,
    w_self_ref,
    w_agg_ref,
    w_out_ref,
    agg_ref,
    hidden_ref,
    updated_ref,
    window_ref,
    sems,
):
    step = pl.program_id(0)
    slots, rows = tiles_ref.shape[1], tiles_ref.shape[2]
    span = group * rows
    hits = own_ref.shape[0]

    @pl.when(step == 0)
    def _():
        copies = [
            pltpu.make_async_copy(piece, window_ref.at[pl.ds(k * hits, hits)], sems.at[k])
            for k, piece in enumerate((below_ref, own_ref, above_ref, sibling_ref, cross_ref))
        ]
        for copy in copies:
            copy.start()
        window_ref[pl.ds(5 * hits, rows), :] = jnp.zeros((rows, window_ref.shape[1]), BF16)
        for copy in copies:
            copy.wait()

    aggregated = aggregate_group(index_ref, tiles_ref, window_ref, step, group, slots, rows)
    own = window_ref[pl.ds(pl.multiple_of(hits + step * span, span), span), :]
    hidden, updated = node_update(own, aggregated, w_self_ref[...], w_agg_ref[...], w_out_ref[...])
    agg_ref[...] = aggregated
    hidden_ref[...] = hidden
    updated_ref[...] = updated.astype(F32)


def gather_kernel(list_ref, bound_ref, anchor_ref, z_ref, *refs):
    outs, (anchor_out, buf_ref) = refs[:5], refs[5:]
    triplets, width = anchor_out.shape
    stride = list_ref.shape[0] // 5

    def anchors(i, carry):
        at = pl.multiple_of(i * 16, 16)
        anchor_out[pl.ds(at, 16), :] = jnp.concatenate(
            [z_ref[pl.ds(anchor_ref[i * 16 + u], 1), :] for u in range(16)], axis=0
        ).astype(BF16)
        return carry

    lax.fori_loop(0, triplets // 16, anchors, 0)
    zeros = jnp.zeros((64, width), F32)

    def clear(i, carry):
        buf_ref[pl.ds(pl.multiple_of(i * 64, 64), 64), :] = zeros
        return carry

    lax.fori_loop(0, 2 * triplets // 64, clear, 0)
    for j in range(5):

        def fetch(i, carry, j=j):
            for u in range(8):
                entry = list_ref[j * stride + i * 8 + u]
                row = z_ref[pl.ds(lax.shift_right_logical(entry, ENTRY_BITS), 1), :]
                buf_ref[pl.ds(lax.bitwise_and(entry, ENTRY_MASK), 1), :] = row
            return carry

        lax.fori_loop(bound_ref[2 * j], bound_ref[2 * j + 1], fetch, 0)

        def subtract(i, carry, j=j):
            at = pl.multiple_of(i * 64, 64)
            value = buf_ref[pl.ds(triplets + at, 64), :] - buf_ref[pl.ds(at, 64), :]
            outs[j][pl.ds(at, 64), :] = value.astype(BF16)
            buf_ref[pl.ds(triplets + at, 64), :] = zeros
            buf_ref[pl.ds(at, 64), :] = zeros
            return carry

        lax.fori_loop(0, triplets // 64, subtract, 0)


ENTRY_BITS = 12
ENTRY_MASK = (1 << ENTRY_BITS) - 1
PARTS = 4


def contrast_kernel(
    inv_root,
    self_ref,
    sib_ref,
    cross_ref,
    near_ref,
    far_ref,
    anchor_ref,
    loss_ref,
    ganchor_ref,
    asib_ref,
    across_ref,
    adirect_ref,
    afar_ref,
    coef_out,
    coefs_out,
    change_ref,
    sib_in,
    cross_in,
    far_send,
    far_in,
    near_send,
    near_in,
    *sems,
):
    s = [sems[2 * i : 2 * i + 2] for i in range(9)]
    direct, sibling, onward, source, near_adds = peers()
    roles = role_targets()
    size = anchor_ref.shape[0] // PARTS
    greet((direct, sibling, onward, source, roles[1], roles[3]))

    def rows(i):
        return pl.ds(i * size, size)

    def copies(k, src, dst, target):
        return [
            remote(src.at[rows(i)], dst.at[rows(i)], s[k][0].at[i], s[k][1].at[i], target)
            for i in range(PARTS)
        ]

    crosses = copies(0, cross_ref, cross_in, sibling)
    sibs = copies(1, sib_ref, sib_in, sibling)
    hops = copies(2, far_send, far_in, source)
    nears = copies(3, near_send, near_in, direct)
    to_direct = copies(4, anchor_ref, adirect_ref, direct)
    to_sibling = copies(5, anchor_ref, asib_ref, sibling)
    relays = copies(6, adirect_ref, afar_ref, onward)
    cross_a = copies(7, adirect_ref, across_ref, sibling)
    cross_b = copies(7, afar_ref, across_ref, sibling)
    coefs = [
        remote(coef_out, coefs_out.at[j], s[8][0].at[j], s[8][1].at[j], target)
        for j, target in enumerate(roles)
    ]
    for copy in crosses:
        copy.start()
    for copy in sibs:
        copy.start()
    for i in range(PARTS):
        crosses[i].wait_recv()
        extra = jnp.where(near_adds, 0.0, cross_in[rows(i), :].astype(F32))
        far_send[rows(i), :] = (far_ref[rows(i), :].astype(F32) + extra).astype(BF16)
        hops[i].start()
    for i in range(PARTS):
        to_direct[i].start()
        hops[i].wait_recv()
        extra = jnp.where(near_adds, cross_in[rows(i), :].astype(F32), 0.0)
        near_send[rows(i), :] = (
            near_ref[rows(i), :].astype(F32) + extra + far_in[rows(i), :].astype(F32)
        ).astype(BF16)
        nears[i].start()
    for i in range(PARTS):
        to_sibling[i].start()
        to_direct[i].wait_recv()
        relays[i].start()

        @pl.when(near_adds)
        def _():
            cross_a[i].start()

    gaps = []
    for i in range(PARTS):
        sibs[i].wait_recv()
        nears[i].wait_recv()
        change = (
            near_in[rows(i), :].astype(F32)
            + self_ref[rows(i), :].astype(F32)
            + sib_in[rows(i), :].astype(F32)
        )
        change_ref[rows(i), :] = change
        product = anchor_ref[rows(i), :].astype(F32) * change
        for u in range(size // 128):
            gaps.append(
                jnp.sum(product[u * 128 : (u + 1) * 128].T, axis=0, keepdims=True) * inv_root
            )
    gap = jnp.concatenate(gaps, axis=0)
    coef_out[...] = jax.nn.sigmoid(gap) * (inv_root / loss_divisor)
    for copy in coefs:
        copy.start()
    soft = jnp.maximum(gap, 0.0) + jnp.log1p(jnp.exp(-jnp.abs(gap)))
    loss_ref[...] = jnp.broadcast_to(jnp.sum(soft, keepdims=True), loss_ref.shape)
    for i in range(PARTS):
        relays[i].wait_recv()

        @pl.when(jnp.logical_not(near_adds))
        def _():
            cross_b[i].start()

    size = 128
    eye = lax.broadcasted_iota(jnp.int32, (size, size), 0) == lax.broadcasted_iota(
        jnp.int32, (size, size), 1
    )
    for i in range(coef_out.shape[0]):
        coef = coef_out[pl.ds(i, 1), :]
        column = jnp.sum(jnp.where(eye, coef, 0.0), axis=1, keepdims=True)
        here = pl.ds(i * size, size)
        ganchor_ref[here, :] = column * change_ref[here, :]
    for copy in coefs:
        copy.wait()
    for i in range(PARTS):
        crosses[i].wait_send()
        sibs[i].wait_send()
        hops[i].wait_send()
        nears[i].wait_send()
        to_direct[i].wait_send()
        to_sibling[i].wait()
        relays[i].wait_send()
        cross_a[i].wait()


def node_backward(
    gradient, hidden_ref, before_ref, agg_ref, w_out, gout_ref, gself_ref, gagg_ref, step
):
    upstream = gradient.astype(BF16)
    hidden = hidden_ref[...]
    hidden_grad = dot(upstream, w_out, 1, 1)
    act_grad = jnp.where(hidden.astype(F32) > 0, hidden_grad, 0.0).astype(BF16)

    @pl.when(step == 0)
    def _():
        gout_ref[...] = jnp.zeros(gout_ref.shape, F32)
        gself_ref[...] = jnp.zeros(gself_ref.shape, F32)
        gagg_ref[...] = jnp.zeros(gagg_ref.shape, F32)

    gout_ref[...] += dot(hidden, upstream, 0, 0)
    gself_ref[...] += dot(before_ref[...], act_grad, 0, 0)
    gagg_ref[...] += dot(agg_ref[...], act_grad, 0, 0)
    return act_grad


def spread_group(index_ref, tiles_ref, adj_ref, agg_grad_t, step, group, slots, rows):
    for g in range(group):
        tile = jnp.concatenate([tiles_ref[g, s] for s in range(slots)], axis=1)
        contrib = dot(agg_grad_t[:, g * rows : (g + 1) * rows], tile, 1, 0)
        for s in range(slots):
            at = index_ref[(step * group + g) * slots + s]
            adj_ref[at] = adj_ref[at] + contrib[:, s * rows : (s + 1) * rows]


def clear_blocks(adj_ref):
    def clear(i, carry):
        adj_ref[i] = jnp.zeros(adj_ref.shape[1:], F32)
        return carry

    lax.fori_loop(0, adj_ref.shape[0], clear, 0)


def scatter_rows(
    list_ref, bound_ref, anchor_ref, ganchor_ref, coef_ref, coefs_ref, rows_in, moved_ref, sums
):
    triplets, width = ganchor_ref.shape
    hits = sums[0].shape[0]
    stride = list_ref.shape[0] // 5
    span = 2 * triplets + 8
    zeros = jnp.zeros((64, width), F32)

    def clear(i, carry):
        for target in sums:
            target[pl.ds(pl.multiple_of(i * 64, 64), 64), :] = zeros
        return carry

    lax.fori_loop(0, hits // 64, clear, 0)
    eye = lax.broadcasted_iota(jnp.int32, (128, 128), 0) == lax.broadcasted_iota(
        jnp.int32, (128, 128), 1
    )
    for j, source in enumerate(rows_in):
        for i in range(triplets // 128):
            coef = coef_ref[pl.ds(i, 1), :] if j == 0 else coefs_ref[j - 1, pl.ds(i, 1), :]
            spread = jnp.where(eye, coef, 0.0)
            high = spread.astype(BF16)
            low = (spread - high.astype(F32)).astype(BF16)
            part = source[pl.ds(i * 128, 128), :]
            value = dot(high, part, 1, 0) + dot(low, part, 1, 0)
            moved_ref[pl.ds(j * span + i * 128, 128), :] = -value
            moved_ref[pl.ds(j * span + triplets + i * 128, 128), :] = value
        moved_ref[pl.ds(j * span + 2 * triplets, 8), :] = zeros[:8]

    def anchors(i, carry):
        for u in range(8):
            t = i * 8 + u
            here = pl.ds(anchor_ref[t], 1)
            target = sums[u % 4]
            target[here, :] = target[here, :] + ganchor_ref[pl.ds(t, 1), :]
        return carry

    lax.fori_loop(0, triplets // 8, anchors, 0)
    for j in range(5):

        def add(i, carry, j=j):
            for u in range(8):
                entry = list_ref[j * stride + i * 8 + u]
                here = pl.ds(lax.shift_right_logical(entry, ENTRY_BITS), 1)
                target = sums[u % 4]
                moved = moved_ref[pl.ds(j * span + lax.bitwise_and(entry, ENTRY_MASK), 1), :]
                target[here, :] = target[here, :] + moved
            return carry

        lax.fori_loop(bound_ref[2 * j], bound_ref[2 * j + 1], add, 0)


def last_backward(
    group,
    steps,
    index_ref,
    list_ref,
    bound_ref,
    anchor_ref,
    tiles_ref,
    ganchor_ref,
    coef_ref,
    coefs_ref,
    aself_ref,
    asib_ref,
    across_ref,
    adirect_ref,
    afar_ref,
    hidden_ref,
    before_ref,
    agg_ref,
    w_self_ref,
    w_agg_ref,
    w_out_ref,
    gout_ref,
    gself_ref,
    gagg_ref,
    direct_ref,
    obelow_ref,
    oown_ref,
    oabove_ref,
    osibling_ref,
    ocross_ref,
    adj_ref,
    moved_ref,
    *sums,
):
    step = pl.program_id(0)
    slots, rows = tiles_ref.shape[1], tiles_ref.shape[2]
    span = group * rows

    @pl.when(step == 0)
    def _():
        clear_blocks(adj_ref)
        scatter_rows(
            list_ref, bound_ref, anchor_ref, ganchor_ref, coef_ref, coefs_ref,
            (aself_ref, asib_ref, across_ref, adirect_ref, afar_ref), moved_ref, sums,
        )

    here = pl.ds(pl.multiple_of(step * span, span), span)
    gradient = (sums[0][here, :] + sums[1][here, :]) + (sums[2][here, :] + sums[3][here, :])
    act_grad = node_backward(
        gradient, hidden_ref, before_ref, agg_ref, w_out_ref[...], gout_ref, gself_ref, gagg_ref, step
    )
    direct_ref[...] = gradient + dot(act_grad, w_self_ref[...], 1, 1)
    agg_grad_t = dot(w_agg_ref[...], act_grad, 1, 1).astype(BF16)
    spread_group(index_ref, tiles_ref, adj_ref, agg_grad_t, step, group, slots, rows)

    @pl.when(step == steps - 1)
    def _():
        blocks = oown_ref.shape[0]
        for k, target in enumerate((obelow_ref, oown_ref, oabove_ref, osibling_ref, ocross_ref)):

            def store(i, carry, k=k, target=target):
                target[i] = adj_ref[k * blocks + i].astype(target.dtype)
                return carry

            lax.fori_loop(0, blocks, store, 0)


def first_backward(
    group,
    steps,
    index_ref,
    tiles_ref,
    direct_ref,
    own_ref,
    total_ref,
    sib_ref,
    hidden_ref,
    before_ref,
    agg_ref,
    w_self_ref,
    w_agg_ref,
    w_out_ref,
    feats_ref,
    wcat_ref,
    wcat_t_ref,
    gout_ref,
    gself_ref,
    gagg_ref,
    genc_ref,
    adj_ref,
):
    step = pl.program_id(0)
    slots, rows = tiles_ref.shape[1], tiles_ref.shape[2]
    span = group * rows
    total = feats_ref.shape[1]

    @pl.when(step == 0)
    def _():
        clear_blocks(adj_ref)
        genc_ref[...] = jnp.zeros(genc_ref.shape, F32)

    pieces = []
    for g in range(group):
        returned = own_ref[g] + (
            total_ref[g].astype(F32) + sib_ref[g].astype(F32)
        )
        pieces.append(returned.T)
    gradient = direct_ref[...] + jnp.concatenate(pieces, axis=0)
    act_grad = node_backward(
        gradient, hidden_ref, before_ref, agg_ref, w_out_ref[...], gout_ref, gself_ref, gagg_ref, step
    )
    direct = gradient + dot(act_grad, w_self_ref[...], 1, 1)
    here = feats_ref[:, pl.ds(pl.multiple_of(total // 5 + step * span, span), span)]
    squashed = jnp.tanh(dot(here, wcat_ref[...], 0, 0))
    genc_ref[...] += dot(here, (direct * (1.0 - squashed * squashed)).astype(BF16), 1, 0)
    agg_grad_t = dot(w_agg_ref[...], act_grad, 1, 1).astype(BF16)
    spread_group(index_ref, tiles_ref, adj_ref, agg_grad_t, step, group, slots, rows)

    @pl.when(step == steps - 1)
    def _():
        per = 4

        def encode(i, carry):
            at = pl.multiple_of(i * (per * rows), per * rows)
            feats = feats_ref[:, pl.ds(at, per * rows)]
            squashed_t = jnp.tanh(dot(wcat_t_ref[...], feats, 1, 0))
            grad_t = jnp.concatenate([adj_ref[i * per + u] for u in range(per)], axis=1)
            grad_t = (grad_t * (1.0 - squashed_t * squashed_t)).astype(BF16)
            return carry + dot(feats, grad_t, 1, 1)

        genc_ref[...] += lax.fori_loop(
            0, total // (per * rows), encode, jnp.zeros(genc_ref.shape, F32)
        )


def body(
    hit_feats,
    layer_ids,
    edge_tiles,
    src_blocks,
    live_slots,
    anchor_hits,
    positive_hits,
    negative_hits,
    w_enc,
    layer_table,
    w_self,
    w_agg,
    w_out,
):
    blocks, slots, rows, _ = edge_tiles.shape
    width = w_enc.shape[1]
    features = hit_feats.shape[0]
    kinds = layer_table.shape[0]
    hits = blocks * rows
    layer_total = w_self.shape[0]
    triplets = anchor_hits.shape[0]
    group = 4
    steps = blocks // group
    span = group * rows
    me = lax.axis_index("phi")
    is_even = me % 2 == 0
    even_pair = (me // 2) % 2 == 0

    def place(part):
        spots = (
            jnp.where(even_pair, 2, 0),
            jnp.where(is_even, 4, 3),
            1,
            jnp.where(is_even, 3, 4),
            jnp.where(even_pair, 0, 2),
        )
        return sum(jnp.where(part == k, spot, 0) for k, spot in enumerate(spots))

    live = jnp.arange(slots, dtype=jnp.int32)[None, :] < live_slots[:, None]
    index = jnp.where(
        live, place(src_blocks // blocks) * blocks + src_blocks % blocks, 5 * blocks
    ).reshape(blocks * slots)
    wanted = jnp.concatenate([positive_hits, negative_hits])
    keys = wanted * (2 * triplets) + jnp.arange(2 * triplets, dtype=jnp.int32)
    ranks = jnp.sum((keys[None, :] < keys[:, None]).astype(jnp.int32), axis=1)
    owner = wanted // hits
    counts = jnp.sum(
        (owner[None, :] == jnp.arange(8, dtype=jnp.int32)[:, None]).astype(jnp.int32), axis=1
    )
    padded = -(-counts // 8) * 8
    earlier = jnp.arange(8)[:, None] > jnp.arange(8)[None, :]
    aligned = jnp.sum(jnp.where(earlier, padded[None, :], 0), axis=1)
    shift = aligned - jnp.sum(jnp.where(earlier, counts[None, :], 0), axis=1)
    place_of = ranks + sum(jnp.where(owner == k, shift[k], 0) for k in range(5))
    listed = 2 * triplets // 128 + 1
    places = jnp.arange(listed * 128, dtype=jnp.int32)
    slot = jnp.arange(2 * triplets, dtype=jnp.int32)
    entry = (wanted % hits) * (1 << ENTRY_BITS) + slot - 2 * triplets
    entries = jnp.sum(
        jnp.where(place_of[None, :] == places[:, None], entry[None, :], 0), axis=1
    ) + 2 * triplets
    starts = jnp.pad((aligned // 8).reshape(1, 8), ((0, 6), (0, 120)))
    keys = jnp.concatenate([entries.reshape(listed, 128), starts], axis=0)
    pad = -(features + 1) % 16
    packed = jnp.concatenate(
        [hit_feats, layer_ids.astype(BF16)[None, :], jnp.zeros((pad, hits), BF16)], axis=0
    )
    packed = jnp.concatenate(
        [
            permute(packed, direct_target),
            packed,
            permute(packed, relayed_target),
            permute(packed, sibling_target),
            permute(packed, cross_target),
        ],
        axis=1,
    )
    feature_pad = -features % 16
    onehot = (
        jnp.arange(kinds, dtype=jnp.int32)[:, None].astype(BF16) == packed[features][None, :]
    ).astype(BF16)
    feats = jnp.concatenate(
        [packed[:features], jnp.zeros((feature_pad, 5 * hits), BF16), onehot], axis=0
    )
    wcat = jnp.concatenate([w_enc, jnp.zeros((feature_pad, width), BF16), layer_table], axis=0)
    depth = wcat.shape[0]

    tile_spec = pl.BlockSpec((group, slots, rows, rows), lambda i, *_: (i, 0, 0, 0))
    row_spec = pl.BlockSpec((span, width), lambda i, *_: (i, 0))
    block_spec = pl.BlockSpec((group, width, rows), lambda i, *_: (i, 0, 0))
    weight_spec = full((width, width))
    any_spec = pl.BlockSpec(memory_space=pl.ANY)
    row_shape = jax.ShapeDtypeStruct((hits, width), BF16)
    weight_shape = jax.ShapeDtypeStruct((width, width), F32)

    before0, agg0, hidden0, latents = pl.pallas_call(
        functools.partial(first_forward, group),
        grid_spec=pltpu.PrefetchScalarGridSpec(
            num_scalar_prefetch=1,
            grid=(steps,),
            in_specs=[tile_spec, full((depth, 5 * hits)), full((depth, width))] + [weight_spec] * 3,
            out_specs=[row_spec] * 4,
            scratch_shapes=[pltpu.VMEM((5 * hits + rows, width), BF16)],
        ),
        out_shape=[row_shape] * 4,
        compiler_params=params(),
        name="first_forward",
    )(index, edge_tiles, feats, wcat, w_self[0], w_agg[0], w_out[0])
    wide_shape = jax.ShapeDtypeStruct((hits, width), F32)
    pieces, lists = window_pieces(latents, keys)
    latents1 = latents
    agg1, hidden1, latents2 = pl.pallas_call(
        functools.partial(later_forward, group),
        grid_spec=pltpu.PrefetchScalarGridSpec(
            num_scalar_prefetch=1,
            grid=(steps,),
            in_specs=[tile_spec] + [any_spec] * 5 + [weight_spec] * 3,
            out_specs=[row_spec] * 3,
            scratch_shapes=[
                pltpu.VMEM((5 * hits + rows, width), BF16),
                pltpu.SemaphoreType.DMA((5,)),
            ],
        ),
        out_shape=[row_shape] * 2 + [wide_shape],
        compiler_params=params(),
        name="later_forward",
    )(index, edge_tiles, *pieces, w_self[1], w_agg[1], w_out[1])

    lists = jnp.concatenate([keys[None], lists], axis=0)
    odd_core, odd_pair = me % 2, (me // 2) % 2
    bounds = []
    for j, k in enumerate(
        (2, 1 + 2 * odd_core, 3 - 2 * odd_core, 4 * odd_pair, 4 - 4 * odd_pair)
    ):
        bounds.append(lax.dynamic_slice(lists[j, listed], (k,), (2,)))
    bounds = jnp.concatenate(bounds)
    lists = lists[:, :listed].reshape(-1)
    move_shape = jax.ShapeDtypeStruct((triplets, width), BF16)
    wide_move = jax.ShapeDtypeStruct((triplets, width), F32)
    move_spec = full((triplets, width))
    *found, anchors = pl.pallas_call(
        gather_kernel,
        grid_spec=pltpu.PrefetchScalarGridSpec(
            num_scalar_prefetch=3,
            grid=(1,),
            in_specs=[full((hits, width))],
            out_specs=[move_spec] * 6,
            scratch_shapes=[pltpu.VMEM((2 * triplets + 8, width), F32)],
        ),
        out_shape=[move_shape] * 6,
        compiler_params=params(),
        name="gather",
    )(lists, bounds, anchor_hits, latents2)
    vmem = pl.BlockSpec(memory_space=pltpu.VMEM)
    coef_shape = (triplets // 128, 128)
    loss_part, ganchor, *moves, coef, coefs = pl.pallas_call(
        functools.partial(contrast_kernel, 1.0 / math.sqrt(width)),
        in_specs=[vmem] * 6,
        out_specs=[vmem] * 8,
        out_shape=[jax.ShapeDtypeStruct((8, width), F32), wide_move]
        + [move_shape] * 4
        + [jax.ShapeDtypeStruct(coef_shape, F32), jax.ShapeDtypeStruct((4,) + coef_shape, F32)],
        scratch_shapes=[pltpu.VMEM((triplets, width), F32)]
        + [pltpu.VMEM((triplets, width), BF16)] * 6
        + [pltpu.SemaphoreType.DMA((PARTS,))] * 16
        + [pltpu.SemaphoreType.DMA((4,))] * 2,
        compiler_params=pltpu.CompilerParams(
            collective_id=4, has_side_effects=True, vmem_limit_bytes=VMEM_BYTES
        ),
        name="contrast",
    )(*found, anchors)

    t_shape = jax.ShapeDtypeStruct((blocks, width, rows), F32)
    t_half = jax.ShapeDtypeStruct((blocks, width, rows), BF16)
    t_full = pl.BlockSpec(
        (blocks, width, rows), lambda *_: (0, 0, 0), pipeline_mode=pl.Buffered(1)
    )
    adj_shape = pltpu.VMEM((5 * blocks + 1, width, rows), F32)
    gout1, gself1, gagg1, direct, obelow, own, oabove, osibling, ocross = pl.pallas_call(
        functools.partial(last_backward, group, steps),
        grid_spec=pltpu.PrefetchScalarGridSpec(
            num_scalar_prefetch=4,
            grid=(steps,),
            in_specs=[tile_spec, move_spec, full(coef_shape), full((4,) + coef_shape)]
            + [move_spec] * 5
            + [row_spec] * 3
            + [weight_spec] * 3,
            out_specs=[weight_spec] * 3 + [row_spec] + [t_full] * 5,
            scratch_shapes=[adj_shape, pltpu.VMEM((10 * triplets + 40, width), F32)]
            + [pltpu.VMEM((hits, width), F32)] * 4,
        ),
        out_shape=[weight_shape] * 3 + [wide_shape] + [t_shape] * 3 + [t_half] * 2,
        compiler_params=params(),
        name="last_backward",
    )(
        index, lists, bounds, anchor_hits, edge_tiles, ganchor, coef, coefs, anchors, *moves, hidden1, latents1, agg1,
        w_self[1], w_agg[1], w_out[1],
    )
    total, sib = return_pieces(obelow, oabove, osibling, ocross)
    gout0, gself0, gagg0, genc = pl.pallas_call(
        functools.partial(first_backward, group, steps),
        grid_spec=pltpu.PrefetchScalarGridSpec(
            num_scalar_prefetch=1,
            grid=(steps,),
            in_specs=[tile_spec, row_spec]
            + [block_spec] * 3
            + [row_spec] * 3
            + [weight_spec] * 3
            + [full((depth, 5 * hits)), full((depth, width)), full((width, depth))],
            out_specs=[weight_spec] * 3 + [full((depth, width))],
            scratch_shapes=[adj_shape],
        ),
        out_shape=[weight_shape] * 3 + [jax.ShapeDtypeStruct((depth, width), F32)],
        compiler_params=params(),
        name="first_backward",
    )(
        index, edge_tiles, direct, own, total, sib, hidden0, before0, agg0,
        w_self[0], w_agg[0], w_out[0], feats, wcat, wcat.T,
    )
    late = sum_all(
        jnp.concatenate([gout0, gout1, gself0, gself1, gagg0, gagg1, genc, loss_part], axis=0)
    )

    triplet_total = triplets * lax.axis_size("phi")
    base = 6 * width
    loss = (late[base + depth, 0] / triplet_total).reshape(1)
    grad_enc = late[base : base + features]
    grad_table = late[base + depth - kinds : base + depth]

    def pair(k):
        return late[2 * k * width : 2 * (k + 1) * width].reshape(layer_total, width, width)

    return (loss, grad_enc, grad_table, pair(1), pair(2), pair(0))


def solution(mesh):
    both = ("event", "phi")
    in_specs = (
        P(None, both),
        P(both),
        P(both, None, None, None),
        P(both, None),
        P(both),
        P(both),
        P(both),
        P(both),
        P(),
        P(),
        P(),
        P(),
        P(),
    )
    out_specs = (
        P("event"),
        P("event", None),
        P("event", None),
        P("event", None, None),
        P("event", None, None),
        P("event", None, None),
    )
    return jax.shard_map(body, mesh=mesh, in_specs=in_specs, out_specs=out_specs, check_vma=False)
```

```python
import functools
import math

import jax
import jax.numpy as jnp
from jax import lax
from jax.experimental import pallas as pl
from jax.experimental.pallas import tpu as pltpu
from jax.sharding import PartitionSpec as P

loss_divisor = 64.0
F32 = jnp.float32
BF16 = jnp.bfloat16
VMEM_BYTES = 60 * 1024 * 1024


def dot(left, right, left_dim, right_dim):
    return lax.dot_general(
        left, right, (((left_dim,), (right_dim,)), ((), ())), preferred_element_type=F32
    )


def full(shape):
    return pl.BlockSpec(shape, lambda *_: (0,) * len(shape))


def params():
    return pltpu.CompilerParams(
        dimension_semantics=("arbitrary",), vmem_limit_bytes=VMEM_BYTES
    )


CHUNKS = 8


def permute(value, target_of):
    count = lax.axis_size("phi")
    return lax.ppermute(value, "phi", [(s, target_of(s) % count) for s in range(count)])


def direct_target(s):
    return s ^ 2


def relayed_target(s):
    return s + 2 if (s // 2) % 2 else s - 2


def sibling_target(s):
    return s ^ 1


def cross_target(s):
    return s + 1 if s % 2 else s - 1


def peers():
    count = lax.axis_size("phi")
    me = lax.axis_index("phi")
    odd_pair = (me // 2) % 2
    odd_core = me % 2
    direct = me + 2 - 4 * odd_pair
    sibling = me + 1 - 2 * odd_core
    stride = 4 - 8 * odd_pair
    onward = (me + stride + count) % count
    source = (me - stride + count) % count
    return direct, sibling, onward, source, odd_pair == odd_core


def remote(src, dst, send, recv, target):
    return pltpu.make_async_remote_copy(
        src_ref=src,
        dst_ref=dst,
        send_sem=send,
        recv_sem=recv,
        device_id={"phi": target},
        device_id_type=pl.DeviceIdType.MESH,
    )


def greet(targets):
    barrier = pltpu.get_barrier_semaphore()
    for target in targets:
        pl.semaphore_signal(
            barrier, inc=1, device_id={"phi": target}, device_id_type=pl.DeviceIdType.MESH
        )
    pl.semaphore_wait(barrier, len(targets))


def role_targets():
    count = lax.axis_size("phi")
    me = lax.axis_index("phi")
    odd_pair = (me // 2) % 2
    odd_core = me % 2
    sibling = me + 1 - 2 * odd_core
    across = (me - 1 + 2 * odd_core + count) % count
    direct = me + 2 - 4 * odd_pair
    far = (me - 2 + 4 * odd_pair + count) % count
    return sibling, across, direct, far


def exchange_kernel(own, keys, direct_out, relay_out, sib_out, cross_out, lists_out, *sems):
    ys, yr, zs, zr, cs, cr, ss, sr, ls, lr = sems
    direct, sibling, onward, source, direct_crosses = peers()
    size = own.shape[0] // CHUNKS
    roles = role_targets()
    greet((direct, sibling, source, roles[1], roles[3]))
    lists = [
        remote(keys, lists_out.at[j], ls.at[j], lr.at[j], target)
        for j, target in enumerate(roles)
    ]
    for copy in lists:
        copy.start()

    def part(ref, i):
        return ref.at[pl.ds(i * size, size)]

    first = [
        remote(part(own, i), part(direct_out, i), ys.at[i], yr.at[i], direct) for i in range(CHUNKS)
    ]
    second = [
        remote(part(direct_out, i), part(relay_out, i), zs.at[i], zr.at[i], onward)
        for i in range(CHUNKS)
    ]
    cross_a = [
        remote(part(direct_out, i), part(cross_out, i), cs.at[i], cr.at[i], sibling)
        for i in range(CHUNKS)
    ]
    cross_b = [
        remote(part(relay_out, i), part(cross_out, i), cs.at[i], cr.at[i], sibling)
        for i in range(CHUNKS)
    ]
    near = remote(own, sib_out, ss.at[0], sr.at[0], sibling)
    for copy in first:
        copy.start()
    near.start()
    for i in range(CHUNKS):
        first[i].wait_recv()
        second[i].start()

        @pl.when(direct_crosses)
        def _():
            cross_a[i].start()

    for i in range(CHUNKS):
        second[i].wait_recv()

        @pl.when(jnp.logical_not(direct_crosses))
        def _():
            cross_b[i].start()

    near.wait()
    for i in range(CHUNKS):
        first[i].wait_send()
        second[i].wait_send()
        cross_a[i].wait()
    for copy in lists:
        copy.wait()


def window_pieces(latents, keys):
    hits, width = latents.shape
    any_spec = pl.BlockSpec(memory_space=pl.ANY)
    direct, relayed, sibling, cross, lists = pl.pallas_call(
        exchange_kernel,
        in_specs=[any_spec] * 2,
        out_specs=[any_spec] * 5,
        out_shape=[jax.ShapeDtypeStruct((hits, width), BF16)] * 4
        + [jax.ShapeDtypeStruct((4,) + keys.shape, keys.dtype)],
        scratch_shapes=[pltpu.SemaphoreType.DMA((CHUNKS,))] * 6
        + [pltpu.SemaphoreType.DMA((1,))] * 2
        + [pltpu.SemaphoreType.DMA((4,))] * 2,
        compiler_params=pltpu.CompilerParams(collective_id=1, has_side_effects=True),
        name="exchange",
    )(latents, keys)
    return (direct, latents, relayed, sibling, cross), lists


def aggregate_group(index_ref, tiles_ref, window_ref, step, group, slots, rows):
    results = []
    for g in range(group):
        tile = jnp.concatenate([tiles_ref[g, s] for s in range(slots)], axis=1)
        source = jnp.concatenate(
            [
                window_ref[
                    pl.ds(
                        pl.multiple_of(index_ref[(step * group + g) * slots + s] * rows, rows),
                        rows,
                    ),
                    :,
                ]
                for s in range(slots)
            ],
            axis=0,
        )
        results.append(dot(tile, source, 1, 0).astype(BF16))
    return jnp.concatenate(results, axis=0)


def node_update(own, aggregated, w_self, w_agg, w_out):
    activation = dot(own, w_self, 1, 0) + dot(aggregated, w_agg, 1, 0)
    hidden = jnp.maximum(activation, 0.0).astype(BF16)
    updated = (own.astype(F32) + dot(hidden, w_out, 1, 0)).astype(BF16)
    return hidden, updated


def first_forward(
    group,
    index_ref,
    tiles_ref,
    feats_ref,
    wcat_ref,
    w_self_ref,
    w_agg_ref,
    w_out_ref,
    before_ref,
    agg_ref,
    hidden_ref,
    updated_ref,
    window_ref,
):
    step = pl.program_id(0)
    slots, rows = tiles_ref.shape[1], tiles_ref.shape[2]
    span = group * rows
    total = feats_ref.shape[1]

    @pl.when(step == 0)
    def _():
        def encode(i, carry):
            at = pl.multiple_of(i * 512, 512)
            encoded = dot(feats_ref[:, pl.ds(at, 512)], wcat_ref[...], 0, 0)
            window_ref[pl.ds(at, 512), :] = jnp.tanh(encoded).astype(BF16)
            return carry

        lax.fori_loop(0, total // 512, encode, 0)
        window_ref[pl.ds(total, rows), :] = jnp.zeros((rows, window_ref.shape[1]), BF16)

    aggregated = aggregate_group(index_ref, tiles_ref, window_ref, step, group, slots, rows)
    own = window_ref[pl.ds(pl.multiple_of(total // 5 + step * span, span), span), :]
    hidden, updated = node_update(own, aggregated, w_self_ref[...], w_agg_ref[...], w_out_ref[...])
    before_ref[...] = own
    agg_ref[...] = aggregated
    hidden_ref[...] = hidden
    updated_ref[...] = updated


def later_forward(
    group,
    index_ref,
    tiles_ref,
    below_ref,
    own_ref,
    above_ref,
    sibling_ref,
    cross_ref,
    w_self_ref,
    w_agg_ref,
    w_out_ref,
    agg_ref,
    hidden_ref,
    updated_ref,
    window_ref,
    sems,
):
    step = pl.program_id(0)
    slots, rows = tiles_ref.shape[1], tiles_ref.shape[2]
    span = group * rows
    hits = own_ref.shape[0]

    @pl.when(step == 0)
    def _():
        copies = [
            pltpu.make_async_copy(piece, window_ref.at[pl.ds(k * hits, hits)], sems.at[k])
            for k, piece in enumerate((below_ref, own_ref, above_ref, sibling_ref, cross_ref))
        ]
        for copy in copies:
            copy.start()
        window_ref[pl.ds(5 * hits, rows), :] = jnp.zeros((rows, window_ref.shape[1]), BF16)
        for copy in copies:
            copy.wait()

    aggregated = aggregate_group(index_ref, tiles_ref, window_ref, step, group, slots, rows)
    own = window_ref[pl.ds(pl.multiple_of(hits + step * span, span), span), :]
    hidden, updated = node_update(own, aggregated, w_self_ref[...], w_agg_ref[...], w_out_ref[...])
    agg_ref[...] = aggregated
    hidden_ref[...] = hidden
    updated_ref[...] = updated.astype(F32)


def gather_kernel(list_ref, bound_ref, anchor_ref, z_ref, *refs):
    outs, (anchor_out, buf_ref) = refs[:5], refs[5:]
    triplets, width = anchor_out.shape
    stride = list_ref.shape[0] // 5

    def anchors(i, carry):
        at = pl.multiple_of(i * 16, 16)
        anchor_out[pl.ds(at, 16), :] = jnp.concatenate(
            [z_ref[pl.ds(anchor_ref[i * 16 + u], 1), :] for u in range(16)], axis=0
        ).astype(BF16)
        return carry

    lax.fori_loop(0, triplets // 16, anchors, 0)
    zeros = jnp.zeros((64, width), F32)

    def clear(i, carry):
        buf_ref[pl.ds(pl.multiple_of(i * 64, 64), 64), :] = zeros
        return carry

    lax.fori_loop(0, 2 * triplets // 64, clear, 0)
    for j in range(5):

        def fetch(i, carry, j=j):
            for u in range(8):
                entry = list_ref[j * stride + i * 8 + u]
                row = z_ref[pl.ds(lax.shift_right_logical(entry, ENTRY_BITS), 1), :]
                buf_ref[pl.ds(lax.bitwise_and(entry, ENTRY_MASK), 1), :] = row
            return carry

        lax.fori_loop(bound_ref[2 * j], bound_ref[2 * j + 1], fetch, 0)

        def subtract(i, carry, j=j):
            at = pl.multiple_of(i * 64, 64)
            value = buf_ref[pl.ds(triplets + at, 64), :] - buf_ref[pl.ds(at, 64), :]
            outs[j][pl.ds(at, 64), :] = value.astype(BF16)
            buf_ref[pl.ds(triplets + at, 64), :] = zeros
            buf_ref[pl.ds(at, 64), :] = zeros
            return carry

        lax.fori_loop(0, triplets // 64, subtract, 0)


ENTRY_BITS = 12
ENTRY_MASK = (1 << ENTRY_BITS) - 1
PARTS = 4


def contrast_kernel(
    inv_root,
    self_ref,
    sib_ref,
    cross_ref,
    near_ref,
    far_ref,
    anchor_ref,
    loss_ref,
    ganchor_ref,
    asib_ref,
    across_ref,
    adirect_ref,
    afar_ref,
    coef_out,
    coefs_out,
    change_ref,
    sib_in,
    cross_in,
    far_send,
    far_in,
    near_send,
    near_in,
    *sems,
):
    s = [sems[2 * i : 2 * i + 2] for i in range(9)]
    direct, sibling, onward, source, near_adds = peers()
    roles = role_targets()
    size = anchor_ref.shape[0] // PARTS
    greet((direct, sibling, onward, source, roles[1], roles[3]))

    def rows(i):
        return pl.ds(i * size, size)

    def copies(k, src, dst, target):
        return [
            remote(src.at[rows(i)], dst.at[rows(i)], s[k][0].at[i], s[k][1].at[i], target)
            for i in range(PARTS)
        ]

    crosses = copies(0, cross_ref, cross_in, sibling)
    sibs = copies(1, sib_ref, sib_in, sibling)
    hops = copies(2, far_send, far_in, source)
    nears = copies(3, near_send, near_in, direct)
    to_direct = copies(4, anchor_ref, adirect_ref, direct)
    to_sibling = copies(5, anchor_ref, asib_ref, sibling)
    relays = copies(6, adirect_ref, afar_ref, onward)
    cross_a = copies(7, adirect_ref, across_ref, sibling)
    cross_b = copies(7, afar_ref, across_ref, sibling)
    coefs = [
        remote(coef_out, coefs_out.at[j], s[8][0].at[j], s[8][1].at[j], target)
        for j, target in enumerate(roles)
    ]
    for copy in crosses:
        copy.start()
    for copy in sibs:
        copy.start()
    for i in range(PARTS):
        crosses[i].wait_recv()
        extra = jnp.where(near_adds, 0.0, cross_in[rows(i), :].astype(F32))
        far_send[rows(i), :] = (far_ref[rows(i), :].astype(F32) + extra).astype(BF16)
        hops[i].start()
    for i in range(PARTS):
        to_direct[i].start()
        hops[i].wait_recv()
        extra = jnp.where(near_adds, cross_in[rows(i), :].astype(F32), 0.0)
        near_send[rows(i), :] = (
            near_ref[rows(i), :].astype(F32) + extra + far_in[rows(i), :].astype(F32)
        ).astype(BF16)
        nears[i].start()
    for i in range(PARTS):
        to_sibling[i].start()
        to_direct[i].wait_recv()
        relays[i].start()

        @pl.when(near_adds)
        def _():
            cross_a[i].start()

    gaps = []
    for i in range(PARTS):
        sibs[i].wait_recv()
        nears[i].wait_recv()
        change = (
            near_in[rows(i), :].astype(F32)
            + self_ref[rows(i), :].astype(F32)
            + sib_in[rows(i), :].astype(F32)
        )
        change_ref[rows(i), :] = change
        product = anchor_ref[rows(i), :].astype(F32) * change
        for u in range(size // 128):
            gaps.append(
                jnp.sum(product[u * 128 : (u + 1) * 128].T, axis=0, keepdims=True) * inv_root
            )
    gap = jnp.concatenate(gaps, axis=0)
    coef_out[...] = jax.nn.sigmoid(gap) * (inv_root / loss_divisor)
    for copy in coefs:
        copy.start()
    soft = jnp.maximum(gap, 0.0) + jnp.log1p(jnp.exp(-jnp.abs(gap)))
    loss_ref[...] = jnp.broadcast_to(jnp.sum(soft, keepdims=True), loss_ref.shape)
    for i in range(PARTS):
        relays[i].wait_recv()

        @pl.when(jnp.logical_not(near_adds))
        def _():
            cross_b[i].start()

    size = 128
    eye = lax.broadcasted_iota(jnp.int32, (size, size), 0) == lax.broadcasted_iota(
        jnp.int32, (size, size), 1
    )
    for i in range(coef_out.shape[0]):
        coef = coef_out[pl.ds(i, 1), :]
        column = jnp.sum(jnp.where(eye, coef, 0.0), axis=1, keepdims=True)
        here = pl.ds(i * size, size)
        ganchor_ref[here, :] = column * change_ref[here, :]
    for copy in coefs:
        copy.wait()
    for i in range(PARTS):
        crosses[i].wait_send()
        sibs[i].wait_send()
        hops[i].wait_send()
        nears[i].wait_send()
        to_direct[i].wait_send()
        to_sibling[i].wait()
        relays[i].wait_send()
        cross_a[i].wait()


def node_backward(
    gradient, hidden_ref, before_ref, agg_ref, w_out, gout_ref, gself_ref, gagg_ref, step
):
    upstream = gradient.astype(BF16)
    hidden = hidden_ref[...]
    hidden_grad = dot(upstream, w_out, 1, 1)
    act_grad = jnp.where(hidden.astype(F32) > 0, hidden_grad, 0.0).astype(BF16)

    @pl.when(step == 0)
    def _():
        gout_ref[...] = jnp.zeros(gout_ref.shape, F32)
        gself_ref[...] = jnp.zeros(gself_ref.shape, F32)
        gagg_ref[...] = jnp.zeros(gagg_ref.shape, F32)

    gout_ref[...] += dot(hidden, upstream, 0, 0)
    gself_ref[...] += dot(before_ref[...], act_grad, 0, 0)
    gagg_ref[...] += dot(agg_ref[...], act_grad, 0, 0)
    return act_grad


def spread_group(index_ref, tiles_ref, adj_ref, agg_grad_t, step, group, slots, rows):
    for g in range(group):
        tile = jnp.concatenate([tiles_ref[g, s] for s in range(slots)], axis=1)
        contrib = dot(agg_grad_t[:, g * rows : (g + 1) * rows], tile, 1, 0)
        for s in range(slots):
            at = index_ref[(step * group + g) * slots + s]
            adj_ref[at] = adj_ref[at] + contrib[:, s * rows : (s + 1) * rows]


def clear_blocks(adj_ref):
    def clear(i, carry):
        adj_ref[i] = jnp.zeros(adj_ref.shape[1:], F32)
        return carry

    lax.fori_loop(0, adj_ref.shape[0], clear, 0)


def scatter_rows(
    list_ref, bound_ref, anchor_ref, ganchor_ref, coef_ref, coefs_ref, rows_in, moved_ref, sums
):
    triplets, width = ganchor_ref.shape
    hits = sums[0].shape[0]
    stride = list_ref.shape[0] // 5
    span = 2 * triplets + 8
    zeros = jnp.zeros((64, width), F32)

    def clear(i, carry):
        for target in sums:
            target[pl.ds(pl.multiple_of(i * 64, 64), 64), :] = zeros
        return carry

    lax.fori_loop(0, hits // 64, clear, 0)
    eye = lax.broadcasted_iota(jnp.int32, (128, 128), 0) == lax.broadcasted_iota(
        jnp.int32, (128, 128), 1
    )
    for j, source in enumerate(rows_in):
        for i in range(triplets // 128):
            coef = coef_ref[pl.ds(i, 1), :] if j == 0 else coefs_ref[j - 1, pl.ds(i, 1), :]
            spread = jnp.where(eye, coef, 0.0)
            high = spread.astype(BF16)
            low = (spread - high.astype(F32)).astype(BF16)
            part = source[pl.ds(i * 128, 128), :]
            value = dot(high, part, 1, 0) + dot(low, part, 1, 0)
            moved_ref[pl.ds(j * span + i * 128, 128), :] = -value
            moved_ref[pl.ds(j * span + triplets + i * 128, 128), :] = value
        moved_ref[pl.ds(j * span + 2 * triplets, 8), :] = zeros[:8]

    def anchors(i, carry):
        for u in range(8):
            t = i * 8 + u
            here = pl.ds(anchor_ref[t], 1)
            target = sums[u % 4]
            target[here, :] = target[here, :] + ganchor_ref[pl.ds(t, 1), :]
        return carry

    lax.fori_loop(0, triplets // 8, anchors, 0)
    for j in range(5):

        def add(i, carry, j=j):
            for u in range(8):
                entry = list_ref[j * stride + i * 8 + u]
                here = pl.ds(lax.shift_right_logical(entry, ENTRY_BITS), 1)
                target = sums[u % 4]
                moved = moved_ref[pl.ds(j * span + lax.bitwise_and(entry, ENTRY_MASK), 1), :]
                target[here, :] = target[here, :] + moved
            return carry

        lax.fori_loop(bound_ref[2 * j], bound_ref[2 * j + 1], add, 0)


def last_backward(
    group,
    steps,
    index_ref,
    list_ref,
    bound_ref,
    anchor_ref,
    tiles_ref,
    ganchor_ref,
    coef_ref,
    coefs_ref,
    aself_ref,
    asib_ref,
    across_ref,
    adirect_ref,
    afar_ref,
    hidden_ref,
    before_ref,
    agg_ref,
    w_self_ref,
    w_agg_ref,
    w_out_ref,
    gout_ref,
    gself_ref,
    gagg_ref,
    direct_ref,
    obelow_ref,
    oown_ref,
    oabove_ref,
    osibling_ref,
    ocross_ref,
    adj_ref,
    moved_ref,
    *sums,
):
    step = pl.program_id(0)
    slots, rows = tiles_ref.shape[1], tiles_ref.shape[2]
    span = group * rows

    @pl.when(step == 0)
    def _():
        clear_blocks(adj_ref)
        scatter_rows(
            list_ref, bound_ref, anchor_ref, ganchor_ref, coef_ref, coefs_ref,
            (aself_ref, asib_ref, across_ref, adirect_ref, afar_ref), moved_ref, sums,
        )

    here = pl.ds(pl.multiple_of(step * span, span), span)
    gradient = (sums[0][here, :] + sums[1][here, :]) + (sums[2][here, :] + sums[3][here, :])
    act_grad = node_backward(
        gradient, hidden_ref, before_ref, agg_ref, w_out_ref[...], gout_ref, gself_ref, gagg_ref, step
    )
    direct_ref[...] = gradient + dot(act_grad, w_self_ref[...], 1, 1)
    agg_grad_t = dot(w_agg_ref[...], act_grad, 1, 1).astype(BF16)
    spread_group(index_ref, tiles_ref, adj_ref, agg_grad_t, step, group, slots, rows)

    @pl.when(step == steps - 1)
    def _():
        blocks = oown_ref.shape[0]
        for k, target in enumerate((obelow_ref, oown_ref, oabove_ref, osibling_ref, ocross_ref)):

            def store(i, carry, k=k, target=target):
                target[i] = adj_ref[k * blocks + i].astype(target.dtype)
                return carry

            lax.fori_loop(0, blocks, store, 0)


def back_kernel(
    pairs,
    index_ref,
    cross_hbm,
    sib_hbm,
    relay_hbm,
    direct_hbm,
    own_hbm,
    grad_hbm,
    hidden_hbm,
    before_hbm,
    agg_hbm,
    tiles_hbm,
    feats_ref,
    wcat_ref,
    wcat_t_ref,
    w_self_ref,
    w_agg_ref,
    w_out_ref,
    gout1_ref,
    gself1_ref,
    gagg1_ref,
    loss_ref,
    gself_out,
    gagg_out,
    gout_out,
    tail_out,
    cross_in,
    sib_in,
    relay_in,
    total_in,
    relay_send,
    direct_send,
    relay_ref,
    direct_ref,
    own_ref,
    grad_ref,
    hidden_ref,
    before_ref,
    agg_ref,
    tiles_ref,
    slope_ref,
    block_feats_ref,
    x_ref,
    half_in,
    acc_ref,
    slots_in,
    all_ref,
    local_sem,
    *sems,
):
    ys, yr, zs, zr, cs, cr, ss, sr, s0, r0, s1, r1, s2, r2, s3, r3 = sems
    direct, sibling, onward, source, to_direct = peers()
    me = lax.axis_index("phi")
    pair, core = me // 2, me % 2
    others = [((pair + d) % pairs) * 2 + core for d in range(1, pairs)]
    blocks, slots, rows, _ = tiles_ref.shape
    depth, width = wcat_ref.shape
    window = feats_ref.shape[1] // rows
    size = grad_ref.shape[0] // CHUNKS
    group = blocks // CHUNKS
    loads = [
        pltpu.make_async_copy(src, dst, local_sem.at[k])
        for k, (src, dst) in enumerate(
            (
                (relay_hbm, relay_ref),
                (direct_hbm, direct_ref),
                (own_hbm, own_ref),
                (grad_hbm, grad_ref),
                (hidden_hbm, hidden_ref),
                (before_hbm, before_ref),
                (agg_hbm, agg_ref),
                (tiles_hbm, tiles_ref),
            )
        )
    ]
    for copy in loads:
        copy.start()
    greet([sibling] + others)

    def span(i):
        return pl.ds(pl.multiple_of(i * size, size), size)

    def crosses(i):
        return remote(cross_hbm.at[span(i)], cross_in.at[span(i)], cs.at[i], cr.at[i], sibling)

    def first(i):
        return remote(relay_send.at[span(i)], relay_in.at[span(i)], zs.at[i], zr.at[i], source)

    def second(i):
        return remote(direct_send.at[span(i)], total_in.at[span(i)], ys.at[i], yr.at[i], direct)

    near = remote(sib_hbm, sib_in, ss.at[0], sr.at[0], sibling)
    lax.fori_loop(0, CHUNKS, lambda i, c: (crosses(i).start(), c)[1], 0)
    near.start()

    per = window // (2 * CHUNKS)

    def slopes(i):
        for u in range(0, per, 2):
            at = pl.multiple_of((i * per + u) * rows, 2 * rows)
            feats = feats_ref[:, pl.ds(at, 2 * rows)]
            squashed = jnp.tanh(dot(wcat_t_ref[...], feats, 1, 0))
            slope = 1.0 - squashed * squashed
            for v in range(2):
                slope_ref[i * per + u + v] = slope[:, v * rows : (v + 1) * rows]
                block_feats_ref[i * per + u + v] = feats[:, v * rows : (v + 1) * rows]

    x_ref[...] = jnp.zeros(x_ref.shape, F32)
    for k, value in enumerate((gout1_ref, gself1_ref, gagg1_ref)):
        x_ref[(2 * k + 1) * width : (2 * k + 2) * width, :] = value[...]
    base = 6 * width
    x_ref[base + depth : base + depth + 8, :] = loss_ref[...]
    slope_ref[window] = jnp.zeros(slope_ref.shape[1:], F32)
    block_feats_ref[window] = jnp.zeros(block_feats_ref.shape[1:], BF16)
    loads[0].wait()

    def relay_step(i, carry):
        here = span(i)
        crosses(i).wait_recv()
        extra = jnp.where(to_direct, 0.0, cross_in[here, :].astype(F32))
        relay_send[here, :] = (relay_ref[here, :] + extra).astype(BF16)
        first(i).start()
        slopes(i)
        return carry

    lax.fori_loop(0, CHUNKS, relay_step, 0)
    loads[1].wait()

    def direct_step(i, carry):
        here = span(i)
        first(i).wait_recv()
        extra = jnp.where(to_direct, cross_in[here, :].astype(F32), 0.0)
        direct_send[here, :] = (
            direct_ref[here, :] + extra + relay_in[here, :].astype(F32)
        ).astype(BF16)
        second(i).start()
        slopes(CHUNKS + i)
        return carry

    lax.fori_loop(0, CHUNKS, direct_step, 0)
    for copy in loads[2:]:
        copy.wait()
    near.wait()

    def layer_step(i, carry):
        here = span(i)
        second(i).wait_recv()
        returned = own_ref[here, :] + (
            total_in[here, :].astype(F32) + sib_in[here, :].astype(F32)
        )
        gradient = grad_ref[here, :] + jnp.concatenate(
            [returned[g * width : (g + 1) * width].T for g in range(group)], axis=0
        )
        upstream = gradient.astype(BF16)
        hidden = hidden_ref[here, :]
        hidden_grad = dot(upstream, w_out_ref[...], 1, 1)
        act_grad = jnp.where(hidden.astype(F32) > 0, hidden_grad, 0.0).astype(BF16)
        agg_grad_t = dot(w_agg_ref[...], act_grad, 1, 1).astype(BF16)
        x_ref[0:width, :] += dot(hidden, upstream, 0, 0)
        x_ref[2 * width : 3 * width, :] += dot(before_ref[here, :], act_grad, 0, 0)
        x_ref[4 * width : 5 * width, :] += dot(agg_ref[here, :], act_grad, 0, 0)
        own_grad = gradient + dot(act_grad, w_self_ref[...], 1, 1)
        feats = feats_ref[:, pl.ds(pl.multiple_of((window // 5) * rows + i * size, size), size)]
        squashed = jnp.tanh(dot(feats, wcat_ref[...], 0, 0))
        genc = dot(feats, (own_grad * (1.0 - squashed * squashed)).astype(BF16), 1, 0)
        for g in range(group):
            block = i * group + g
            tile = jnp.concatenate([tiles_ref[block, s] for s in range(slots)], axis=1)
            contrib = dot(agg_grad_t[:, g * rows : (g + 1) * rows], tile, 1, 0)
            places = [index_ref[block * slots + s] for s in range(slots)]
            slope = jnp.concatenate([slope_ref[at] for at in places], axis=1)
            source_feats = jnp.concatenate([block_feats_ref[at] for at in places], axis=1)
            genc = genc + dot(source_feats, (contrib * slope).astype(BF16), 1, 1)
        x_ref[base : base + depth, :] += genc
        return carry

    lax.fori_loop(0, CHUNKS, layer_step, 0)

    def drain(i, carry):
        crosses(i).wait_send()
        first(i).wait_send()
        second(i).wait_send()
        return carry

    lax.fori_loop(0, CHUNKS, drain, 0)

    half = x_ref.shape[0] // 2
    chunk = half // pairs

    def part(start, length):
        return pl.ds(pl.multiple_of(start, 8), length)

    swap = remote(x_ref.at[part((1 - core) * half, half)], half_in, s0.at[0], r0.at[0], sibling)
    swap.start()
    swap.wait()
    acc_ref[...] = x_ref[part(core * half, half), :] + half_in[...]
    scatter = [
        remote(
            acc_ref.at[part(((pair + d) % pairs) * chunk, chunk)],
            slots_in.at[d - 1],
            s1.at[d - 1],
            r1.at[d - 1],
            others[d - 1],
        )
        for d in range(1, pairs)
    ]
    for copy in scatter:
        copy.start()
    total = acc_ref[part(pair * chunk, chunk), :]
    for d in range(1, pairs):
        scatter[d - 1].wait_recv()
        total = total + slots_in[d - 1]
    mine = part(core * half + pair * chunk, chunk)
    all_ref[mine, :] = total
    gather = [
        remote(all_ref.at[mine], all_ref.at[mine], s2.at[d - 1], r2.at[d - 1], others[d - 1])
        for d in range(1, pairs)
    ]
    for copy in gather:
        copy.start()
    for copy in gather:
        copy.wait()
    for copy in scatter:
        copy.wait_send()
    whole = part(core * half, half)
    last = remote(all_ref.at[whole], all_ref.at[whole], s3.at[0], r3.at[0], sibling)
    last.start()
    last.wait()
    for k, out in enumerate((gout_out, gself_out, gagg_out)):
        for layer in range(2):
            at = (2 * k + layer) * width
            out[layer] = all_ref[at : at + width, :]
    tail_out[...] = all_ref[base : base + depth + 8, :]


def body(
    hit_feats,
    layer_ids,
    edge_tiles,
    src_blocks,
    live_slots,
    anchor_hits,
    positive_hits,
    negative_hits,
    w_enc,
    layer_table,
    w_self,
    w_agg,
    w_out,
):
    blocks, slots, rows, _ = edge_tiles.shape
    width = w_enc.shape[1]
    features = hit_feats.shape[0]
    kinds = layer_table.shape[0]
    hits = blocks * rows
    layer_total = w_self.shape[0]
    triplets = anchor_hits.shape[0]
    group = 4
    steps = blocks // group
    span = group * rows
    me = lax.axis_index("phi")
    is_even = me % 2 == 0
    even_pair = (me // 2) % 2 == 0

    def place(part):
        spots = (
            jnp.where(even_pair, 2, 0),
            jnp.where(is_even, 4, 3),
            1,
            jnp.where(is_even, 3, 4),
            jnp.where(even_pair, 0, 2),
        )
        return sum(jnp.where(part == k, spot, 0) for k, spot in enumerate(spots))

    live = jnp.arange(slots, dtype=jnp.int32)[None, :] < live_slots[:, None]
    index = jnp.where(
        live, place(src_blocks // blocks) * blocks + src_blocks % blocks, 5 * blocks
    ).reshape(blocks * slots)
    wanted = jnp.concatenate([positive_hits, negative_hits])
    keys = wanted * (2 * triplets) + jnp.arange(2 * triplets, dtype=jnp.int32)
    ranks = jnp.sum((keys[None, :] < keys[:, None]).astype(jnp.int32), axis=1)
    owner = wanted // hits
    counts = jnp.sum(
        (owner[None, :] == jnp.arange(8, dtype=jnp.int32)[:, None]).astype(jnp.int32), axis=1
    )
    padded = -(-counts // 8) * 8
    earlier = jnp.arange(8)[:, None] > jnp.arange(8)[None, :]
    aligned = jnp.sum(jnp.where(earlier, padded[None, :], 0), axis=1)
    shift = aligned - jnp.sum(jnp.where(earlier, counts[None, :], 0), axis=1)
    place_of = ranks + sum(jnp.where(owner == k, shift[k], 0) for k in range(5))
    listed = 2 * triplets // 128 + 1
    places = jnp.arange(listed * 128, dtype=jnp.int32)
    slot = jnp.arange(2 * triplets, dtype=jnp.int32)
    entry = (wanted % hits) * (1 << ENTRY_BITS) + slot - 2 * triplets
    entries = jnp.sum(
        jnp.where(place_of[None, :] == places[:, None], entry[None, :], 0), axis=1
    ) + 2 * triplets
    starts = jnp.pad((aligned // 8).reshape(1, 8), ((0, 6), (0, 120)))
    keys = jnp.concatenate([entries.reshape(listed, 128), starts], axis=0)
    pad = -(features + 1) % 16
    packed = jnp.concatenate(
        [hit_feats, layer_ids.astype(BF16)[None, :], jnp.zeros((pad, hits), BF16)], axis=0
    )
    packed = jnp.concatenate(
        [
            permute(packed, direct_target),
            packed,
            permute(packed, relayed_target),
            permute(packed, sibling_target),
            permute(packed, cross_target),
        ],
        axis=1,
    )
    feature_pad = -features % 16
    onehot = (
        jnp.arange(kinds, dtype=jnp.int32)[:, None].astype(BF16) == packed[features][None, :]
    ).astype(BF16)
    feats = jnp.concatenate(
        [packed[:features], jnp.zeros((feature_pad, 5 * hits), BF16), onehot], axis=0
    )
    wcat = jnp.concatenate([w_enc, jnp.zeros((feature_pad, width), BF16), layer_table], axis=0)
    depth = wcat.shape[0]

    tile_spec = pl.BlockSpec((group, slots, rows, rows), lambda i, *_: (i, 0, 0, 0))
    row_spec = pl.BlockSpec((span, width), lambda i, *_: (i, 0))
    weight_spec = full((width, width))
    any_spec = pl.BlockSpec(memory_space=pl.ANY)
    row_shape = jax.ShapeDtypeStruct((hits, width), BF16)
    weight_shape = jax.ShapeDtypeStruct((width, width), F32)

    before0, agg0, hidden0, latents = pl.pallas_call(
        functools.partial(first_forward, group),
        grid_spec=pltpu.PrefetchScalarGridSpec(
            num_scalar_prefetch=1,
            grid=(steps,),
            in_specs=[tile_spec, full((depth, 5 * hits)), full((depth, width))] + [weight_spec] * 3,
            out_specs=[row_spec] * 4,
            scratch_shapes=[pltpu.VMEM((5 * hits + rows, width), BF16)],
        ),
        out_shape=[row_shape] * 4,
        compiler_params=params(),
        name="first_forward",
    )(index, edge_tiles, feats, wcat, w_self[0], w_agg[0], w_out[0])
    wide_shape = jax.ShapeDtypeStruct((hits, width), F32)
    pieces, lists = window_pieces(latents, keys)
    latents1 = latents
    agg1, hidden1, latents2 = pl.pallas_call(
        functools.partial(later_forward, group),
        grid_spec=pltpu.PrefetchScalarGridSpec(
            num_scalar_prefetch=1,
            grid=(steps,),
            in_specs=[tile_spec] + [any_spec] * 5 + [weight_spec] * 3,
            out_specs=[row_spec] * 3,
            scratch_shapes=[
                pltpu.VMEM((5 * hits + rows, width), BF16),
                pltpu.SemaphoreType.DMA((5,)),
            ],
        ),
        out_shape=[row_shape] * 2 + [wide_shape],
        compiler_params=params(),
        name="later_forward",
    )(index, edge_tiles, *pieces, w_self[1], w_agg[1], w_out[1])

    lists = jnp.concatenate([keys[None], lists], axis=0)
    odd_core, odd_pair = me % 2, (me // 2) % 2
    bounds = []
    for j, k in enumerate(
        (2, 1 + 2 * odd_core, 3 - 2 * odd_core, 4 * odd_pair, 4 - 4 * odd_pair)
    ):
        bounds.append(lax.dynamic_slice(lists[j, listed], (k,), (2,)))
    bounds = jnp.concatenate(bounds)
    lists = lists[:, :listed].reshape(-1)
    move_shape = jax.ShapeDtypeStruct((triplets, width), BF16)
    wide_move = jax.ShapeDtypeStruct((triplets, width), F32)
    move_spec = full((triplets, width))
    *found, anchors = pl.pallas_call(
        gather_kernel,
        grid_spec=pltpu.PrefetchScalarGridSpec(
            num_scalar_prefetch=3,
            grid=(1,),
            in_specs=[full((hits, width))],
            out_specs=[move_spec] * 6,
            scratch_shapes=[pltpu.VMEM((2 * triplets + 8, width), F32)],
        ),
        out_shape=[move_shape] * 6,
        compiler_params=params(),
        name="gather",
    )(lists, bounds, anchor_hits, latents2)
    vmem = pl.BlockSpec(memory_space=pltpu.VMEM)
    coef_shape = (triplets // 128, 128)
    loss_part, ganchor, *moves, coef, coefs = pl.pallas_call(
        functools.partial(contrast_kernel, 1.0 / math.sqrt(width)),
        in_specs=[vmem] * 6,
        out_specs=[vmem] * 8,
        out_shape=[jax.ShapeDtypeStruct((8, width), F32), wide_move]
        + [move_shape] * 4
        + [jax.ShapeDtypeStruct(coef_shape, F32), jax.ShapeDtypeStruct((4,) + coef_shape, F32)],
        scratch_shapes=[pltpu.VMEM((triplets, width), F32)]
        + [pltpu.VMEM((triplets, width), BF16)] * 6
        + [pltpu.SemaphoreType.DMA((PARTS,))] * 16
        + [pltpu.SemaphoreType.DMA((4,))] * 2,
        compiler_params=pltpu.CompilerParams(
            collective_id=4, has_side_effects=True, vmem_limit_bytes=VMEM_BYTES
        ),
        name="contrast",
    )(*found, anchors)

    t_shape = jax.ShapeDtypeStruct((blocks, width, rows), F32)
    t_half = jax.ShapeDtypeStruct((blocks, width, rows), BF16)
    t_full = pl.BlockSpec(
        (blocks, width, rows), lambda *_: (0, 0, 0), pipeline_mode=pl.Buffered(1)
    )
    adj_shape = pltpu.VMEM((5 * blocks + 1, width, rows), F32)
    gout1, gself1, gagg1, direct, obelow, own, oabove, osibling, ocross = pl.pallas_call(
        functools.partial(last_backward, group, steps),
        grid_spec=pltpu.PrefetchScalarGridSpec(
            num_scalar_prefetch=4,
            grid=(steps,),
            in_specs=[tile_spec, move_spec, full(coef_shape), full((4,) + coef_shape)]
            + [move_spec] * 5
            + [row_spec] * 3
            + [weight_spec] * 3,
            out_specs=[weight_spec] * 3 + [row_spec] + [t_full] * 5,
            scratch_shapes=[adj_shape, pltpu.VMEM((10 * triplets + 40, width), F32)]
            + [pltpu.VMEM((hits, width), F32)] * 4,
        ),
        out_shape=[weight_shape] * 3 + [wide_shape] + [t_shape] * 3 + [t_half] * 2,
        compiler_params=params(),
        name="last_backward",
    )(
        index, lists, bounds, anchor_hits, edge_tiles, ganchor, coef, coefs, anchors, *moves, hidden1, latents1, agg1,
        w_self[1], w_agg[1], w_out[1],
    )
    pairs = lax.axis_size("phi") // 2
    sum_chunk = -(-(6 * width + depth + 8) // (16 * pairs)) * 8
    sum_rows = 2 * pairs * sum_chunk
    one = pltpu.SemaphoreType.DMA((1,))
    many = pltpu.SemaphoreType.DMA((pairs - 1,))
    smem = pl.BlockSpec(memory_space=pltpu.SMEM)
    flat = (hits, width)
    gself, gagg, gout, tail = pl.pallas_call(
        functools.partial(back_kernel, pairs),
        in_specs=[smem] + [any_spec] * 10 + [vmem] * 10,
        out_specs=[vmem] * 4,
        out_shape=[jax.ShapeDtypeStruct((2, width, width), F32)] * 3
        + [jax.ShapeDtypeStruct((depth + 8, width), F32)],
        scratch_shapes=[pltpu.VMEM(flat, BF16)] * 6
        + [pltpu.VMEM(flat, F32)] * 4
        + [pltpu.VMEM(flat, BF16)] * 3
        + [
            pltpu.VMEM(edge_tiles.shape, BF16),
            pltpu.VMEM((5 * blocks + 1, width, rows), F32),
            pltpu.VMEM((5 * blocks + 1, depth, rows), BF16),
            pltpu.VMEM((sum_rows, width), F32),
            pltpu.VMEM((sum_rows // 2, width), F32),
            pltpu.VMEM((sum_rows // 2, width), F32),
            pltpu.VMEM((pairs - 1, sum_chunk, width), F32),
            pltpu.VMEM((sum_rows, width), F32),
            pltpu.SemaphoreType.DMA((8,)),
        ]
        + [pltpu.SemaphoreType.DMA((CHUNKS,))] * 6
        + [one, one, one, one, many, many, many, many, one, one],
        compiler_params=pltpu.CompilerParams(
            collective_id=3, has_side_effects=True, vmem_limit_bytes=VMEM_BYTES
        ),
        name="back",
    )(
        index, ocross.reshape(flat), osibling.reshape(flat), oabove.reshape(flat),
        obelow.reshape(flat), own.reshape(flat), direct, hidden0, before0, agg0, edge_tiles,
        feats, wcat, wcat.T, w_self[0], w_agg[0], w_out[0], gout1, gself1, gagg1, loss_part,
    )
    triplet_total = triplets * lax.axis_size("phi")
    loss = (tail[depth, 0] / triplet_total).reshape(1)
    return (loss, tail[:features], tail[depth - kinds : depth], gself, gagg, gout)


def solution(mesh):
    both = ("event", "phi")
    in_specs = (
        P(None, both),
        P(both),
        P(both, None, None, None),
        P(both, None),
        P(both),
        P(both),
        P(both),
        P(both),
        P(),
        P(),
        P(),
        P(),
        P(),
    )
    out_specs = (
        P("event"),
        P("event", None),
        P("event", None),
        P("event", None, None),
        P("event", None, None),
        P("event", None, None),
    )
    return jax.shard_map(body, mesh=mesh, in_specs=in_specs, out_specs=out_specs, check_vma=False)
```

```python
import functools
import math

import jax
import jax.numpy as jnp
from jax import lax
from jax.experimental import pallas as pl
from jax.experimental.pallas import tpu as pltpu
from jax.sharding import PartitionSpec as P

loss_divisor = 64.0
F32 = jnp.float32
BF16 = jnp.bfloat16
VMEM_BYTES = 60 * 1024 * 1024


def dot(left, right, left_dim, right_dim):
    return lax.dot_general(
        left, right, (((left_dim,), (right_dim,)), ((), ())), preferred_element_type=F32
    )


def full(shape):
    return pl.BlockSpec(shape, lambda *_: (0,) * len(shape))


def params():
    return pltpu.CompilerParams(
        dimension_semantics=("arbitrary",), vmem_limit_bytes=VMEM_BYTES
    )


CHUNKS = 8


def peers():
    count = lax.axis_size("phi")
    me = lax.axis_index("phi")
    odd_pair = (me // 2) % 2
    odd_core = me % 2
    direct = me + 2 - 4 * odd_pair
    sibling = me + 1 - 2 * odd_core
    stride = 4 - 8 * odd_pair
    onward = (me + stride + count) % count
    source = (me - stride + count) % count
    return direct, sibling, onward, source, odd_pair == odd_core


def remote(src, dst, send, recv, target):
    return pltpu.make_async_remote_copy(
        src_ref=src,
        dst_ref=dst,
        send_sem=send,
        recv_sem=recv,
        device_id={"phi": target},
        device_id_type=pl.DeviceIdType.MESH,
    )


def greet(targets):
    barrier = pltpu.get_barrier_semaphore()
    for target in targets:
        pl.semaphore_signal(
            barrier, inc=1, device_id={"phi": target}, device_id_type=pl.DeviceIdType.MESH
        )
    pl.semaphore_wait(barrier, len(targets))


def role_targets():
    count = lax.axis_size("phi")
    me = lax.axis_index("phi")
    odd_pair = (me // 2) % 2
    odd_core = me % 2
    sibling = me + 1 - 2 * odd_core
    across = (me - 1 + 2 * odd_core + count) % count
    direct = me + 2 - 4 * odd_pair
    far = (me - 2 + 4 * odd_pair + count) % count
    return sibling, across, direct, far


def aggregate_group(index_ref, tiles_ref, window_ref, step, group, slots, rows):
    results = []
    for g in range(group):
        tile = jnp.concatenate([tiles_ref[step * group + g, s] for s in range(slots)], axis=1)
        source = jnp.concatenate(
            [
                window_ref[index_ref[(step * group + g) * slots + s]] for s in range(slots)
            ],
            axis=0,
        )
        results.append(dot(tile, source, 1, 0).astype(BF16))
    return jnp.concatenate(results, axis=0)


def node_update(own, aggregated, w_self, w_agg, w_out):
    activation = dot(own, w_self, 1, 0) + dot(aggregated, w_agg, 1, 0)
    hidden = jnp.maximum(activation, 0.0).astype(BF16)
    updated = (own.astype(F32) + dot(hidden, w_out, 1, 0)).astype(BF16)
    return hidden, updated


FEAT_CHUNKS = 2


def forward_kernel(
    features,
    index_ref,
    packed_ref,
    keys_hbm,
    tiles_hbm,
    wcat_ref,
    w_self_ref,
    w_agg_ref,
    w_out_ref,
    before_out,
    agg0_out,
    hidden0_out,
    latents_out,
    agg1_out,
    hidden1_out,
    z_out,
    lists_out,
    feats_out,
    packs_ref,
    feats_ref,
    window_ref,
    later_ref,
    agg0_ref,
    hidden0_ref,
    agg1_ref,
    hidden1_ref,
    z_ref,
    tiles_ref,
    tile_sem,
    out_sem,
    late_sem,
    *sems,
):
    fys, fyr, fzs, fzr, fcs, fcr, ls, lr = sems[:8]
    ys, yr, zs, zr, cs, cr, ss, sr = sems[8:16]
    fss, fsr = sems[16:]
    direct, sibling, onward, source, direct_crosses = peers()
    roles = role_targets()
    blocks, slots, rows, _ = tiles_ref.shape
    hits = packed_ref.shape[1]
    width = wcat_ref.shape[1]
    group = blocks // CHUNKS
    span = group * rows

    def tile_load(i):
        part = pl.ds(i * group, group)
        return pltpu.make_async_copy(tiles_hbm.at[part], tiles_ref.at[part], tile_sem.at[i])

    lax.fori_loop(0, CHUNKS, lambda i, c: (tile_load(i).start(), c)[1], 0)
    greet((direct, sibling, onward, source, roles[1], roles[3]))
    columns = hits // FEAT_CHUNKS

    def pack(k, i):
        return packs_ref.at[k, :, pl.ds(i * columns, columns)]

    chunks = range(FEAT_CHUNKS)
    f_first = [
        remote(
            packed_ref.at[:, pl.ds(i * columns, columns)], pack(0, i), fys.at[i], fyr.at[i], direct
        )
        for i in chunks
    ]
    f_second = [remote(pack(0, i), pack(2, i), fzs.at[i], fzr.at[i], onward) for i in chunks]
    f_cross_a = [remote(pack(0, i), pack(4, i), fcs.at[i], fcr.at[i], sibling) for i in chunks]
    f_cross_b = [remote(pack(2, i), pack(4, i), fcs.at[i], fcr.at[i], sibling) for i in chunks]
    f_near = remote(packed_ref, packs_ref.at[3], fss.at[0], fsr.at[0], sibling)
    lists = [
        remote(keys_hbm, lists_out.at[j], ls.at[j], lr.at[j], target)
        for j, target in enumerate(roles)
    ]
    for copy in f_first:
        copy.start()
    f_near.start()
    for copy in lists:
        copy.start()

    def encode(k, ref):
        step = 512
        is_feature = lax.broadcasted_iota(jnp.int32, (16, step), 0) < features
        kind = lax.broadcasted_iota(jnp.int32, (16, step), 0).astype(F32)

        def run(i, carry):
            at = pl.multiple_of(i * step, step)
            data = ref[:, pl.ds(at, step)].astype(F32)
            onehot = jnp.where(kind == data[features : features + 1], 1.0, 0.0)
            feats = jnp.concatenate([jnp.where(is_feature, data, 0.0), onehot], axis=0).astype(BF16)
            feats_ref[:, pl.ds(pl.multiple_of(k * hits + i * step, step), step)] = feats
            encoded = dot(feats, wcat_ref[...], 0, 0)
            squashed = jnp.tanh(encoded).astype(BF16)
            for u in range(step // rows):
                window_ref[k * blocks + i * (step // rows) + u] = squashed[
                    u * rows : (u + 1) * rows
                ]
            return carry

        lax.fori_loop(0, hits // step, run, 0)

    encode(1, packed_ref)
    for i in chunks:
        f_first[i].wait_recv()
        f_second[i].start()

        @pl.when(direct_crosses)
        def _():
            f_cross_a[i].start()

    f_near.wait_recv()
    encode(3, packs_ref.at[3])
    encode(0, packs_ref.at[0])
    for i in chunks:
        f_second[i].wait_recv()

        @pl.when(jnp.logical_not(direct_crosses))
        def _():
            f_cross_b[i].start()

    encode(2, packs_ref.at[2])
    for i in chunks:
        f_cross_a[i].wait_recv()
    encode(4, packs_ref.at[4])
    window_ref[5 * blocks] = jnp.zeros((rows, width), BF16)
    later_ref[5 * blocks] = jnp.zeros((rows, width), BF16)

    def part(k, i):
        return pl.ds(k * blocks + i * group, group)

    def first(i):
        return remote(later_ref.at[part(1, i)], later_ref.at[part(0, i)], ys.at[i], yr.at[i], direct)

    def near(i):
        return remote(later_ref.at[part(1, i)], later_ref.at[part(3, i)], ss.at[i], sr.at[i], sibling)

    def second(i):
        return remote(later_ref.at[part(0, i)], later_ref.at[part(2, i)], zs.at[i], zr.at[i], onward)

    def cross_a(i):
        return remote(later_ref.at[part(0, i)], later_ref.at[part(4, i)], cs.at[i], cr.at[i], sibling)

    def cross_b(i):
        return remote(later_ref.at[part(2, i)], later_ref.at[part(4, i)], cs.at[i], cr.at[i], sibling)

    def relay(i):
        first(i).wait_recv()
        second(i).start()

        @pl.when(direct_crosses)
        def _():
            cross_a(i).start()

    lag = 3

    def layer0(i, carry):
        tile_load(i).wait()
        here = pl.ds(pl.multiple_of(i * span, span), span)
        aggregated = aggregate_group(index_ref, tiles_ref, window_ref, i, group, slots, rows)
        own = window_ref[part(1, i)].reshape(span, width)
        hidden, updated = node_update(own, aggregated, w_self_ref[0], w_agg_ref[0], w_out_ref[0])
        later_ref[part(1, i)] = updated.reshape(group, rows, width)
        first(i).start()
        near(i).start()
        agg0_ref[here, :] = aggregated
        hidden0_ref[here, :] = hidden

        @pl.when(i >= lag)
        def _():
            relay(i - lag)

        return carry

    lax.fori_loop(0, CHUNKS, layer0, 0)
    own = pl.ds(blocks, blocks)
    saves = [
        pltpu.make_async_copy(src, dst, out_sem.at[k])
        for k, (src, dst) in enumerate(
            (
                (window_ref.at[own], before_out),
                (agg0_ref, agg0_out),
                (hidden0_ref, hidden0_out),
                (later_ref.at[own], latents_out),
                (feats_ref, feats_out),
            )
        )
    ]
    for copy in saves:
        copy.start()

    def relay_rest(i, carry):
        relay(i)
        return carry

    lax.fori_loop(CHUNKS - lag, CHUNKS, relay_rest, 0)

    def land(i, carry):
        second(i).wait_recv()

        @pl.when(jnp.logical_not(direct_crosses))
        def _():
            cross_b(i).start()

        return carry

    lax.fori_loop(0, CHUNKS, land, 0)

    def settle(i, carry):
        near(i).wait()
        cross_a(i).wait_recv()
        return carry

    lax.fori_loop(0, CHUNKS, settle, 0)

    def late_saves(i):
        here = pl.ds(pl.multiple_of(i * span, span), span)
        return [
            pltpu.make_async_copy(src.at[here], dst.at[here], late_sem.at[k * CHUNKS + i])
            for k, (src, dst) in enumerate(
                ((agg1_ref, agg1_out), (hidden1_ref, hidden1_out), (z_ref, z_out))
            )
        ]

    def layer1(i, carry):
        here = pl.ds(pl.multiple_of(i * span, span), span)
        aggregated = aggregate_group(index_ref, tiles_ref, later_ref, i, group, slots, rows)
        own = later_ref[part(1, i)].reshape(span, width)
        hidden, updated = node_update(own, aggregated, w_self_ref[1], w_agg_ref[1], w_out_ref[1])
        agg1_ref[here, :] = aggregated
        hidden1_ref[here, :] = hidden
        z_ref[here, :] = updated.astype(F32)
        for copy in late_saves(i):
            copy.start()
        return carry

    lax.fori_loop(0, CHUNKS, layer1, 0)

    def drain(i, carry):
        first(i).wait_send()
        second(i).wait_send()
        cross_a(i).wait_send()
        for copy in late_saves(i):
            copy.wait()
        return carry

    lax.fori_loop(0, CHUNKS, drain, 0)
    for i in chunks:
        f_first[i].wait_send()
        f_second[i].wait_send()
        f_cross_a[i].wait_send()
    f_near.wait_send()
    for copy in lists:
        copy.wait()
    for copy in saves:
        copy.wait()


def gather_kernel(list_ref, bound_ref, anchor_ref, z_ref, *refs):
    outs, (anchor_out, buf_ref) = refs[:5], refs[5:]
    triplets, width = anchor_out.shape
    stride = list_ref.shape[0] // 5

    def anchors(i, carry):
        at = pl.multiple_of(i * 16, 16)
        anchor_out[pl.ds(at, 16), :] = jnp.concatenate(
            [z_ref[pl.ds(anchor_ref[i * 16 + u], 1), :] for u in range(16)], axis=0
        ).astype(BF16)
        return carry

    lax.fori_loop(0, triplets // 16, anchors, 0)
    zeros = jnp.zeros((64, width), F32)

    def clear(i, carry):
        buf_ref[pl.ds(pl.multiple_of(i * 64, 64), 64), :] = zeros
        return carry

    lax.fori_loop(0, 2 * triplets // 64, clear, 0)
    for j in range(5):

        def fetch(i, carry, j=j):
            for u in range(8):
                entry = list_ref[j * stride + i * 8 + u]
                row = z_ref[pl.ds(lax.shift_right_logical(entry, ENTRY_BITS), 1), :]
                buf_ref[pl.ds(lax.bitwise_and(entry, ENTRY_MASK), 1), :] = row
            return carry

        lax.fori_loop(bound_ref[2 * j], bound_ref[2 * j + 1], fetch, 0)

        def subtract(i, carry, j=j):
            at = pl.multiple_of(i * 64, 64)
            value = buf_ref[pl.ds(triplets + at, 64), :] - buf_ref[pl.ds(at, 64), :]
            outs[j][pl.ds(at, 64), :] = value.astype(BF16)
            buf_ref[pl.ds(triplets + at, 64), :] = zeros
            buf_ref[pl.ds(at, 64), :] = zeros
            return carry

        lax.fori_loop(0, triplets // 64, subtract, 0)


ENTRY_BITS = 12
ENTRY_MASK = (1 << ENTRY_BITS) - 1
PARTS = 4


def contrast_kernel(
    inv_root,
    self_ref,
    sib_ref,
    cross_ref,
    near_ref,
    far_ref,
    anchor_ref,
    loss_ref,
    ganchor_ref,
    asib_ref,
    across_ref,
    adirect_ref,
    afar_ref,
    coef_out,
    coefs_out,
    change_ref,
    sib_in,
    cross_in,
    far_send,
    far_in,
    near_send,
    near_in,
    *sems,
):
    s = [sems[2 * i : 2 * i + 2] for i in range(9)]
    direct, sibling, onward, source, near_adds = peers()
    roles = role_targets()
    size = anchor_ref.shape[0] // PARTS
    greet((direct, sibling, onward, source, roles[1], roles[3]))

    def rows(i):
        return pl.ds(i * size, size)

    def copies(k, src, dst, target):
        return [
            remote(src.at[rows(i)], dst.at[rows(i)], s[k][0].at[i], s[k][1].at[i], target)
            for i in range(PARTS)
        ]

    crosses = copies(0, cross_ref, cross_in, sibling)
    sibs = copies(1, sib_ref, sib_in, sibling)
    hops = copies(2, far_send, far_in, source)
    nears = copies(3, near_send, near_in, direct)
    to_direct = copies(4, anchor_ref, adirect_ref, direct)
    to_sibling = copies(5, anchor_ref, asib_ref, sibling)
    relays = copies(6, adirect_ref, afar_ref, onward)
    cross_a = copies(7, adirect_ref, across_ref, sibling)
    cross_b = copies(7, afar_ref, across_ref, sibling)
    coefs = [
        remote(coef_out, coefs_out.at[j], s[8][0].at[j], s[8][1].at[j], target)
        for j, target in enumerate(roles)
    ]
    for copy in crosses:
        copy.start()
    for copy in sibs:
        copy.start()
    for i in range(PARTS):
        crosses[i].wait_recv()
        extra = jnp.where(near_adds, 0.0, cross_in[rows(i), :].astype(F32))
        far_send[rows(i), :] = (far_ref[rows(i), :].astype(F32) + extra).astype(BF16)
        hops[i].start()
    for i in range(PARTS):
        to_direct[i].start()
        hops[i].wait_recv()
        extra = jnp.where(near_adds, cross_in[rows(i), :].astype(F32), 0.0)
        near_send[rows(i), :] = (
            near_ref[rows(i), :].astype(F32) + extra + far_in[rows(i), :].astype(F32)
        ).astype(BF16)
        nears[i].start()
    for i in range(PARTS):
        to_sibling[i].start()
        to_direct[i].wait_recv()
        relays[i].start()

        @pl.when(near_adds)
        def _():
            cross_a[i].start()

    gaps = []
    for i in range(PARTS):
        sibs[i].wait_recv()
        nears[i].wait_recv()
        change = (
            near_in[rows(i), :].astype(F32)
            + self_ref[rows(i), :].astype(F32)
            + sib_in[rows(i), :].astype(F32)
        )
        change_ref[rows(i), :] = change
        product = anchor_ref[rows(i), :].astype(F32) * change
        for u in range(size // 128):
            gaps.append(
                jnp.sum(product[u * 128 : (u + 1) * 128].T, axis=0, keepdims=True) * inv_root
            )
    gap = jnp.concatenate(gaps, axis=0)
    coef_out[...] = jax.nn.sigmoid(gap) * (inv_root / loss_divisor)
    for copy in coefs:
        copy.start()
    soft = jnp.maximum(gap, 0.0) + jnp.log1p(jnp.exp(-jnp.abs(gap)))
    loss_ref[...] = jnp.broadcast_to(jnp.sum(soft, keepdims=True), loss_ref.shape)
    for i in range(PARTS):
        relays[i].wait_recv()

        @pl.when(jnp.logical_not(near_adds))
        def _():
            cross_b[i].start()

    size = 128
    eye = lax.broadcasted_iota(jnp.int32, (size, size), 0) == lax.broadcasted_iota(
        jnp.int32, (size, size), 1
    )
    for i in range(coef_out.shape[0]):
        coef = coef_out[pl.ds(i, 1), :]
        column = jnp.sum(jnp.where(eye, coef, 0.0), axis=1, keepdims=True)
        here = pl.ds(i * size, size)
        ganchor_ref[here, :] = column * change_ref[here, :]
    for copy in coefs:
        copy.wait()
    for i in range(PARTS):
        crosses[i].wait_send()
        sibs[i].wait_send()
        hops[i].wait_send()
        nears[i].wait_send()
        to_direct[i].wait_send()
        to_sibling[i].wait()
        relays[i].wait_send()
        cross_a[i].wait()


def node_backward(
    gradient, hidden_ref, before_ref, agg_ref, w_out, gout_ref, gself_ref, gagg_ref, step
):
    upstream = gradient.astype(BF16)
    hidden = hidden_ref[...]
    hidden_grad = dot(upstream, w_out, 1, 1)
    act_grad = jnp.where(hidden.astype(F32) > 0, hidden_grad, 0.0).astype(BF16)

    @pl.when(step == 0)
    def _():
        gout_ref[...] = jnp.zeros(gout_ref.shape, F32)
        gself_ref[...] = jnp.zeros(gself_ref.shape, F32)
        gagg_ref[...] = jnp.zeros(gagg_ref.shape, F32)

    gout_ref[...] += dot(hidden, upstream, 0, 0)
    gself_ref[...] += dot(before_ref[...], act_grad, 0, 0)
    gagg_ref[...] += dot(agg_ref[...], act_grad, 0, 0)
    return act_grad


def spread_group(index_ref, tiles_ref, adj_ref, agg_grad_t, step, group, slots, rows):
    for g in range(group):
        tile = jnp.concatenate([tiles_ref[g, s] for s in range(slots)], axis=1)
        contrib = dot(agg_grad_t[:, g * rows : (g + 1) * rows], tile, 1, 0)
        for s in range(slots):
            at = index_ref[(step * group + g) * slots + s]
            adj_ref[at] = adj_ref[at] + contrib[:, s * rows : (s + 1) * rows]


def clear_blocks(adj_ref):
    def clear(i, carry):
        adj_ref[i] = jnp.zeros(adj_ref.shape[1:], F32)
        return carry

    lax.fori_loop(0, adj_ref.shape[0], clear, 0)


def scatter_rows(
    list_ref, bound_ref, anchor_ref, ganchor_ref, coef_ref, coefs_ref, rows_in, moved_ref, sums
):
    triplets, width = ganchor_ref.shape
    hits = sums[0].shape[0]
    stride = list_ref.shape[0] // 5
    span = 2 * triplets + 8
    zeros = jnp.zeros((64, width), F32)

    def clear(i, carry):
        for target in sums:
            target[pl.ds(pl.multiple_of(i * 64, 64), 64), :] = zeros
        return carry

    lax.fori_loop(0, hits // 64, clear, 0)
    eye = lax.broadcasted_iota(jnp.int32, (128, 128), 0) == lax.broadcasted_iota(
        jnp.int32, (128, 128), 1
    )
    for j, source in enumerate(rows_in):
        for i in range(triplets // 128):
            coef = coef_ref[pl.ds(i, 1), :] if j == 0 else coefs_ref[j - 1, pl.ds(i, 1), :]
            spread = jnp.where(eye, coef, 0.0)
            high = spread.astype(BF16)
            low = (spread - high.astype(F32)).astype(BF16)
            part = source[pl.ds(i * 128, 128), :]
            value = dot(high, part, 1, 0) + dot(low, part, 1, 0)
            moved_ref[pl.ds(j * span + i * 128, 128), :] = -value
            moved_ref[pl.ds(j * span + triplets + i * 128, 128), :] = value
        moved_ref[pl.ds(j * span + 2 * triplets, 8), :] = zeros[:8]

    def anchors(i, carry):
        for u in range(8):
            t = i * 8 + u
            here = pl.ds(anchor_ref[t], 1)
            target = sums[u % 4]
            target[here, :] = target[here, :] + ganchor_ref[pl.ds(t, 1), :]
        return carry

    lax.fori_loop(0, triplets // 8, anchors, 0)
    for j in range(5):

        def add(i, carry, j=j):
            for u in range(8):
                entry = list_ref[j * stride + i * 8 + u]
                here = pl.ds(lax.shift_right_logical(entry, ENTRY_BITS), 1)
                target = sums[u % 4]
                moved = moved_ref[pl.ds(j * span + lax.bitwise_and(entry, ENTRY_MASK), 1), :]
                target[here, :] = target[here, :] + moved
            return carry

        lax.fori_loop(bound_ref[2 * j], bound_ref[2 * j + 1], add, 0)


def last_backward(
    group,
    steps,
    index_ref,
    list_ref,
    bound_ref,
    anchor_ref,
    tiles_ref,
    ganchor_ref,
    coef_ref,
    coefs_ref,
    aself_ref,
    asib_ref,
    across_ref,
    adirect_ref,
    afar_ref,
    hidden_ref,
    before_ref,
    agg_ref,
    w_self_ref,
    w_agg_ref,
    w_out_ref,
    gout_ref,
    gself_ref,
    gagg_ref,
    direct_ref,
    obelow_ref,
    oown_ref,
    oabove_ref,
    osibling_ref,
    ocross_ref,
    adj_ref,
    moved_ref,
    *sums,
):
    step = pl.program_id(0)
    slots, rows = tiles_ref.shape[1], tiles_ref.shape[2]
    span = group * rows

    @pl.when(step == 0)
    def _():
        clear_blocks(adj_ref)
        scatter_rows(
            list_ref, bound_ref, anchor_ref, ganchor_ref, coef_ref, coefs_ref,
            (aself_ref, asib_ref, across_ref, adirect_ref, afar_ref), moved_ref, sums,
        )

    here = pl.ds(pl.multiple_of(step * span, span), span)
    gradient = (sums[0][here, :] + sums[1][here, :]) + (sums[2][here, :] + sums[3][here, :])
    act_grad = node_backward(
        gradient, hidden_ref, before_ref, agg_ref, w_out_ref[...], gout_ref, gself_ref, gagg_ref, step
    )
    direct_ref[...] = gradient + dot(act_grad, w_self_ref[...], 1, 1)
    agg_grad_t = dot(w_agg_ref[...], act_grad, 1, 1).astype(BF16)
    spread_group(index_ref, tiles_ref, adj_ref, agg_grad_t, step, group, slots, rows)

    @pl.when(step == steps - 1)
    def _():
        blocks = oown_ref.shape[0]
        for k, target in enumerate((obelow_ref, oown_ref, oabove_ref, osibling_ref, ocross_ref)):

            def store(i, carry, k=k, target=target):
                target[i] = adj_ref[k * blocks + i].astype(target.dtype)
                return carry

            lax.fori_loop(0, blocks, store, 0)


def back_kernel(
    pairs,
    index_ref,
    cross_hbm,
    sib_hbm,
    relay_hbm,
    direct_hbm,
    own_hbm,
    grad_hbm,
    hidden_hbm,
    before_hbm,
    agg_hbm,
    tiles_hbm,
    feats_ref,
    wcat_ref,
    wcat_t_ref,
    w_self_ref,
    w_agg_ref,
    w_out_ref,
    gout1_ref,
    gself1_ref,
    gagg1_ref,
    loss_ref,
    gself_out,
    gagg_out,
    gout_out,
    tail_out,
    cross_in,
    sib_in,
    relay_in,
    total_in,
    relay_send,
    direct_send,
    relay_ref,
    direct_ref,
    own_ref,
    grad_ref,
    hidden_ref,
    before_ref,
    agg_ref,
    tiles_ref,
    slope_ref,
    block_feats_ref,
    x_ref,
    half_in,
    acc_ref,
    slots_in,
    all_ref,
    local_sem,
    *sems,
):
    ys, yr, zs, zr, cs, cr, ss, sr, s0, r0, s1, r1, s2, r2, s3, r3 = sems
    direct, sibling, onward, source, to_direct = peers()
    me = lax.axis_index("phi")
    pair, core = me // 2, me % 2
    others = [((pair + d) % pairs) * 2 + core for d in range(1, pairs)]
    blocks, slots, rows, _ = tiles_ref.shape
    depth, width = wcat_ref.shape
    window = feats_ref.shape[1] // rows
    size = grad_ref.shape[0] // CHUNKS
    group = blocks // CHUNKS
    loads = [
        pltpu.make_async_copy(src, dst, local_sem.at[k])
        for k, (src, dst) in enumerate(
            (
                (relay_hbm, relay_ref),
                (direct_hbm, direct_ref),
                (own_hbm, own_ref),
                (grad_hbm, grad_ref),
                (hidden_hbm, hidden_ref),
                (before_hbm, before_ref),
                (agg_hbm, agg_ref),
                (tiles_hbm, tiles_ref),
            )
        )
    ]
    for copy in loads:
        copy.start()
    greet([sibling] + others)

    def span(i):
        return pl.ds(pl.multiple_of(i * size, size), size)

    def crosses(i):
        return remote(cross_hbm.at[span(i)], cross_in.at[span(i)], cs.at[i], cr.at[i], sibling)

    def first(i):
        return remote(relay_send.at[span(i)], relay_in.at[span(i)], zs.at[i], zr.at[i], source)

    def second(i):
        return remote(direct_send.at[span(i)], total_in.at[span(i)], ys.at[i], yr.at[i], direct)

    near = remote(sib_hbm, sib_in, ss.at[0], sr.at[0], sibling)
    lax.fori_loop(0, CHUNKS, lambda i, c: (crosses(i).start(), c)[1], 0)
    near.start()

    per = window // (2 * CHUNKS)

    def slopes(i):
        for u in range(0, per, 2):
            at = pl.multiple_of((i * per + u) * rows, 2 * rows)
            feats = feats_ref[:, pl.ds(at, 2 * rows)]
            squashed = jnp.tanh(dot(wcat_t_ref[...], feats, 1, 0))
            slope = 1.0 - squashed * squashed
            for v in range(2):
                slope_ref[i * per + u + v] = slope[:, v * rows : (v + 1) * rows]
                block_feats_ref[i * per + u + v] = feats[:, v * rows : (v + 1) * rows]

    x_ref[...] = jnp.zeros(x_ref.shape, F32)
    for k, value in enumerate((gout1_ref, gself1_ref, gagg1_ref)):
        x_ref[(2 * k + 1) * width : (2 * k + 2) * width, :] = value[...]
    base = 6 * width
    x_ref[base + depth : base + depth + 8, :] = loss_ref[...]
    slope_ref[window] = jnp.zeros(slope_ref.shape[1:], F32)
    block_feats_ref[window] = jnp.zeros(block_feats_ref.shape[1:], BF16)
    loads[0].wait()

    def relay_step(i, carry):
        here = span(i)
        crosses(i).wait_recv()
        extra = jnp.where(to_direct, 0.0, cross_in[here, :].astype(F32))
        relay_send[here, :] = (relay_ref[here, :] + extra).astype(BF16)
        first(i).start()
        slopes(i)
        return carry

    lax.fori_loop(0, CHUNKS, relay_step, 0)
    loads[1].wait()

    def direct_step(i, carry):
        here = span(i)
        first(i).wait_recv()
        extra = jnp.where(to_direct, cross_in[here, :].astype(F32), 0.0)
        direct_send[here, :] = (
            direct_ref[here, :] + extra + relay_in[here, :].astype(F32)
        ).astype(BF16)
        second(i).start()
        slopes(CHUNKS + i)
        return carry

    lax.fori_loop(0, CHUNKS, direct_step, 0)
    for copy in loads[2:]:
        copy.wait()
    near.wait()

    def layer_step(i, carry):
        here = span(i)
        second(i).wait_recv()
        returned = own_ref[here, :] + (
            total_in[here, :].astype(F32) + sib_in[here, :].astype(F32)
        )
        gradient = grad_ref[here, :] + jnp.concatenate(
            [returned[g * width : (g + 1) * width].T for g in range(group)], axis=0
        )
        upstream = gradient.astype(BF16)
        hidden = hidden_ref[here, :]
        hidden_grad = dot(upstream, w_out_ref[...], 1, 1)
        act_grad = jnp.where(hidden.astype(F32) > 0, hidden_grad, 0.0).astype(BF16)
        agg_grad_t = dot(w_agg_ref[...], act_grad, 1, 1).astype(BF16)
        x_ref[0:width, :] += dot(hidden, upstream, 0, 0)
        x_ref[2 * width : 3 * width, :] += dot(before_ref[here, :], act_grad, 0, 0)
        x_ref[4 * width : 5 * width, :] += dot(agg_ref[here, :], act_grad, 0, 0)
        own_grad = gradient + dot(act_grad, w_self_ref[...], 1, 1)
        feats = feats_ref[:, pl.ds(pl.multiple_of((window // 5) * rows + i * size, size), size)]
        squashed = jnp.tanh(dot(feats, wcat_ref[...], 0, 0))
        genc = dot(feats, (own_grad * (1.0 - squashed * squashed)).astype(BF16), 1, 0)
        for g in range(group):
            block = i * group + g
            tile = jnp.concatenate([tiles_ref[block, s] for s in range(slots)], axis=1)
            contrib = dot(agg_grad_t[:, g * rows : (g + 1) * rows], tile, 1, 0)
            places = [index_ref[block * slots + s] for s in range(slots)]
            slope = jnp.concatenate([slope_ref[at] for at in places], axis=1)
            source_feats = jnp.concatenate([block_feats_ref[at] for at in places], axis=1)
            genc = genc + dot(source_feats, (contrib * slope).astype(BF16), 1, 1)
        x_ref[base : base + depth, :] += genc
        return carry

    lax.fori_loop(0, CHUNKS, layer_step, 0)

    def drain(i, carry):
        crosses(i).wait_send()
        first(i).wait_send()
        second(i).wait_send()
        return carry

    lax.fori_loop(0, CHUNKS, drain, 0)

    half = x_ref.shape[0] // 2
    chunk = half // pairs

    def part(start, length):
        return pl.ds(pl.multiple_of(start, 8), length)

    swap = remote(x_ref.at[part((1 - core) * half, half)], half_in, s0.at[0], r0.at[0], sibling)
    swap.start()
    swap.wait()
    acc_ref[...] = x_ref[part(core * half, half), :] + half_in[...]
    scatter = [
        remote(
            acc_ref.at[part(((pair + d) % pairs) * chunk, chunk)],
            slots_in.at[d - 1],
            s1.at[d - 1],
            r1.at[d - 1],
            others[d - 1],
        )
        for d in range(1, pairs)
    ]
    for copy in scatter:
        copy.start()
    total = acc_ref[part(pair * chunk, chunk), :]
    for d in range(1, pairs):
        scatter[d - 1].wait_recv()
        total = total + slots_in[d - 1]
    mine = part(core * half + pair * chunk, chunk)
    all_ref[mine, :] = total
    gather = [
        remote(all_ref.at[mine], all_ref.at[mine], s2.at[d - 1], r2.at[d - 1], others[d - 1])
        for d in range(1, pairs)
    ]
    for copy in gather:
        copy.start()
    for copy in gather:
        copy.wait()
    for copy in scatter:
        copy.wait_send()
    whole = part(core * half, half)
    last = remote(all_ref.at[whole], all_ref.at[whole], s3.at[0], r3.at[0], sibling)
    last.start()
    last.wait()
    for k, out in enumerate((gout_out, gself_out, gagg_out)):
        for layer in range(2):
            at = (2 * k + layer) * width
            out[layer] = all_ref[at : at + width, :]
    tail_out[...] = all_ref[base : base + depth + 8, :]


def body(
    hit_feats,
    layer_ids,
    edge_tiles,
    src_blocks,
    live_slots,
    anchor_hits,
    positive_hits,
    negative_hits,
    w_enc,
    layer_table,
    w_self,
    w_agg,
    w_out,
):
    blocks, slots, rows, _ = edge_tiles.shape
    width = w_enc.shape[1]
    features = hit_feats.shape[0]
    kinds = layer_table.shape[0]
    hits = blocks * rows
    layer_total = w_self.shape[0]
    triplets = anchor_hits.shape[0]
    group = 4
    steps = blocks // group
    span = group * rows
    me = lax.axis_index("phi")
    is_even = me % 2 == 0
    even_pair = (me // 2) % 2 == 0

    def place(part):
        spots = (
            jnp.where(even_pair, 2, 0),
            jnp.where(is_even, 4, 3),
            1,
            jnp.where(is_even, 3, 4),
            jnp.where(even_pair, 0, 2),
        )
        return sum(jnp.where(part == k, spot, 0) for k, spot in enumerate(spots))

    live = jnp.arange(slots, dtype=jnp.int32)[None, :] < live_slots[:, None]
    index = jnp.where(
        live, place(src_blocks // blocks) * blocks + src_blocks % blocks, 5 * blocks
    ).reshape(blocks * slots)
    wanted = jnp.concatenate([positive_hits, negative_hits])
    keys = wanted * (2 * triplets) + jnp.arange(2 * triplets, dtype=jnp.int32)
    ranks = jnp.sum((keys[None, :] < keys[:, None]).astype(jnp.int32), axis=1)
    owner = wanted // hits
    counts = jnp.sum(
        (owner[None, :] == jnp.arange(8, dtype=jnp.int32)[:, None]).astype(jnp.int32), axis=1
    )
    padded = -(-counts // 8) * 8
    earlier = jnp.arange(8)[:, None] > jnp.arange(8)[None, :]
    aligned = jnp.sum(jnp.where(earlier, padded[None, :], 0), axis=1)
    shift = aligned - jnp.sum(jnp.where(earlier, counts[None, :], 0), axis=1)
    place_of = ranks + sum(jnp.where(owner == k, shift[k], 0) for k in range(5))
    listed = 2 * triplets // 128 + 1
    places = jnp.arange(listed * 128, dtype=jnp.int32)
    slot = jnp.arange(2 * triplets, dtype=jnp.int32)
    entry = (wanted % hits) * (1 << ENTRY_BITS) + slot - 2 * triplets
    entries = jnp.sum(
        jnp.where(place_of[None, :] == places[:, None], entry[None, :], 0), axis=1
    ) + 2 * triplets
    starts = jnp.pad((aligned // 8).reshape(1, 8), ((0, 6), (0, 120)))
    keys = jnp.concatenate([entries.reshape(listed, 128), starts], axis=0)
    pad = -(features + 1) % 16
    packed = jnp.concatenate(
        [hit_feats, layer_ids.astype(BF16)[None, :], jnp.zeros((pad, hits), BF16)], axis=0
    )
    feature_pad = -features % 16
    wcat = jnp.concatenate([w_enc, jnp.zeros((feature_pad, width), BF16), layer_table], axis=0)
    depth = wcat.shape[0]

    tile_spec = pl.BlockSpec((group, slots, rows, rows), lambda i, *_: (i, 0, 0, 0))
    row_spec = pl.BlockSpec((span, width), lambda i, *_: (i, 0))
    weight_spec = full((width, width))
    any_spec = pl.BlockSpec(memory_space=pl.ANY)
    row_shape = jax.ShapeDtypeStruct((hits, width), BF16)
    weight_shape = jax.ShapeDtypeStruct((width, width), F32)

    wide_shape = jax.ShapeDtypeStruct((hits, width), F32)
    vmem = pl.BlockSpec(memory_space=pltpu.VMEM)
    smem = pl.BlockSpec(memory_space=pltpu.SMEM)
    few = pltpu.SemaphoreType.DMA((FEAT_CHUNKS,))
    each = pltpu.SemaphoreType.DMA((CHUNKS,))
    one = pltpu.SemaphoreType.DMA((1,))
    four = pltpu.SemaphoreType.DMA((4,))
    block_shape = jax.ShapeDtypeStruct((blocks, rows, width), BF16)
    before0, agg0, hidden0, latents1, agg1, hidden1, latents2, lists, feats = pl.pallas_call(
        functools.partial(forward_kernel, features),
        in_specs=[smem, vmem, any_spec, any_spec] + [vmem] * 4,
        out_specs=[any_spec] * 9,
        out_shape=[block_shape, row_shape, row_shape, block_shape, row_shape, row_shape]
        + [
            wide_shape,
            jax.ShapeDtypeStruct((4,) + keys.shape, keys.dtype),
            jax.ShapeDtypeStruct((depth, 5 * hits), BF16),
        ],
        scratch_shapes=[
            pltpu.VMEM((5,) + packed.shape, BF16),
            pltpu.VMEM((depth, 5 * hits), BF16),
            pltpu.VMEM((5 * blocks + 1, rows, width), BF16),
            pltpu.VMEM((5 * blocks + 1, rows, width), BF16),
        ]
        + [pltpu.VMEM((hits, width), BF16)] * 4
        + [
            pltpu.VMEM((hits, width), F32),
            pltpu.VMEM(edge_tiles.shape, BF16),
            each,
            pltpu.SemaphoreType.DMA((5,)),
            pltpu.SemaphoreType.DMA((3 * CHUNKS,)),
        ]
        + [few] * 6
        + [four] * 2
        + [each] * 8
        + [one] * 2,
        compiler_params=pltpu.CompilerParams(
            collective_id=1, has_side_effects=True, vmem_limit_bytes=VMEM_BYTES
        ),
        name="forward",
    )(index, packed, keys, edge_tiles, wcat, w_self, w_agg, w_out)

    before0, latents1 = before0.reshape(hits, width), latents1.reshape(hits, width)
    lists = jnp.concatenate([keys[None], lists], axis=0)
    odd_core, odd_pair = me % 2, (me // 2) % 2
    bounds = []
    for j, k in enumerate(
        (2, 1 + 2 * odd_core, 3 - 2 * odd_core, 4 * odd_pair, 4 - 4 * odd_pair)
    ):
        bounds.append(lax.dynamic_slice(lists[j, listed], (k,), (2,)))
    bounds = jnp.concatenate(bounds)
    lists = lists[:, :listed].reshape(-1)
    move_shape = jax.ShapeDtypeStruct((triplets, width), BF16)
    wide_move = jax.ShapeDtypeStruct((triplets, width), F32)
    move_spec = full((triplets, width))
    *found, anchors = pl.pallas_call(
        gather_kernel,
        grid_spec=pltpu.PrefetchScalarGridSpec(
            num_scalar_prefetch=3,
            grid=(1,),
            in_specs=[full((hits, width))],
            out_specs=[move_spec] * 6,
            scratch_shapes=[pltpu.VMEM((2 * triplets + 8, width), F32)],
        ),
        out_shape=[move_shape] * 6,
        compiler_params=params(),
        name="gather",
    )(lists, bounds, anchor_hits, latents2)
    coef_shape = (triplets // 128, 128)
    loss_part, ganchor, *moves, coef, coefs = pl.pallas_call(
        functools.partial(contrast_kernel, 1.0 / math.sqrt(width)),
        in_specs=[vmem] * 6,
        out_specs=[vmem] * 8,
        out_shape=[jax.ShapeDtypeStruct((8, width), F32), wide_move]
        + [move_shape] * 4
        + [jax.ShapeDtypeStruct(coef_shape, F32), jax.ShapeDtypeStruct((4,) + coef_shape, F32)],
        scratch_shapes=[pltpu.VMEM((triplets, width), F32)]
        + [pltpu.VMEM((triplets, width), BF16)] * 6
        + [pltpu.SemaphoreType.DMA((PARTS,))] * 16
        + [pltpu.SemaphoreType.DMA((4,))] * 2,
        compiler_params=pltpu.CompilerParams(
            collective_id=4, has_side_effects=True, vmem_limit_bytes=VMEM_BYTES
        ),
        name="contrast",
    )(*found, anchors)

    t_shape = jax.ShapeDtypeStruct((blocks, width, rows), F32)
    t_half = jax.ShapeDtypeStruct((blocks, width, rows), BF16)
    t_full = pl.BlockSpec(
        (blocks, width, rows), lambda *_: (0, 0, 0), pipeline_mode=pl.Buffered(1)
    )
    adj_shape = pltpu.VMEM((5 * blocks + 1, width, rows), F32)
    gout1, gself1, gagg1, direct, obelow, own, oabove, osibling, ocross = pl.pallas_call(
        functools.partial(last_backward, group, steps),
        grid_spec=pltpu.PrefetchScalarGridSpec(
            num_scalar_prefetch=4,
            grid=(steps,),
            in_specs=[tile_spec, move_spec, full(coef_shape), full((4,) + coef_shape)]
            + [move_spec] * 5
            + [row_spec] * 3
            + [weight_spec] * 3,
            out_specs=[weight_spec] * 3 + [row_spec] + [t_full] * 5,
            scratch_shapes=[adj_shape, pltpu.VMEM((10 * triplets + 40, width), F32)]
            + [pltpu.VMEM((hits, width), F32)] * 4,
        ),
        out_shape=[weight_shape] * 3 + [wide_shape] + [t_shape] * 3 + [t_half] * 2,
        compiler_params=params(),
        name="last_backward",
    )(
        index, lists, bounds, anchor_hits, edge_tiles, ganchor, coef, coefs, anchors, *moves, hidden1, latents1, agg1,
        w_self[1], w_agg[1], w_out[1],
    )
    pairs = lax.axis_size("phi") // 2
    sum_chunk = -(-(6 * width + depth + 8) // (16 * pairs)) * 8
    sum_rows = 2 * pairs * sum_chunk
    many = pltpu.SemaphoreType.DMA((pairs - 1,))
    flat = (hits, width)
    gself, gagg, gout, tail = pl.pallas_call(
        functools.partial(back_kernel, pairs),
        in_specs=[smem] + [any_spec] * 10 + [vmem] * 10,
        out_specs=[vmem] * 4,
        out_shape=[jax.ShapeDtypeStruct((2, width, width), F32)] * 3
        + [jax.ShapeDtypeStruct((depth + 8, width), F32)],
        scratch_shapes=[pltpu.VMEM(flat, BF16)] * 6
        + [pltpu.VMEM(flat, F32)] * 4
        + [pltpu.VMEM(flat, BF16)] * 3
        + [
            pltpu.VMEM(edge_tiles.shape, BF16),
            pltpu.VMEM((5 * blocks + 1, width, rows), F32),
            pltpu.VMEM((5 * blocks + 1, depth, rows), BF16),
            pltpu.VMEM((sum_rows, width), F32),
            pltpu.VMEM((sum_rows // 2, width), F32),
            pltpu.VMEM((sum_rows // 2, width), F32),
            pltpu.VMEM((pairs - 1, sum_chunk, width), F32),
            pltpu.VMEM((sum_rows, width), F32),
            pltpu.SemaphoreType.DMA((8,)),
        ]
        + [pltpu.SemaphoreType.DMA((CHUNKS,))] * 6
        + [one, one, one, one, many, many, many, many, one, one],
        compiler_params=pltpu.CompilerParams(
            collective_id=3, has_side_effects=True, vmem_limit_bytes=VMEM_BYTES
        ),
        name="back",
    )(
        index, ocross.reshape(flat), osibling.reshape(flat), oabove.reshape(flat),
        obelow.reshape(flat), own.reshape(flat), direct, hidden0, before0, agg0, edge_tiles,
        feats, wcat, wcat.T, w_self[0], w_agg[0], w_out[0], gout1, gself1, gagg1, loss_part,
    )
    triplet_total = triplets * lax.axis_size("phi")
    loss = (tail[depth, 0] / triplet_total).reshape(1)
    return (loss, tail[:features], tail[depth - kinds : depth], gself, gagg, gout)


def solution(mesh):
    both = ("event", "phi")
    in_specs = (
        P(None, both),
        P(both),
        P(both, None, None, None),
        P(both, None),
        P(both),
        P(both),
        P(both),
        P(both),
        P(),
        P(),
        P(),
        P(),
        P(),
    )
    out_specs = (
        P("event"),
        P("event", None),
        P("event", None),
        P("event", None, None),
        P("event", None, None),
        P("event", None, None),
    )
    return jax.shard_map(body, mesh=mesh, in_specs=in_specs, out_specs=out_specs, check_vma=False)
```

```python
import functools
import math

import jax
import jax.numpy as jnp
from jax import lax
from jax.experimental import pallas as pl
from jax.experimental.pallas import tpu as pltpu
from jax.sharding import PartitionSpec as P

loss_divisor = 64.0
F32 = jnp.float32
BF16 = jnp.bfloat16
VMEM_BYTES = 60 * 1024 * 1024


def dot(left, right, left_dim, right_dim):
    return lax.dot_general(
        left, right, (((left_dim,), (right_dim,)), ((), ())), preferred_element_type=F32
    )


def full(shape):
    return pl.BlockSpec(shape, lambda *_: (0,) * len(shape))


def params():
    return pltpu.CompilerParams(
        dimension_semantics=("arbitrary",), vmem_limit_bytes=VMEM_BYTES
    )


CHUNKS = 8


def peers():
    count = lax.axis_size("phi")
    me = lax.axis_index("phi")
    odd_pair = (me // 2) % 2
    odd_core = me % 2
    direct = me + 2 - 4 * odd_pair
    sibling = me + 1 - 2 * odd_core
    stride = 4 - 8 * odd_pair
    onward = (me + stride + count) % count
    source = (me - stride + count) % count
    return direct, sibling, onward, source, odd_pair == odd_core


def remote(src, dst, send, recv, target):
    return pltpu.make_async_remote_copy(
        src_ref=src,
        dst_ref=dst,
        send_sem=send,
        recv_sem=recv,
        device_id={"phi": target},
        device_id_type=pl.DeviceIdType.MESH,
    )


def greet(targets):
    barrier = pltpu.get_barrier_semaphore()
    for target in targets:
        pl.semaphore_signal(
            barrier, inc=1, device_id={"phi": target}, device_id_type=pl.DeviceIdType.MESH
        )
    pl.semaphore_wait(barrier, len(targets))


def role_targets():
    count = lax.axis_size("phi")
    me = lax.axis_index("phi")
    odd_pair = (me // 2) % 2
    odd_core = me % 2
    sibling = me + 1 - 2 * odd_core
    across = (me - 1 + 2 * odd_core + count) % count
    direct = me + 2 - 4 * odd_pair
    far = (me - 2 + 4 * odd_pair + count) % count
    return sibling, across, direct, far


def aggregate_group(index_ref, tiles_ref, window_ref, step, group, slots, rows):
    results = []
    for g in range(group):
        tile = jnp.concatenate([tiles_ref[step * group + g, s] for s in range(slots)], axis=1)
        source = jnp.concatenate(
            [
                window_ref[index_ref[(step * group + g) * slots + s]] for s in range(slots)
            ],
            axis=0,
        )
        results.append(dot(tile, source, 1, 0).astype(BF16))
    return jnp.concatenate(results, axis=0)


def node_update(own, aggregated, w_self, w_agg, w_out):
    activation = dot(own, w_self, 1, 0) + dot(aggregated, w_agg, 1, 0)
    hidden = jnp.maximum(activation, 0.0).astype(BF16)
    updated = (own.astype(F32) + dot(hidden, w_out, 1, 0)).astype(BF16)
    return hidden, updated


FEAT_CHUNKS = 2


def forward_kernel(
    features,
    index_ref,
    hit_ref,
    id_ref,
    positive_ref,
    negative_ref,
    tiles_hbm,
    enc_ref,
    table_ref,
    w_self_ref,
    w_agg_ref,
    w_out_ref,
    before_out,
    agg0_out,
    hidden0_out,
    latents_out,
    agg1_out,
    hidden1_out,
    z_out,
    lists_out,
    feats_out,
    wcat_out,
    packed_ref,
    wcat_ref,
    keys_ref,
    key_cols,
    place_cols,
    entry_cols,
    packs_ref,
    feats_ref,
    window_ref,
    later_ref,
    agg0_ref,
    hidden0_ref,
    agg1_ref,
    hidden1_ref,
    z_ref,
    tiles_ref,
    tile_sem,
    out_sem,
    late_sem,
    list_sem,
    *sems,
):
    fys, fyr, fzs, fzr, fcs, fcr, ls, lr = sems[:8]
    ys, yr, zs, zr, cs, cr, ss, sr = sems[8:16]
    fss, fsr = sems[16:]
    direct, sibling, onward, source, direct_crosses = peers()
    roles = role_targets()
    blocks, slots, rows, _ = tiles_ref.shape
    hits = packed_ref.shape[1]
    group = blocks // CHUNKS
    span = group * rows

    def tile_load(i):
        part = pl.ds(i * group, group)
        return pltpu.make_async_copy(tiles_hbm.at[part], tiles_ref.at[part], tile_sem.at[i])

    lax.fori_loop(0, CHUNKS, lambda i, c: (tile_load(i).start(), c)[1], 0)
    kinds, width = table_ref.shape
    filler = jnp.zeros((16 - features, width), F32)
    wcat_ref[...] = jnp.concatenate(
        [enc_ref[...].astype(F32), filler, table_ref[...].astype(F32)], axis=0
    ).astype(BF16)

    def gather_input(i, carry):
        at = pl.ds(pl.multiple_of(i * 512, 512), 512)
        packed_ref[:, at] = jnp.concatenate(
            [
                hit_ref[:, at].astype(F32),
                id_ref[:, at].astype(F32),
                jnp.zeros((15 - features, 512), F32),
            ],
            axis=0,
        ).astype(BF16)
        return carry

    lax.fori_loop(0, hits // 512, gather_input, 0)
    greet((direct, sibling, onward, source, roles[1], roles[3]))
    columns = hits // FEAT_CHUNKS

    def pack(k, i):
        return packs_ref.at[k, :, pl.ds(i * columns, columns)]

    chunks = range(FEAT_CHUNKS)
    f_first = [
        remote(
            packed_ref.at[:, pl.ds(i * columns, columns)], pack(0, i), fys.at[i], fyr.at[i], direct
        )
        for i in chunks
    ]
    f_second = [remote(pack(0, i), pack(2, i), fzs.at[i], fzr.at[i], onward) for i in chunks]
    f_cross_a = [remote(pack(0, i), pack(4, i), fcs.at[i], fcr.at[i], sibling) for i in chunks]
    f_cross_b = [remote(pack(2, i), pack(4, i), fcs.at[i], fcr.at[i], sibling) for i in chunks]
    f_near = remote(packed_ref, packs_ref.at[3], fss.at[0], fsr.at[0], sibling)
    for copy in f_first:
        copy.start()
    f_near.start()

    def encode(k, ref):
        step = 512
        is_feature = lax.broadcasted_iota(jnp.int32, (16, step), 0) < features
        kind = lax.broadcasted_iota(jnp.int32, (16, step), 0).astype(F32)

        def run(i, carry):
            at = pl.multiple_of(i * step, step)
            data = ref[:, pl.ds(at, step)].astype(F32)
            onehot = jnp.where(kind == data[features : features + 1], 1.0, 0.0)
            feats = jnp.concatenate([jnp.where(is_feature, data, 0.0), onehot], axis=0).astype(BF16)
            feats_ref[:, pl.ds(pl.multiple_of(k * hits + i * step, step), step)] = feats
            encoded = dot(feats, wcat_ref[...], 0, 0)
            squashed = jnp.tanh(encoded).astype(BF16)
            for u in range(step // rows):
                window_ref[k * blocks + i * (step // rows) + u] = squashed[
                    u * rows : (u + 1) * rows
                ]
            return carry

        lax.fori_loop(0, hits // step, run, 0)

    encode(1, packed_ref)
    for i in chunks:
        f_first[i].wait_recv()
        f_second[i].start()

        @pl.when(direct_crosses)
        def _():
            f_cross_a[i].start()

    f_near.wait_recv()
    encode(3, packs_ref.at[3])
    encode(0, packs_ref.at[0])
    for i in chunks:
        f_second[i].wait_recv()

        @pl.when(jnp.logical_not(direct_crosses))
        def _():
            f_cross_b[i].start()

    encode(2, packs_ref.at[2])
    for i in chunks:
        f_cross_a[i].wait_recv()
    encode(4, packs_ref.at[4])
    window_ref[5 * blocks] = jnp.zeros((rows, width), BF16)
    later_ref[5 * blocks] = jnp.zeros((rows, width), BF16)

    def part(k, i):
        return pl.ds(k * blocks + i * group, group)

    def first(i):
        return remote(later_ref.at[part(1, i)], later_ref.at[part(0, i)], ys.at[i], yr.at[i], direct)

    def near(i):
        return remote(later_ref.at[part(1, i)], later_ref.at[part(3, i)], ss.at[i], sr.at[i], sibling)

    def second(i):
        return remote(later_ref.at[part(0, i)], later_ref.at[part(2, i)], zs.at[i], zr.at[i], onward)

    def cross_a(i):
        return remote(later_ref.at[part(0, i)], later_ref.at[part(4, i)], cs.at[i], cr.at[i], sibling)

    def cross_b(i):
        return remote(later_ref.at[part(2, i)], later_ref.at[part(4, i)], cs.at[i], cr.at[i], sibling)

    def relay(i):
        first(i).wait_recv()
        second(i).start()

        @pl.when(direct_crosses)
        def _():
            cross_a(i).start()

    lag = 3

    def layer0(i, carry):
        tile_load(i).wait()
        here = pl.ds(pl.multiple_of(i * span, span), span)
        aggregated = aggregate_group(index_ref, tiles_ref, window_ref, i, group, slots, rows)
        own = window_ref[part(1, i)].reshape(span, width)
        hidden, updated = node_update(own, aggregated, w_self_ref[0], w_agg_ref[0], w_out_ref[0])
        later_ref[part(1, i)] = updated.reshape(group, rows, width)
        first(i).start()
        near(i).start()
        agg0_ref[here, :] = aggregated
        hidden0_ref[here, :] = hidden

        @pl.when(i >= lag)
        def _():
            relay(i - lag)

        return carry

    lax.fori_loop(0, CHUNKS, layer0, 0)
    own = pl.ds(blocks, blocks)
    saves = [
        pltpu.make_async_copy(src, dst, out_sem.at[k])
        for k, (src, dst) in enumerate(
            (
                (window_ref.at[own], before_out),
                (agg0_ref, agg0_out),
                (hidden0_ref, hidden0_out),
                (later_ref.at[own], latents_out),
                (feats_ref, feats_out),
                (wcat_ref, wcat_out),
            )
        )
    ]
    for copy in saves:
        copy.start()

    wanted = jnp.concatenate([positive_ref[...], negative_ref[...]], axis=0)
    lines = wanted.shape[0]
    pairs_of = lines * 128
    line = lax.broadcasted_iota(jnp.int32, (lines, 128), 0)
    lane = lax.broadcasted_iota(jnp.int32, (lines, 128), 1)
    keys = wanted * pairs_of + (line * 128 + lane)
    tall = jnp.concatenate(
        [wanted.astype(F32), jnp.zeros((128 - lines, 128), F32)], axis=0
    ).T.astype(jnp.int32)
    down = lax.broadcasted_iota(jnp.int32, (128, 1), 0)
    counts = []
    for k in range(5):
        mine = jnp.logical_and(wanted >= k * hits, wanted < (k + 1) * hits)
        counted = jnp.sum(jnp.where(mine, 1.0, 0.0), axis=1, keepdims=True)
        counts.append(jnp.sum(counted, axis=0, keepdims=True).astype(jnp.int32))
    aligned, shift = [jnp.zeros((1, 1), jnp.int32)], [jnp.zeros((1, 1), jnp.int32)]
    for k in range(5):
        filled = lax.bitwise_and(counts[k] + 7, -8)
        aligned.append(aligned[k] + filled)
        shift.append(shift[k] + filled - counts[k])
    for c in range(lines):
        column = tall[:, c : c + 1]
        slot = down + c * 128
        moved = jnp.zeros((128, 1), jnp.int32)
        first_row = jnp.zeros((128, 1), jnp.int32)
        for k in range(5):
            mine = jnp.logical_and(column >= k * hits, column < (k + 1) * hits)
            moved = moved + jnp.where(mine, shift[k], 0)
            first_row = first_row + jnp.where(mine, k * hits, 0)
        entry = (column - first_row) * (1 << ENTRY_BITS) + slot - pairs_of
        key_cols[c] = jnp.broadcast_to(column * pairs_of + slot, (128, 128))
        place_cols[c] = jnp.broadcast_to(moved, (128, 128))
        entry_cols[c] = jnp.broadcast_to(entry, (128, 128))

    def rank(c, carry):
        column = key_cols[c]
        count = jnp.zeros((128, 128), F32)
        for r in range(lines):
            count = count + jnp.where(keys[r : r + 1] < column, 1.0, 0.0)
        total = jnp.sum(count, axis=1, keepdims=True).astype(jnp.int32)
        place_cols[c] = place_cols[c] + jnp.broadcast_to(total, (128, 128))
        return carry

    relay(CHUNKS - 3)
    lax.fori_loop(0, lines, rank, 0)
    relay(CHUNKS - 2)
    keys_ref[...] = jnp.zeros(keys_ref.shape, jnp.int32)

    def put(q, carry):
        target = lax.broadcasted_iota(jnp.int32, (128, 128), 1) + q * 128

        def match(c, total):
            return total + jnp.where(place_cols[c] == target, entry_cols[c], 0)

        total = lax.fori_loop(0, lines, match, jnp.zeros((128, 128), jnp.int32))
        found = jnp.sum(total.astype(F32), axis=0, keepdims=True).astype(jnp.int32)
        keys_ref[pl.ds(q, 1), :] = found + pairs_of
        return carry

    lax.fori_loop(0, (lines + 1) // 2, put, 0)
    relay(CHUNKS - 1)
    lax.fori_loop((lines + 1) // 2, lines + 1, put, 0)
    lane = lax.broadcasted_iota(jnp.int32, (1, 128), 1)
    keys_ref[pl.ds(lines + 1, 1), :] = sum(
        jnp.where(lane == k, aligned[k] // 8, 0) for k in range(6)
    )
    lists = [
        remote(keys_ref, lists_out.at[j + 1], ls.at[j], lr.at[j], target)
        for j, target in enumerate(roles)
    ]
    for copy in lists:
        copy.start()
    own_list = pltpu.make_async_copy(keys_ref, lists_out.at[0], list_sem.at[0])
    own_list.start()

    def land(i, carry):
        second(i).wait_recv()

        @pl.when(jnp.logical_not(direct_crosses))
        def _():
            cross_b(i).start()

        return carry

    lax.fori_loop(0, CHUNKS, land, 0)

    def settle(i, carry):
        near(i).wait()
        cross_a(i).wait_recv()
        return carry

    lax.fori_loop(0, CHUNKS, settle, 0)

    def late_saves(i):
        here = pl.ds(pl.multiple_of(i * span, span), span)
        return [
            pltpu.make_async_copy(src.at[here], dst.at[here], late_sem.at[k * CHUNKS + i])
            for k, (src, dst) in enumerate(
                ((agg1_ref, agg1_out), (hidden1_ref, hidden1_out), (z_ref, z_out))
            )
        ]

    def layer1(i, carry):
        here = pl.ds(pl.multiple_of(i * span, span), span)
        aggregated = aggregate_group(index_ref, tiles_ref, later_ref, i, group, slots, rows)
        own = later_ref[part(1, i)].reshape(span, width)
        hidden, updated = node_update(own, aggregated, w_self_ref[1], w_agg_ref[1], w_out_ref[1])
        agg1_ref[here, :] = aggregated
        hidden1_ref[here, :] = hidden
        z_ref[here, :] = updated.astype(F32)
        for copy in late_saves(i):
            copy.start()
        return carry

    lax.fori_loop(0, CHUNKS, layer1, 0)

    def drain(i, carry):
        first(i).wait_send()
        second(i).wait_send()
        cross_a(i).wait_send()
        for copy in late_saves(i):
            copy.wait()
        return carry

    lax.fori_loop(0, CHUNKS, drain, 0)
    for i in chunks:
        f_first[i].wait_send()
        f_second[i].wait_send()
        f_cross_a[i].wait_send()
    f_near.wait_send()
    own_list.wait()
    for copy in lists:
        copy.wait()
    for copy in saves:
        copy.wait()


def segments(list_ref, stride, listed):
    me = lax.axis_index("phi")
    odd_core, odd_pair = lax.rem(me, 2), lax.rem(lax.div(me, 2), 2)
    places = (2, 1 + 2 * odd_core, 3 - 2 * odd_core, 4 * odd_pair, 4 - 4 * odd_pair)
    starts = [j * stride + listed + k for j, k in enumerate(places)]
    return [(list_ref[at], list_ref[at + 1]) for at in starts]


def gather_kernel(list_ref, anchor_ref, z_ref, *refs):
    outs, (anchor_out, buf_ref) = refs[:5], refs[5:]
    triplets, width = anchor_out.shape
    stride = list_ref.shape[0] // 5
    bounds = segments(list_ref, stride, 2 * triplets + 128)

    def anchors(i, carry):
        at = pl.multiple_of(i * 16, 16)
        anchor_out[pl.ds(at, 16), :] = jnp.concatenate(
            [z_ref[pl.ds(anchor_ref[i * 16 + u], 1), :] for u in range(16)], axis=0
        ).astype(BF16)
        return carry

    lax.fori_loop(0, triplets // 16, anchors, 0)
    zeros = jnp.zeros((64, width), F32)

    def clear(i, carry):
        buf_ref[pl.ds(pl.multiple_of(i * 64, 64), 64), :] = zeros
        return carry

    lax.fori_loop(0, 2 * triplets // 64, clear, 0)
    for j in range(5):

        def fetch(i, carry, j=j):
            for u in range(8):
                entry = list_ref[j * stride + i * 8 + u]
                row = z_ref[pl.ds(lax.shift_right_logical(entry, ENTRY_BITS), 1), :]
                buf_ref[pl.ds(lax.bitwise_and(entry, ENTRY_MASK), 1), :] = row
            return carry

        lax.fori_loop(bounds[j][0], bounds[j][1], fetch, 0)

        def subtract(i, carry, j=j):
            at = pl.multiple_of(i * 64, 64)
            value = buf_ref[pl.ds(triplets + at, 64), :] - buf_ref[pl.ds(at, 64), :]
            outs[j][pl.ds(at, 64), :] = value.astype(BF16)
            buf_ref[pl.ds(triplets + at, 64), :] = zeros
            buf_ref[pl.ds(at, 64), :] = zeros
            return carry

        lax.fori_loop(0, triplets // 64, subtract, 0)


ENTRY_BITS = 12
ENTRY_MASK = (1 << ENTRY_BITS) - 1
PARTS = 4


def contrast_kernel(
    inv_root,
    self_ref,
    sib_ref,
    cross_ref,
    near_ref,
    far_ref,
    anchor_ref,
    loss_ref,
    ganchor_ref,
    asib_ref,
    across_ref,
    adirect_ref,
    afar_ref,
    coef_out,
    coefs_out,
    change_ref,
    sib_in,
    cross_in,
    far_send,
    far_in,
    near_send,
    near_in,
    *sems,
):
    s = [sems[2 * i : 2 * i + 2] for i in range(9)]
    direct, sibling, onward, source, near_adds = peers()
    roles = role_targets()
    size = anchor_ref.shape[0] // PARTS
    greet((direct, sibling, onward, source, roles[1], roles[3]))

    def rows(i):
        return pl.ds(i * size, size)

    def copies(k, src, dst, target):
        return [
            remote(src.at[rows(i)], dst.at[rows(i)], s[k][0].at[i], s[k][1].at[i], target)
            for i in range(PARTS)
        ]

    crosses = copies(0, cross_ref, cross_in, sibling)
    sibs = copies(1, sib_ref, sib_in, sibling)
    hops = copies(2, far_send, far_in, source)
    nears = copies(3, near_send, near_in, direct)
    to_direct = copies(4, anchor_ref, adirect_ref, direct)
    to_sibling = copies(5, anchor_ref, asib_ref, sibling)
    relays = copies(6, adirect_ref, afar_ref, onward)
    cross_a = copies(7, adirect_ref, across_ref, sibling)
    cross_b = copies(7, afar_ref, across_ref, sibling)
    coefs = [
        remote(coef_out, coefs_out.at[j], s[8][0].at[j], s[8][1].at[j], target)
        for j, target in enumerate(roles)
    ]
    for copy in crosses:
        copy.start()
    for copy in sibs:
        copy.start()
    for i in range(PARTS):
        crosses[i].wait_recv()
        extra = jnp.where(near_adds, 0.0, cross_in[rows(i), :].astype(F32))
        far_send[rows(i), :] = (far_ref[rows(i), :].astype(F32) + extra).astype(BF16)
        hops[i].start()
    for i in range(PARTS):
        to_direct[i].start()
        hops[i].wait_recv()
        extra = jnp.where(near_adds, cross_in[rows(i), :].astype(F32), 0.0)
        near_send[rows(i), :] = (
            near_ref[rows(i), :].astype(F32) + extra + far_in[rows(i), :].astype(F32)
        ).astype(BF16)
        nears[i].start()
    for i in range(PARTS):
        to_sibling[i].start()
        to_direct[i].wait_recv()
        relays[i].start()

        @pl.when(near_adds)
        def _():
            cross_a[i].start()

    gaps = []
    for i in range(PARTS):
        sibs[i].wait_recv()
        nears[i].wait_recv()
        change = (
            near_in[rows(i), :].astype(F32)
            + self_ref[rows(i), :].astype(F32)
            + sib_in[rows(i), :].astype(F32)
        )
        change_ref[rows(i), :] = change
        product = anchor_ref[rows(i), :].astype(F32) * change
        for u in range(size // 128):
            gaps.append(
                jnp.sum(product[u * 128 : (u + 1) * 128].T, axis=0, keepdims=True) * inv_root
            )
    gap = jnp.concatenate(gaps, axis=0)
    coef_out[...] = jax.nn.sigmoid(gap) * (inv_root / loss_divisor)
    for copy in coefs:
        copy.start()
    soft = jnp.maximum(gap, 0.0) + jnp.log1p(jnp.exp(-jnp.abs(gap)))
    loss_ref[...] = jnp.broadcast_to(jnp.sum(soft, keepdims=True), loss_ref.shape)
    for i in range(PARTS):
        relays[i].wait_recv()

        @pl.when(jnp.logical_not(near_adds))
        def _():
            cross_b[i].start()

    size = 128
    eye = lax.broadcasted_iota(jnp.int32, (size, size), 0) == lax.broadcasted_iota(
        jnp.int32, (size, size), 1
    )
    for i in range(coef_out.shape[0]):
        coef = coef_out[pl.ds(i, 1), :]
        column = jnp.sum(jnp.where(eye, coef, 0.0), axis=1, keepdims=True)
        here = pl.ds(i * size, size)
        ganchor_ref[here, :] = column * change_ref[here, :]
    for copy in coefs:
        copy.wait()
    for i in range(PARTS):
        crosses[i].wait_send()
        sibs[i].wait_send()
        hops[i].wait_send()
        nears[i].wait_send()
        to_direct[i].wait_send()
        to_sibling[i].wait()
        relays[i].wait_send()
        cross_a[i].wait()


def node_backward(
    gradient, hidden_ref, before_ref, agg_ref, w_out, gout_ref, gself_ref, gagg_ref, step
):
    upstream = gradient.astype(BF16)
    hidden = hidden_ref[...]
    hidden_grad = dot(upstream, w_out, 1, 1)
    act_grad = jnp.where(hidden.astype(F32) > 0, hidden_grad, 0.0).astype(BF16)

    @pl.when(step == 0)
    def _():
        gout_ref[...] = jnp.zeros(gout_ref.shape, F32)
        gself_ref[...] = jnp.zeros(gself_ref.shape, F32)
        gagg_ref[...] = jnp.zeros(gagg_ref.shape, F32)

    gout_ref[...] += dot(hidden, upstream, 0, 0)
    gself_ref[...] += dot(before_ref[...], act_grad, 0, 0)
    gagg_ref[...] += dot(agg_ref[...], act_grad, 0, 0)
    return act_grad


def spread_group(index_ref, tiles_ref, adj_ref, agg_grad_t, step, group, slots, rows):
    for g in range(group):
        tile = jnp.concatenate([tiles_ref[g, s] for s in range(slots)], axis=1)
        contrib = dot(agg_grad_t[:, g * rows : (g + 1) * rows], tile, 1, 0)
        for s in range(slots):
            at = index_ref[(step * group + g) * slots + s]
            adj_ref[at] = adj_ref[at] + contrib[:, s * rows : (s + 1) * rows]


def clear_blocks(adj_ref):
    def clear(i, carry):
        adj_ref[i] = jnp.zeros(adj_ref.shape[1:], F32)
        return carry

    lax.fori_loop(0, adj_ref.shape[0], clear, 0)


def scatter_rows(
    list_ref, anchor_ref, ganchor_ref, coef_ref, coefs_ref, rows_in, moved_ref, sums
):
    triplets, width = ganchor_ref.shape
    hits = sums[0].shape[0]
    stride = list_ref.shape[0] // 5
    span = 2 * triplets + 8
    bounds = segments(list_ref, stride, 2 * triplets + 128)
    zeros = jnp.zeros((64, width), F32)

    def clear(i, carry):
        for target in sums:
            target[pl.ds(pl.multiple_of(i * 64, 64), 64), :] = zeros
        return carry

    lax.fori_loop(0, hits // 64, clear, 0)
    eye = lax.broadcasted_iota(jnp.int32, (128, 128), 0) == lax.broadcasted_iota(
        jnp.int32, (128, 128), 1
    )
    for j, source in enumerate(rows_in):
        for i in range(triplets // 128):
            coef = coef_ref[pl.ds(i, 1), :] if j == 0 else coefs_ref[j - 1, pl.ds(i, 1), :]
            spread = jnp.where(eye, coef, 0.0)
            high = spread.astype(BF16)
            low = (spread - high.astype(F32)).astype(BF16)
            part = source[pl.ds(i * 128, 128), :]
            value = dot(high, part, 1, 0) + dot(low, part, 1, 0)
            moved_ref[pl.ds(j * span + i * 128, 128), :] = -value
            moved_ref[pl.ds(j * span + triplets + i * 128, 128), :] = value
        moved_ref[pl.ds(j * span + 2 * triplets, 8), :] = zeros[:8]

    def anchors(i, carry):
        for u in range(8):
            t = i * 8 + u
            here = pl.ds(anchor_ref[t], 1)
            target = sums[u % 4]
            target[here, :] = target[here, :] + ganchor_ref[pl.ds(t, 1), :]
        return carry

    lax.fori_loop(0, triplets // 8, anchors, 0)
    for j in range(5):

        def add(i, carry, j=j):
            for u in range(8):
                entry = list_ref[j * stride + i * 8 + u]
                here = pl.ds(lax.shift_right_logical(entry, ENTRY_BITS), 1)
                target = sums[u % 4]
                moved = moved_ref[pl.ds(j * span + lax.bitwise_and(entry, ENTRY_MASK), 1), :]
                target[here, :] = target[here, :] + moved
            return carry

        lax.fori_loop(bounds[j][0], bounds[j][1], add, 0)


def last_backward(
    group,
    steps,
    index_ref,
    list_ref,
    anchor_ref,
    tiles_ref,
    ganchor_ref,
    coef_ref,
    coefs_ref,
    aself_ref,
    asib_ref,
    across_ref,
    adirect_ref,
    afar_ref,
    hidden_ref,
    before_ref,
    agg_ref,
    w_self_ref,
    w_agg_ref,
    w_out_ref,
    gout_ref,
    gself_ref,
    gagg_ref,
    direct_ref,
    obelow_ref,
    oown_ref,
    oabove_ref,
    osibling_ref,
    ocross_ref,
    adj_ref,
    moved_ref,
    *sums,
):
    step = pl.program_id(0)
    slots, rows = tiles_ref.shape[1], tiles_ref.shape[2]
    span = group * rows

    @pl.when(step == 0)
    def _():
        clear_blocks(adj_ref)
        scatter_rows(
            list_ref, anchor_ref, ganchor_ref, coef_ref, coefs_ref,
            (aself_ref, asib_ref, across_ref, adirect_ref, afar_ref), moved_ref, sums,
        )

    here = pl.ds(pl.multiple_of(step * span, span), span)
    gradient = (sums[0][here, :] + sums[1][here, :]) + (sums[2][here, :] + sums[3][here, :])
    act_grad = node_backward(
        gradient, hidden_ref, before_ref, agg_ref, w_out_ref[...], gout_ref, gself_ref, gagg_ref, step
    )
    direct_ref[...] = gradient + dot(act_grad, w_self_ref[...], 1, 1)
    agg_grad_t = dot(w_agg_ref[...], act_grad, 1, 1).astype(BF16)
    spread_group(index_ref, tiles_ref, adj_ref, agg_grad_t, step, group, slots, rows)

    @pl.when(step == steps - 1)
    def _():
        blocks = oown_ref.shape[0]
        for k, target in enumerate((obelow_ref, oown_ref, oabove_ref, osibling_ref, ocross_ref)):

            def store(i, carry, k=k, target=target):
                target[i] = adj_ref[k * blocks + i].astype(target.dtype)
                return carry

            lax.fori_loop(0, blocks, store, 0)


def back_kernel(
    pairs,
    index_ref,
    cross_hbm,
    sib_hbm,
    relay_hbm,
    direct_hbm,
    own_hbm,
    grad_hbm,
    hidden_hbm,
    before_hbm,
    agg_hbm,
    tiles_hbm,
    feats_ref,
    wcat_ref,
    w_self_ref,
    w_agg_ref,
    w_out_ref,
    gout1_ref,
    gself1_ref,
    gagg1_ref,
    loss_ref,
    all_ref,
    wcat_t_ref,
    cross_in,
    sib_in,
    relay_in,
    total_in,
    relay_send,
    direct_send,
    relay_ref,
    direct_ref,
    own_ref,
    grad_ref,
    hidden_ref,
    before_ref,
    agg_ref,
    tiles_ref,
    slope_ref,
    block_feats_ref,
    x_ref,
    half_in,
    acc_ref,
    slots_in,
    local_sem,
    *sems,
):
    ys, yr, zs, zr, cs, cr, ss, sr, s0, r0, s1, r1, s2, r2, s3, r3 = sems
    direct, sibling, onward, source, to_direct = peers()
    me = lax.axis_index("phi")
    pair, core = me // 2, me % 2
    others = [((pair + d) % pairs) * 2 + core for d in range(1, pairs)]
    blocks, slots, rows, _ = tiles_ref.shape
    depth, width = wcat_ref.shape
    window = feats_ref.shape[1] // rows
    size = grad_ref.shape[0] // CHUNKS
    group = blocks // CHUNKS
    loads = [
        pltpu.make_async_copy(src, dst, local_sem.at[k])
        for k, (src, dst) in enumerate(
            (
                (relay_hbm, relay_ref),
                (direct_hbm, direct_ref),
                (own_hbm, own_ref),
                (grad_hbm, grad_ref),
                (hidden_hbm, hidden_ref),
                (before_hbm, before_ref),
                (agg_hbm, agg_ref),
                (tiles_hbm, tiles_ref),
            )
        )
    ]
    for copy in loads:
        copy.start()
    greet([sibling] + others)

    def span(i):
        return pl.ds(pl.multiple_of(i * size, size), size)

    def crosses(i):
        return remote(cross_hbm.at[span(i)], cross_in.at[span(i)], cs.at[i], cr.at[i], sibling)

    def first(i):
        return remote(relay_send.at[span(i)], relay_in.at[span(i)], zs.at[i], zr.at[i], source)

    def second(i):
        return remote(direct_send.at[span(i)], total_in.at[span(i)], ys.at[i], yr.at[i], direct)

    near = remote(sib_hbm, sib_in, ss.at[0], sr.at[0], sibling)
    lax.fori_loop(0, CHUNKS, lambda i, c: (crosses(i).start(), c)[1], 0)
    near.start()

    per = window // (2 * CHUNKS)

    def slopes(i):
        for u in range(0, per, 2):
            at = pl.multiple_of((i * per + u) * rows, 2 * rows)
            feats = feats_ref[:, pl.ds(at, 2 * rows)]
            squashed = jnp.tanh(dot(wcat_t_ref[...], feats, 1, 0))
            slope = 1.0 - squashed * squashed
            for v in range(2):
                slope_ref[i * per + u + v] = slope[:, v * rows : (v + 1) * rows]
                block_feats_ref[i * per + u + v] = feats[:, v * rows : (v + 1) * rows]

    wcat_t_ref[...] = (
        jnp.concatenate([wcat_ref[...].astype(F32), jnp.zeros((width - depth, width), F32)], axis=0)
        .T[:, :depth]
        .astype(BF16)
    )
    x_ref[...] = jnp.zeros(x_ref.shape, F32)
    for k, value in enumerate((gout1_ref, gself1_ref, gagg1_ref)):
        x_ref[(2 * k + 1) * width : (2 * k + 2) * width, :] = value[...]
    base = 6 * width
    x_ref[base + depth : base + depth + 8, :] = loss_ref[...]
    slope_ref[window] = jnp.zeros(slope_ref.shape[1:], F32)
    block_feats_ref[window] = jnp.zeros(block_feats_ref.shape[1:], BF16)
    loads[0].wait()

    def relay_step(i, carry):
        here = span(i)
        crosses(i).wait_recv()
        extra = jnp.where(to_direct, 0.0, cross_in[here, :].astype(F32))
        relay_send[here, :] = (relay_ref[here, :] + extra).astype(BF16)
        first(i).start()
        slopes(i)
        return carry

    lax.fori_loop(0, CHUNKS, relay_step, 0)
    loads[1].wait()

    def direct_step(i, carry):
        here = span(i)
        first(i).wait_recv()
        extra = jnp.where(to_direct, cross_in[here, :].astype(F32), 0.0)
        direct_send[here, :] = (
            direct_ref[here, :] + extra + relay_in[here, :].astype(F32)
        ).astype(BF16)
        second(i).start()
        slopes(CHUNKS + i)
        return carry

    lax.fori_loop(0, CHUNKS, direct_step, 0)
    for copy in loads[2:]:
        copy.wait()
    near.wait()

    def layer_step(i, carry):
        here = span(i)
        second(i).wait_recv()
        returned = own_ref[here, :] + (
            total_in[here, :].astype(F32) + sib_in[here, :].astype(F32)
        )
        gradient = grad_ref[here, :] + jnp.concatenate(
            [returned[g * width : (g + 1) * width].T for g in range(group)], axis=0
        )
        upstream = gradient.astype(BF16)
        hidden = hidden_ref[here, :]
        hidden_grad = dot(upstream, w_out_ref[...], 1, 1)
        act_grad = jnp.where(hidden.astype(F32) > 0, hidden_grad, 0.0).astype(BF16)
        agg_grad_t = dot(w_agg_ref[...], act_grad, 1, 1).astype(BF16)
        x_ref[0:width, :] += dot(hidden, upstream, 0, 0)
        x_ref[2 * width : 3 * width, :] += dot(before_ref[here, :], act_grad, 0, 0)
        x_ref[4 * width : 5 * width, :] += dot(agg_ref[here, :], act_grad, 0, 0)
        own_grad = gradient + dot(act_grad, w_self_ref[...], 1, 1)
        feats = feats_ref[:, pl.ds(pl.multiple_of((window // 5) * rows + i * size, size), size)]
        squashed = jnp.tanh(dot(feats, wcat_ref[...], 0, 0))
        genc = dot(feats, (own_grad * (1.0 - squashed * squashed)).astype(BF16), 1, 0)
        for g in range(group):
            block = i * group + g
            tile = jnp.concatenate([tiles_ref[block, s] for s in range(slots)], axis=1)
            contrib = dot(agg_grad_t[:, g * rows : (g + 1) * rows], tile, 1, 0)
            places = [index_ref[block * slots + s] for s in range(slots)]
            slope = jnp.concatenate([slope_ref[at] for at in places], axis=1)
            source_feats = jnp.concatenate([block_feats_ref[at] for at in places], axis=1)
            genc = genc + dot(source_feats, (contrib * slope).astype(BF16), 1, 1)
        x_ref[base : base + depth, :] += genc
        return carry

    lax.fori_loop(0, CHUNKS, layer_step, 0)

    def drain(i, carry):
        crosses(i).wait_send()
        first(i).wait_send()
        second(i).wait_send()
        return carry

    lax.fori_loop(0, CHUNKS, drain, 0)

    half = x_ref.shape[0] // 2
    chunk = half // pairs

    def part(start, length):
        return pl.ds(pl.multiple_of(start, 8), length)

    swap = remote(x_ref.at[part((1 - core) * half, half)], half_in, s0.at[0], r0.at[0], sibling)
    swap.start()
    swap.wait()
    acc_ref[...] = x_ref[part(core * half, half), :] + half_in[...]
    scatter = [
        remote(
            acc_ref.at[part(((pair + d) % pairs) * chunk, chunk)],
            slots_in.at[d - 1],
            s1.at[d - 1],
            r1.at[d - 1],
            others[d - 1],
        )
        for d in range(1, pairs)
    ]
    for copy in scatter:
        copy.start()
    total = acc_ref[part(pair * chunk, chunk), :]
    for d in range(1, pairs):
        scatter[d - 1].wait_recv()
        total = total + slots_in[d - 1]
    mine = part(core * half + pair * chunk, chunk)
    all_ref[mine, :] = total
    gather = [
        remote(all_ref.at[mine], all_ref.at[mine], s2.at[d - 1], r2.at[d - 1], others[d - 1])
        for d in range(1, pairs)
    ]
    for copy in gather:
        copy.start()
    for copy in gather:
        copy.wait()
    for copy in scatter:
        copy.wait_send()
    whole = part(core * half, half)
    last = remote(all_ref.at[whole], all_ref.at[whole], s3.at[0], r3.at[0], sibling)
    last.start()
    last.wait()


def finish_kernel(
    triplet_total,
    sum_ref,
    loss_out,
    genc_out,
    gtable_out,
    gself_out,
    gagg_out,
    gout_out,
):
    width = gself_out.shape[1]
    for k, out in enumerate((gout_out, gself_out, gagg_out)):
        for layer in range(2):
            at = (2 * k + layer) * width
            out[layer] = sum_ref[at : at + width, :]
    base = 6 * width
    genc_out[...] = sum_ref[base : base + genc_out.shape[0], :]
    gtable_out[...] = sum_ref[base + 16 : base + 16 + gtable_out.shape[0], :]
    at = base + 16 + gtable_out.shape[0]
    loss_out[...] = sum_ref[at : at + 1, 0:1] / triplet_total


def body(
    hit_feats,
    layer_ids,
    edge_tiles,
    src_blocks,
    live_slots,
    anchor_hits,
    positive_hits,
    negative_hits,
    w_enc,
    layer_table,
    w_self,
    w_agg,
    w_out,
):
    blocks, slots, rows, _ = edge_tiles.shape
    width = w_enc.shape[1]
    features = hit_feats.shape[0]
    kinds = layer_table.shape[0]
    hits = blocks * rows
    layer_total = w_self.shape[0]
    triplets = anchor_hits.shape[0]
    group = 4
    steps = blocks // group
    span = group * rows
    me = lax.axis_index("phi")
    is_even = me % 2 == 0
    even_pair = (me // 2) % 2 == 0

    def place(part):
        spots = (
            jnp.where(even_pair, 2, 0),
            jnp.where(is_even, 4, 3),
            1,
            jnp.where(is_even, 3, 4),
            jnp.where(even_pair, 0, 2),
        )
        return sum(jnp.where(part == k, spot, 0) for k, spot in enumerate(spots))

    live = jnp.arange(slots, dtype=jnp.int32)[None, :] < live_slots[:, None]
    index = jnp.where(
        live, place(src_blocks // blocks) * blocks + src_blocks % blocks, 5 * blocks
    ).reshape(blocks * slots)
    depth = 16 + kinds
    listed = 2 * triplets // 128 + 1
    list_shape = (-(-(listed + 1) // 8) * 8, 128)

    tile_spec = pl.BlockSpec((group, slots, rows, rows), lambda i, *_: (i, 0, 0, 0))
    row_spec = pl.BlockSpec((span, width), lambda i, *_: (i, 0))
    weight_spec = full((width, width))
    any_spec = pl.BlockSpec(memory_space=pl.ANY)
    row_shape = jax.ShapeDtypeStruct((hits, width), BF16)
    weight_shape = jax.ShapeDtypeStruct((width, width), F32)

    wide_shape = jax.ShapeDtypeStruct((hits, width), F32)
    vmem = pl.BlockSpec(memory_space=pltpu.VMEM)
    smem = pl.BlockSpec(memory_space=pltpu.SMEM)
    few = pltpu.SemaphoreType.DMA((FEAT_CHUNKS,))
    each = pltpu.SemaphoreType.DMA((CHUNKS,))
    one = pltpu.SemaphoreType.DMA((1,))
    four = pltpu.SemaphoreType.DMA((4,))
    block_shape = jax.ShapeDtypeStruct((blocks, rows, width), BF16)
    before0, agg0, hidden0, latents1, agg1, hidden1, latents2, lists, feats, wcat = pl.pallas_call(
        functools.partial(forward_kernel, features),
        in_specs=[smem] + [vmem] * 4 + [any_spec] + [vmem] * 5,
        out_specs=[any_spec] * 10,
        out_shape=[block_shape, row_shape, row_shape, block_shape, row_shape, row_shape]
        + [
            wide_shape,
            jax.ShapeDtypeStruct((5,) + list_shape, jnp.int32),
            jax.ShapeDtypeStruct((depth, 5 * hits), BF16),
            jax.ShapeDtypeStruct((depth, width), BF16),
        ],
        scratch_shapes=[
            pltpu.VMEM((16, hits), BF16),
            pltpu.VMEM((depth, width), BF16),
            pltpu.VMEM(list_shape, jnp.int32),
            pltpu.VMEM((listed - 1, 128, 128), jnp.int32),
            pltpu.VMEM((listed - 1, 128, 128), jnp.int32),
            pltpu.VMEM((listed - 1, 128, 128), jnp.int32),
            pltpu.VMEM((5, 16, hits), BF16),
            pltpu.VMEM((depth, 5 * hits), BF16),
            pltpu.VMEM((5 * blocks + 1, rows, width), BF16),
            pltpu.VMEM((5 * blocks + 1, rows, width), BF16),
        ]
        + [pltpu.VMEM((hits, width), BF16)] * 4
        + [
            pltpu.VMEM((hits, width), F32),
            pltpu.VMEM(edge_tiles.shape, BF16),
            each,
            pltpu.SemaphoreType.DMA((6,)),
            pltpu.SemaphoreType.DMA((3 * CHUNKS,)),
            one,
        ]
        + [few] * 6
        + [four] * 2
        + [each] * 8
        + [one] * 2,
        compiler_params=pltpu.CompilerParams(
            collective_id=1, has_side_effects=True, vmem_limit_bytes=VMEM_BYTES
        ),
        name="forward",
    )(
        index,
        hit_feats,
        layer_ids.reshape(1, hits),
        positive_hits.reshape(triplets // 128, 128),
        negative_hits.reshape(triplets // 128, 128),
        edge_tiles,
        w_enc,
        layer_table,
        w_self,
        w_agg,
        w_out,
    )

    before0, latents1 = before0.reshape(hits, width), latents1.reshape(hits, width)
    lists = lists.reshape(-1)
    move_shape = jax.ShapeDtypeStruct((triplets, width), BF16)
    wide_move = jax.ShapeDtypeStruct((triplets, width), F32)
    move_spec = full((triplets, width))
    *found, anchors = pl.pallas_call(
        gather_kernel,
        grid_spec=pltpu.PrefetchScalarGridSpec(
            num_scalar_prefetch=2,
            grid=(1,),
            in_specs=[full((hits, width))],
            out_specs=[move_spec] * 6,
            scratch_shapes=[pltpu.VMEM((2 * triplets + 8, width), F32)],
        ),
        out_shape=[move_shape] * 6,
        compiler_params=params(),
        name="gather",
    )(lists, anchor_hits, latents2)
    coef_shape = (triplets // 128, 128)
    loss_part, ganchor, *moves, coef, coefs = pl.pallas_call(
        functools.partial(contrast_kernel, 1.0 / math.sqrt(width)),
        in_specs=[vmem] * 6,
        out_specs=[vmem] * 8,
        out_shape=[jax.ShapeDtypeStruct((8, width), F32), wide_move]
        + [move_shape] * 4
        + [jax.ShapeDtypeStruct(coef_shape, F32), jax.ShapeDtypeStruct((4,) + coef_shape, F32)],
        scratch_shapes=[pltpu.VMEM((triplets, width), F32)]
        + [pltpu.VMEM((triplets, width), BF16)] * 6
        + [pltpu.SemaphoreType.DMA((PARTS,))] * 16
        + [pltpu.SemaphoreType.DMA((4,))] * 2,
        compiler_params=pltpu.CompilerParams(
            collective_id=4, has_side_effects=True, vmem_limit_bytes=VMEM_BYTES
        ),
        name="contrast",
    )(*found, anchors)

    t_shape = jax.ShapeDtypeStruct((blocks, width, rows), F32)
    t_half = jax.ShapeDtypeStruct((blocks, width, rows), BF16)
    t_full = pl.BlockSpec(
        (blocks, width, rows), lambda *_: (0, 0, 0), pipeline_mode=pl.Buffered(1)
    )
    adj_shape = pltpu.VMEM((5 * blocks + 1, width, rows), F32)
    gout1, gself1, gagg1, direct, obelow, own, oabove, osibling, ocross = pl.pallas_call(
        functools.partial(last_backward, group, steps),
        grid_spec=pltpu.PrefetchScalarGridSpec(
            num_scalar_prefetch=3,
            grid=(steps,),
            in_specs=[tile_spec, move_spec, full(coef_shape), full((4,) + coef_shape)]
            + [move_spec] * 5
            + [row_spec] * 3
            + [weight_spec] * 3,
            out_specs=[weight_spec] * 3 + [row_spec] + [t_full] * 5,
            scratch_shapes=[adj_shape, pltpu.VMEM((10 * triplets + 40, width), F32)]
            + [pltpu.VMEM((hits, width), F32)] * 4,
        ),
        out_shape=[weight_shape] * 3 + [wide_shape] + [t_shape] * 3 + [t_half] * 2,
        compiler_params=params(),
        name="last_backward",
    )(
        index, lists, anchor_hits, edge_tiles, ganchor, coef, coefs, anchors, *moves, hidden1, latents1, agg1,
        w_self[1], w_agg[1], w_out[1],
    )
    pairs = lax.axis_size("phi") // 2
    sum_chunk = -(-(6 * width + depth + 8) // (16 * pairs)) * 8
    sum_rows = 2 * pairs * sum_chunk
    many = pltpu.SemaphoreType.DMA((pairs - 1,))
    flat = (hits, width)
    summed = pl.pallas_call(
        functools.partial(back_kernel, pairs),
        in_specs=[smem] + [any_spec] * 10 + [vmem] * 9,
        out_specs=vmem,
        out_shape=jax.ShapeDtypeStruct((sum_rows, width), F32),
        scratch_shapes=[pltpu.VMEM((width, depth), BF16)]
        + [pltpu.VMEM(flat, BF16)] * 6
        + [pltpu.VMEM(flat, F32)] * 4
        + [pltpu.VMEM(flat, BF16)] * 3
        + [
            pltpu.VMEM(edge_tiles.shape, BF16),
            pltpu.VMEM((5 * blocks + 1, width, rows), F32),
            pltpu.VMEM((5 * blocks + 1, depth, rows), BF16),
            pltpu.VMEM((sum_rows, width), F32),
            pltpu.VMEM((sum_rows // 2, width), F32),
            pltpu.VMEM((sum_rows // 2, width), F32),
            pltpu.VMEM((pairs - 1, sum_chunk, width), F32),
            pltpu.SemaphoreType.DMA((8,)),
        ]
        + [pltpu.SemaphoreType.DMA((CHUNKS,))] * 6
        + [one, one, one, one, many, many, many, many, one, one],
        compiler_params=pltpu.CompilerParams(
            collective_id=3, has_side_effects=True, vmem_limit_bytes=VMEM_BYTES
        ),
        name="back",
    )(
        index, ocross.reshape(flat), osibling.reshape(flat), oabove.reshape(flat),
        obelow.reshape(flat), own.reshape(flat), direct, hidden0, before0, agg0, edge_tiles,
        feats, wcat, w_self[0], w_agg[0], w_out[0], gout1, gself1, gagg1, loss_part,
    )
    stack = jax.ShapeDtypeStruct((2, width, width), F32)
    loss, genc, gtable, gself, gagg, gout = pl.pallas_call(
        functools.partial(finish_kernel, float(triplets * lax.axis_size("phi"))),
        in_specs=[vmem],
        out_specs=[vmem] * 6,
        out_shape=[
            jax.ShapeDtypeStruct((1, 1), F32),
            jax.ShapeDtypeStruct((features, width), F32),
            jax.ShapeDtypeStruct((kinds, width), F32),
            stack, stack, stack,
        ],
        name="finish",
    )(summed)
    return (loss.reshape(1), genc, gtable, gself, gagg, gout)


def solution(mesh):
    both = ("event", "phi")
    in_specs = (
        P(None, both),
        P(both),
        P(both, None, None, None),
        P(both, None),
        P(both),
        P(both),
        P(both),
        P(both),
        P(),
        P(),
        P(),
        P(),
        P(),
    )
    out_specs = (
        P("event"),
        P("event", None),
        P("event", None),
        P("event", None, None),
        P("event", None, None),
        P("event", None, None),
    )
    return jax.shard_map(body, mesh=mesh, in_specs=in_specs, out_specs=out_specs, check_vma=False)
```

```python
import functools
import math

import jax
import jax.numpy as jnp
from jax import lax
from jax.experimental import pallas as pl
from jax.experimental.pallas import tpu as pltpu
from jax.sharding import PartitionSpec as P

loss_divisor = 64.0
F32 = jnp.float32
BF16 = jnp.bfloat16
VMEM_BYTES = 60 * 1024 * 1024


def dot(left, right, left_dim, right_dim):
    return lax.dot_general(
        left, right, (((left_dim,), (right_dim,)), ((), ())), preferred_element_type=F32
    )


def full(shape):
    return pl.BlockSpec(shape, lambda *_: (0,) * len(shape))


def params():
    return pltpu.CompilerParams(
        dimension_semantics=("arbitrary",), vmem_limit_bytes=VMEM_BYTES
    )


CHUNKS = 16
LATER_STEPS = 8


def peers():
    count = lax.axis_size("phi")
    me = lax.axis_index("phi")
    odd_pair = (me // 2) % 2
    odd_core = me % 2
    direct = me + 2 - 4 * odd_pair
    sibling = me + 1 - 2 * odd_core
    stride = 4 - 8 * odd_pair
    onward = (me + stride + count) % count
    source = (me - stride + count) % count
    return direct, sibling, onward, source, odd_pair == odd_core


def remote(src, dst, send, recv, target):
    return pltpu.make_async_remote_copy(
        src_ref=src,
        dst_ref=dst,
        send_sem=send,
        recv_sem=recv,
        device_id={"phi": target},
        device_id_type=pl.DeviceIdType.MESH,
    )


def greet(targets):
    barrier = pltpu.get_barrier_semaphore()
    for target in targets:
        pl.semaphore_signal(
            barrier, inc=1, device_id={"phi": target}, device_id_type=pl.DeviceIdType.MESH
        )
    pl.semaphore_wait(barrier, len(targets))


def role_targets():
    count = lax.axis_size("phi")
    me = lax.axis_index("phi")
    odd_pair = (me // 2) % 2
    odd_core = me % 2
    sibling = me + 1 - 2 * odd_core
    across = (me - 1 + 2 * odd_core + count) % count
    direct = me + 2 - 4 * odd_pair
    far = (me - 2 + 4 * odd_pair + count) % count
    return sibling, across, direct, far


def aggregate_group(index_ref, tiles_ref, window_ref, step, group, slots, rows):
    results = []
    for g in range(group):
        tile = jnp.concatenate([tiles_ref[step * group + g, s] for s in range(slots)], axis=1)
        source = jnp.concatenate(
            [
                window_ref[index_ref[(step * group + g) * slots + s]] for s in range(slots)
            ],
            axis=0,
        )
        results.append(dot(tile, source, 1, 0).astype(BF16))
    return jnp.concatenate(results, axis=0)


def node_update(own, aggregated, w_self, w_agg, w_out):
    activation = dot(own, w_self, 1, 0) + dot(aggregated, w_agg, 1, 0)
    hidden = jnp.maximum(activation, 0.0).astype(BF16)
    updated = (own.astype(F32) + dot(hidden, w_out, 1, 0)).astype(BF16)
    return hidden, updated


FEAT_CHUNKS = 2


def forward_kernel(
    features,
    index_ref,
    hit_ref,
    id_ref,
    positive_ref,
    negative_ref,
    tiles_hbm,
    enc_ref,
    table_ref,
    w_self_ref,
    w_agg_ref,
    w_out_ref,
    before_out,
    agg0_out,
    hidden0_out,
    latents_out,
    agg1_out,
    hidden1_out,
    z_out,
    lists_out,
    feats_out,
    wcat_out,
    packed_ref,
    wcat_ref,
    keys_ref,
    key_cols,
    place_cols,
    entry_cols,
    packs_ref,
    feats_ref,
    window_ref,
    later_ref,
    agg0_ref,
    hidden0_ref,
    agg1_ref,
    hidden1_ref,
    z_ref,
    tiles_ref,
    tile_sem,
    out_sem,
    late_sem,
    list_sem,
    *sems,
):
    fys, fyr, fzs, fzr, fcs, fcr, ls, lr = sems[:8]
    ys, yr, zs, zr, cs, cr, ss, sr = sems[8:16]
    fss, fsr = sems[16:]
    direct, sibling, onward, source, direct_crosses = peers()
    roles = role_targets()
    blocks, slots, rows, _ = tiles_ref.shape
    hits = packed_ref.shape[1]
    group = blocks // CHUNKS
    span = group * rows

    def tile_load(i):
        part = pl.ds(i * group, group)
        return pltpu.make_async_copy(tiles_hbm.at[part], tiles_ref.at[part], tile_sem.at[i])

    lax.fori_loop(0, CHUNKS, lambda i, c: (tile_load(i).start(), c)[1], 0)
    kinds, width = table_ref.shape
    filler = jnp.zeros((16 - features, width), F32)
    wcat_ref[...] = jnp.concatenate(
        [enc_ref[...].astype(F32), filler, table_ref[...].astype(F32)], axis=0
    ).astype(BF16)

    def gather_input(i, carry):
        at = pl.ds(pl.multiple_of(i * 512, 512), 512)
        packed_ref[:, at] = jnp.concatenate(
            [
                hit_ref[:, at].astype(F32),
                id_ref[:, at].astype(F32),
                jnp.zeros((15 - features, 512), F32),
            ],
            axis=0,
        ).astype(BF16)
        return carry

    lax.fori_loop(0, hits // 512, gather_input, 0)
    greet((direct, sibling, onward, source, roles[1], roles[3]))
    columns = hits // FEAT_CHUNKS

    def pack(k, i):
        return packs_ref.at[k, :, pl.ds(i * columns, columns)]

    chunks = range(FEAT_CHUNKS)
    f_first = [
        remote(
            packed_ref.at[:, pl.ds(i * columns, columns)], pack(0, i), fys.at[i], fyr.at[i], direct
        )
        for i in chunks
    ]
    f_second = [remote(pack(0, i), pack(2, i), fzs.at[i], fzr.at[i], onward) for i in chunks]
    f_cross_a = [remote(pack(0, i), pack(4, i), fcs.at[i], fcr.at[i], sibling) for i in chunks]
    f_cross_b = [remote(pack(2, i), pack(4, i), fcs.at[i], fcr.at[i], sibling) for i in chunks]
    f_near = remote(packed_ref, packs_ref.at[3], fss.at[0], fsr.at[0], sibling)
    for copy in f_first:
        copy.start()
    f_near.start()

    def encode(k, ref):
        step = 512
        is_feature = lax.broadcasted_iota(jnp.int32, (16, step), 0) < features
        kind = lax.broadcasted_iota(jnp.int32, (16, step), 0).astype(F32)

        def run(i, carry):
            at = pl.multiple_of(i * step, step)
            data = ref[:, pl.ds(at, step)].astype(F32)
            onehot = jnp.where(kind == data[features : features + 1], 1.0, 0.0)
            feats = jnp.concatenate([jnp.where(is_feature, data, 0.0), onehot], axis=0).astype(BF16)
            feats_ref[:, pl.ds(pl.multiple_of(k * hits + i * step, step), step)] = feats
            encoded = dot(feats, wcat_ref[...], 0, 0)
            squashed = jnp.tanh(encoded).astype(BF16)
            for u in range(step // rows):
                window_ref[k * blocks + i * (step // rows) + u] = squashed[
                    u * rows : (u + 1) * rows
                ]
            return carry

        lax.fori_loop(0, hits // step, run, 0)

    encode(1, packed_ref)
    for i in chunks:
        f_first[i].wait_recv()
        f_second[i].start()

        @pl.when(direct_crosses)
        def _():
            f_cross_a[i].start()

    f_near.wait_recv()
    encode(3, packs_ref.at[3])
    encode(0, packs_ref.at[0])
    for i in chunks:
        f_second[i].wait_recv()

        @pl.when(jnp.logical_not(direct_crosses))
        def _():
            f_cross_b[i].start()

    encode(2, packs_ref.at[2])
    for i in chunks:
        f_cross_a[i].wait_recv()
    encode(4, packs_ref.at[4])
    window_ref[5 * blocks] = jnp.zeros((rows, width), BF16)
    later_ref[5 * blocks] = jnp.zeros((rows, width), BF16)

    def part(k, i):
        return pl.ds(k * blocks + i * group, group)

    def first(i):
        return remote(later_ref.at[part(1, i)], later_ref.at[part(0, i)], ys.at[i], yr.at[i], direct)

    def near(i):
        return remote(later_ref.at[part(1, i)], later_ref.at[part(3, i)], ss.at[i], sr.at[i], sibling)

    def second(i):
        return remote(later_ref.at[part(0, i)], later_ref.at[part(2, i)], zs.at[i], zr.at[i], onward)

    def cross_a(i):
        return remote(later_ref.at[part(0, i)], later_ref.at[part(4, i)], cs.at[i], cr.at[i], sibling)

    def cross_b(i):
        return remote(later_ref.at[part(2, i)], later_ref.at[part(4, i)], cs.at[i], cr.at[i], sibling)

    def relay(i):
        first(i).wait_recv()
        second(i).start()

        @pl.when(direct_crosses)
        def _():
            cross_a(i).start()

    def land(i):
        second(i).wait_recv()

        @pl.when(jnp.logical_not(direct_crosses))
        def _():
            cross_b(i).start()

    lead = 5
    relayed = (CHUNKS - lead + 1) // 2

    def layer0(i, carry):
        tile_load(i).wait()
        here = pl.ds(pl.multiple_of(i * span, span), span)
        aggregated = aggregate_group(index_ref, tiles_ref, window_ref, i, group, slots, rows)
        own = window_ref[part(1, i)].reshape(span, width)
        hidden, updated = node_update(own, aggregated, w_self_ref[0], w_agg_ref[0], w_out_ref[0])
        later_ref[part(1, i)] = updated.reshape(group, rows, width)
        first(i).start()
        near(i).start()
        agg0_ref[here, :] = aggregated
        hidden0_ref[here, :] = hidden

        @pl.when(jnp.logical_and(i >= lead, lax.rem(i, 2) == 1))
        def _():
            relay(lax.div(i - lead, 2))

        return carry

    lax.fori_loop(0, CHUNKS, layer0, 0)
    own = pl.ds(blocks, blocks)
    saves = [
        pltpu.make_async_copy(src, dst, out_sem.at[k])
        for k, (src, dst) in enumerate(
            (
                (window_ref.at[own], before_out),
                (agg0_ref, agg0_out),
                (hidden0_ref, hidden0_out),
                (later_ref.at[own], latents_out),
                (feats_ref, feats_out),
                (wcat_ref, wcat_out),
            )
        )
    ]
    for copy in saves:
        copy.start()

    wanted = jnp.concatenate([positive_ref[...], negative_ref[...]], axis=0)
    lines = wanted.shape[0]
    pairs_of = lines * 128
    line = lax.broadcasted_iota(jnp.int32, (lines, 128), 0)
    lane = lax.broadcasted_iota(jnp.int32, (lines, 128), 1)
    keys = wanted * pairs_of + (line * 128 + lane)
    tall = jnp.concatenate(
        [wanted.astype(F32), jnp.zeros((128 - lines, 128), F32)], axis=0
    ).T.astype(jnp.int32)
    down = lax.broadcasted_iota(jnp.int32, (128, 1), 0)
    counts = []
    for k in range(5):
        mine = jnp.logical_and(wanted >= k * hits, wanted < (k + 1) * hits)
        counted = jnp.sum(jnp.where(mine, 1.0, 0.0), axis=1, keepdims=True)
        counts.append(jnp.sum(counted, axis=0, keepdims=True).astype(jnp.int32))
    aligned, shift = [jnp.zeros((1, 1), jnp.int32)], [jnp.zeros((1, 1), jnp.int32)]
    for k in range(5):
        filled = lax.bitwise_and(counts[k] + 7, -8)
        aligned.append(aligned[k] + filled)
        shift.append(shift[k] + filled - counts[k])
    for c in range(lines):
        column = tall[:, c : c + 1]
        slot = down + c * 128
        moved = jnp.zeros((128, 1), jnp.int32)
        first_row = jnp.zeros((128, 1), jnp.int32)
        for k in range(5):
            mine = jnp.logical_and(column >= k * hits, column < (k + 1) * hits)
            moved = moved + jnp.where(mine, shift[k], 0)
            first_row = first_row + jnp.where(mine, k * hits, 0)
        entry = (column - first_row) * (1 << ENTRY_BITS) + slot - pairs_of
        key_cols[c] = jnp.broadcast_to(column * pairs_of + slot, (128, 128))
        place_cols[c] = jnp.broadcast_to(moved, (128, 128))
        entry_cols[c] = jnp.broadcast_to(entry, (128, 128))

    def rank(c, carry):
        column = key_cols[c]
        count = jnp.zeros((128, 128), F32)
        for r in range(lines):
            count = count + jnp.where(keys[r : r + 1] < column, 1.0, 0.0)
        total = jnp.sum(count, axis=1, keepdims=True).astype(jnp.int32)
        place_cols[c] = place_cols[c] + jnp.broadcast_to(total, (128, 128))
        return carry

    keys_ref[...] = jnp.zeros(keys_ref.shape, jnp.int32)

    def put(q, carry):
        target = lax.broadcasted_iota(jnp.int32, (128, 128), 1) + q * 128

        def match(c, total):
            return total + jnp.where(place_cols[c] == target, entry_cols[c], 0)

        total = lax.fori_loop(0, lines, match, jnp.zeros((128, 128), jnp.int32))
        found = jnp.sum(total.astype(F32), axis=0, keepdims=True).astype(jnp.int32)
        keys_ref[pl.ds(q, 1), :] = found + pairs_of
        return carry

    turns = 3
    for k in range(turns):
        relay(relayed + k)
        land(k)
        lax.fori_loop(lines * k // turns, lines * (k + 1) // turns, rank, 0)
    put_turns = CHUNKS - relayed - turns - 2
    for k in range(put_turns):
        relay(relayed + turns + k)
        land(turns + k)
        lax.fori_loop(
            (lines + 1) * k // put_turns, (lines + 1) * (k + 1) // put_turns, put, 0
        )
    lane = lax.broadcasted_iota(jnp.int32, (1, 128), 1)
    keys_ref[pl.ds(lines + 1, 1), :] = sum(
        jnp.where(lane == k, aligned[k] // 8, 0) for k in range(6)
    )
    lists = [
        remote(keys_ref, lists_out.at[j + 1], ls.at[j], lr.at[j], target)
        for j, target in enumerate(roles)
    ]
    for copy in lists:
        copy.start()
    own_list = pltpu.make_async_copy(keys_ref, lists_out.at[0], list_sem.at[0])
    own_list.start()

    for k in range(CHUNKS - 2, CHUNKS):
        relay(k)
    for k in range(turns + put_turns, CHUNKS):
        land(k)

    def settle(i, carry):
        near(i).wait()
        cross_a(i).wait_recv()
        return carry

    lax.fori_loop(0, CHUNKS, settle, 0)

    later_group = blocks // LATER_STEPS
    later_span = later_group * rows

    def late_saves(i):
        here = pl.ds(pl.multiple_of(i * later_span, later_span), later_span)
        return [
            pltpu.make_async_copy(src.at[here], dst.at[here], late_sem.at[k * LATER_STEPS + i])
            for k, (src, dst) in enumerate(
                ((agg1_ref, agg1_out), (hidden1_ref, hidden1_out), (z_ref, z_out))
            )
        ]

    def layer1(i, carry):
        here = pl.ds(pl.multiple_of(i * later_span, later_span), later_span)
        aggregated = aggregate_group(index_ref, tiles_ref, later_ref, i, later_group, slots, rows)
        own = later_ref[pl.ds(blocks + i * later_group, later_group)].reshape(later_span, width)
        hidden, updated = node_update(own, aggregated, w_self_ref[1], w_agg_ref[1], w_out_ref[1])
        agg1_ref[here, :] = aggregated
        hidden1_ref[here, :] = hidden
        z_ref[here, :] = updated.astype(F32)
        for copy in late_saves(i):
            copy.start()
        return carry

    lax.fori_loop(0, LATER_STEPS, layer1, 0)

    def drain(i, carry):
        first(i).wait_send()
        second(i).wait_send()
        cross_a(i).wait_send()
        return carry

    lax.fori_loop(0, CHUNKS, drain, 0)

    def saved(i, carry):
        for copy in late_saves(i):
            copy.wait()
        return carry

    lax.fori_loop(0, LATER_STEPS, saved, 0)
    for i in chunks:
        f_first[i].wait_send()
        f_second[i].wait_send()
        f_cross_a[i].wait_send()
    f_near.wait_send()
    own_list.wait()
    for copy in lists:
        copy.wait()
    for copy in saves:
        copy.wait()


def segments(list_ref, stride, listed):
    me = lax.axis_index("phi")
    odd_core, odd_pair = lax.rem(me, 2), lax.rem(lax.div(me, 2), 2)
    places = (2, 1 + 2 * odd_core, 3 - 2 * odd_core, 4 * odd_pair, 4 - 4 * odd_pair)
    starts = [j * stride + listed + k for j, k in enumerate(places)]
    return [(list_ref[at], list_ref[at + 1]) for at in starts]


def gather_kernel(list_ref, anchor_ref, z_ref, *refs):
    outs, (anchor_out, buf_ref) = refs[:5], refs[5:]
    triplets, width = anchor_out.shape
    stride = list_ref.shape[0] // 5
    bounds = segments(list_ref, stride, 2 * triplets + 128)

    def anchors(i, carry):
        at = pl.multiple_of(i * 16, 16)
        anchor_out[pl.ds(at, 16), :] = jnp.concatenate(
            [z_ref[pl.ds(anchor_ref[i * 16 + u], 1), :] for u in range(16)], axis=0
        ).astype(BF16)
        return carry

    lax.fori_loop(0, triplets // 16, anchors, 0)
    zeros = jnp.zeros((64, width), F32)

    def clear(i, carry):
        buf_ref[pl.ds(pl.multiple_of(i * 64, 64), 64), :] = zeros
        return carry

    lax.fori_loop(0, 2 * triplets // 64, clear, 0)
    for j in range(5):

        def fetch(i, carry, j=j):
            for u in range(8):
                entry = list_ref[j * stride + i * 8 + u]
                row = z_ref[pl.ds(lax.shift_right_logical(entry, ENTRY_BITS), 1), :]
                buf_ref[pl.ds(lax.bitwise_and(entry, ENTRY_MASK), 1), :] = row
            return carry

        lax.fori_loop(bounds[j][0], bounds[j][1], fetch, 0)

        def subtract(i, carry, j=j):
            at = pl.multiple_of(i * 64, 64)
            value = buf_ref[pl.ds(triplets + at, 64), :] - buf_ref[pl.ds(at, 64), :]
            outs[j][pl.ds(at, 64), :] = value.astype(BF16)
            buf_ref[pl.ds(triplets + at, 64), :] = zeros
            buf_ref[pl.ds(at, 64), :] = zeros
            return carry

        lax.fori_loop(0, triplets // 64, subtract, 0)


ENTRY_BITS = 12
ENTRY_MASK = (1 << ENTRY_BITS) - 1
PARTS = 8


def contrast_kernel(
    inv_root,
    self_ref,
    sib_ref,
    cross_ref,
    near_ref,
    far_ref,
    anchor_ref,
    loss_ref,
    ganchor_ref,
    asib_ref,
    across_ref,
    adirect_ref,
    afar_ref,
    coef_out,
    coefs_out,
    change_ref,
    sib_in,
    cross_in,
    far_send,
    far_in,
    near_send,
    near_in,
    *sems,
):
    s = [sems[2 * i : 2 * i + 2] for i in range(9)]
    direct, sibling, onward, source, near_adds = peers()
    roles = role_targets()
    size = anchor_ref.shape[0] // PARTS
    greet((direct, sibling, onward, source, roles[1], roles[3]))

    def rows(i):
        return pl.ds(i * size, size)

    def copies(k, src, dst, target):
        return [
            remote(src.at[rows(i)], dst.at[rows(i)], s[k][0].at[i], s[k][1].at[i], target)
            for i in range(PARTS)
        ]

    crosses = copies(0, cross_ref, cross_in, sibling)
    sibs = copies(1, sib_ref, sib_in, sibling)
    hops = copies(2, far_send, far_in, source)
    nears = copies(3, near_send, near_in, direct)
    to_direct = copies(4, anchor_ref, adirect_ref, direct)
    to_sibling = copies(5, anchor_ref, asib_ref, sibling)
    relays = copies(6, adirect_ref, afar_ref, onward)
    cross_a = copies(7, adirect_ref, across_ref, sibling)
    cross_b = copies(7, afar_ref, across_ref, sibling)
    coefs = [
        remote(coef_out, coefs_out.at[j], s[8][0].at[j], s[8][1].at[j], target)
        for j, target in enumerate(roles)
    ]
    for copy in crosses:
        copy.start()
    for copy in sibs:
        copy.start()
    for i in range(PARTS):
        crosses[i].wait_recv()
        extra = jnp.where(near_adds, 0.0, cross_in[rows(i), :].astype(F32))
        far_send[rows(i), :] = (far_ref[rows(i), :].astype(F32) + extra).astype(BF16)
        hops[i].start()
        if i < PARTS // 2:
            to_direct[i].start()
    for i in range(PARTS):
        hops[i].wait_recv()
        extra = jnp.where(near_adds, cross_in[rows(i), :].astype(F32), 0.0)
        near_send[rows(i), :] = (
            near_ref[rows(i), :].astype(F32) + extra + far_in[rows(i), :].astype(F32)
        ).astype(BF16)
        nears[i].start()
    for i in range(PARTS // 2, PARTS):
        to_direct[i].start()

    def relay(i):
        to_sibling[i].start()
        to_direct[i].wait_recv()
        relays[i].start()

        @pl.when(near_adds)
        def _():
            cross_a[i].start()

    gaps = []
    for i in range(PARTS):
        if i < PARTS // 2:
            relay(i)
        sibs[i].wait_recv()
        nears[i].wait_recv()
        change = (
            near_in[rows(i), :].astype(F32)
            + self_ref[rows(i), :].astype(F32)
            + sib_in[rows(i), :].astype(F32)
        )
        change_ref[rows(i), :] = change
        product = anchor_ref[rows(i), :].astype(F32) * change
        for u in range(size // 128):
            gaps.append(
                jnp.sum(product[u * 128 : (u + 1) * 128].T, axis=0, keepdims=True) * inv_root
            )
    gap = jnp.concatenate(gaps, axis=0)
    coef_out[...] = jax.nn.sigmoid(gap) * (inv_root / loss_divisor)
    for copy in coefs:
        copy.start()
    soft = jnp.maximum(gap, 0.0) + jnp.log1p(jnp.exp(-jnp.abs(gap)))
    loss_ref[...] = jnp.broadcast_to(jnp.sum(soft, keepdims=True), loss_ref.shape)
    for i in range(PARTS // 2, PARTS):
        relay(i)
    for i in range(PARTS):
        relays[i].wait_recv()

        @pl.when(jnp.logical_not(near_adds))
        def _():
            cross_b[i].start()

    size = 128
    eye = lax.broadcasted_iota(jnp.int32, (size, size), 0) == lax.broadcasted_iota(
        jnp.int32, (size, size), 1
    )
    for i in range(coef_out.shape[0]):
        coef = coef_out[pl.ds(i, 1), :]
        column = jnp.sum(jnp.where(eye, coef, 0.0), axis=1, keepdims=True)
        here = pl.ds(i * size, size)
        ganchor_ref[here, :] = column * change_ref[here, :]
    for copy in coefs:
        copy.wait()
    for i in range(PARTS):
        crosses[i].wait_send()
        sibs[i].wait_send()
        hops[i].wait_send()
        nears[i].wait_send()
        to_direct[i].wait_send()
        to_sibling[i].wait()
        relays[i].wait_send()
        cross_a[i].wait()


def node_backward(
    gradient, hidden_ref, before_ref, agg_ref, w_out, gout_ref, gself_ref, gagg_ref, step
):
    upstream = gradient.astype(BF16)
    hidden = hidden_ref[...]
    hidden_grad = dot(upstream, w_out, 1, 1)
    act_grad = jnp.where(hidden.astype(F32) > 0, hidden_grad, 0.0).astype(BF16)

    @pl.when(step == 0)
    def _():
        gout_ref[...] = jnp.zeros(gout_ref.shape, F32)
        gself_ref[...] = jnp.zeros(gself_ref.shape, F32)
        gagg_ref[...] = jnp.zeros(gagg_ref.shape, F32)

    gout_ref[...] += dot(hidden, upstream, 0, 0)
    gself_ref[...] += dot(before_ref[...], act_grad, 0, 0)
    gagg_ref[...] += dot(agg_ref[...], act_grad, 0, 0)
    return act_grad


def spread_group(index_ref, tiles_ref, adj_ref, agg_grad_t, step, group, slots, rows):
    for g in range(group):
        tile = jnp.concatenate([tiles_ref[g, s] for s in range(slots)], axis=1)
        contrib = dot(agg_grad_t[:, g * rows : (g + 1) * rows], tile, 1, 0)
        for s in range(slots):
            at = index_ref[(step * group + g) * slots + s]
            adj_ref[at] = adj_ref[at] + contrib[:, s * rows : (s + 1) * rows]


def clear_blocks(adj_ref):
    def clear(i, carry):
        adj_ref[i] = jnp.zeros(adj_ref.shape[1:], F32)
        return carry

    lax.fori_loop(0, adj_ref.shape[0], clear, 0)


def scatter_rows(
    list_ref, anchor_ref, ganchor_ref, coef_ref, coefs_ref, rows_in, moved_ref, sums
):
    triplets, width = ganchor_ref.shape
    hits = sums[0].shape[0]
    stride = list_ref.shape[0] // 5
    span = 2 * triplets + 8
    bounds = segments(list_ref, stride, 2 * triplets + 128)
    zeros = jnp.zeros((64, width), F32)

    def clear(i, carry):
        for target in sums:
            target[pl.ds(pl.multiple_of(i * 64, 64), 64), :] = zeros
        return carry

    lax.fori_loop(0, hits // 64, clear, 0)
    eye = lax.broadcasted_iota(jnp.int32, (128, 128), 0) == lax.broadcasted_iota(
        jnp.int32, (128, 128), 1
    )
    for j, source in enumerate(rows_in):
        for i in range(triplets // 128):
            coef = coef_ref[pl.ds(i, 1), :] if j == 0 else coefs_ref[j - 1, pl.ds(i, 1), :]
            spread = jnp.where(eye, coef, 0.0)
            high = spread.astype(BF16)
            low = (spread - high.astype(F32)).astype(BF16)
            part = source[pl.ds(i * 128, 128), :]
            value = dot(high, part, 1, 0) + dot(low, part, 1, 0)
            moved_ref[pl.ds(j * span + i * 128, 128), :] = -value
            moved_ref[pl.ds(j * span + triplets + i * 128, 128), :] = value
        moved_ref[pl.ds(j * span + 2 * triplets, 8), :] = zeros[:8]

    def anchors(i, carry):
        for u in range(8):
            t = i * 8 + u
            here = pl.ds(anchor_ref[t], 1)
            target = sums[u % 4]
            target[here, :] = target[here, :] + ganchor_ref[pl.ds(t, 1), :]
        return carry

    lax.fori_loop(0, triplets // 8, anchors, 0)
    for j in range(5):

        def add(i, carry, j=j):
            for u in range(8):
                entry = list_ref[j * stride + i * 8 + u]
                here = pl.ds(lax.shift_right_logical(entry, ENTRY_BITS), 1)
                target = sums[u % 4]
                moved = moved_ref[pl.ds(j * span + lax.bitwise_and(entry, ENTRY_MASK), 1), :]
                target[here, :] = target[here, :] + moved
            return carry

        lax.fori_loop(bounds[j][0], bounds[j][1], add, 0)


def last_backward(
    group,
    steps,
    index_ref,
    list_ref,
    anchor_ref,
    tiles_ref,
    ganchor_ref,
    coef_ref,
    coefs_ref,
    aself_ref,
    asib_ref,
    across_ref,
    adirect_ref,
    afar_ref,
    hidden_ref,
    before_ref,
    agg_ref,
    w_self_ref,
    w_agg_ref,
    w_out_ref,
    gout_ref,
    gself_ref,
    gagg_ref,
    direct_ref,
    obelow_ref,
    oown_ref,
    oabove_ref,
    osibling_ref,
    ocross_ref,
    adj_ref,
    moved_ref,
    *sums,
):
    step = pl.program_id(0)
    slots, rows = tiles_ref.shape[1], tiles_ref.shape[2]
    span = group * rows

    @pl.when(step == 0)
    def _():
        clear_blocks(adj_ref)
        scatter_rows(
            list_ref, anchor_ref, ganchor_ref, coef_ref, coefs_ref,
            (aself_ref, asib_ref, across_ref, adirect_ref, afar_ref), moved_ref, sums,
        )

    here = pl.ds(pl.multiple_of(step * span, span), span)
    gradient = (sums[0][here, :] + sums[1][here, :]) + (sums[2][here, :] + sums[3][here, :])
    act_grad = node_backward(
        gradient, hidden_ref, before_ref, agg_ref, w_out_ref[1], gout_ref, gself_ref, gagg_ref, step
    )
    direct_ref[...] = gradient + dot(act_grad, w_self_ref[1], 1, 1)
    agg_grad_t = dot(w_agg_ref[1], act_grad, 1, 1).astype(BF16)
    spread_group(index_ref, tiles_ref, adj_ref, agg_grad_t, step, group, slots, rows)

    @pl.when(step == steps - 1)
    def _():
        blocks = oown_ref.shape[0]
        for k, target in enumerate((obelow_ref, oown_ref, oabove_ref, osibling_ref, ocross_ref)):

            def store(i, carry, k=k, target=target):
                target[i] = adj_ref[k * blocks + i].astype(target.dtype)
                return carry

            lax.fori_loop(0, blocks, store, 0)


def summer(pairs, x_ref, half_in, acc_ref, slots_in, all_ref, sems):
    s0, r0, s1, r1, s2, r2, s3, r3 = sems
    me = lax.axis_index("phi")
    pair, core = me // 2, me % 2
    sibling = me + 1 - 2 * core
    others = [((pair + d) % pairs) * 2 + core for d in range(1, pairs)]
    half = x_ref.shape[0] // 2
    chunk = half // pairs

    def part(start, length):
        return pl.ds(pl.multiple_of(start, 8), length)

    swap = remote(x_ref.at[part((1 - core) * half, half)], half_in, s0.at[0], r0.at[0], sibling)
    scatter = [
        remote(
            acc_ref.at[part(((pair + d) % pairs) * chunk, chunk)],
            slots_in.at[d - 1],
            s1.at[d - 1],
            r1.at[d - 1],
            others[d - 1],
        )
        for d in range(1, pairs)
    ]
    mine = part(core * half + pair * chunk, chunk)
    gather = [
        remote(all_ref.at[mine], all_ref.at[mine], s2.at[d - 1], r2.at[d - 1], others[d - 1])
        for d in range(1, pairs)
    ]
    whole = part(core * half, half)
    last = remote(all_ref.at[whole], all_ref.at[whole], s3.at[0], r3.at[0], sibling)

    def scatter_stage():
        swap.wait()
        acc_ref[...] = x_ref[part(core * half, half), :] + half_in[...]
        for copy in scatter:
            copy.start()

    def gather_stage():
        total = acc_ref[part(pair * chunk, chunk), :]
        for d in range(1, pairs):
            scatter[d - 1].wait_recv()
            total = total + slots_in[d - 1]
        all_ref[mine, :] = total
        for copy in gather:
            copy.start()

    def last_stage():
        for copy in gather:
            copy.wait()
        for copy in scatter:
            copy.wait_send()
        last.start()

    return swap.start, scatter_stage, gather_stage, last_stage, last.wait


def back_kernel(
    pairs,
    index_ref,
    cross_hbm,
    sib_hbm,
    relay_hbm,
    direct_hbm,
    own_hbm,
    grad_hbm,
    hidden_hbm,
    before_hbm,
    agg_hbm,
    tiles_hbm,
    feats_ref,
    wcat_ref,
    w_self_ref,
    w_agg_ref,
    w_out_ref,
    gout1_ref,
    gself1_ref,
    gagg1_ref,
    loss_ref,
    early_ref,
    all_ref,
    wcat_t_ref,
    cross_in,
    sib_in,
    relay_in,
    total_in,
    relay_send,
    direct_send,
    relay_ref,
    direct_ref,
    own_ref,
    grad_ref,
    hidden_ref,
    before_ref,
    agg_ref,
    tiles_ref,
    slope_ref,
    block_feats_ref,
    x_ref,
    half_in,
    acc_ref,
    slots_in,
    early_x,
    early_half,
    early_acc,
    early_slots,
    local_sem,
    *sems,
):
    ys, yr, zs, zr, cs, cr, ss, sr = sems[:8]
    direct, sibling, onward, source, to_direct = peers()
    me = lax.axis_index("phi")
    pair, core = me // 2, me % 2
    others = [((pair + d) % pairs) * 2 + core for d in range(1, pairs)]
    blocks, slots, rows, _ = tiles_ref.shape
    depth, width = wcat_ref.shape
    window = feats_ref.shape[1] // rows
    size = grad_ref.shape[0] // CHUNKS
    group = blocks // CHUNKS
    loads = [
        pltpu.make_async_copy(src, dst, local_sem.at[k])
        for k, (src, dst) in enumerate(
            (
                (relay_hbm, relay_ref),
                (direct_hbm, direct_ref),
                (own_hbm, own_ref),
                (grad_hbm, grad_ref),
                (hidden_hbm, hidden_ref),
                (before_hbm, before_ref),
                (agg_hbm, agg_ref),
                (tiles_hbm, tiles_ref),
            )
        )
    ]
    for copy in loads:
        copy.start()
    greet([sibling] + others)

    def span(i):
        return pl.ds(pl.multiple_of(i * size, size), size)

    def crosses(i):
        return remote(cross_hbm.at[span(i)], cross_in.at[span(i)], cs.at[i], cr.at[i], sibling)

    def first(i):
        return remote(relay_send.at[span(i)], relay_in.at[span(i)], zs.at[i], zr.at[i], source)

    def second(i):
        return remote(direct_send.at[span(i)], total_in.at[span(i)], ys.at[i], yr.at[i], direct)

    near = remote(sib_hbm, sib_in, ss.at[0], sr.at[0], sibling)
    lax.fori_loop(0, CHUNKS, lambda i, c: (crosses(i).start(), c)[1], 0)
    near.start()

    early = summer(pairs, early_x, early_half, early_acc, early_slots, early_ref, sems[8:16])
    final = summer(pairs, x_ref, half_in, acc_ref, slots_in, all_ref, sems[16:24])
    for k, value in enumerate((gout1_ref, gself1_ref, gagg1_ref)):
        early_x[k * width : (k + 1) * width, :] = value[...]
    if early_x.shape[0] > 3 * width:
        early_x[3 * width :, :] = jnp.zeros((early_x.shape[0] - 3 * width, width), F32)
    early[0]()
    per = window // CHUNKS

    def slopes(i):
        for u in range(0, per, 2):
            at = pl.multiple_of((i * per + u) * rows, 2 * rows)
            feats = feats_ref[:, pl.ds(at, 2 * rows)]
            squashed = jnp.tanh(dot(wcat_t_ref[...], feats, 1, 0))
            slope = 1.0 - squashed * squashed
            for v in range(2):
                slope_ref[i * per + u + v] = slope[:, v * rows : (v + 1) * rows]
                block_feats_ref[i * per + u + v] = feats[:, v * rows : (v + 1) * rows]

    wcat_t_ref[...] = (
        jnp.concatenate([wcat_ref[...].astype(F32), jnp.zeros((width - depth, width), F32)], axis=0)
        .T[:, :depth]
        .astype(BF16)
    )
    x_ref[...] = jnp.zeros(x_ref.shape, F32)
    base = 3 * width
    x_ref[base + depth : base + depth + 8, :] = loss_ref[...]
    slope_ref[window] = jnp.zeros(slope_ref.shape[1:], F32)
    block_feats_ref[window] = jnp.zeros(block_feats_ref.shape[1:], BF16)
    loads[0].wait()

    def relay_step(i, carry):
        here = span(i)
        crosses(i).wait_recv()
        extra = jnp.where(to_direct, 0.0, cross_in[here, :].astype(F32))
        relay_send[here, :] = (relay_ref[here, :].astype(F32) + extra).astype(BF16)
        first(i).start()
        return carry

    lax.fori_loop(0, CHUNKS, relay_step, 0)
    early[1]()
    loads[1].wait()

    def direct_step(i, carry):
        here = span(i)
        first(i).wait_recv()
        extra = jnp.where(to_direct, cross_in[here, :].astype(F32), 0.0)
        direct_send[here, :] = (
            direct_ref[here, :].astype(F32) + extra + relay_in[here, :].astype(F32)
        ).astype(BF16)
        second(i).start()
        slopes(i)
        return carry

    lax.fori_loop(0, CHUNKS, direct_step, 0)
    early[2]()
    for copy in loads[2:]:
        copy.wait()
    near.wait()

    def layer_step(i, carry):
        here = span(i)
        second(i).wait_recv()
        returned = own_ref[here, :] + (
            total_in[here, :].astype(F32) + sib_in[here, :].astype(F32)
        )
        gradient = grad_ref[here, :] + jnp.concatenate(
            [returned[g * width : (g + 1) * width].T for g in range(group)], axis=0
        )
        upstream = gradient.astype(BF16)
        hidden = hidden_ref[here, :]
        hidden_grad = dot(upstream, w_out_ref[0], 1, 1)
        act_grad = jnp.where(hidden.astype(F32) > 0, hidden_grad, 0.0).astype(BF16)
        agg_grad_t = dot(w_agg_ref[0], act_grad, 1, 1).astype(BF16)
        x_ref[0:width, :] += dot(hidden, upstream, 0, 0)
        x_ref[width : 2 * width, :] += dot(before_ref[here, :], act_grad, 0, 0)
        x_ref[2 * width : 3 * width, :] += dot(agg_ref[here, :], act_grad, 0, 0)
        own_grad = gradient + dot(act_grad, w_self_ref[0], 1, 1)
        feats = feats_ref[:, pl.ds(pl.multiple_of((window // 5) * rows + i * size, size), size)]
        squashed = jnp.tanh(dot(feats, wcat_ref[...], 0, 0))
        genc = dot(feats, (own_grad * (1.0 - squashed * squashed)).astype(BF16), 1, 0)
        for g in range(group):
            block = i * group + g
            tile = jnp.concatenate([tiles_ref[block, s] for s in range(slots)], axis=1)
            contrib = dot(agg_grad_t[:, g * rows : (g + 1) * rows], tile, 1, 0)
            places = [index_ref[block * slots + s] for s in range(slots)]
            slope = jnp.concatenate([slope_ref[at] for at in places], axis=1)
            source_feats = jnp.concatenate([block_feats_ref[at] for at in places], axis=1)
            genc = genc + dot(source_feats, (contrib * slope).astype(BF16), 1, 1)
        x_ref[base : base + depth, :] += genc
        return carry

    lax.fori_loop(0, CHUNKS, layer_step, 0)
    final[0]()
    early[3]()

    def drain(i, carry):
        crosses(i).wait_send()
        first(i).wait_send()
        second(i).wait_send()
        return carry

    lax.fori_loop(0, CHUNKS, drain, 0)

    for stage in final[1:]:
        stage()
    early[4]()


def finish_kernel(
    triplet_total,
    early_ref,
    sum_ref,
    loss_out,
    genc_out,
    gtable_out,
    gself_out,
    gagg_out,
    gout_out,
):
    width = gself_out.shape[1]
    for k, out in enumerate((gout_out, gself_out, gagg_out)):
        for layer, source in enumerate((sum_ref, early_ref)):
            out[layer] = source[k * width : (k + 1) * width, :]
    base = 3 * width
    genc_out[...] = sum_ref[base : base + genc_out.shape[0], :]
    gtable_out[...] = sum_ref[base + 16 : base + 16 + gtable_out.shape[0], :]
    at = base + 16 + gtable_out.shape[0]
    loss_out[...] = sum_ref[at : at + 1, 0:1] / triplet_total


def body(
    hit_feats,
    layer_ids,
    edge_tiles,
    src_blocks,
    live_slots,
    anchor_hits,
    positive_hits,
    negative_hits,
    w_enc,
    layer_table,
    w_self,
    w_agg,
    w_out,
):
    blocks, slots, rows, _ = edge_tiles.shape
    width = w_enc.shape[1]
    features = hit_feats.shape[0]
    kinds = layer_table.shape[0]
    hits = blocks * rows
    layer_total = w_self.shape[0]
    triplets = anchor_hits.shape[0]
    group = 4
    steps = blocks // group
    span = group * rows
    me = lax.axis_index("phi")
    is_even = me % 2 == 0
    even_pair = (me // 2) % 2 == 0

    def place(part):
        spots = (
            jnp.where(even_pair, 2, 0),
            jnp.where(is_even, 4, 3),
            1,
            jnp.where(is_even, 3, 4),
            jnp.where(even_pair, 0, 2),
        )
        return sum(jnp.where(part == k, spot, 0) for k, spot in enumerate(spots))

    live = jnp.arange(slots, dtype=jnp.int32)[None, :] < live_slots[:, None]
    index = jnp.where(
        live, place(src_blocks // blocks) * blocks + src_blocks % blocks, 5 * blocks
    ).reshape(blocks * slots)
    depth = 16 + kinds
    listed = 2 * triplets // 128 + 1
    list_shape = (-(-(listed + 1) // 8) * 8, 128)

    tile_spec = pl.BlockSpec((group, slots, rows, rows), lambda i, *_: (i, 0, 0, 0))
    row_spec = pl.BlockSpec((span, width), lambda i, *_: (i, 0))
    weight_spec = full((width, width))
    any_spec = pl.BlockSpec(memory_space=pl.ANY)
    row_shape = jax.ShapeDtypeStruct((hits, width), BF16)
    weight_shape = jax.ShapeDtypeStruct((width, width), F32)

    wide_shape = jax.ShapeDtypeStruct((hits, width), F32)
    vmem = pl.BlockSpec(memory_space=pltpu.VMEM)
    smem = pl.BlockSpec(memory_space=pltpu.SMEM)
    few = pltpu.SemaphoreType.DMA((FEAT_CHUNKS,))
    each = pltpu.SemaphoreType.DMA((CHUNKS,))
    one = pltpu.SemaphoreType.DMA((1,))
    four = pltpu.SemaphoreType.DMA((4,))
    block_shape = jax.ShapeDtypeStruct((blocks, rows, width), BF16)
    before0, agg0, hidden0, latents1, agg1, hidden1, latents2, lists, feats, wcat = pl.pallas_call(
        functools.partial(forward_kernel, features),
        in_specs=[smem] + [vmem] * 4 + [any_spec] + [vmem] * 5,
        out_specs=[any_spec] * 10,
        out_shape=[block_shape, row_shape, row_shape, block_shape, row_shape, row_shape]
        + [
            wide_shape,
            jax.ShapeDtypeStruct((5,) + list_shape, jnp.int32),
            jax.ShapeDtypeStruct((depth, 5 * hits), BF16),
            jax.ShapeDtypeStruct((depth, width), BF16),
        ],
        scratch_shapes=[
            pltpu.VMEM((16, hits), BF16),
            pltpu.VMEM((depth, width), BF16),
            pltpu.VMEM(list_shape, jnp.int32),
            pltpu.VMEM((listed - 1, 128, 128), jnp.int32),
            pltpu.VMEM((listed - 1, 128, 128), jnp.int32),
            pltpu.VMEM((listed - 1, 128, 128), jnp.int32),
            pltpu.VMEM((5, 16, hits), BF16),
            pltpu.VMEM((depth, 5 * hits), BF16),
            pltpu.VMEM((5 * blocks + 1, rows, width), BF16),
            pltpu.VMEM((5 * blocks + 1, rows, width), BF16),
        ]
        + [pltpu.VMEM((hits, width), BF16)] * 4
        + [
            pltpu.VMEM((hits, width), F32),
            pltpu.VMEM(edge_tiles.shape, BF16),
            each,
            pltpu.SemaphoreType.DMA((6,)),
            pltpu.SemaphoreType.DMA((3 * LATER_STEPS,)),
            one,
        ]
        + [few] * 6
        + [four] * 2
        + [each] * 8
        + [one] * 2,
        compiler_params=pltpu.CompilerParams(
            collective_id=1, has_side_effects=True, vmem_limit_bytes=VMEM_BYTES
        ),
        name="forward",
    )(
        index,
        hit_feats,
        layer_ids.reshape(1, hits),
        positive_hits.reshape(triplets // 128, 128),
        negative_hits.reshape(triplets // 128, 128),
        edge_tiles,
        w_enc,
        layer_table,
        w_self,
        w_agg,
        w_out,
    )

    before0, latents1 = before0.reshape(hits, width), latents1.reshape(hits, width)
    lists = lists.reshape(-1)
    move_shape = jax.ShapeDtypeStruct((triplets, width), BF16)
    wide_move = jax.ShapeDtypeStruct((triplets, width), F32)
    move_spec = full((triplets, width))
    *found, anchors = pl.pallas_call(
        gather_kernel,
        grid_spec=pltpu.PrefetchScalarGridSpec(
            num_scalar_prefetch=2,
            grid=(1,),
            in_specs=[full((hits, width))],
            out_specs=[move_spec] * 6,
            scratch_shapes=[pltpu.VMEM((2 * triplets + 8, width), F32)],
        ),
        out_shape=[move_shape] * 6,
        compiler_params=params(),
        name="gather",
    )(lists, anchor_hits, latents2)
    coef_shape = (triplets // 128, 128)
    loss_part, ganchor, *moves, coef, coefs = pl.pallas_call(
        functools.partial(contrast_kernel, 1.0 / math.sqrt(width)),
        in_specs=[vmem] * 6,
        out_specs=[vmem] * 8,
        out_shape=[jax.ShapeDtypeStruct((8, width), F32), wide_move]
        + [move_shape] * 4
        + [jax.ShapeDtypeStruct(coef_shape, F32), jax.ShapeDtypeStruct((4,) + coef_shape, F32)],
        scratch_shapes=[pltpu.VMEM((triplets, width), F32)]
        + [pltpu.VMEM((triplets, width), BF16)] * 6
        + [pltpu.SemaphoreType.DMA((PARTS,))] * 16
        + [pltpu.SemaphoreType.DMA((4,))] * 2,
        compiler_params=pltpu.CompilerParams(
            collective_id=4, has_side_effects=True, vmem_limit_bytes=VMEM_BYTES
        ),
        name="contrast",
    )(*found, anchors)

    t_shape = jax.ShapeDtypeStruct((blocks, width, rows), F32)
    t_half = jax.ShapeDtypeStruct((blocks, width, rows), BF16)
    t_full = pl.BlockSpec(
        (blocks, width, rows), lambda *_: (0, 0, 0), pipeline_mode=pl.Buffered(1)
    )
    adj_shape = pltpu.VMEM((5 * blocks + 1, width, rows), F32)
    gout1, gself1, gagg1, direct, obelow, own, oabove, osibling, ocross = pl.pallas_call(
        functools.partial(last_backward, group, steps),
        grid_spec=pltpu.PrefetchScalarGridSpec(
            num_scalar_prefetch=3,
            grid=(steps,),
            in_specs=[tile_spec, move_spec, full(coef_shape), full((4,) + coef_shape)]
            + [move_spec] * 5
            + [row_spec] * 3
            + [full((2, width, width))] * 3,
            out_specs=[weight_spec] * 3 + [row_spec] + [t_full] * 5,
            scratch_shapes=[adj_shape, pltpu.VMEM((10 * triplets + 40, width), F32)]
            + [pltpu.VMEM((hits, width), F32)] * 4,
        ),
        out_shape=[weight_shape] * 3 + [wide_shape] + [t_half, t_shape] + [t_half] * 3,
        compiler_params=params(),
        name="last_backward",
    )(
        index, lists, anchor_hits, edge_tiles, ganchor, coef, coefs, anchors, *moves, hidden1, latents1, agg1,
        w_self, w_agg, w_out,
    )
    pairs = lax.axis_size("phi") // 2

    def sum_sizes(count):
        chunk = -(-count // (16 * pairs)) * 8
        total = 2 * pairs * chunk
        return jax.ShapeDtypeStruct((total, width), F32), [
            pltpu.VMEM((total, width), F32),
            pltpu.VMEM((total // 2, width), F32),
            pltpu.VMEM((total // 2, width), F32),
            pltpu.VMEM((pairs - 1, chunk, width), F32),
        ]

    early_shape, early_scratch = sum_sizes(3 * width)
    final_shape, final_scratch = sum_sizes(3 * width + depth + 8)
    many = pltpu.SemaphoreType.DMA((pairs - 1,))
    flat = (hits, width)
    sums = pl.pallas_call(
        functools.partial(back_kernel, pairs),
        in_specs=[smem] + [any_spec] * 10 + [vmem] * 9,
        out_specs=[vmem] * 2,
        out_shape=[early_shape, final_shape],
        scratch_shapes=[pltpu.VMEM((width, depth), BF16)]
        + [pltpu.VMEM(flat, BF16)] * 8
        + [pltpu.VMEM(flat, F32)] * 2
        + [pltpu.VMEM(flat, BF16)] * 3
        + [
            pltpu.VMEM(edge_tiles.shape, BF16),
            pltpu.VMEM((5 * blocks + 1, width, rows), F32),
            pltpu.VMEM((5 * blocks + 1, depth, rows), BF16),
        ]
        + final_scratch
        + early_scratch
        + [pltpu.SemaphoreType.DMA((8,))]
        + [pltpu.SemaphoreType.DMA((CHUNKS,))] * 6
        + [one, one]
        + [one, one, many, many, many, many, one, one] * 2,
        compiler_params=pltpu.CompilerParams(
            collective_id=3, has_side_effects=True, vmem_limit_bytes=VMEM_BYTES
        ),
        name="back",
    )(
        index, ocross.reshape(flat), osibling.reshape(flat), oabove.reshape(flat),
        obelow.reshape(flat), own.reshape(flat), direct, hidden0, before0, agg0, edge_tiles,
        feats, wcat, w_self, w_agg, w_out, gout1, gself1, gagg1, loss_part,
    )
    stack = jax.ShapeDtypeStruct((2, width, width), F32)
    loss, genc, gtable, gself, gagg, gout = pl.pallas_call(
        functools.partial(finish_kernel, float(triplets * lax.axis_size("phi"))),
        in_specs=[vmem] * 2,
        out_specs=[vmem] * 6,
        out_shape=[
            jax.ShapeDtypeStruct((1, 1), F32),
            jax.ShapeDtypeStruct((features, width), F32),
            jax.ShapeDtypeStruct((kinds, width), F32),
            stack, stack, stack,
        ],
        name="finish",
    )(*sums)
    return (loss.reshape(1), genc, gtable, gself, gagg, gout)


def solution(mesh):
    both = ("event", "phi")
    in_specs = (
        P(None, both),
        P(both),
        P(both, None, None, None),
        P(both, None),
        P(both),
        P(both),
        P(both),
        P(both),
        P(),
        P(),
        P(),
        P(),
        P(),
    )
    out_specs = (
        P("event"),
        P("event", None),
        P("event", None),
        P("event", None, None),
        P("event", None, None),
        P("event", None, None),
    )
    return jax.shard_map(body, mesh=mesh, in_specs=in_specs, out_specs=out_specs, check_vma=False)
```

```python
import functools
import math

import jax
import jax.numpy as jnp
from jax import lax
from jax.experimental import pallas as pl
from jax.experimental.pallas import tpu as pltpu
from jax.sharding import PartitionSpec as P

loss_divisor = 64.0
F32 = jnp.float32
BF16 = jnp.bfloat16
VMEM_BYTES = 60 * 1024 * 1024


def dot(left, right, left_dim, right_dim):
    return lax.dot_general(
        left, right, (((left_dim,), (right_dim,)), ((), ())), preferred_element_type=F32
    )


def full(shape):
    return pl.BlockSpec(shape, lambda *_: (0,) * len(shape))


def params():
    return pltpu.CompilerParams(
        dimension_semantics=("arbitrary",), vmem_limit_bytes=VMEM_BYTES
    )


CHUNKS = 16
LATER_STEPS = 8


def peers():
    count = lax.axis_size("phi")
    me = lax.axis_index("phi")
    odd_pair = (me // 2) % 2
    odd_core = me % 2
    direct = me + 2 - 4 * odd_pair
    sibling = me + 1 - 2 * odd_core
    stride = 4 - 8 * odd_pair
    onward = (me + stride + count) % count
    source = (me - stride + count) % count
    return direct, sibling, onward, source, odd_pair == odd_core


def remote(src, dst, send, recv, target):
    return pltpu.make_async_remote_copy(
        src_ref=src,
        dst_ref=dst,
        send_sem=send,
        recv_sem=recv,
        device_id={"phi": target},
        device_id_type=pl.DeviceIdType.MESH,
    )


def greet(targets):
    barrier = pltpu.get_barrier_semaphore()
    for target in targets:
        pl.semaphore_signal(
            barrier, inc=1, device_id={"phi": target}, device_id_type=pl.DeviceIdType.MESH
        )
    pl.semaphore_wait(barrier, len(targets))


def role_targets():
    count = lax.axis_size("phi")
    me = lax.axis_index("phi")
    odd_pair = (me // 2) % 2
    odd_core = me % 2
    sibling = me + 1 - 2 * odd_core
    across = (me - 1 + 2 * odd_core + count) % count
    direct = me + 2 - 4 * odd_pair
    far = (me - 2 + 4 * odd_pair + count) % count
    return sibling, across, direct, far


def aggregate_group(index_ref, tiles_ref, window_ref, step, group, slots, rows):
    results = []
    for g in range(group):
        tile = jnp.concatenate([tiles_ref[step * group + g, s] for s in range(slots)], axis=1)
        source = jnp.concatenate(
            [
                window_ref[index_ref[(step * group + g) * slots + s]] for s in range(slots)
            ],
            axis=0,
        )
        results.append(dot(tile, source, 1, 0).astype(BF16))
    return jnp.concatenate(results, axis=0)


def node_update(own, aggregated, w_self, w_agg, w_out):
    activation = dot(own, w_self, 1, 0) + dot(aggregated, w_agg, 1, 0)
    hidden = jnp.maximum(activation, 0.0).astype(BF16)
    updated = (own.astype(F32) + dot(hidden, w_out, 1, 0)).astype(BF16)
    return hidden, updated


FEAT_CHUNKS = 2


def forward_kernel(
    features,
    index_ref,
    hit_ref,
    id_ref,
    positive_ref,
    negative_ref,
    tiles_hbm,
    enc_ref,
    table_ref,
    w_self_ref,
    w_agg_ref,
    w_out_ref,
    before_out,
    agg0_out,
    hidden0_out,
    latents_out,
    agg1_out,
    hidden1_out,
    z_out,
    lists_out,
    feats_out,
    wcat_out,
    packed_ref,
    wcat_ref,
    keys_ref,
    key_cols,
    place_cols,
    entry_cols,
    packs_ref,
    feats_ref,
    window_ref,
    later_ref,
    agg0_ref,
    hidden0_ref,
    agg1_ref,
    hidden1_ref,
    z_ref,
    tiles_ref,
    tile_sem,
    out_sem,
    late_sem,
    list_sem,
    *sems,
):
    fys, fyr, fzs, fzr, fcs, fcr, ls, lr = sems[:8]
    ys, yr, zs, zr, cs, cr, ss, sr = sems[8:16]
    fss, fsr = sems[16:]
    direct, sibling, onward, source, direct_crosses = peers()
    roles = role_targets()
    blocks, slots, rows, _ = tiles_ref.shape
    hits = packed_ref.shape[1]
    group = blocks // CHUNKS
    span = group * rows

    def tile_load(i):
        part = pl.ds(i * group, group)
        return pltpu.make_async_copy(tiles_hbm.at[part], tiles_ref.at[part], tile_sem.at[i])

    lax.fori_loop(0, CHUNKS, lambda i, c: (tile_load(i).start(), c)[1], 0)
    kinds, width = table_ref.shape
    filler = jnp.zeros((16 - features, width), F32)
    wcat_ref[...] = jnp.concatenate(
        [enc_ref[...].astype(F32), filler, table_ref[...].astype(F32)], axis=0
    ).astype(BF16)

    def gather_input(i, carry):
        at = pl.ds(pl.multiple_of(i * 512, 512), 512)
        packed_ref[:, at] = jnp.concatenate(
            [
                hit_ref[:, at].astype(F32),
                id_ref[:, at].astype(F32),
                jnp.zeros((15 - features, 512), F32),
            ],
            axis=0,
        ).astype(BF16)
        return carry

    lax.fori_loop(0, hits // 512, gather_input, 0)
    beside = [t + 1 - 2 * lax.rem(t, 2) for t in (onward, source)]
    greet((direct, sibling, onward, source, beside[0], beside[1], roles[1], roles[3]))
    columns = hits // FEAT_CHUNKS

    def pack(k, i):
        return packs_ref.at[k, :, pl.ds(i * columns, columns)]

    chunks = range(FEAT_CHUNKS)
    f_first = [
        remote(
            packed_ref.at[:, pl.ds(i * columns, columns)], pack(0, i), fys.at[i], fyr.at[i], direct
        )
        for i in chunks
    ]
    f_second = [remote(pack(0, i), pack(2, i), fzs.at[i], fzr.at[i], onward) for i in chunks]
    f_cross_a = [remote(pack(0, i), pack(4, i), fcs.at[i], fcr.at[i], sibling) for i in chunks]
    f_cross_b = [remote(pack(0, i), pack(4, i), fcs.at[i], fcr.at[i], beside[0]) for i in chunks]
    f_near = remote(packed_ref, packs_ref.at[3], fss.at[0], fsr.at[0], sibling)
    for copy in f_first:
        copy.start()
    f_near.start()

    def encode(k, ref):
        step = 512
        is_feature = lax.broadcasted_iota(jnp.int32, (16, step), 0) < features
        kind = lax.broadcasted_iota(jnp.int32, (16, step), 0).astype(F32)

        def run(i, carry):
            at = pl.multiple_of(i * step, step)
            data = ref[:, pl.ds(at, step)].astype(F32)
            onehot = jnp.where(kind == data[features : features + 1], 1.0, 0.0)
            feats = jnp.concatenate([jnp.where(is_feature, data, 0.0), onehot], axis=0).astype(BF16)
            feats_ref[:, pl.ds(pl.multiple_of(k * hits + i * step, step), step)] = feats
            encoded = dot(feats, wcat_ref[...], 0, 0)
            squashed = jnp.tanh(encoded).astype(BF16)
            for u in range(step // rows):
                window_ref[k * blocks + i * (step // rows) + u] = squashed[
                    u * rows : (u + 1) * rows
                ]
            return carry

        lax.fori_loop(0, hits // step, run, 0)

    encode(1, packed_ref)
    for i in chunks:
        f_first[i].wait_recv()
        f_second[i].start()

        @pl.when(direct_crosses)
        def _():
            f_cross_a[i].start()

        @pl.when(jnp.logical_not(direct_crosses))
        def _():
            f_cross_b[i].start()

    f_near.wait_recv()
    encode(3, packs_ref.at[3])
    encode(0, packs_ref.at[0])
    for i in chunks:
        f_second[i].wait_recv()
    encode(2, packs_ref.at[2])
    for i in chunks:
        f_cross_a[i].wait_recv()
    encode(4, packs_ref.at[4])
    window_ref[5 * blocks] = jnp.zeros((rows, width), BF16)
    later_ref[5 * blocks] = jnp.zeros((rows, width), BF16)

    def part(k, i):
        return pl.ds(k * blocks + i * group, group)

    def first(i):
        return remote(later_ref.at[part(1, i)], later_ref.at[part(0, i)], ys.at[i], yr.at[i], direct)

    def near(i):
        return remote(later_ref.at[part(1, i)], later_ref.at[part(3, i)], ss.at[i], sr.at[i], sibling)

    def second(i):
        return remote(later_ref.at[part(0, i)], later_ref.at[part(2, i)], zs.at[i], zr.at[i], onward)

    def cross_a(i):
        return remote(later_ref.at[part(0, i)], later_ref.at[part(4, i)], cs.at[i], cr.at[i], sibling)

    def cross_b(i):
        return remote(later_ref.at[part(2, i)], later_ref.at[part(4, i)], cs.at[i], cr.at[i], sibling)

    def relay(i):
        first(i).wait_recv()
        second(i).start()

        @pl.when(direct_crosses)
        def _():
            cross_a(i).start()

    def land(i):
        second(i).wait_recv()

        @pl.when(jnp.logical_not(direct_crosses))
        def _():
            cross_b(i).start()

    lead = 5
    relayed = (CHUNKS - lead + 1) // 2

    def layer0(i, carry):
        tile_load(i).wait()
        here = pl.ds(pl.multiple_of(i * span, span), span)
        aggregated = aggregate_group(index_ref, tiles_ref, window_ref, i, group, slots, rows)
        own = window_ref[part(1, i)].reshape(span, width)
        hidden, updated = node_update(own, aggregated, w_self_ref[0], w_agg_ref[0], w_out_ref[0])
        later_ref[part(1, i)] = updated.reshape(group, rows, width)
        first(i).start()
        near(i).start()
        agg0_ref[here, :] = aggregated
        hidden0_ref[here, :] = hidden

        @pl.when(jnp.logical_and(i >= lead, lax.rem(i, 2) == 1))
        def _():
            relay(lax.div(i - lead, 2))

        return carry

    lax.fori_loop(0, CHUNKS, layer0, 0)
    own = pl.ds(blocks, blocks)
    saves = [
        pltpu.make_async_copy(src, dst, out_sem.at[k])
        for k, (src, dst) in enumerate(
            (
                (window_ref.at[own], before_out),
                (agg0_ref, agg0_out),
                (hidden0_ref, hidden0_out),
                (later_ref.at[own], latents_out),
                (feats_ref, feats_out),
                (wcat_ref, wcat_out),
            )
        )
    ]
    for copy in saves:
        copy.start()

    wanted = jnp.concatenate([positive_ref[...], negative_ref[...]], axis=0)
    lines = wanted.shape[0]
    pairs_of = lines * 128
    line = lax.broadcasted_iota(jnp.int32, (lines, 128), 0)
    lane = lax.broadcasted_iota(jnp.int32, (lines, 128), 1)
    keys = wanted * pairs_of + (line * 128 + lane)
    tall = jnp.concatenate(
        [wanted.astype(F32), jnp.zeros((128 - lines, 128), F32)], axis=0
    ).T.astype(jnp.int32)
    down = lax.broadcasted_iota(jnp.int32, (128, 1), 0)
    counts = []
    for k in range(5):
        mine = jnp.logical_and(wanted >= k * hits, wanted < (k + 1) * hits)
        counted = jnp.sum(jnp.where(mine, 1.0, 0.0), axis=1, keepdims=True)
        counts.append(jnp.sum(counted, axis=0, keepdims=True).astype(jnp.int32))
    aligned, shift = [jnp.zeros((1, 1), jnp.int32)], [jnp.zeros((1, 1), jnp.int32)]
    for k in range(5):
        filled = lax.bitwise_and(counts[k] + 7, -8)
        aligned.append(aligned[k] + filled)
        shift.append(shift[k] + filled - counts[k])
    for c in range(lines):
        column = tall[:, c : c + 1]
        slot = down + c * 128
        moved = jnp.zeros((128, 1), jnp.int32)
        first_row = jnp.zeros((128, 1), jnp.int32)
        for k in range(5):
            mine = jnp.logical_and(column >= k * hits, column < (k + 1) * hits)
            moved = moved + jnp.where(mine, shift[k], 0)
            first_row = first_row + jnp.where(mine, k * hits, 0)
        entry = (column - first_row) * (1 << ENTRY_BITS) + slot - pairs_of
        key_cols[c] = jnp.broadcast_to(column * pairs_of + slot, (128, 128))
        place_cols[c] = jnp.broadcast_to(moved, (128, 128))
        entry_cols[c] = jnp.broadcast_to(entry, (128, 128))

    def rank(c, carry):
        column = key_cols[c]
        count = jnp.zeros((128, 128), F32)
        for r in range(lines):
            count = count + jnp.where(keys[r : r + 1] < column, 1.0, 0.0)
        total = jnp.sum(count, axis=1, keepdims=True).astype(jnp.int32)
        place_cols[c] = place_cols[c] + jnp.broadcast_to(total, (128, 128))
        return carry

    keys_ref[...] = jnp.zeros(keys_ref.shape, jnp.int32)

    def put(q, carry):
        target = lax.broadcasted_iota(jnp.int32, (128, 128), 1) + q * 128

        def match(c, total):
            return total + jnp.where(place_cols[c] == target, entry_cols[c], 0)

        total = lax.fori_loop(0, lines, match, jnp.zeros((128, 128), jnp.int32))
        found = jnp.sum(total.astype(F32), axis=0, keepdims=True).astype(jnp.int32)
        keys_ref[pl.ds(q, 1), :] = found + pairs_of
        return carry

    turns = 3
    for k in range(turns):
        relay(relayed + k)
        land(k)
        lax.fori_loop(lines * k // turns, lines * (k + 1) // turns, rank, 0)
    put_turns = CHUNKS - relayed - turns - 2
    for k in range(put_turns):
        relay(relayed + turns + k)
        land(turns + k)
        lax.fori_loop(
            (lines + 1) * k // put_turns, (lines + 1) * (k + 1) // put_turns, put, 0
        )
    lane = lax.broadcasted_iota(jnp.int32, (1, 128), 1)
    keys_ref[pl.ds(lines + 1, 1), :] = sum(
        jnp.where(lane == k, aligned[k] // 8, 0) for k in range(6)
    )
    lists = [
        remote(keys_ref, lists_out.at[j + 1], ls.at[j], lr.at[j], target)
        for j, target in enumerate(roles)
    ]
    for copy in lists:
        copy.start()
    own_list = pltpu.make_async_copy(keys_ref, lists_out.at[0], list_sem.at[0])
    own_list.start()

    for k in range(CHUNKS - 2, CHUNKS):
        relay(k)
    for k in range(turns + put_turns, CHUNKS):
        land(k)

    def settle(i, carry):
        near(i).wait()
        cross_a(i).wait_recv()
        return carry

    lax.fori_loop(0, CHUNKS, settle, 0)

    later_group = blocks // LATER_STEPS
    later_span = later_group * rows

    def late_saves(i):
        here = pl.ds(pl.multiple_of(i * later_span, later_span), later_span)
        return [
            pltpu.make_async_copy(src.at[here], dst.at[here], late_sem.at[k * LATER_STEPS + i])
            for k, (src, dst) in enumerate(
                ((agg1_ref, agg1_out), (hidden1_ref, hidden1_out), (z_ref, z_out))
            )
        ]

    def layer1(i, carry):
        here = pl.ds(pl.multiple_of(i * later_span, later_span), later_span)
        aggregated = aggregate_group(index_ref, tiles_ref, later_ref, i, later_group, slots, rows)
        own = later_ref[pl.ds(blocks + i * later_group, later_group)].reshape(later_span, width)
        hidden, updated = node_update(own, aggregated, w_self_ref[1], w_agg_ref[1], w_out_ref[1])
        agg1_ref[here, :] = aggregated
        hidden1_ref[here, :] = hidden
        z_ref[here, :] = updated.astype(F32)
        for copy in late_saves(i):
            copy.start()
        return carry

    lax.fori_loop(0, LATER_STEPS, layer1, 0)

    def drain(i, carry):
        first(i).wait_send()
        second(i).wait_send()
        cross_a(i).wait_send()
        return carry

    lax.fori_loop(0, CHUNKS, drain, 0)

    def saved(i, carry):
        for copy in late_saves(i):
            copy.wait()
        return carry

    lax.fori_loop(0, LATER_STEPS, saved, 0)
    for i in chunks:
        f_first[i].wait_send()
        f_second[i].wait_send()
        f_cross_a[i].wait_send()
    f_near.wait_send()
    own_list.wait()
    for copy in lists:
        copy.wait()
    for copy in saves:
        copy.wait()


def segments(list_ref, stride, listed):
    me = lax.axis_index("phi")
    odd_core, odd_pair = lax.rem(me, 2), lax.rem(lax.div(me, 2), 2)
    places = (2, 1 + 2 * odd_core, 3 - 2 * odd_core, 4 * odd_pair, 4 - 4 * odd_pair)
    starts = [j * stride + listed + k for j, k in enumerate(places)]
    return [(list_ref[at], list_ref[at + 1]) for at in starts]


def gather_kernel(list_ref, anchor_ref, z_ref, *refs):
    outs, (anchor_out, buf_ref) = refs[:5], refs[5:]
    triplets, width = anchor_out.shape
    stride = list_ref.shape[0] // 5
    bounds = segments(list_ref, stride, 2 * triplets + 128)

    def anchors(i, carry):
        at = pl.multiple_of(i * 16, 16)
        anchor_out[pl.ds(at, 16), :] = jnp.concatenate(
            [z_ref[pl.ds(anchor_ref[i * 16 + u], 1), :] for u in range(16)], axis=0
        ).astype(BF16)
        return carry

    lax.fori_loop(0, triplets // 16, anchors, 0)
    zeros = jnp.zeros((64, width), F32)

    def clear(i, carry):
        buf_ref[pl.ds(pl.multiple_of(i * 64, 64), 64), :] = zeros
        return carry

    lax.fori_loop(0, 2 * triplets // 64, clear, 0)
    for j in range(5):

        def fetch(i, carry, j=j):
            for u in range(8):
                entry = list_ref[j * stride + i * 8 + u]
                row = z_ref[pl.ds(lax.shift_right_logical(entry, ENTRY_BITS), 1), :]
                buf_ref[pl.ds(lax.bitwise_and(entry, ENTRY_MASK), 1), :] = row
            return carry

        lax.fori_loop(bounds[j][0], bounds[j][1], fetch, 0)

        def subtract(i, carry, j=j):
            at = pl.multiple_of(i * 64, 64)
            value = buf_ref[pl.ds(triplets + at, 64), :] - buf_ref[pl.ds(at, 64), :]
            outs[j][pl.ds(at, 64), :] = value.astype(BF16)
            buf_ref[pl.ds(triplets + at, 64), :] = zeros
            buf_ref[pl.ds(at, 64), :] = zeros
            return carry

        lax.fori_loop(0, triplets // 64, subtract, 0)


ENTRY_BITS = 12
ENTRY_MASK = (1 << ENTRY_BITS) - 1
PARTS = 8


def contrast_kernel(
    inv_root,
    self_ref,
    sib_ref,
    cross_ref,
    near_ref,
    far_ref,
    anchor_ref,
    loss_ref,
    ganchor_ref,
    asib_ref,
    across_ref,
    adirect_ref,
    afar_ref,
    coef_out,
    coefs_out,
    change_ref,
    sib_in,
    cross_in,
    far_send,
    far_in,
    near_send,
    near_in,
    *sems,
):
    s = [sems[2 * i : 2 * i + 2] for i in range(9)]
    direct, sibling, onward, source, near_adds = peers()
    roles = role_targets()
    size = anchor_ref.shape[0] // PARTS
    greet((direct, sibling, onward, source, roles[1], roles[3]))

    def rows(i):
        return pl.ds(i * size, size)

    def copies(k, src, dst, target):
        return [
            remote(src.at[rows(i)], dst.at[rows(i)], s[k][0].at[i], s[k][1].at[i], target)
            for i in range(PARTS)
        ]

    crosses = copies(0, cross_ref, cross_in, sibling)
    sibs = copies(1, sib_ref, sib_in, sibling)
    hops = copies(2, far_send, far_in, source)
    nears = copies(3, near_send, near_in, direct)
    to_direct = copies(4, anchor_ref, adirect_ref, direct)
    to_sibling = copies(5, anchor_ref, asib_ref, sibling)
    relays = copies(6, adirect_ref, afar_ref, onward)
    cross_a = copies(7, adirect_ref, across_ref, sibling)
    cross_b = copies(7, afar_ref, across_ref, sibling)
    coefs = [
        remote(coef_out, coefs_out.at[j], s[8][0].at[j], s[8][1].at[j], target)
        for j, target in enumerate(roles)
    ]
    for copy in crosses:
        copy.start()
    for copy in sibs:
        copy.start()
    for i in range(PARTS):
        crosses[i].wait_recv()
        extra = jnp.where(near_adds, 0.0, cross_in[rows(i), :].astype(F32))
        far_send[rows(i), :] = (far_ref[rows(i), :].astype(F32) + extra).astype(BF16)
        hops[i].start()
        if i < PARTS // 2:
            to_direct[i].start()
    for i in range(PARTS):
        hops[i].wait_recv()
        extra = jnp.where(near_adds, cross_in[rows(i), :].astype(F32), 0.0)
        near_send[rows(i), :] = (
            near_ref[rows(i), :].astype(F32) + extra + far_in[rows(i), :].astype(F32)
        ).astype(BF16)
        nears[i].start()
    for i in range(PARTS // 2, PARTS):
        to_direct[i].start()

    def relay(i):
        to_sibling[i].start()
        to_direct[i].wait_recv()
        relays[i].start()

        @pl.when(near_adds)
        def _():
            cross_a[i].start()

    gaps = []
    for i in range(PARTS):
        if i < PARTS // 2:
            relay(i)
        sibs[i].wait_recv()
        nears[i].wait_recv()
        change = (
            near_in[rows(i), :].astype(F32)
            + self_ref[rows(i), :].astype(F32)
            + sib_in[rows(i), :].astype(F32)
        )
        change_ref[rows(i), :] = change
        product = anchor_ref[rows(i), :].astype(F32) * change
        for u in range(size // 128):
            gaps.append(
                jnp.sum(product[u * 128 : (u + 1) * 128].T, axis=0, keepdims=True) * inv_root
            )
    gap = jnp.concatenate(gaps, axis=0)
    coef_out[...] = jax.nn.sigmoid(gap) * (inv_root / loss_divisor)
    for copy in coefs:
        copy.start()
    soft = jnp.maximum(gap, 0.0) + jnp.log1p(jnp.exp(-jnp.abs(gap)))
    loss_ref[...] = jnp.broadcast_to(jnp.sum(soft, keepdims=True), loss_ref.shape)
    for i in range(PARTS // 2, PARTS):
        relay(i)
    for i in range(PARTS):
        relays[i].wait_recv()

        @pl.when(jnp.logical_not(near_adds))
        def _():
            cross_b[i].start()

    size = 128
    eye = lax.broadcasted_iota(jnp.int32, (size, size), 0) == lax.broadcasted_iota(
        jnp.int32, (size, size), 1
    )
    for i in range(coef_out.shape[0]):
        coef = coef_out[pl.ds(i, 1), :]
        column = jnp.sum(jnp.where(eye, coef, 0.0), axis=1, keepdims=True)
        here = pl.ds(i * size, size)
        ganchor_ref[here, :] = column * change_ref[here, :]
    for copy in coefs:
        copy.wait()
    for i in range(PARTS):
        crosses[i].wait_send()
        sibs[i].wait_send()
        hops[i].wait_send()
        nears[i].wait_send()
        to_direct[i].wait_send()
        to_sibling[i].wait()
        relays[i].wait_send()
        cross_a[i].wait()


def spread_group(index_ref, tiles_ref, adj_ref, agg_grad_t, step, group, slots, rows):
    for g in range(group):
        tile = jnp.concatenate([tiles_ref[g, s] for s in range(slots)], axis=1)
        contrib = dot(agg_grad_t[:, g * rows : (g + 1) * rows], tile, 1, 0)
        for s in range(slots):
            at = index_ref[(step * group + g) * slots + s]
            adj_ref[at] = adj_ref[at] + contrib[:, s * rows : (s + 1) * rows]


def clear_blocks(adj_ref):
    def clear(i, carry):
        adj_ref[i] = jnp.zeros(adj_ref.shape[1:], F32)
        return carry

    lax.fori_loop(0, adj_ref.shape[0], clear, 0)


def scatter_rows(
    list_ref, anchor_ref, ganchor_ref, coef_ref, coefs_ref, rows_in, moved_ref, sums
):
    triplets, width = ganchor_ref.shape
    hits = sums[0].shape[0]
    stride = list_ref.shape[0] // 5
    span = 2 * triplets + 8
    bounds = segments(list_ref, stride, 2 * triplets + 128)
    zeros = jnp.zeros((64, width), F32)

    def clear(i, carry):
        for target in sums:
            target[pl.ds(pl.multiple_of(i * 64, 64), 64), :] = zeros
        return carry

    lax.fori_loop(0, hits // 64, clear, 0)
    eye = lax.broadcasted_iota(jnp.int32, (128, 128), 0) == lax.broadcasted_iota(
        jnp.int32, (128, 128), 1
    )
    for j, source in enumerate(rows_in):
        for i in range(triplets // 128):
            coef = coef_ref[pl.ds(i, 1), :] if j == 0 else coefs_ref[j - 1, pl.ds(i, 1), :]
            spread = jnp.where(eye, coef, 0.0)
            high = spread.astype(BF16)
            low = (spread - high.astype(F32)).astype(BF16)
            part = source[pl.ds(i * 128, 128), :]
            value = dot(high, part, 1, 0) + dot(low, part, 1, 0)
            moved_ref[pl.ds(j * span + i * 128, 128), :] = -value
            moved_ref[pl.ds(j * span + triplets + i * 128, 128), :] = value
        moved_ref[pl.ds(j * span + 2 * triplets, 8), :] = zeros[:8]

    def anchors(i, carry):
        for u in range(8):
            t = i * 8 + u
            here = pl.ds(anchor_ref[t], 1)
            target = sums[u % 4]
            target[here, :] = target[here, :] + ganchor_ref[pl.ds(t, 1), :]
        return carry

    lax.fori_loop(0, triplets // 8, anchors, 0)
    for j in range(5):

        def add(i, carry, j=j):
            for u in range(8):
                entry = list_ref[j * stride + i * 8 + u]
                here = pl.ds(lax.shift_right_logical(entry, ENTRY_BITS), 1)
                target = sums[u % 4]
                moved = moved_ref[pl.ds(j * span + lax.bitwise_and(entry, ENTRY_MASK), 1), :]
                target[here, :] = target[here, :] + moved
            return carry

        lax.fori_loop(bounds[j][0], bounds[j][1], add, 0)


def last_backward(
    group,
    steps,
    index_ref,
    list_ref,
    anchor_ref,
    tiles_ref,
    ganchor_ref,
    coef_ref,
    coefs_ref,
    aself_ref,
    asib_ref,
    across_ref,
    adirect_ref,
    afar_ref,
    hidden_ref,
    w_agg_ref,
    w_out_ref,
    upstream_ref,
    act_ref,
    gradient_ref,
    obelow_ref,
    oown_ref,
    oabove_ref,
    osibling_ref,
    ocross_ref,
    adj_ref,
    moved_ref,
    *sums,
):
    step = pl.program_id(0)
    slots, rows = tiles_ref.shape[1], tiles_ref.shape[2]
    span = group * rows

    @pl.when(step == 0)
    def _():
        clear_blocks(adj_ref)
        scatter_rows(
            list_ref, anchor_ref, ganchor_ref, coef_ref, coefs_ref,
            (aself_ref, asib_ref, across_ref, adirect_ref, afar_ref), moved_ref, sums,
        )

    here = pl.ds(pl.multiple_of(step * span, span), span)
    gradient = (sums[0][here, :] + sums[1][here, :]) + (sums[2][here, :] + sums[3][here, :])
    upstream = gradient.astype(BF16)
    hidden_grad = dot(upstream, w_out_ref[1], 1, 1)
    act_grad = jnp.where(hidden_ref[...].astype(F32) > 0, hidden_grad, 0.0).astype(BF16)
    upstream_ref[...] = upstream
    act_ref[...] = act_grad
    gradient_ref[...] = gradient
    agg_grad_t = dot(w_agg_ref[1], act_grad, 1, 1).astype(BF16)
    spread_group(index_ref, tiles_ref, adj_ref, agg_grad_t, step, group, slots, rows)

    @pl.when(step == steps - 1)
    def _():
        blocks = oown_ref.shape[0]
        for k, target in enumerate((obelow_ref, oown_ref, oabove_ref, osibling_ref, ocross_ref)):

            def store(i, carry, k=k, target=target):
                target[i] = adj_ref[k * blocks + i].astype(target.dtype)
                return carry

            lax.fori_loop(0, blocks, store, 0)


def summer(pairs, x_ref, half_in, acc_ref, slots_in, all_ref, sems):
    s0, r0, s1, r1, s2, r2, s3, r3 = sems
    me = lax.axis_index("phi")
    pair, core = me // 2, me % 2
    sibling = me + 1 - 2 * core
    others = [((pair + d) % pairs) * 2 + core for d in range(1, pairs)]
    half = x_ref.shape[0] // 2
    chunk = half // pairs

    def part(start, length):
        return pl.ds(pl.multiple_of(start, 8), length)

    swap = remote(x_ref.at[part((1 - core) * half, half)], half_in, s0.at[0], r0.at[0], sibling)
    scatter = [
        remote(
            acc_ref.at[part(((pair + d) % pairs) * chunk, chunk)],
            slots_in.at[d - 1],
            s1.at[d - 1],
            r1.at[d - 1],
            others[d - 1],
        )
        for d in range(1, pairs)
    ]
    mine = part(core * half + pair * chunk, chunk)
    gather = [
        remote(all_ref.at[mine], all_ref.at[mine], s2.at[d - 1], r2.at[d - 1], others[d - 1])
        for d in range(1, pairs)
    ]
    whole = part(core * half, half)
    last = remote(all_ref.at[whole], all_ref.at[whole], s3.at[0], r3.at[0], sibling)

    def scatter_stage():
        swap.wait()
        acc_ref[...] = x_ref[part(core * half, half), :] + half_in[...]
        for copy in scatter:
            copy.start()

    def gather_stage():
        total = acc_ref[part(pair * chunk, chunk), :]
        for d in range(1, pairs):
            scatter[d - 1].wait_recv()
            total = total + slots_in[d - 1]
        all_ref[mine, :] = total
        for copy in gather:
            copy.start()

    def last_stage():
        for copy in gather:
            copy.wait()
        for copy in scatter:
            copy.wait_send()
        last.start()

    return swap.start, scatter_stage, gather_stage, last_stage, last.wait


def back_kernel(
    pairs,
    index_ref,
    cross_hbm,
    sib_hbm,
    relay_hbm,
    direct_hbm,
    own_hbm,
    grad_hbm,
    hidden_hbm,
    before_hbm,
    agg_hbm,
    tiles_hbm,
    upstream1_hbm,
    act1_hbm,
    hidden1_hbm,
    before1_hbm,
    agg1_hbm,
    feats_ref,
    wcat_ref,
    w_self_ref,
    w_agg_ref,
    w_out_ref,
    loss_ref,
    early_ref,
    all_ref,
    wcat_t_ref,
    cross_in,
    sib_in,
    relay_in,
    total_in,
    relay_send,
    direct_send,
    relay_ref,
    direct_ref,
    own_ref,
    grad_ref,
    hidden_ref,
    before_ref,
    agg_ref,
    upstream1_ref,
    act1_ref,
    hidden1_ref,
    before1_ref,
    agg1_ref,
    tiles_ref,
    slope_ref,
    block_feats_ref,
    x_ref,
    half_in,
    acc_ref,
    slots_in,
    early_x,
    early_half,
    early_acc,
    early_slots,
    local_sem,
    *sems,
):
    ys, yr, zs, zr, cs, cr, ss, sr = sems[:8]
    direct, sibling, onward, source, to_direct = peers()
    me = lax.axis_index("phi")
    pair, core = me // 2, me % 2
    others = [((pair + d) % pairs) * 2 + core for d in range(1, pairs)]
    blocks, slots, rows, _ = tiles_ref.shape
    depth, width = wcat_ref.shape
    window = feats_ref.shape[1] // rows
    size = grad_ref.shape[0] // CHUNKS
    group = blocks // CHUNKS
    loads = [
        pltpu.make_async_copy(src, dst, local_sem.at[k])
        for k, (src, dst) in enumerate(
            (
                (relay_hbm, relay_ref),
                (direct_hbm, direct_ref),
                (own_hbm, own_ref),
                (grad_hbm, grad_ref),
                (hidden_hbm, hidden_ref),
                (before_hbm, before_ref),
                (agg_hbm, agg_ref),
                (tiles_hbm, tiles_ref),
                (upstream1_hbm, upstream1_ref),
                (act1_hbm, act1_ref),
                (hidden1_hbm, hidden1_ref),
                (before1_hbm, before1_ref),
                (agg1_hbm, agg1_ref),
            )
        )
    ]
    for copy in loads:
        copy.start()
    greet([sibling] + others)

    def span(i):
        return pl.ds(pl.multiple_of(i * size, size), size)

    def crosses(i):
        return remote(cross_hbm.at[span(i)], cross_in.at[span(i)], cs.at[i], cr.at[i], sibling)

    def first(i):
        return remote(relay_send.at[span(i)], relay_in.at[span(i)], zs.at[i], zr.at[i], source)

    def second(i):
        return remote(direct_send.at[span(i)], total_in.at[span(i)], ys.at[i], yr.at[i], direct)

    near = remote(sib_hbm, sib_in, ss.at[0], sr.at[0], sibling)
    lax.fori_loop(0, CHUNKS, lambda i, c: (crosses(i).start(), c)[1], 0)
    near.start()

    early = summer(pairs, early_x, early_half, early_acc, early_slots, early_ref, sems[8:16])
    final = summer(pairs, x_ref, half_in, acc_ref, slots_in, all_ref, sems[16:24])
    early_x[...] = jnp.zeros(early_x.shape, F32)
    per = window // CHUNKS

    def slopes(i):
        for u in range(0, per, 2):
            at = pl.multiple_of((i * per + u) * rows, 2 * rows)
            feats = feats_ref[:, pl.ds(at, 2 * rows)]
            squashed = jnp.tanh(dot(wcat_t_ref[...], feats, 1, 0))
            slope = 1.0 - squashed * squashed
            for v in range(2):
                slope_ref[i * per + u + v] = slope[:, v * rows : (v + 1) * rows]
                block_feats_ref[i * per + u + v] = feats[:, v * rows : (v + 1) * rows]

    wcat_t_ref[...] = (
        jnp.concatenate([wcat_ref[...].astype(F32), jnp.zeros((width - depth, width), F32)], axis=0)
        .T[:, :depth]
        .astype(BF16)
    )
    x_ref[...] = jnp.zeros(x_ref.shape, F32)
    base = 3 * width
    x_ref[base + depth : base + depth + 8, :] = loss_ref[...]
    slope_ref[window] = jnp.zeros(slope_ref.shape[1:], F32)
    block_feats_ref[window] = jnp.zeros(block_feats_ref.shape[1:], BF16)
    loads[0].wait()

    lag = 4

    def relay_step(i, carry):
        here = span(i)
        crosses(i).wait_recv()
        extra = jnp.where(to_direct, 0.0, cross_in[here, :].astype(F32))
        relay_send[here, :] = (relay_ref[here, :].astype(F32) + extra).astype(BF16)
        first(i).start()

        @pl.when(i < CHUNKS - 2 * lag)
        def _():
            slopes(i)

        return carry

    lax.fori_loop(0, CHUNKS, relay_step, 0)
    for copy in loads[1:]:
        copy.wait()
    near.wait()

    def direct_step(i):
        here = span(i)
        first(i).wait_recv()
        extra = jnp.where(to_direct, cross_in[here, :].astype(F32), 0.0)
        direct_send[here, :] = (
            direct_ref[here, :].astype(F32) + extra + relay_in[here, :].astype(F32)
        ).astype(BF16)
        second(i).start()

    def upper_step(i):
        here = pl.ds(pl.multiple_of(i * 2 * size, 2 * size), 2 * size)
        act_grad = act1_ref[here, :]
        early_x[0:width, :] += dot(hidden1_ref[here, :], upstream1_ref[here, :], 0, 0)
        early_x[width : 2 * width, :] += dot(before1_ref[here, :], act_grad, 0, 0)
        early_x[2 * width : 3 * width, :] += dot(agg1_ref[here, :], act_grad, 0, 0)
        grad_ref[here, :] = grad_ref[here, :] + dot(act_grad, w_self_ref[1], 1, 1)

    def layer_step(i):
        here = span(i)
        second(i).wait_recv()
        returned = own_ref[here, :] + (
            total_in[here, :].astype(F32) + sib_in[here, :].astype(F32)
        )
        gradient = grad_ref[here, :] + jnp.concatenate(
            [returned[g * width : (g + 1) * width].T for g in range(group)], axis=0
        )
        upstream = gradient.astype(BF16)
        hidden = hidden_ref[here, :]
        hidden_grad = dot(upstream, w_out_ref[0], 1, 1)
        act_grad = jnp.where(hidden.astype(F32) > 0, hidden_grad, 0.0).astype(BF16)
        agg_grad_t = dot(w_agg_ref[0], act_grad, 1, 1).astype(BF16)
        x_ref[0:width, :] += dot(hidden, upstream, 0, 0)
        x_ref[width : 2 * width, :] += dot(before_ref[here, :], act_grad, 0, 0)
        x_ref[2 * width : 3 * width, :] += dot(agg_ref[here, :], act_grad, 0, 0)
        own_grad = gradient + dot(act_grad, w_self_ref[0], 1, 1)
        feats = feats_ref[:, pl.ds(pl.multiple_of((window // 5) * rows + i * size, size), size)]
        squashed = jnp.tanh(dot(feats, wcat_ref[...], 0, 0))
        genc = dot(feats, (own_grad * (1.0 - squashed * squashed)).astype(BF16), 1, 0)
        for g in range(group):
            block = i * group + g
            tile = jnp.concatenate([tiles_ref[block, s] for s in range(slots)], axis=1)
            contrib = dot(agg_grad_t[:, g * rows : (g + 1) * rows], tile, 1, 0)
            places = [index_ref[block * slots + s] for s in range(slots)]
            slope = jnp.concatenate([slope_ref[at] for at in places], axis=1)
            source_feats = jnp.concatenate([block_feats_ref[at] for at in places], axis=1)
            genc = genc + dot(source_feats, (contrib * slope).astype(BF16), 1, 1)
        x_ref[base : base + depth, :] += genc

    turn = CHUNKS // 2

    def opening(i, carry):
        direct_step(i)
        upper_step(i)

        @pl.when(i < lag)
        def _():
            slopes(CHUNKS - 2 * lag + 2 * i)
            slopes(CHUNKS - 2 * lag + 2 * i + 1)

        @pl.when(i >= lag)
        def _():
            layer_step(i - lag)

        return carry

    def middle(i, carry):
        direct_step(i)
        layer_step(i - lag)
        return carry

    def closing(i, carry):
        layer_step(i)
        return carry

    lax.fori_loop(0, turn, opening, 0)
    early[0]()
    lax.fori_loop(turn, turn + 4, middle, 0)
    early[1]()
    lax.fori_loop(turn + 4, CHUNKS, middle, 0)
    early[2]()
    lax.fori_loop(CHUNKS - lag, CHUNKS, closing, 0)
    final[0]()
    early[3]()

    def drain(i, carry):
        crosses(i).wait_send()
        first(i).wait_send()
        second(i).wait_send()
        return carry

    lax.fori_loop(0, CHUNKS, drain, 0)

    for stage in final[1:]:
        stage()
    early[4]()


def finish_kernel(
    triplet_total,
    early_ref,
    sum_ref,
    loss_out,
    genc_out,
    gtable_out,
    gself_out,
    gagg_out,
    gout_out,
):
    width = gself_out.shape[1]
    for k, out in enumerate((gout_out, gself_out, gagg_out)):
        for layer, source in enumerate((sum_ref, early_ref)):
            out[layer] = source[k * width : (k + 1) * width, :]
    base = 3 * width
    genc_out[...] = sum_ref[base : base + genc_out.shape[0], :]
    gtable_out[...] = sum_ref[base + 16 : base + 16 + gtable_out.shape[0], :]
    at = base + 16 + gtable_out.shape[0]
    loss_out[...] = sum_ref[at : at + 1, 0:1] / triplet_total


def body(
    hit_feats,
    layer_ids,
    edge_tiles,
    src_blocks,
    live_slots,
    anchor_hits,
    positive_hits,
    negative_hits,
    w_enc,
    layer_table,
    w_self,
    w_agg,
    w_out,
):
    blocks, slots, rows, _ = edge_tiles.shape
    width = w_enc.shape[1]
    features = hit_feats.shape[0]
    kinds = layer_table.shape[0]
    hits = blocks * rows
    layer_total = w_self.shape[0]
    triplets = anchor_hits.shape[0]
    group = 4
    steps = blocks // group
    span = group * rows
    me = lax.axis_index("phi")
    is_even = me % 2 == 0
    even_pair = (me // 2) % 2 == 0

    def place(part):
        spots = (
            jnp.where(even_pair, 2, 0),
            jnp.where(is_even, 4, 3),
            1,
            jnp.where(is_even, 3, 4),
            jnp.where(even_pair, 0, 2),
        )
        return sum(jnp.where(part == k, spot, 0) for k, spot in enumerate(spots))

    live = jnp.arange(slots, dtype=jnp.int32)[None, :] < live_slots[:, None]
    index = jnp.where(
        live, place(src_blocks // blocks) * blocks + src_blocks % blocks, 5 * blocks
    ).reshape(blocks * slots)
    depth = 16 + kinds
    listed = 2 * triplets // 128 + 1
    list_shape = (-(-(listed + 1) // 8) * 8, 128)

    tile_spec = pl.BlockSpec((group, slots, rows, rows), lambda i, *_: (i, 0, 0, 0))
    row_spec = pl.BlockSpec((span, width), lambda i, *_: (i, 0))
    weight_spec = full((width, width))
    any_spec = pl.BlockSpec(memory_space=pl.ANY)
    row_shape = jax.ShapeDtypeStruct((hits, width), BF16)
    weight_shape = jax.ShapeDtypeStruct((width, width), F32)

    wide_shape = jax.ShapeDtypeStruct((hits, width), F32)
    vmem = pl.BlockSpec(memory_space=pltpu.VMEM)
    smem = pl.BlockSpec(memory_space=pltpu.SMEM)
    few = pltpu.SemaphoreType.DMA((FEAT_CHUNKS,))
    each = pltpu.SemaphoreType.DMA((CHUNKS,))
    one = pltpu.SemaphoreType.DMA((1,))
    four = pltpu.SemaphoreType.DMA((4,))
    block_shape = jax.ShapeDtypeStruct((blocks, rows, width), BF16)
    before0, agg0, hidden0, latents1, agg1, hidden1, latents2, lists, feats, wcat = pl.pallas_call(
        functools.partial(forward_kernel, features),
        in_specs=[smem] + [vmem] * 4 + [any_spec] + [vmem] * 5,
        out_specs=[any_spec] * 10,
        out_shape=[block_shape, row_shape, row_shape, block_shape, row_shape, row_shape]
        + [
            wide_shape,
            jax.ShapeDtypeStruct((5,) + list_shape, jnp.int32),
            jax.ShapeDtypeStruct((depth, 5 * hits), BF16),
            jax.ShapeDtypeStruct((depth, width), BF16),
        ],
        scratch_shapes=[
            pltpu.VMEM((16, hits), BF16),
            pltpu.VMEM((depth, width), BF16),
            pltpu.VMEM(list_shape, jnp.int32),
            pltpu.VMEM((listed - 1, 128, 128), jnp.int32),
            pltpu.VMEM((listed - 1, 128, 128), jnp.int32),
            pltpu.VMEM((listed - 1, 128, 128), jnp.int32),
            pltpu.VMEM((5, 16, hits), BF16),
            pltpu.VMEM((depth, 5 * hits), BF16),
            pltpu.VMEM((5 * blocks + 1, rows, width), BF16),
            pltpu.VMEM((5 * blocks + 1, rows, width), BF16),
        ]
        + [pltpu.VMEM((hits, width), BF16)] * 4
        + [
            pltpu.VMEM((hits, width), F32),
            pltpu.VMEM(edge_tiles.shape, BF16),
            each,
            pltpu.SemaphoreType.DMA((6,)),
            pltpu.SemaphoreType.DMA((3 * LATER_STEPS,)),
            one,
        ]
        + [few] * 6
        + [four] * 2
        + [each] * 8
        + [one] * 2,
        compiler_params=pltpu.CompilerParams(
            collective_id=1, has_side_effects=True, vmem_limit_bytes=VMEM_BYTES
        ),
        name="forward",
    )(
        index,
        hit_feats,
        layer_ids.reshape(1, hits),
        positive_hits.reshape(triplets // 128, 128),
        negative_hits.reshape(triplets // 128, 128),
        edge_tiles,
        w_enc,
        layer_table,
        w_self,
        w_agg,
        w_out,
    )

    before0, latents1 = before0.reshape(hits, width), latents1.reshape(hits, width)
    lists = lists.reshape(-1)
    move_shape = jax.ShapeDtypeStruct((triplets, width), BF16)
    wide_move = jax.ShapeDtypeStruct((triplets, width), F32)
    move_spec = full((triplets, width))
    *found, anchors = pl.pallas_call(
        gather_kernel,
        grid_spec=pltpu.PrefetchScalarGridSpec(
            num_scalar_prefetch=2,
            grid=(1,),
            in_specs=[full((hits, width))],
            out_specs=[move_spec] * 6,
            scratch_shapes=[pltpu.VMEM((2 * triplets + 8, width), F32)],
        ),
        out_shape=[move_shape] * 6,
        compiler_params=params(),
        name="gather",
    )(lists, anchor_hits, latents2)
    coef_shape = (triplets // 128, 128)
    loss_part, ganchor, *moves, coef, coefs = pl.pallas_call(
        functools.partial(contrast_kernel, 1.0 / math.sqrt(width)),
        in_specs=[vmem] * 6,
        out_specs=[vmem] * 8,
        out_shape=[jax.ShapeDtypeStruct((8, width), F32), wide_move]
        + [move_shape] * 4
        + [jax.ShapeDtypeStruct(coef_shape, F32), jax.ShapeDtypeStruct((4,) + coef_shape, F32)],
        scratch_shapes=[pltpu.VMEM((triplets, width), F32)]
        + [pltpu.VMEM((triplets, width), BF16)] * 6
        + [pltpu.SemaphoreType.DMA((PARTS,))] * 16
        + [pltpu.SemaphoreType.DMA((4,))] * 2,
        compiler_params=pltpu.CompilerParams(
            collective_id=4, has_side_effects=True, vmem_limit_bytes=VMEM_BYTES
        ),
        name="contrast",
    )(*found, anchors)

    t_shape = jax.ShapeDtypeStruct((blocks, width, rows), F32)
    t_half = jax.ShapeDtypeStruct((blocks, width, rows), BF16)
    t_full = pl.BlockSpec(
        (blocks, width, rows), lambda *_: (0, 0, 0), pipeline_mode=pl.Buffered(1)
    )
    adj_shape = pltpu.VMEM((5 * blocks + 1, width, rows), F32)
    upstream1, act1, gradient2, obelow, own, oabove, osibling, ocross = pl.pallas_call(
        functools.partial(last_backward, group, steps),
        grid_spec=pltpu.PrefetchScalarGridSpec(
            num_scalar_prefetch=3,
            grid=(steps,),
            in_specs=[tile_spec, move_spec, full(coef_shape), full((4,) + coef_shape)]
            + [move_spec] * 5
            + [row_spec]
            + [full((2, width, width))] * 2,
            out_specs=[row_spec] * 3 + [t_full] * 5,
            scratch_shapes=[adj_shape, pltpu.VMEM((10 * triplets + 40, width), F32)]
            + [pltpu.VMEM((hits, width), F32)] * 4,
        ),
        out_shape=[row_shape] * 2 + [wide_shape] + [t_half, t_shape] + [t_half] * 3,
        compiler_params=params(),
        name="last_backward",
    )(
        index, lists, anchor_hits, edge_tiles, ganchor, coef, coefs, anchors, *moves, hidden1, w_agg, w_out,
    )
    pairs = lax.axis_size("phi") // 2

    def sum_sizes(count):
        chunk = -(-count // (16 * pairs)) * 8
        total = 2 * pairs * chunk
        return jax.ShapeDtypeStruct((total, width), F32), [
            pltpu.VMEM((total, width), F32),
            pltpu.VMEM((total // 2, width), F32),
            pltpu.VMEM((total // 2, width), F32),
            pltpu.VMEM((pairs - 1, chunk, width), F32),
        ]

    early_shape, early_scratch = sum_sizes(3 * width)
    final_shape, final_scratch = sum_sizes(3 * width + depth + 8)
    many = pltpu.SemaphoreType.DMA((pairs - 1,))
    flat = (hits, width)
    sums = pl.pallas_call(
        functools.partial(back_kernel, pairs),
        in_specs=[smem] + [any_spec] * 15 + [vmem] * 6,
        out_specs=[vmem] * 2,
        out_shape=[early_shape, final_shape],
        scratch_shapes=[pltpu.VMEM((width, depth), BF16)]
        + [pltpu.VMEM(flat, BF16)] * 8
        + [pltpu.VMEM(flat, F32)] * 2
        + [pltpu.VMEM(flat, BF16)] * 8
        + [
            pltpu.VMEM(edge_tiles.shape, BF16),
            pltpu.VMEM((5 * blocks + 1, width, rows), F32),
            pltpu.VMEM((5 * blocks + 1, depth, rows), BF16),
        ]
        + final_scratch
        + early_scratch
        + [pltpu.SemaphoreType.DMA((13,))]
        + [pltpu.SemaphoreType.DMA((CHUNKS,))] * 6
        + [one, one]
        + [one, one, many, many, many, many, one, one] * 2,
        compiler_params=pltpu.CompilerParams(
            collective_id=3, has_side_effects=True, vmem_limit_bytes=VMEM_BYTES
        ),
        name="back",
    )(
        index, ocross.reshape(flat), osibling.reshape(flat), oabove.reshape(flat),
        obelow.reshape(flat), own.reshape(flat), gradient2, hidden0, before0, agg0, edge_tiles,
        upstream1, act1, hidden1, latents1, agg1,
        feats, wcat, w_self, w_agg, w_out, loss_part,
    )
    stack = jax.ShapeDtypeStruct((2, width, width), F32)
    loss, genc, gtable, gself, gagg, gout = pl.pallas_call(
        functools.partial(finish_kernel, float(triplets * lax.axis_size("phi"))),
        in_specs=[vmem] * 2,
        out_specs=[vmem] * 6,
        out_shape=[
            jax.ShapeDtypeStruct((1, 1), F32),
            jax.ShapeDtypeStruct((features, width), F32),
            jax.ShapeDtypeStruct((kinds, width), F32),
            stack, stack, stack,
        ],
        name="finish",
    )(*sums)
    return (loss.reshape(1), genc, gtable, gself, gagg, gout)


def solution(mesh):
    both = ("event", "phi")
    in_specs = (
        P(None, both),
        P(both),
        P(both, None, None, None),
        P(both, None),
        P(both),
        P(both),
        P(both),
        P(both),
        P(),
        P(),
        P(),
        P(),
        P(),
    )
    out_specs = (
        P("event"),
        P("event", None),
        P("event", None),
        P("event", None, None),
        P("event", None, None),
        P("event", None, None),
    )
    return jax.shard_map(body, mesh=mesh, in_specs=in_specs, out_specs=out_specs, check_vma=False)
```

```python
import functools
import math

import jax
import jax.numpy as jnp
from jax import lax
from jax.experimental import pallas as pl
from jax.experimental.pallas import tpu as pltpu
from jax.sharding import PartitionSpec as P

loss_divisor = 64.0
F32 = jnp.float32
BF16 = jnp.bfloat16
VMEM_BYTES = 60 * 1024 * 1024


def dot(left, right, left_dim, right_dim):
    return lax.dot_general(
        left, right, (((left_dim,), (right_dim,)), ((), ())), preferred_element_type=F32
    )


def full(shape):
    return pl.BlockSpec(shape, lambda *_: (0,) * len(shape))


def params():
    return pltpu.CompilerParams(
        dimension_semantics=("arbitrary",), vmem_limit_bytes=VMEM_BYTES
    )


CHUNKS = 16
LATER_STEPS = 8


def peers():
    count = lax.axis_size("phi")
    me = lax.axis_index("phi")
    odd_pair = (me // 2) % 2
    odd_core = me % 2
    direct = me + 2 - 4 * odd_pair
    sibling = me + 1 - 2 * odd_core
    stride = 4 - 8 * odd_pair
    onward = (me + stride + count) % count
    source = (me - stride + count) % count
    return direct, sibling, onward, source, odd_pair == odd_core


def remote(src, dst, send, recv, target):
    return pltpu.make_async_remote_copy(
        src_ref=src,
        dst_ref=dst,
        send_sem=send,
        recv_sem=recv,
        device_id={"phi": target},
        device_id_type=pl.DeviceIdType.MESH,
    )


def greet(targets):
    barrier = pltpu.get_barrier_semaphore()
    for target in targets:
        pl.semaphore_signal(
            barrier, inc=1, device_id={"phi": target}, device_id_type=pl.DeviceIdType.MESH
        )
    pl.semaphore_wait(barrier, len(targets))


def role_targets():
    count = lax.axis_size("phi")
    me = lax.axis_index("phi")
    odd_pair = (me // 2) % 2
    odd_core = me % 2
    sibling = me + 1 - 2 * odd_core
    across = (me - 1 + 2 * odd_core + count) % count
    direct = me + 2 - 4 * odd_pair
    far = (me - 2 + 4 * odd_pair + count) % count
    return sibling, across, direct, far


def aggregate_group(index_ref, tiles_ref, window_ref, step, group, slots, rows):
    results = []
    for g in range(group):
        tile = jnp.concatenate([tiles_ref[step * group + g, s] for s in range(slots)], axis=1)
        source = jnp.concatenate(
            [
                window_ref[index_ref[(step * group + g) * slots + s]] for s in range(slots)
            ],
            axis=0,
        )
        results.append(dot(tile, source, 1, 0).astype(BF16))
    return jnp.concatenate(results, axis=0)


def node_update(own, aggregated, w_self, w_agg, w_out):
    activation = dot(own, w_self, 1, 0) + dot(aggregated, w_agg, 1, 0)
    hidden = jnp.maximum(activation, 0.0).astype(BF16)
    updated = (own.astype(F32) + dot(hidden, w_out, 1, 0)).astype(BF16)
    return hidden, updated


FEAT_CHUNKS = 2


def forward_kernel(
    features,
    index_ref,
    hit_ref,
    id_ref,
    positive_ref,
    negative_ref,
    tiles_hbm,
    enc_ref,
    table_ref,
    w_self_ref,
    w_agg_ref,
    w_out_ref,
    before_out,
    agg0_out,
    hidden0_out,
    latents_out,
    agg1_out,
    hidden1_out,
    z_out,
    lists_out,
    feats_out,
    wcat_out,
    packed_ref,
    wcat_ref,
    keys_ref,
    key_cols,
    place_cols,
    entry_cols,
    packs_ref,
    feats_ref,
    window_ref,
    later_ref,
    agg0_ref,
    hidden0_ref,
    agg1_ref,
    hidden1_ref,
    z_ref,
    tiles_ref,
    tile_sem,
    out_sem,
    late_sem,
    list_sem,
    *sems,
):
    fys, fyr, fzs, fzr, fcs, fcr, ls, lr = sems[:8]
    ys, yr, zs, zr, cs, cr, ss, sr = sems[8:16]
    fss, fsr = sems[16:]
    direct, sibling, onward, source, direct_crosses = peers()
    roles = role_targets()
    blocks, slots, rows, _ = tiles_ref.shape
    hits = packed_ref.shape[1]
    group = blocks // CHUNKS
    span = group * rows

    def tile_load(i):
        part = pl.ds(i * group, group)
        return pltpu.make_async_copy(tiles_hbm.at[part], tiles_ref.at[part], tile_sem.at[i])

    lax.fori_loop(0, CHUNKS, lambda i, c: (tile_load(i).start(), c)[1], 0)
    kinds, width = table_ref.shape
    filler = jnp.zeros((16 - features, width), F32)
    wcat_ref[...] = jnp.concatenate(
        [enc_ref[...].astype(F32), filler, table_ref[...].astype(F32)], axis=0
    ).astype(BF16)

    def gather_input(i, carry):
        at = pl.ds(pl.multiple_of(i * 512, 512), 512)
        packed_ref[:, at] = jnp.concatenate(
            [
                hit_ref[:, at].astype(F32),
                id_ref[:, at].astype(F32),
                jnp.zeros((15 - features, 512), F32),
            ],
            axis=0,
        ).astype(BF16)
        return carry

    lax.fori_loop(0, hits // 512, gather_input, 0)
    beside = [t + 1 - 2 * lax.rem(t, 2) for t in (onward, source)]
    greet((direct, sibling, onward, source, beside[0], beside[1], roles[1], roles[3]))
    columns = hits // FEAT_CHUNKS

    def pack(k, i):
        return packs_ref.at[k, :, pl.ds(i * columns, columns)]

    chunks = range(FEAT_CHUNKS)
    f_first = [
        remote(
            packed_ref.at[:, pl.ds(i * columns, columns)], pack(0, i), fys.at[i], fyr.at[i], direct
        )
        for i in chunks
    ]
    f_second = [remote(pack(0, i), pack(2, i), fzs.at[i], fzr.at[i], onward) for i in chunks]
    f_cross_a = [remote(pack(0, i), pack(4, i), fcs.at[i], fcr.at[i], sibling) for i in chunks]
    f_cross_b = [remote(pack(0, i), pack(4, i), fcs.at[i], fcr.at[i], beside[0]) for i in chunks]
    f_near = remote(packed_ref, packs_ref.at[3], fss.at[0], fsr.at[0], sibling)
    for copy in f_first:
        copy.start()
    f_near.start()

    def encode(k, ref):
        step = 512
        is_feature = lax.broadcasted_iota(jnp.int32, (16, step), 0) < features
        kind = lax.broadcasted_iota(jnp.int32, (16, step), 0).astype(F32)

        def run(i, carry):
            at = pl.multiple_of(i * step, step)
            data = ref[:, pl.ds(at, step)].astype(F32)
            onehot = jnp.where(kind == data[features : features + 1], 1.0, 0.0)
            feats = jnp.concatenate([jnp.where(is_feature, data, 0.0), onehot], axis=0).astype(BF16)
            feats_ref[:, pl.ds(pl.multiple_of(k * hits + i * step, step), step)] = feats
            encoded = dot(feats, wcat_ref[...], 0, 0)
            squashed = jnp.tanh(encoded).astype(BF16)
            for u in range(step // rows):
                window_ref[k * blocks + i * (step // rows) + u] = squashed[
                    u * rows : (u + 1) * rows
                ]
            return carry

        lax.fori_loop(0, hits // step, run, 0)

    encode(1, packed_ref)
    for i in chunks:
        f_first[i].wait_recv()
        f_second[i].start()

        @pl.when(direct_crosses)
        def _():
            f_cross_a[i].start()

        @pl.when(jnp.logical_not(direct_crosses))
        def _():
            f_cross_b[i].start()

    f_near.wait_recv()
    encode(3, packs_ref.at[3])
    encode(0, packs_ref.at[0])
    for i in chunks:
        f_second[i].wait_recv()
    encode(2, packs_ref.at[2])
    for i in chunks:
        f_cross_a[i].wait_recv()
    encode(4, packs_ref.at[4])
    window_ref[5 * blocks] = jnp.zeros((rows, width), BF16)
    later_ref[5 * blocks] = jnp.zeros((rows, width), BF16)

    def part(k, i):
        return pl.ds(k * blocks + i * group, group)

    def first(i):
        return remote(later_ref.at[part(1, i)], later_ref.at[part(0, i)], ys.at[i], yr.at[i], direct)

    def near(i):
        return remote(later_ref.at[part(1, i)], later_ref.at[part(3, i)], ss.at[i], sr.at[i], sibling)

    def second(i):
        return remote(later_ref.at[part(0, i)], later_ref.at[part(2, i)], zs.at[i], zr.at[i], onward)

    def cross_a(i):
        return remote(later_ref.at[part(0, i)], later_ref.at[part(4, i)], cs.at[i], cr.at[i], sibling)

    def cross_b(i):
        return remote(later_ref.at[part(2, i)], later_ref.at[part(4, i)], cs.at[i], cr.at[i], sibling)

    def cross_c(i):
        return remote(
            later_ref.at[part(0, i)], later_ref.at[part(4, i)], cs.at[i], cr.at[i], beside[0]
        )

    def relay(i):
        first(i).wait_recv()
        second(i).start()

        @pl.when(direct_crosses)
        def _():
            cross_a(i).start()

        if isinstance(i, int) and i == CHUNKS - 1:

            @pl.when(jnp.logical_not(direct_crosses))
            def _():
                cross_c(i).start()

    def land(i):
        second(i).wait_recv()

        if not (isinstance(i, int) and i == CHUNKS - 1):

            @pl.when(jnp.logical_not(direct_crosses))
            def _():
                cross_b(i).start()

    lead = 5
    relayed = (CHUNKS - lead + 1) // 2

    def layer0(i, carry):
        tile_load(i).wait()
        here = pl.ds(pl.multiple_of(i * span, span), span)
        aggregated = aggregate_group(index_ref, tiles_ref, window_ref, i, group, slots, rows)
        own = window_ref[part(1, i)].reshape(span, width)
        hidden, updated = node_update(own, aggregated, w_self_ref[0], w_agg_ref[0], w_out_ref[0])
        later_ref[part(1, i)] = updated.reshape(group, rows, width)
        first(i).start()
        near(i).start()
        agg0_ref[here, :] = aggregated
        hidden0_ref[here, :] = hidden

        @pl.when(jnp.logical_and(i >= lead, lax.rem(i, 2) == 1))
        def _():
            relay(lax.div(i - lead, 2))

        return carry

    lax.fori_loop(0, CHUNKS, layer0, 0)
    own = pl.ds(blocks, blocks)
    saves = [
        pltpu.make_async_copy(src, dst, out_sem.at[k])
        for k, (src, dst) in enumerate(
            (
                (window_ref.at[own], before_out),
                (agg0_ref, agg0_out),
                (hidden0_ref, hidden0_out),
                (later_ref.at[own], latents_out),
                (feats_ref, feats_out),
                (wcat_ref, wcat_out),
            )
        )
    ]
    for copy in saves:
        copy.start()

    wanted = jnp.concatenate([positive_ref[...], negative_ref[...]], axis=0)
    lines = wanted.shape[0]
    pairs_of = lines * 128
    line = lax.broadcasted_iota(jnp.int32, (lines, 128), 0)
    lane = lax.broadcasted_iota(jnp.int32, (lines, 128), 1)
    keys = wanted * pairs_of + (line * 128 + lane)
    tall = jnp.concatenate(
        [wanted.astype(F32), jnp.zeros((128 - lines, 128), F32)], axis=0
    ).T.astype(jnp.int32)
    down = lax.broadcasted_iota(jnp.int32, (128, 1), 0)
    counts = []
    for k in range(5):
        mine = jnp.logical_and(wanted >= k * hits, wanted < (k + 1) * hits)
        counted = jnp.sum(jnp.where(mine, 1.0, 0.0), axis=1, keepdims=True)
        counts.append(jnp.sum(counted, axis=0, keepdims=True).astype(jnp.int32))
    aligned, shift = [jnp.zeros((1, 1), jnp.int32)], [jnp.zeros((1, 1), jnp.int32)]
    for k in range(5):
        filled = lax.bitwise_and(counts[k] + 7, -8)
        aligned.append(aligned[k] + filled)
        shift.append(shift[k] + filled - counts[k])
    for c in range(lines):
        column = tall[:, c : c + 1]
        slot = down + c * 128
        moved = jnp.zeros((128, 1), jnp.int32)
        first_row = jnp.zeros((128, 1), jnp.int32)
        for k in range(5):
            mine = jnp.logical_and(column >= k * hits, column < (k + 1) * hits)
            moved = moved + jnp.where(mine, shift[k], 0)
            first_row = first_row + jnp.where(mine, k * hits, 0)
        entry = (column - first_row) * (1 << ENTRY_BITS) + slot - pairs_of
        key_cols[c] = jnp.broadcast_to(column * pairs_of + slot, (128, 128))
        place_cols[c] = jnp.broadcast_to(moved, (128, 128))
        entry_cols[c] = jnp.broadcast_to(entry, (128, 128))

    def rank(c, carry):
        column = key_cols[c]
        count = jnp.zeros((128, 128), F32)
        for r in range(lines):
            count = count + jnp.where(keys[r : r + 1] < column, 1.0, 0.0)
        total = jnp.sum(count, axis=1, keepdims=True).astype(jnp.int32)
        place_cols[c] = place_cols[c] + jnp.broadcast_to(total, (128, 128))
        return carry

    keys_ref[...] = jnp.zeros(keys_ref.shape, jnp.int32)

    def put(q, carry):
        target = lax.broadcasted_iota(jnp.int32, (128, 128), 1) + q * 128

        def match(c, total):
            return total + jnp.where(place_cols[c] == target, entry_cols[c], 0)

        total = lax.fori_loop(0, lines, match, jnp.zeros((128, 128), jnp.int32))
        found = jnp.sum(total.astype(F32), axis=0, keepdims=True).astype(jnp.int32)
        keys_ref[pl.ds(q, 1), :] = found + pairs_of
        return carry

    turns = 3
    for k in range(turns):
        relay(relayed + k)
        land(k)
        lax.fori_loop(lines * k // turns, lines * (k + 1) // turns, rank, 0)
    put_turns = CHUNKS - relayed - turns - 2
    for k in range(put_turns):
        relay(relayed + turns + k)
        land(turns + k)
        lax.fori_loop(
            (lines + 1) * k // put_turns, (lines + 1) * (k + 1) // put_turns, put, 0
        )
    lane = lax.broadcasted_iota(jnp.int32, (1, 128), 1)
    keys_ref[pl.ds(lines + 1, 1), :] = sum(
        jnp.where(lane == k, aligned[k] // 8, 0) for k in range(6)
    )
    lists = [
        remote(keys_ref, lists_out.at[j + 1], ls.at[j], lr.at[j], target)
        for j, target in enumerate(roles)
    ]
    for copy in lists:
        copy.start()
    own_list = pltpu.make_async_copy(keys_ref, lists_out.at[0], list_sem.at[0])
    own_list.start()

    for k in range(CHUNKS - 2, CHUNKS):
        relay(k)
    for k in range(turns + put_turns, CHUNKS):
        land(k)

    def settle(i, carry):
        near(i).wait()
        cross_a(i).wait_recv()
        return carry

    lax.fori_loop(0, CHUNKS, settle, 0)

    later_group = blocks // LATER_STEPS
    later_span = later_group * rows

    def late_saves(i):
        here = pl.ds(pl.multiple_of(i * later_span, later_span), later_span)
        return [
            pltpu.make_async_copy(src.at[here], dst.at[here], late_sem.at[k * LATER_STEPS + i])
            for k, (src, dst) in enumerate(
                ((agg1_ref, agg1_out), (hidden1_ref, hidden1_out), (z_ref, z_out))
            )
        ]

    def layer1(i, carry):
        here = pl.ds(pl.multiple_of(i * later_span, later_span), later_span)
        aggregated = aggregate_group(index_ref, tiles_ref, later_ref, i, later_group, slots, rows)
        own = later_ref[pl.ds(blocks + i * later_group, later_group)].reshape(later_span, width)
        hidden, updated = node_update(own, aggregated, w_self_ref[1], w_agg_ref[1], w_out_ref[1])
        agg1_ref[here, :] = aggregated
        hidden1_ref[here, :] = hidden
        z_ref[here, :] = updated.astype(F32)
        for copy in late_saves(i):
            copy.start()
        return carry

    lax.fori_loop(0, LATER_STEPS, layer1, 0)

    def drain(i, carry):
        first(i).wait_send()
        second(i).wait_send()
        cross_a(i).wait_send()
        return carry

    lax.fori_loop(0, CHUNKS, drain, 0)

    def saved(i, carry):
        for copy in late_saves(i):
            copy.wait()
        return carry

    lax.fori_loop(0, LATER_STEPS, saved, 0)
    for i in chunks:
        f_first[i].wait_send()
        f_second[i].wait_send()
        f_cross_a[i].wait_send()
    f_near.wait_send()
    own_list.wait()
    for copy in lists:
        copy.wait()
    for copy in saves:
        copy.wait()


def segments(list_ref, stride, listed):
    me = lax.axis_index("phi")
    odd_core, odd_pair = lax.rem(me, 2), lax.rem(lax.div(me, 2), 2)
    places = (2, 1 + 2 * odd_core, 3 - 2 * odd_core, 4 * odd_pair, 4 - 4 * odd_pair)
    starts = [j * stride + listed + k for j, k in enumerate(places)]
    return [(list_ref[at], list_ref[at + 1]) for at in starts]


def gather_kernel(list_ref, anchor_ref, z_ref, *refs):
    outs, (anchor_out, buf_ref) = refs[:5], refs[5:]
    triplets, width = anchor_out.shape
    stride = list_ref.shape[0] // 5
    bounds = segments(list_ref, stride, 2 * triplets + 128)

    def anchors(i, carry):
        at = pl.multiple_of(i * 16, 16)
        anchor_out[pl.ds(at, 16), :] = jnp.concatenate(
            [z_ref[pl.ds(anchor_ref[i * 16 + u], 1), :] for u in range(16)], axis=0
        ).astype(BF16)
        return carry

    lax.fori_loop(0, triplets // 16, anchors, 0)
    zeros = jnp.zeros((64, width), F32)

    def clear(i, carry):
        buf_ref[pl.ds(pl.multiple_of(i * 64, 64), 64), :] = zeros
        return carry

    lax.fori_loop(0, 2 * triplets // 64, clear, 0)
    for j in range(5):

        def fetch(i, carry, j=j):
            for u in range(8):
                entry = list_ref[j * stride + i * 8 + u]
                row = z_ref[pl.ds(lax.shift_right_logical(entry, ENTRY_BITS), 1), :]
                buf_ref[pl.ds(lax.bitwise_and(entry, ENTRY_MASK), 1), :] = row
            return carry

        lax.fori_loop(bounds[j][0], bounds[j][1], fetch, 0)

        def subtract(i, carry, j=j):
            at = pl.multiple_of(i * 64, 64)
            value = buf_ref[pl.ds(triplets + at, 64), :] - buf_ref[pl.ds(at, 64), :]
            outs[j][pl.ds(at, 64), :] = value.astype(BF16)
            buf_ref[pl.ds(triplets + at, 64), :] = zeros
            buf_ref[pl.ds(at, 64), :] = zeros
            return carry

        lax.fori_loop(0, triplets // 64, subtract, 0)


ENTRY_BITS = 12
ENTRY_MASK = (1 << ENTRY_BITS) - 1
PARTS = 8


def contrast_kernel(
    inv_root,
    self_ref,
    sib_ref,
    cross_ref,
    near_ref,
    far_ref,
    anchor_ref,
    loss_ref,
    ganchor_ref,
    asib_ref,
    across_ref,
    adirect_ref,
    afar_ref,
    coef_out,
    coefs_out,
    change_ref,
    sib_in,
    cross_in,
    far_send,
    far_in,
    near_send,
    near_in,
    *sems,
):
    s = [sems[2 * i : 2 * i + 2] for i in range(9)]
    direct, sibling, onward, source, near_adds = peers()
    roles = role_targets()
    size = anchor_ref.shape[0] // PARTS
    greet((direct, sibling, onward, source, roles[1], roles[3]))

    def rows(i):
        return pl.ds(i * size, size)

    def copies(k, src, dst, target):
        return [
            remote(src.at[rows(i)], dst.at[rows(i)], s[k][0].at[i], s[k][1].at[i], target)
            for i in range(PARTS)
        ]

    crosses = copies(0, cross_ref, cross_in, sibling)
    sibs = copies(1, sib_ref, sib_in, sibling)
    hops = copies(2, far_send, far_in, source)
    nears = copies(3, near_send, near_in, direct)
    to_direct = copies(4, anchor_ref, adirect_ref, direct)
    to_sibling = copies(5, anchor_ref, asib_ref, sibling)
    relays = copies(6, adirect_ref, afar_ref, onward)
    cross_a = copies(7, adirect_ref, across_ref, sibling)
    cross_b = copies(7, afar_ref, across_ref, sibling)
    coefs = [
        remote(coef_out, coefs_out.at[j], s[8][0].at[j], s[8][1].at[j], target)
        for j, target in enumerate(roles)
    ]
    for copy in crosses:
        copy.start()
    for copy in sibs:
        copy.start()
    for i in range(PARTS):
        @pl.when(near_adds)
        def _():
            far_send[rows(i), :] = far_ref[rows(i), :]

        @pl.when(jnp.logical_not(near_adds))
        def _():
            crosses[i].wait_recv()
            far_send[rows(i), :] = (
                far_ref[rows(i), :].astype(F32) + cross_in[rows(i), :].astype(F32)
            ).astype(BF16)

        hops[i].start()
        if i < PARTS // 2:
            to_direct[i].start()
    for i in range(PARTS):
        hops[i].wait_recv()
        value = near_ref[rows(i), :].astype(F32) + far_in[rows(i), :].astype(F32)

        @pl.when(near_adds)
        def _():
            crosses[i].wait_recv()
            near_send[rows(i), :] = (value + cross_in[rows(i), :].astype(F32)).astype(BF16)

        @pl.when(jnp.logical_not(near_adds))
        def _():
            near_send[rows(i), :] = value.astype(BF16)

        nears[i].start()
    for i in range(PARTS // 2, PARTS):
        to_direct[i].start()

    def relay(i):
        to_sibling[i].start()
        to_direct[i].wait_recv()
        relays[i].start()

        @pl.when(near_adds)
        def _():
            cross_a[i].start()

    gaps = []
    for i in range(PARTS):
        if i < PARTS // 2:
            relay(i)
        sibs[i].wait_recv()
        nears[i].wait_recv()
        change = (
            near_in[rows(i), :].astype(F32)
            + self_ref[rows(i), :].astype(F32)
            + sib_in[rows(i), :].astype(F32)
        )
        change_ref[rows(i), :] = change
        product = anchor_ref[rows(i), :].astype(F32) * change
        for u in range(size // 128):
            gaps.append(
                jnp.sum(product[u * 128 : (u + 1) * 128].T, axis=0, keepdims=True) * inv_root
            )
    gap = jnp.concatenate(gaps, axis=0)
    coef_out[...] = jax.nn.sigmoid(gap) * (inv_root / loss_divisor)
    for copy in coefs:
        copy.start()
    soft = jnp.maximum(gap, 0.0) + jnp.log1p(jnp.exp(-jnp.abs(gap)))
    loss_ref[...] = jnp.broadcast_to(jnp.sum(soft, keepdims=True), loss_ref.shape)
    for i in range(PARTS // 2, PARTS):
        relay(i)
    for i in range(PARTS):
        relays[i].wait_recv()

        @pl.when(jnp.logical_not(near_adds))
        def _():
            cross_b[i].start()

    size = 128
    eye = lax.broadcasted_iota(jnp.int32, (size, size), 0) == lax.broadcasted_iota(
        jnp.int32, (size, size), 1
    )
    for i in range(coef_out.shape[0]):
        coef = coef_out[pl.ds(i, 1), :]
        column = jnp.sum(jnp.where(eye, coef, 0.0), axis=1, keepdims=True)
        here = pl.ds(i * size, size)
        ganchor_ref[here, :] = column * change_ref[here, :]
    for copy in coefs:
        copy.wait()
    for i in range(PARTS):
        crosses[i].wait_send()
        sibs[i].wait_send()
        hops[i].wait_send()
        nears[i].wait_send()
        to_direct[i].wait_send()
        to_sibling[i].wait()
        relays[i].wait_send()
        cross_a[i].wait()


def spread_group(index_ref, tiles_ref, adj_ref, agg_grad_t, step, group, slots, rows):
    for g in range(group):
        tile = jnp.concatenate([tiles_ref[g, s] for s in range(slots)], axis=1)
        contrib = dot(agg_grad_t[:, g * rows : (g + 1) * rows], tile, 1, 0)
        for s in range(slots):
            at = index_ref[(step * group + g) * slots + s]
            adj_ref[at] = adj_ref[at] + contrib[:, s * rows : (s + 1) * rows]


def clear_blocks(adj_ref):
    def clear(i, carry):
        adj_ref[i] = jnp.zeros(adj_ref.shape[1:], F32)
        return carry

    lax.fori_loop(0, adj_ref.shape[0], clear, 0)


def scatter_rows(
    list_ref, anchor_ref, ganchor_ref, coef_ref, coefs_ref, rows_in, moved_ref, sums
):
    triplets, width = ganchor_ref.shape
    hits = sums[0].shape[0]
    stride = list_ref.shape[0] // 5
    span = 2 * triplets + 8
    bounds = segments(list_ref, stride, 2 * triplets + 128)
    zeros = jnp.zeros((64, width), F32)

    def clear(i, carry):
        for target in sums:
            target[pl.ds(pl.multiple_of(i * 64, 64), 64), :] = zeros
        return carry

    lax.fori_loop(0, hits // 64, clear, 0)
    eye = lax.broadcasted_iota(jnp.int32, (128, 128), 0) == lax.broadcasted_iota(
        jnp.int32, (128, 128), 1
    )
    for j, source in enumerate(rows_in):
        for i in range(triplets // 128):
            coef = coef_ref[pl.ds(i, 1), :] if j == 0 else coefs_ref[j - 1, pl.ds(i, 1), :]
            spread = jnp.where(eye, coef, 0.0)
            high = spread.astype(BF16)
            low = (spread - high.astype(F32)).astype(BF16)
            part = source[pl.ds(i * 128, 128), :]
            value = dot(high, part, 1, 0) + dot(low, part, 1, 0)
            moved_ref[pl.ds(j * span + i * 128, 128), :] = -value
            moved_ref[pl.ds(j * span + triplets + i * 128, 128), :] = value
        moved_ref[pl.ds(j * span + 2 * triplets, 8), :] = zeros[:8]

    def anchors(i, carry):
        for u in range(8):
            t = i * 8 + u
            here = pl.ds(anchor_ref[t], 1)
            target = sums[u % 4]
            target[here, :] = target[here, :] + ganchor_ref[pl.ds(t, 1), :]
        return carry

    lax.fori_loop(0, triplets // 8, anchors, 0)
    for j in range(5):

        def add(i, carry, j=j):
            for u in range(8):
                entry = list_ref[j * stride + i * 8 + u]
                here = pl.ds(lax.shift_right_logical(entry, ENTRY_BITS), 1)
                target = sums[u % 4]
                moved = moved_ref[pl.ds(j * span + lax.bitwise_and(entry, ENTRY_MASK), 1), :]
                target[here, :] = target[here, :] + moved
            return carry

        lax.fori_loop(bounds[j][0], bounds[j][1], add, 0)


def last_backward(
    group,
    steps,
    index_ref,
    list_ref,
    anchor_ref,
    tiles_ref,
    ganchor_ref,
    coef_ref,
    coefs_ref,
    aself_ref,
    asib_ref,
    across_ref,
    adirect_ref,
    afar_ref,
    hidden_ref,
    w_agg_ref,
    w_out_ref,
    upstream_ref,
    act_ref,
    gradient_ref,
    obelow_ref,
    oown_ref,
    oabove_ref,
    osibling_ref,
    ocross_ref,
    adj_ref,
    moved_ref,
    stage_ref,
    piece_sem,
    *sums,
):
    step = pl.program_id(0)
    slots, rows = tiles_ref.shape[1], tiles_ref.shape[2]
    span = group * rows

    @pl.when(step == 0)
    def _():
        clear_blocks(adj_ref)
        scatter_rows(
            list_ref, anchor_ref, ganchor_ref, coef_ref, coefs_ref,
            (aself_ref, asib_ref, across_ref, adirect_ref, afar_ref), moved_ref, sums,
        )

    here = pl.ds(pl.multiple_of(step * span, span), span)
    gradient = (sums[0][here, :] + sums[1][here, :]) + (sums[2][here, :] + sums[3][here, :])
    upstream = gradient.astype(BF16)
    hidden_grad = dot(upstream, w_out_ref[1], 1, 1)
    act_grad = jnp.where(hidden_ref[...].astype(F32) > 0, hidden_grad, 0.0).astype(BF16)
    upstream_ref[...] = upstream
    act_ref[...] = act_grad
    gradient_ref[...] = gradient
    agg_grad_t = dot(w_agg_ref[1], act_grad, 1, 1).astype(BF16)
    spread_group(index_ref, tiles_ref, adj_ref, agg_grad_t, step, group, slots, rows)

    @pl.when(step == steps - 1)
    def _():
        blocks = oown_ref.shape[0]
        copies = [
            pltpu.make_async_copy(
                adj_ref.at[pl.ds(blocks, blocks)], oown_ref, piece_sem.at[4]
            )
        ]
        copies[0].start()
        for j, (k, target) in enumerate(
            ((4, ocross_ref), (3, osibling_ref), (2, oabove_ref), (0, obelow_ref))
        ):

            def store(i, carry, k=k, j=j):
                for u in range(2):
                    stage_ref[j, 2 * i + u] = adj_ref[k * blocks + 2 * i + u].astype(BF16)
                return carry

            lax.fori_loop(0, blocks // 2, store, 0)
            copies.append(pltpu.make_async_copy(stage_ref.at[j], target, piece_sem.at[j]))
            copies[-1].start()
        for copy in copies:
            copy.wait()


def summer(pairs, x_ref, half_in, acc_ref, slots_in, all_ref, sems):
    s0, r0, s1, r1, s2, r2, s3, r3 = sems
    wire = acc_ref.dtype
    me = lax.axis_index("phi")
    pair, core = me // 2, me % 2
    sibling = me + 1 - 2 * core
    others = [((pair + d) % pairs) * 2 + core for d in range(1, pairs)]
    half = x_ref.shape[0] // 2
    chunk = half // pairs

    def part(start, length):
        return pl.ds(pl.multiple_of(start, 16 if wire == BF16 else 8), length)

    swap = remote(x_ref.at[part((1 - core) * half, half)], half_in, s0.at[0], r0.at[0], sibling)
    scatter = [
        remote(
            acc_ref.at[part(((pair + d) % pairs) * chunk, chunk)],
            slots_in.at[d - 1],
            s1.at[d - 1],
            r1.at[d - 1],
            others[d - 1],
        )
        for d in range(1, pairs)
    ]
    mine = part(core * half + pair * chunk, chunk)
    gather = [
        remote(all_ref.at[mine], all_ref.at[mine], s2.at[d - 1], r2.at[d - 1], others[d - 1])
        for d in range(1, pairs)
    ]
    whole = part(core * half, half)
    last = remote(all_ref.at[whole], all_ref.at[whole], s3.at[0], r3.at[0], sibling)

    def scatter_stage():
        swap.wait()
        acc_ref[...] = (x_ref[part(core * half, half), :] + half_in[...]).astype(wire)
        for copy in scatter:
            copy.start()

    def gather_stage():
        total = x_ref[mine, :] + half_in[part(pair * chunk, chunk), :]
        for d in range(1, pairs):
            scatter[d - 1].wait_recv()
            total = total + slots_in[d - 1].astype(F32)
        all_ref[mine, :] = total.astype(wire)
        for copy in gather:
            copy.start()

    def last_stage():
        for copy in gather:
            copy.wait()
        for copy in scatter:
            copy.wait_send()
        last.start()

    return swap.start, scatter_stage, gather_stage, last_stage, last.wait


def back_kernel(
    pairs,
    index_ref,
    cross_hbm,
    sib_hbm,
    relay_hbm,
    direct_hbm,
    own_hbm,
    grad_hbm,
    hidden_hbm,
    before_hbm,
    agg_hbm,
    tiles_hbm,
    upstream1_hbm,
    act1_hbm,
    hidden1_hbm,
    before1_hbm,
    agg1_hbm,
    feats_ref,
    wcat_ref,
    w_self_ref,
    w_agg_ref,
    w_out_ref,
    loss_ref,
    early_ref,
    all_ref,
    wcat_t_ref,
    cross_in,
    sib_in,
    relay_in,
    total_in,
    relay_send,
    direct_send,
    relay_ref,
    direct_ref,
    own_ref,
    grad_ref,
    hidden_ref,
    before_ref,
    agg_ref,
    upstream1_ref,
    act1_ref,
    hidden1_ref,
    before1_ref,
    agg1_ref,
    tiles_ref,
    slope_ref,
    block_feats_ref,
    x_ref,
    half_in,
    acc_ref,
    slots_in,
    early_x,
    early_half,
    early_acc,
    early_slots,
    local_sem,
    *sems,
):
    ys, yr, zs, zr, cs, cr, ss, sr = sems[:8]
    direct, sibling, onward, source, to_direct = peers()
    me = lax.axis_index("phi")
    pair, core = me // 2, me % 2
    others = [((pair + d) % pairs) * 2 + core for d in range(1, pairs)]
    blocks, slots, rows, _ = tiles_ref.shape
    depth, width = wcat_ref.shape
    window = feats_ref.shape[1] // rows
    size = grad_ref.shape[0] // CHUNKS
    group = blocks // CHUNKS
    loads = [
        pltpu.make_async_copy(src, dst, local_sem.at[k])
        for k, (src, dst) in enumerate(
            (
                (relay_hbm, relay_ref),
                (direct_hbm, direct_ref),
                (own_hbm, own_ref),
                (grad_hbm, grad_ref),
                (hidden_hbm, hidden_ref),
                (before_hbm, before_ref),
                (agg_hbm, agg_ref),
                (tiles_hbm, tiles_ref),
                (upstream1_hbm, upstream1_ref),
                (act1_hbm, act1_ref),
                (hidden1_hbm, hidden1_ref),
                (before1_hbm, before1_ref),
                (agg1_hbm, agg1_ref),
            )
        )
    ]
    for copy in loads:
        copy.start()
    greet([sibling] + others)

    def span(i):
        return pl.ds(pl.multiple_of(i * size, size), size)

    def crosses(i):
        return remote(cross_hbm.at[span(i)], cross_in.at[span(i)], cs.at[i], cr.at[i], sibling)

    def first(i):
        return remote(relay_send.at[span(i)], relay_in.at[span(i)], zs.at[i], zr.at[i], source)

    def second(i):
        return remote(direct_send.at[span(i)], total_in.at[span(i)], ys.at[i], yr.at[i], direct)

    near = remote(sib_hbm, sib_in, ss.at[0], sr.at[0], sibling)
    lax.fori_loop(0, CHUNKS, lambda i, c: (crosses(i).start(), c)[1], 0)
    near.start()

    early = summer(pairs, early_x, early_half, early_acc, early_slots, early_ref, sems[8:16])
    final = summer(pairs, x_ref, half_in, acc_ref, slots_in, all_ref, sems[16:24])
    early_x[...] = jnp.zeros(early_x.shape, F32)
    early_x[3 * width : 3 * width + 8, :] = loss_ref[...]
    per = window // CHUNKS

    def slopes(i):
        for u in range(0, per, 2):
            at = pl.multiple_of((i * per + u) * rows, 2 * rows)
            feats = feats_ref[:, pl.ds(at, 2 * rows)]
            squashed = jnp.tanh(dot(wcat_t_ref[...], feats, 1, 0))
            slope = 1.0 - squashed * squashed
            for v in range(2):
                slope_ref[i * per + u + v] = slope[:, v * rows : (v + 1) * rows]
                block_feats_ref[i * per + u + v] = feats[:, v * rows : (v + 1) * rows]

    wcat_t_ref[...] = (
        jnp.concatenate([wcat_ref[...].astype(F32), jnp.zeros((width - depth, width), F32)], axis=0)
        .T[:, :depth]
        .astype(BF16)
    )
    x_ref[...] = jnp.zeros(x_ref.shape, F32)
    base = 3 * width
    slope_ref[window] = jnp.zeros(slope_ref.shape[1:], F32)
    block_feats_ref[window] = jnp.zeros(block_feats_ref.shape[1:], BF16)
    loads[0].wait()

    lag = 4

    def relay_step(i, carry):
        here = span(i)

        @pl.when(to_direct)
        def _():
            relay_send[here, :] = relay_ref[here, :]

        @pl.when(jnp.logical_not(to_direct))
        def _():
            crosses(i).wait_recv()
            relay_send[here, :] = (
                relay_ref[here, :].astype(F32) + cross_in[here, :].astype(F32)
            ).astype(BF16)

        first(i).start()

        @pl.when(i < CHUNKS - 2 * lag)
        def _():
            slopes(i)

        return carry

    lax.fori_loop(0, CHUNKS, relay_step, 0)
    for copy in loads[1:]:
        copy.wait()
    near.wait()

    def direct_step(i):
        here = span(i)
        first(i).wait_recv()
        value = direct_ref[here, :].astype(F32) + relay_in[here, :].astype(F32)

        @pl.when(to_direct)
        def _():
            crosses(i).wait_recv()
            direct_send[here, :] = (value + cross_in[here, :].astype(F32)).astype(BF16)

        @pl.when(jnp.logical_not(to_direct))
        def _():
            direct_send[here, :] = value.astype(BF16)

        second(i).start()

    def upper_step(i):
        here = pl.ds(pl.multiple_of(i * 2 * size, 2 * size), 2 * size)
        act_grad = act1_ref[here, :]
        early_x[0:width, :] += dot(hidden1_ref[here, :], upstream1_ref[here, :], 0, 0)
        early_x[width : 2 * width, :] += dot(before1_ref[here, :], act_grad, 0, 0)
        early_x[2 * width : 3 * width, :] += dot(agg1_ref[here, :], act_grad, 0, 0)
        grad_ref[here, :] = grad_ref[here, :] + dot(act_grad, w_self_ref[1], 1, 1)

    def layer_step(i):
        here = span(i)
        second(i).wait_recv()
        returned = own_ref[here, :] + (
            total_in[here, :].astype(F32) + sib_in[here, :].astype(F32)
        )
        gradient = grad_ref[here, :] + jnp.concatenate(
            [returned[g * width : (g + 1) * width].T for g in range(group)], axis=0
        )
        upstream = gradient.astype(BF16)
        hidden = hidden_ref[here, :]
        hidden_grad = dot(upstream, w_out_ref[0], 1, 1)
        act_grad = jnp.where(hidden.astype(F32) > 0, hidden_grad, 0.0).astype(BF16)
        agg_grad_t = dot(w_agg_ref[0], act_grad, 1, 1).astype(BF16)
        x_ref[0:width, :] += dot(hidden, upstream, 0, 0)
        x_ref[width : 2 * width, :] += dot(before_ref[here, :], act_grad, 0, 0)
        x_ref[2 * width : 3 * width, :] += dot(agg_ref[here, :], act_grad, 0, 0)
        own_grad = gradient + dot(act_grad, w_self_ref[0], 1, 1)
        feats = feats_ref[:, pl.ds(pl.multiple_of((window // 5) * rows + i * size, size), size)]
        squashed = jnp.tanh(dot(feats, wcat_ref[...], 0, 0))
        genc = dot(feats, (own_grad * (1.0 - squashed * squashed)).astype(BF16), 1, 0)
        for g in range(group):
            block = i * group + g
            tile = jnp.concatenate([tiles_ref[block, s] for s in range(slots)], axis=1)
            contrib = dot(agg_grad_t[:, g * rows : (g + 1) * rows], tile, 1, 0)
            places = [index_ref[block * slots + s] for s in range(slots)]
            slope = jnp.concatenate([slope_ref[at] for at in places], axis=1)
            source_feats = jnp.concatenate([block_feats_ref[at] for at in places], axis=1)
            genc = genc + dot(source_feats, (contrib * slope).astype(BF16), 1, 1)
        x_ref[base : base + depth, :] += genc

    turn = CHUNKS // 2

    def opening(i, carry):
        direct_step(i)
        upper_step(i)

        @pl.when(i < lag)
        def _():
            slopes(CHUNKS - 2 * lag + 2 * i)
            slopes(CHUNKS - 2 * lag + 2 * i + 1)

        @pl.when(i >= lag)
        def _():
            layer_step(i - lag)

        return carry

    def middle(i, carry):
        direct_step(i)
        layer_step(i - lag)
        return carry

    def closing(i, carry):
        layer_step(i)
        return carry

    lax.fori_loop(0, turn, opening, 0)
    early[0]()
    lax.fori_loop(turn, turn + 4, middle, 0)
    early[1]()
    lax.fori_loop(turn + 4, CHUNKS, middle, 0)
    early[2]()
    lax.fori_loop(CHUNKS - lag, CHUNKS, closing, 0)
    final[0]()
    early[3]()

    def drain(i, carry):
        crosses(i).wait_send()
        first(i).wait_send()
        second(i).wait_send()
        return carry

    lax.fori_loop(0, CHUNKS, drain, 0)

    for stage in final[1:]:
        stage()
    early[4]()


def finish_kernel(
    triplet_total,
    early_ref,
    sum_ref,
    loss_out,
    genc_out,
    gtable_out,
    gself_out,
    gagg_out,
    gout_out,
):
    width = gself_out.shape[1]
    for k, out in enumerate((gout_out, gself_out, gagg_out)):
        for layer, source in enumerate((sum_ref, early_ref)):
            out[layer] = source[k * width : (k + 1) * width, :].astype(F32)
    base = 3 * width
    genc_out[...] = sum_ref[base : base + 16, :].astype(F32)[: genc_out.shape[0]]
    gtable_out[...] = sum_ref[base + 16 : base + 16 + gtable_out.shape[0], :].astype(F32)
    loss_out[...] = early_ref[base : base + 1, 0:1] / triplet_total


def body(
    hit_feats,
    layer_ids,
    edge_tiles,
    src_blocks,
    live_slots,
    anchor_hits,
    positive_hits,
    negative_hits,
    w_enc,
    layer_table,
    w_self,
    w_agg,
    w_out,
):
    blocks, slots, rows, _ = edge_tiles.shape
    width = w_enc.shape[1]
    features = hit_feats.shape[0]
    kinds = layer_table.shape[0]
    hits = blocks * rows
    layer_total = w_self.shape[0]
    triplets = anchor_hits.shape[0]
    group = 4
    steps = blocks // group
    span = group * rows
    me = lax.axis_index("phi")
    is_even = me % 2 == 0
    even_pair = (me // 2) % 2 == 0

    def place(part):
        spots = (
            jnp.where(even_pair, 2, 0),
            jnp.where(is_even, 4, 3),
            1,
            jnp.where(is_even, 3, 4),
            jnp.where(even_pair, 0, 2),
        )
        return sum(jnp.where(part == k, spot, 0) for k, spot in enumerate(spots))

    live = jnp.arange(slots, dtype=jnp.int32)[None, :] < live_slots[:, None]
    index = jnp.where(
        live, place(src_blocks // blocks) * blocks + src_blocks % blocks, 5 * blocks
    ).reshape(blocks * slots)
    depth = 16 + kinds
    listed = 2 * triplets // 128 + 1
    list_shape = (-(-(listed + 1) // 8) * 8, 128)

    tile_spec = pl.BlockSpec((group, slots, rows, rows), lambda i, *_: (i, 0, 0, 0))
    row_spec = pl.BlockSpec((span, width), lambda i, *_: (i, 0))
    weight_spec = full((width, width))
    any_spec = pl.BlockSpec(memory_space=pl.ANY)
    row_shape = jax.ShapeDtypeStruct((hits, width), BF16)
    weight_shape = jax.ShapeDtypeStruct((width, width), F32)

    wide_shape = jax.ShapeDtypeStruct((hits, width), F32)
    vmem = pl.BlockSpec(memory_space=pltpu.VMEM)
    smem = pl.BlockSpec(memory_space=pltpu.SMEM)
    few = pltpu.SemaphoreType.DMA((FEAT_CHUNKS,))
    each = pltpu.SemaphoreType.DMA((CHUNKS,))
    one = pltpu.SemaphoreType.DMA((1,))
    four = pltpu.SemaphoreType.DMA((4,))
    block_shape = jax.ShapeDtypeStruct((blocks, rows, width), BF16)
    before0, agg0, hidden0, latents1, agg1, hidden1, latents2, lists, feats, wcat = pl.pallas_call(
        functools.partial(forward_kernel, features),
        in_specs=[smem] + [vmem] * 4 + [any_spec] + [vmem] * 5,
        out_specs=[any_spec] * 10,
        out_shape=[block_shape, row_shape, row_shape, block_shape, row_shape, row_shape]
        + [
            wide_shape,
            jax.ShapeDtypeStruct((5,) + list_shape, jnp.int32),
            jax.ShapeDtypeStruct((depth, 5 * hits), BF16),
            jax.ShapeDtypeStruct((depth, width), BF16),
        ],
        scratch_shapes=[
            pltpu.VMEM((16, hits), BF16),
            pltpu.VMEM((depth, width), BF16),
            pltpu.VMEM(list_shape, jnp.int32),
            pltpu.VMEM((listed - 1, 128, 128), jnp.int32),
            pltpu.VMEM((listed - 1, 128, 128), jnp.int32),
            pltpu.VMEM((listed - 1, 128, 128), jnp.int32),
            pltpu.VMEM((5, 16, hits), BF16),
            pltpu.VMEM((depth, 5 * hits), BF16),
            pltpu.VMEM((5 * blocks + 1, rows, width), BF16),
            pltpu.VMEM((5 * blocks + 1, rows, width), BF16),
        ]
        + [pltpu.VMEM((hits, width), BF16)] * 4
        + [
            pltpu.VMEM((hits, width), F32),
            pltpu.VMEM(edge_tiles.shape, BF16),
            each,
            pltpu.SemaphoreType.DMA((6,)),
            pltpu.SemaphoreType.DMA((3 * LATER_STEPS,)),
            one,
        ]
        + [few] * 6
        + [four] * 2
        + [each] * 8
        + [one] * 2,
        compiler_params=pltpu.CompilerParams(
            collective_id=1, has_side_effects=True, vmem_limit_bytes=VMEM_BYTES
        ),
        name="forward",
    )(
        index,
        hit_feats,
        layer_ids.reshape(1, hits),
        positive_hits.reshape(triplets // 128, 128),
        negative_hits.reshape(triplets // 128, 128),
        edge_tiles,
        w_enc,
        layer_table,
        w_self,
        w_agg,
        w_out,
    )

    before0, latents1 = before0.reshape(hits, width), latents1.reshape(hits, width)
    lists = lists.reshape(-1)
    move_shape = jax.ShapeDtypeStruct((triplets, width), BF16)
    wide_move = jax.ShapeDtypeStruct((triplets, width), F32)
    move_spec = full((triplets, width))
    *found, anchors = pl.pallas_call(
        gather_kernel,
        grid_spec=pltpu.PrefetchScalarGridSpec(
            num_scalar_prefetch=2,
            grid=(1,),
            in_specs=[full((hits, width))],
            out_specs=[move_spec] * 6,
            scratch_shapes=[pltpu.VMEM((2 * triplets + 8, width), F32)],
        ),
        out_shape=[move_shape] * 6,
        compiler_params=params(),
        name="gather",
    )(lists, anchor_hits, latents2)
    coef_shape = (triplets // 128, 128)
    loss_part, ganchor, *moves, coef, coefs = pl.pallas_call(
        functools.partial(contrast_kernel, 1.0 / math.sqrt(width)),
        in_specs=[vmem] * 6,
        out_specs=[vmem] * 8,
        out_shape=[jax.ShapeDtypeStruct((8, width), F32), wide_move]
        + [move_shape] * 4
        + [jax.ShapeDtypeStruct(coef_shape, F32), jax.ShapeDtypeStruct((4,) + coef_shape, F32)],
        scratch_shapes=[pltpu.VMEM((triplets, width), F32)]
        + [pltpu.VMEM((triplets, width), BF16)] * 6
        + [pltpu.SemaphoreType.DMA((PARTS,))] * 16
        + [pltpu.SemaphoreType.DMA((4,))] * 2,
        compiler_params=pltpu.CompilerParams(
            collective_id=4, has_side_effects=True, vmem_limit_bytes=VMEM_BYTES
        ),
        name="contrast",
    )(*found, anchors)

    t_shape = jax.ShapeDtypeStruct((blocks, width, rows), F32)
    t_half = jax.ShapeDtypeStruct((blocks, width, rows), BF16)
    adj_shape = pltpu.VMEM((5 * blocks + 1, width, rows), F32)
    upstream1, act1, gradient2, obelow, own, oabove, osibling, ocross = pl.pallas_call(
        functools.partial(last_backward, group, steps),
        grid_spec=pltpu.PrefetchScalarGridSpec(
            num_scalar_prefetch=3,
            grid=(steps,),
            in_specs=[tile_spec, move_spec, full(coef_shape), full((4,) + coef_shape)]
            + [move_spec] * 5
            + [row_spec]
            + [full((2, width, width))] * 2,
            out_specs=[row_spec] * 3 + [any_spec] * 5,
            scratch_shapes=[
                adj_shape,
                pltpu.VMEM((10 * triplets + 40, width), F32),
                pltpu.VMEM((4, blocks, width, rows), BF16),
                pltpu.SemaphoreType.DMA((5,)),
            ]
            + [pltpu.VMEM((hits, width), F32)] * 4,
        ),
        out_shape=[row_shape] * 2 + [wide_shape] + [t_half, t_shape] + [t_half] * 3,
        compiler_params=params(),
        name="last_backward",
    )(
        index, lists, anchor_hits, edge_tiles, ganchor, coef, coefs, anchors, *moves, hidden1, w_agg, w_out,
    )
    pairs = lax.axis_size("phi") // 2

    def sum_sizes(count, wire):
        chunk = -(-count // (32 * pairs)) * 16
        total = 2 * pairs * chunk
        return jax.ShapeDtypeStruct((total, width), wire), [
            pltpu.VMEM((total, width), F32),
            pltpu.VMEM((total // 2, width), F32),
            pltpu.VMEM((total // 2, width), wire),
            pltpu.VMEM((pairs - 1, chunk, width), wire),
        ]

    early_shape, early_scratch = sum_sizes(3 * width + 8, F32)
    final_shape, final_scratch = sum_sizes(3 * width + depth, BF16)
    many = pltpu.SemaphoreType.DMA((pairs - 1,))
    flat = (hits, width)
    sums = pl.pallas_call(
        functools.partial(back_kernel, pairs),
        in_specs=[smem] + [any_spec] * 15 + [vmem] * 6,
        out_specs=[vmem] * 2,
        out_shape=[early_shape, final_shape],
        scratch_shapes=[pltpu.VMEM((width, depth), BF16)]
        + [pltpu.VMEM(flat, BF16)] * 8
        + [pltpu.VMEM(flat, F32)] * 2
        + [pltpu.VMEM(flat, BF16)] * 8
        + [
            pltpu.VMEM(edge_tiles.shape, BF16),
            pltpu.VMEM((5 * blocks + 1, width, rows), F32),
            pltpu.VMEM((5 * blocks + 1, depth, rows), BF16),
        ]
        + final_scratch
        + early_scratch
        + [pltpu.SemaphoreType.DMA((13,))]
        + [pltpu.SemaphoreType.DMA((CHUNKS,))] * 6
        + [one, one]
        + [one, one, many, many, many, many, one, one] * 2,
        compiler_params=pltpu.CompilerParams(
            collective_id=3, has_side_effects=True, vmem_limit_bytes=VMEM_BYTES
        ),
        name="back",
    )(
        index, ocross.reshape(flat), osibling.reshape(flat), oabove.reshape(flat),
        obelow.reshape(flat), own.reshape(flat), gradient2, hidden0, before0, agg0, edge_tiles,
        upstream1, act1, hidden1, latents1, agg1,
        feats, wcat, w_self, w_agg, w_out, loss_part,
    )
    stack = jax.ShapeDtypeStruct((2, width, width), F32)
    loss, genc, gtable, gself, gagg, gout = pl.pallas_call(
        functools.partial(finish_kernel, float(triplets * lax.axis_size("phi"))),
        in_specs=[vmem] * 2,
        out_specs=[vmem] * 6,
        out_shape=[
            jax.ShapeDtypeStruct((1, 1), F32),
            jax.ShapeDtypeStruct((features, width), F32),
            jax.ShapeDtypeStruct((kinds, width), F32),
            stack, stack, stack,
        ],
        name="finish",
    )(*sums)
    return (loss.reshape(1), genc, gtable, gself, gagg, gout)


def solution(mesh):
    both = ("event", "phi")
    in_specs = (
        P(None, both),
        P(both),
        P(both, None, None, None),
        P(both, None),
        P(both),
        P(both),
        P(both),
        P(both),
        P(),
        P(),
        P(),
        P(),
        P(),
    )
    out_specs = (
        P("event"),
        P("event", None),
        P("event", None),
        P("event", None, None),
        P("event", None, None),
        P("event", None, None),
    )
    return jax.shard_map(body, mesh=mesh, in_specs=in_specs, out_specs=out_specs, check_vma=False)
```

```python
import functools
import math

import jax
import jax.numpy as jnp
from jax import lax
from jax.experimental import pallas as pl
from jax.experimental.pallas import tpu as pltpu
from jax.sharding import PartitionSpec as P

loss_divisor = 64.0
F32 = jnp.float32
BF16 = jnp.bfloat16
VMEM_BYTES = 60 * 1024 * 1024


def dot(left, right, left_dim, right_dim):
    return lax.dot_general(
        left, right, (((left_dim,), (right_dim,)), ((), ())), preferred_element_type=F32
    )


def full(shape):
    return pl.BlockSpec(shape, lambda *_: (0,) * len(shape))


def params():
    return pltpu.CompilerParams(
        dimension_semantics=("arbitrary",), vmem_limit_bytes=VMEM_BYTES
    )


CHUNKS = 16
LATER_STEPS = 8


def peers():
    count = lax.axis_size("phi")
    me = lax.axis_index("phi")
    odd_pair = (me // 2) % 2
    odd_core = me % 2
    direct = me + 2 - 4 * odd_pair
    sibling = me + 1 - 2 * odd_core
    stride = 4 - 8 * odd_pair
    onward = (me + stride + count) % count
    source = (me - stride + count) % count
    return direct, sibling, onward, source, odd_pair == odd_core


def remote(src, dst, send, recv, target):
    return pltpu.make_async_remote_copy(
        src_ref=src,
        dst_ref=dst,
        send_sem=send,
        recv_sem=recv,
        device_id={"phi": target},
        device_id_type=pl.DeviceIdType.MESH,
    )


def greet(targets):
    barrier = pltpu.get_barrier_semaphore()
    for target in targets:
        pl.semaphore_signal(
            barrier, inc=1, device_id={"phi": target}, device_id_type=pl.DeviceIdType.MESH
        )
    pl.semaphore_wait(barrier, len(targets))


def role_targets():
    count = lax.axis_size("phi")
    me = lax.axis_index("phi")
    odd_pair = (me // 2) % 2
    odd_core = me % 2
    sibling = me + 1 - 2 * odd_core
    across = (me - 1 + 2 * odd_core + count) % count
    direct = me + 2 - 4 * odd_pair
    far = (me - 2 + 4 * odd_pair + count) % count
    return sibling, across, direct, far


def aggregate_group(index_ref, tiles_ref, window_ref, step, group, slots, rows):
    results = []
    for g in range(group):
        tile = jnp.concatenate([tiles_ref[step * group + g, s] for s in range(slots)], axis=1)
        source = jnp.concatenate(
            [
                window_ref[index_ref[(step * group + g) * slots + s]] for s in range(slots)
            ],
            axis=0,
        )
        results.append(dot(tile, source, 1, 0).astype(BF16))
    return jnp.concatenate(results, axis=0)


def node_update(own, aggregated, w_self, w_agg, w_out):
    activation = dot(own, w_self, 1, 0) + dot(aggregated, w_agg, 1, 0)
    hidden = jnp.maximum(activation, 0.0).astype(BF16)
    updated = (own.astype(F32) + dot(hidden, w_out, 1, 0)).astype(BF16)
    return hidden, updated


FEAT_CHUNKS = 2


def forward_kernel(
    features,
    index_ref,
    hit_ref,
    id_ref,
    positive_ref,
    negative_ref,
    tiles_hbm,
    enc_ref,
    table_ref,
    w_self_ref,
    w_agg_ref,
    w_out_ref,
    before_out,
    agg0_out,
    hidden0_out,
    latents_out,
    agg1_out,
    hidden1_out,
    z_out,
    lists_out,
    feats_out,
    wcat_out,
    packed_ref,
    wcat_ref,
    keys_ref,
    key_cols,
    place_cols,
    entry_cols,
    packs_ref,
    feats_ref,
    window_ref,
    later_ref,
    agg0_ref,
    hidden0_ref,
    agg1_ref,
    hidden1_ref,
    z_ref,
    tiles_ref,
    tile_sem,
    out_sem,
    late_sem,
    list_sem,
    *sems,
):
    fys, fyr, fzs, fzr, fcs, fcr, ls, lr = sems[:8]
    ys, yr, zs, zr, cs, cr, ss, sr = sems[8:16]
    fss, fsr = sems[16:]
    direct, sibling, onward, source, direct_crosses = peers()
    roles = role_targets()
    blocks, slots, rows, _ = tiles_ref.shape
    hits = packed_ref.shape[1]
    group = blocks // CHUNKS
    span = group * rows

    def tile_load(i):
        part = pl.ds(i * group, group)
        return pltpu.make_async_copy(tiles_hbm.at[part], tiles_ref.at[part], tile_sem.at[i])

    lax.fori_loop(0, CHUNKS, lambda i, c: (tile_load(i).start(), c)[1], 0)
    kinds, width = table_ref.shape
    filler = jnp.zeros((16 - features, width), F32)
    wcat_ref[...] = jnp.concatenate(
        [enc_ref[...].astype(F32), filler, table_ref[...].astype(F32)], axis=0
    ).astype(BF16)

    def gather_input(i, carry):
        at = pl.ds(pl.multiple_of(i * 512, 512), 512)
        packed_ref[:, at] = jnp.concatenate(
            [
                hit_ref[:, at].astype(F32),
                id_ref[:, at].astype(F32),
                jnp.zeros((15 - features, 512), F32),
            ],
            axis=0,
        ).astype(BF16)
        return carry

    lax.fori_loop(0, hits // 512, gather_input, 0)
    beside = [t + 1 - 2 * lax.rem(t, 2) for t in (onward, source)]
    greet((direct, sibling, onward, source, beside[0], beside[1], roles[1], roles[3]))
    columns = hits // FEAT_CHUNKS

    def pack(k, i):
        return packs_ref.at[k, :, pl.ds(i * columns, columns)]

    chunks = range(FEAT_CHUNKS)
    f_first = [
        remote(
            packed_ref.at[:, pl.ds(i * columns, columns)], pack(0, i), fys.at[i], fyr.at[i], direct
        )
        for i in chunks
    ]
    f_second = [remote(pack(0, i), pack(2, i), fzs.at[i], fzr.at[i], onward) for i in chunks]
    f_cross_a = [remote(pack(0, i), pack(4, i), fcs.at[i], fcr.at[i], sibling) for i in chunks]
    f_cross_b = [remote(pack(0, i), pack(4, i), fcs.at[i], fcr.at[i], beside[0]) for i in chunks]
    f_near = remote(packed_ref, packs_ref.at[3], fss.at[0], fsr.at[0], sibling)
    for copy in f_first:
        copy.start()
    f_near.start()

    def encode(k, ref):
        step = 512
        is_feature = lax.broadcasted_iota(jnp.int32, (16, step), 0) < features
        kind = lax.broadcasted_iota(jnp.int32, (16, step), 0).astype(F32)

        def run(i, carry):
            at = pl.multiple_of(i * step, step)
            data = ref[:, pl.ds(at, step)].astype(F32)
            onehot = jnp.where(kind == data[features : features + 1], 1.0, 0.0)
            feats = jnp.concatenate([jnp.where(is_feature, data, 0.0), onehot], axis=0).astype(BF16)
            feats_ref[:, pl.ds(pl.multiple_of(k * hits + i * step, step), step)] = feats
            encoded = dot(feats, wcat_ref[...], 0, 0)
            squashed = jnp.tanh(encoded).astype(BF16)
            for u in range(step // rows):
                window_ref[k * blocks + i * (step // rows) + u] = squashed[
                    u * rows : (u + 1) * rows
                ]
            return carry

        lax.fori_loop(0, hits // step, run, 0)

    encode(1, packed_ref)
    for i in chunks:
        f_first[i].wait_recv()
        f_second[i].start()

        @pl.when(direct_crosses)
        def _():
            f_cross_a[i].start()

        @pl.when(jnp.logical_not(direct_crosses))
        def _():
            f_cross_b[i].start()

    f_near.wait_recv()
    encode(3, packs_ref.at[3])
    encode(0, packs_ref.at[0])
    for i in chunks:
        f_second[i].wait_recv()
    encode(2, packs_ref.at[2])
    for i in chunks:
        f_cross_a[i].wait_recv()
    encode(4, packs_ref.at[4])
    window_ref[5 * blocks] = jnp.zeros((rows, width), BF16)
    later_ref[5 * blocks] = jnp.zeros((rows, width), BF16)

    def part(k, i):
        return pl.ds(k * blocks + i * group, group)

    def first(i):
        return remote(later_ref.at[part(1, i)], later_ref.at[part(0, i)], ys.at[i], yr.at[i], direct)

    def near(i):
        return remote(later_ref.at[part(1, i)], later_ref.at[part(3, i)], ss.at[i], sr.at[i], sibling)

    def second(i):
        return remote(later_ref.at[part(0, i)], later_ref.at[part(2, i)], zs.at[i], zr.at[i], onward)

    def cross_a(i):
        return remote(later_ref.at[part(0, i)], later_ref.at[part(4, i)], cs.at[i], cr.at[i], sibling)

    def cross_b(i):
        return remote(later_ref.at[part(2, i)], later_ref.at[part(4, i)], cs.at[i], cr.at[i], sibling)

    def cross_c(i):
        return remote(
            later_ref.at[part(0, i)], later_ref.at[part(4, i)], cs.at[i], cr.at[i], beside[0]
        )

    def relay(i):
        first(i).wait_recv()
        second(i).start()

        @pl.when(direct_crosses)
        def _():
            cross_a(i).start()

        if isinstance(i, int) and i == CHUNKS - 1:

            @pl.when(jnp.logical_not(direct_crosses))
            def _():
                cross_c(i).start()

    def land(i):
        second(i).wait_recv()

        if not (isinstance(i, int) and i == CHUNKS - 1):

            @pl.when(jnp.logical_not(direct_crosses))
            def _():
                cross_b(i).start()

    lead = 5
    relayed = (CHUNKS - lead + 1) // 2

    def layer0(i, carry):
        tile_load(i).wait()
        here = pl.ds(pl.multiple_of(i * span, span), span)
        aggregated = aggregate_group(index_ref, tiles_ref, window_ref, i, group, slots, rows)
        own = window_ref[part(1, i)].reshape(span, width)
        hidden, updated = node_update(own, aggregated, w_self_ref[0], w_agg_ref[0], w_out_ref[0])
        later_ref[part(1, i)] = updated.reshape(group, rows, width)
        first(i).start()
        near(i).start()
        agg0_ref[here, :] = aggregated
        hidden0_ref[here, :] = hidden

        @pl.when(jnp.logical_and(i >= lead, lax.rem(i, 2) == 1))
        def _():
            relay(lax.div(i - lead, 2))

        return carry

    lax.fori_loop(0, CHUNKS, layer0, 0)
    own = pl.ds(blocks, blocks)
    saves = [
        pltpu.make_async_copy(src, dst, out_sem.at[k])
        for k, (src, dst) in enumerate(
            (
                (window_ref.at[own], before_out),
                (agg0_ref, agg0_out),
                (hidden0_ref, hidden0_out),
                (later_ref.at[own], latents_out),
                (feats_ref, feats_out),
                (wcat_ref, wcat_out),
            )
        )
    ]
    for copy in saves:
        copy.start()

    wanted = jnp.concatenate([positive_ref[...], negative_ref[...]], axis=0)
    lines = wanted.shape[0]
    pairs_of = lines * 128
    line = lax.broadcasted_iota(jnp.int32, (lines, 128), 0)
    lane = lax.broadcasted_iota(jnp.int32, (lines, 128), 1)
    keys = wanted * pairs_of + (line * 128 + lane)
    tall = jnp.concatenate(
        [wanted.astype(F32), jnp.zeros((128 - lines, 128), F32)], axis=0
    ).T.astype(jnp.int32)
    down = lax.broadcasted_iota(jnp.int32, (128, 1), 0)
    counts = []
    for k in range(5):
        mine = jnp.logical_and(wanted >= k * hits, wanted < (k + 1) * hits)
        counted = jnp.sum(jnp.where(mine, 1.0, 0.0), axis=1, keepdims=True)
        counts.append(jnp.sum(counted, axis=0, keepdims=True).astype(jnp.int32))
    aligned, shift = [jnp.zeros((1, 1), jnp.int32)], [jnp.zeros((1, 1), jnp.int32)]
    for k in range(5):
        filled = lax.bitwise_and(counts[k] + 7, -8)
        aligned.append(aligned[k] + filled)
        shift.append(shift[k] + filled - counts[k])
    for c in range(lines):
        column = tall[:, c : c + 1]
        slot = down + c * 128
        moved = jnp.zeros((128, 1), jnp.int32)
        first_row = jnp.zeros((128, 1), jnp.int32)
        for k in range(5):
            mine = jnp.logical_and(column >= k * hits, column < (k + 1) * hits)
            moved = moved + jnp.where(mine, shift[k], 0)
            first_row = first_row + jnp.where(mine, k * hits, 0)
        entry = (column - first_row) * (1 << ENTRY_BITS) + slot - pairs_of
        key_cols[c] = jnp.broadcast_to(column * pairs_of + slot, (128, 128))
        place_cols[c] = jnp.broadcast_to(moved, (128, 128))
        entry_cols[c] = jnp.broadcast_to(entry, (128, 128))

    def rank(c, carry):
        column = key_cols[c]
        count = jnp.zeros((128, 128), F32)
        for r in range(lines):
            count = count + jnp.where(keys[r : r + 1] < column, 1.0, 0.0)
        total = jnp.sum(count, axis=1, keepdims=True).astype(jnp.int32)
        place_cols[c] = place_cols[c] + jnp.broadcast_to(total, (128, 128))
        return carry

    keys_ref[...] = jnp.zeros(keys_ref.shape, jnp.int32)

    def put(q, carry):
        target = lax.broadcasted_iota(jnp.int32, (128, 128), 1) + q * 128

        def match(c, total):
            return total + jnp.where(place_cols[c] == target, entry_cols[c], 0)

        total = lax.fori_loop(0, lines, match, jnp.zeros((128, 128), jnp.int32))
        found = jnp.sum(total.astype(F32), axis=0, keepdims=True).astype(jnp.int32)
        keys_ref[pl.ds(q, 1), :] = found + pairs_of
        return carry

    turns = 3
    for k in range(turns):
        relay(relayed + k)
        land(k)
        lax.fori_loop(lines * k // turns, lines * (k + 1) // turns, rank, 0)
    put_turns = CHUNKS - relayed - turns - 2
    for k in range(put_turns):
        relay(relayed + turns + k)
        land(turns + k)
        lax.fori_loop(
            (lines + 1) * k // put_turns, (lines + 1) * (k + 1) // put_turns, put, 0
        )
    lane = lax.broadcasted_iota(jnp.int32, (1, 128), 1)
    keys_ref[pl.ds(lines + 1, 1), :] = sum(
        jnp.where(lane == k, aligned[k] // 8, 0) for k in range(6)
    )
    lists = [
        remote(keys_ref, lists_out.at[j + 1], ls.at[j], lr.at[j], target)
        for j, target in enumerate(roles)
    ]
    for copy in lists:
        copy.start()
    own_list = pltpu.make_async_copy(keys_ref, lists_out.at[0], list_sem.at[0])
    own_list.start()

    for k in range(CHUNKS - 2, CHUNKS):
        relay(k)
    for k in range(turns + put_turns, CHUNKS):
        land(k)

    def settle(i, carry):
        near(i).wait()
        cross_a(i).wait_recv()
        return carry

    lax.fori_loop(0, CHUNKS, settle, 0)

    later_group = blocks // LATER_STEPS
    later_span = later_group * rows

    def late_saves(i):
        here = pl.ds(pl.multiple_of(i * later_span, later_span), later_span)
        return [
            pltpu.make_async_copy(src.at[here], dst.at[here], late_sem.at[k * LATER_STEPS + i])
            for k, (src, dst) in enumerate(
                ((agg1_ref, agg1_out), (hidden1_ref, hidden1_out), (z_ref, z_out))
            )
        ]

    def layer1(i, carry):
        here = pl.ds(pl.multiple_of(i * later_span, later_span), later_span)
        aggregated = aggregate_group(index_ref, tiles_ref, later_ref, i, later_group, slots, rows)
        own = later_ref[pl.ds(blocks + i * later_group, later_group)].reshape(later_span, width)
        hidden, updated = node_update(own, aggregated, w_self_ref[1], w_agg_ref[1], w_out_ref[1])
        agg1_ref[here, :] = aggregated
        hidden1_ref[here, :] = hidden
        z_ref[here, :] = updated.astype(F32)
        for copy in late_saves(i):
            copy.start()
        return carry

    lax.fori_loop(0, LATER_STEPS, layer1, 0)

    def drain(i, carry):
        first(i).wait_send()
        second(i).wait_send()
        cross_a(i).wait_send()
        return carry

    lax.fori_loop(0, CHUNKS, drain, 0)

    def saved(i, carry):
        for copy in late_saves(i):
            copy.wait()
        return carry

    lax.fori_loop(0, LATER_STEPS, saved, 0)
    for i in chunks:
        f_first[i].wait_send()
        f_second[i].wait_send()
        f_cross_a[i].wait_send()
    f_near.wait_send()
    own_list.wait()
    for copy in lists:
        copy.wait()
    for copy in saves:
        copy.wait()


def segments(list_ref, stride, listed):
    me = lax.axis_index("phi")
    odd_core, odd_pair = lax.rem(me, 2), lax.rem(lax.div(me, 2), 2)
    places = (2, 1 + 2 * odd_core, 3 - 2 * odd_core, 4 * odd_pair, 4 - 4 * odd_pair)
    starts = [j * stride + listed + k for j, k in enumerate(places)]
    return [(list_ref[at], list_ref[at + 1]) for at in starts]


def gather_kernel(list_ref, anchor_ref, z_ref, *refs):
    outs, (anchor_out, buf_ref) = refs[:5], refs[5:]
    triplets, width = anchor_out.shape
    stride = list_ref.shape[0] // 5
    bounds = segments(list_ref, stride, 2 * triplets + 128)

    def anchors(i, carry):
        at = pl.multiple_of(i * 16, 16)
        anchor_out[pl.ds(at, 16), :] = jnp.concatenate(
            [z_ref[pl.ds(anchor_ref[i * 16 + u], 1), :] for u in range(16)], axis=0
        ).astype(BF16)
        return carry

    lax.fori_loop(0, triplets // 16, anchors, 0)
    zeros = jnp.zeros((64, width), F32)

    def clear(i, carry):
        for u in range(4):
            buf_ref[pl.ds(pl.multiple_of(i * 256 + u * 64, 64), 64), :] = zeros
        return carry

    lax.fori_loop(0, 2 * triplets // 256, clear, 0)
    for j in range(5):

        def fetch(i, carry, j=j):
            for u in range(8):
                entry = list_ref[j * stride + i * 8 + u]
                row = z_ref[pl.ds(lax.shift_right_logical(entry, ENTRY_BITS), 1), :]
                buf_ref[pl.ds(lax.bitwise_and(entry, ENTRY_MASK), 1), :] = row
            return carry

        lax.fori_loop(bounds[j][0], bounds[j][1], fetch, 0)

        def subtract(i, carry, j=j):
            for u in range(8):
                at = pl.multiple_of(i * 256 + u * 32, 32)
                value = buf_ref[pl.ds(triplets + at, 32), :] - buf_ref[pl.ds(at, 32), :]
                outs[j][pl.ds(at, 32), :] = value.astype(BF16)
                if j < 4:
                    buf_ref[pl.ds(triplets + at, 32), :] = zeros[:32]
                    buf_ref[pl.ds(at, 32), :] = zeros[:32]
            return carry

        lax.fori_loop(0, triplets // 256, subtract, 0)


ENTRY_BITS = 12
ENTRY_MASK = (1 << ENTRY_BITS) - 1
PARTS = 8


def contrast_kernel(
    inv_root,
    self_ref,
    sib_ref,
    cross_ref,
    near_ref,
    far_ref,
    anchor_ref,
    loss_ref,
    ganchor_ref,
    asib_ref,
    across_ref,
    adirect_ref,
    afar_ref,
    coef_out,
    coefs_out,
    change_ref,
    sib_in,
    cross_in,
    far_send,
    far_in,
    near_send,
    near_in,
    *sems,
):
    s = [sems[2 * i : 2 * i + 2] for i in range(9)]
    direct, sibling, onward, source, near_adds = peers()
    roles = role_targets()
    size = anchor_ref.shape[0] // PARTS
    greet((direct, sibling, onward, source, roles[1], roles[3]))

    def rows(i):
        return pl.ds(i * size, size)

    def copies(k, src, dst, target):
        return [
            remote(src.at[rows(i)], dst.at[rows(i)], s[k][0].at[i], s[k][1].at[i], target)
            for i in range(PARTS)
        ]

    crosses = copies(0, cross_ref, cross_in, sibling)
    sibs = copies(1, sib_ref, sib_in, sibling)
    hops = copies(2, far_send, far_in, source)
    nears = copies(3, near_send, near_in, direct)
    to_direct = copies(4, anchor_ref, adirect_ref, direct)
    to_sibling = copies(5, anchor_ref, asib_ref, sibling)
    relays = copies(6, adirect_ref, afar_ref, onward)
    cross_a = copies(7, adirect_ref, across_ref, sibling)
    cross_b = copies(7, afar_ref, across_ref, sibling)
    coefs = [
        remote(coef_out, coefs_out.at[j], s[8][0].at[j], s[8][1].at[j], target)
        for j, target in enumerate(roles)
    ]
    for copy in crosses:
        copy.start()
    for copy in sibs:
        copy.start()
    for i in range(PARTS):
        @pl.when(near_adds)
        def _():
            far_send[rows(i), :] = far_ref[rows(i), :]

        @pl.when(jnp.logical_not(near_adds))
        def _():
            crosses[i].wait_recv()
            far_send[rows(i), :] = (
                far_ref[rows(i), :].astype(F32) + cross_in[rows(i), :].astype(F32)
            ).astype(BF16)

        hops[i].start()
        if i < PARTS // 2:
            to_direct[i].start()
    for i in range(PARTS):
        hops[i].wait_recv()
        value = near_ref[rows(i), :].astype(F32) + far_in[rows(i), :].astype(F32)

        @pl.when(near_adds)
        def _():
            crosses[i].wait_recv()
            near_send[rows(i), :] = (value + cross_in[rows(i), :].astype(F32)).astype(BF16)

        @pl.when(jnp.logical_not(near_adds))
        def _():
            near_send[rows(i), :] = value.astype(BF16)

        nears[i].start()
    for i in range(PARTS // 2, PARTS):
        to_direct[i].start()

    def relay(i):
        to_sibling[i].start()
        to_direct[i].wait_recv()
        relays[i].start()

        @pl.when(near_adds)
        def _():
            cross_a[i].start()

    gaps = []
    for i in range(PARTS):
        if i < PARTS // 2:
            relay(i)
        sibs[i].wait_recv()
        nears[i].wait_recv()
        change = (
            near_in[rows(i), :].astype(F32)
            + self_ref[rows(i), :].astype(F32)
            + sib_in[rows(i), :].astype(F32)
        )
        change_ref[rows(i), :] = change
        product = anchor_ref[rows(i), :].astype(F32) * change
        for u in range(size // 128):
            gaps.append(
                jnp.sum(product[u * 128 : (u + 1) * 128].T, axis=0, keepdims=True) * inv_root
            )
    gap = jnp.concatenate(gaps, axis=0)
    coef_out[...] = jax.nn.sigmoid(gap) * (inv_root / loss_divisor)
    for copy in coefs:
        copy.start()
    soft = jnp.maximum(gap, 0.0) + jnp.log1p(jnp.exp(-jnp.abs(gap)))
    loss_ref[...] = jnp.broadcast_to(jnp.sum(soft, keepdims=True), loss_ref.shape)
    for i in range(PARTS // 2, PARTS):
        relay(i)
    for i in range(PARTS):
        relays[i].wait_recv()

        @pl.when(jnp.logical_not(near_adds))
        def _():
            cross_b[i].start()

    size = 128
    eye = lax.broadcasted_iota(jnp.int32, (size, size), 0) == lax.broadcasted_iota(
        jnp.int32, (size, size), 1
    )
    for i in range(coef_out.shape[0]):
        coef = coef_out[pl.ds(i, 1), :]
        column = jnp.sum(jnp.where(eye, coef, 0.0), axis=1, keepdims=True)
        here = pl.ds(i * size, size)
        ganchor_ref[here, :] = column * change_ref[here, :]
    for copy in coefs:
        copy.wait()
    for i in range(PARTS):
        crosses[i].wait_send()
        sibs[i].wait_send()
        hops[i].wait_send()
        nears[i].wait_send()
        to_direct[i].wait_send()
        to_sibling[i].wait()
        relays[i].wait_send()
        cross_a[i].wait()


def spread_group(index_ref, tiles_ref, adj_ref, agg_grad_t, step, group, slots, rows):
    for g in range(group):
        block = step * group + g
        tile = jnp.concatenate([tiles_ref[block, s] for s in range(slots)], axis=1)
        contrib = dot(agg_grad_t[:, g * rows : (g + 1) * rows], tile, 1, 0)
        for s in range(slots):
            at = index_ref[(step * group + g) * slots + s]
            adj_ref[at] = adj_ref[at] + contrib[:, s * rows : (s + 1) * rows]


def clear_blocks(adj_ref):
    def clear(i, carry):
        adj_ref[i] = jnp.zeros(adj_ref.shape[1:], F32)
        return carry

    lax.fori_loop(0, adj_ref.shape[0], clear, 0)


def scatter_rows(
    list_ref, anchor_ref, ganchor_ref, coef_ref, coefs_ref, rows_in, moved_ref, sums
):
    triplets, width = ganchor_ref.shape
    hits = sums[0].shape[0]
    stride = list_ref.shape[0] // 5
    span = 2 * triplets + 8
    bounds = segments(list_ref, stride, 2 * triplets + 128)
    zeros = jnp.zeros((64, width), F32)

    def clear(i, carry):
        for target in sums:
            target[pl.ds(pl.multiple_of(i * 64, 64), 64), :] = zeros
        return carry

    lax.fori_loop(0, hits // 64, clear, 0)
    eye = lax.broadcasted_iota(jnp.int32, (128, 128), 0) == lax.broadcasted_iota(
        jnp.int32, (128, 128), 1
    )
    for j, source in enumerate(rows_in):
        for i in range(triplets // 128):
            coef = coef_ref[pl.ds(i, 1), :] if j == 0 else coefs_ref[j - 1, pl.ds(i, 1), :]
            spread = jnp.where(eye, coef, 0.0)
            high = spread.astype(BF16)
            low = (spread - high.astype(F32)).astype(BF16)
            part = source[pl.ds(i * 128, 128), :]
            value = dot(high, part, 1, 0) + dot(low, part, 1, 0)
            moved_ref[pl.ds(j * span + i * 128, 128), :] = -value
            moved_ref[pl.ds(j * span + triplets + i * 128, 128), :] = value
        moved_ref[pl.ds(j * span + 2 * triplets, 8), :] = zeros[:8]

    def anchors(i, carry):
        for u in range(8):
            t = i * 8 + u
            here = pl.ds(anchor_ref[t], 1)
            target = sums[u % 4]
            target[here, :] = target[here, :] + ganchor_ref[pl.ds(t, 1), :]
        return carry

    lax.fori_loop(0, triplets // 8, anchors, 0)
    for j in range(5):

        def add(i, carry, j=j):
            for u in range(8):
                entry = list_ref[j * stride + i * 8 + u]
                here = pl.ds(lax.shift_right_logical(entry, ENTRY_BITS), 1)
                target = sums[u % 4]
                moved = moved_ref[pl.ds(j * span + lax.bitwise_and(entry, ENTRY_MASK), 1), :]
                target[here, :] = target[here, :] + moved
            return carry

        lax.fori_loop(bounds[j][0], bounds[j][1], add, 0)


def last_backward(
    group,
    steps,
    index_ref,
    list_ref,
    anchor_ref,
    tiles_hbm,
    ganchor_ref,
    coef_ref,
    coefs_ref,
    aself_ref,
    asib_ref,
    across_ref,
    adirect_ref,
    afar_ref,
    hidden_ref,
    w_agg_ref,
    w_out_ref,
    upstream_ref,
    act_ref,
    gradient_ref,
    obelow_ref,
    oown_ref,
    oabove_ref,
    osibling_ref,
    ocross_ref,
    adj_ref,
    moved_ref,
    stage_ref,
    tiles_ref,
    tile_sem,
    piece_sem,
    *sums,
):
    step = pl.program_id(0)
    slots, rows = tiles_ref.shape[1], tiles_ref.shape[2]
    span = group * rows

    def tile_load(i):
        part = pl.ds(i * group, group)
        return pltpu.make_async_copy(tiles_hbm.at[part], tiles_ref.at[part], tile_sem.at[i])

    @pl.when(step == 0)
    def _():
        for i in range(steps):
            tile_load(i).start()
        clear_blocks(adj_ref)
        scatter_rows(
            list_ref, anchor_ref, ganchor_ref, coef_ref, coefs_ref,
            (aself_ref, asib_ref, across_ref, adirect_ref, afar_ref), moved_ref, sums,
        )

    here = pl.ds(pl.multiple_of(step * span, span), span)
    gradient = (sums[0][here, :] + sums[1][here, :]) + (sums[2][here, :] + sums[3][here, :])
    upstream = gradient.astype(BF16)
    hidden_grad = dot(upstream, w_out_ref[1], 1, 1)
    act_grad = jnp.where(hidden_ref[...].astype(F32) > 0, hidden_grad, 0.0).astype(BF16)
    upstream_ref[...] = upstream
    act_ref[...] = act_grad
    gradient_ref[...] = gradient
    tile_load(step).wait()
    agg_grad_t = dot(w_agg_ref[1], act_grad, 1, 1).astype(BF16)
    spread_group(index_ref, tiles_ref, adj_ref, agg_grad_t, step, group, slots, rows)

    @pl.when(step == steps - 1)
    def _():
        blocks = oown_ref.shape[0]
        copies = [
            pltpu.make_async_copy(
                adj_ref.at[pl.ds(blocks, blocks)], oown_ref, piece_sem.at[4]
            )
        ]
        copies[0].start()
        for j, (k, target) in enumerate(
            ((4, ocross_ref), (3, osibling_ref), (2, oabove_ref), (0, obelow_ref))
        ):

            def store(i, carry, k=k, j=j):
                for u in range(2):
                    stage_ref[j, 2 * i + u] = adj_ref[k * blocks + 2 * i + u].astype(BF16)
                return carry

            lax.fori_loop(0, blocks // 2, store, 0)
            copies.append(pltpu.make_async_copy(stage_ref.at[j], target, piece_sem.at[j]))
            copies[-1].start()
        for copy in copies:
            copy.wait()


def summer(pairs, x_ref, half_in, acc_ref, slots_in, all_ref, sems):
    s0, r0, s1, r1, s2, r2, s3, r3 = sems
    wire = acc_ref.dtype
    me = lax.axis_index("phi")
    pair, core = me // 2, me % 2
    sibling = me + 1 - 2 * core
    others = [((pair + d) % pairs) * 2 + core for d in range(1, pairs)]
    half = x_ref.shape[0] // 2
    chunk = half // pairs

    def part(start, length):
        return pl.ds(pl.multiple_of(start, 16 if wire == BF16 else 8), length)

    swap = remote(x_ref.at[part((1 - core) * half, half)], half_in, s0.at[0], r0.at[0], sibling)
    scatter = [
        remote(
            acc_ref.at[part(((pair + d) % pairs) * chunk, chunk)],
            slots_in.at[d - 1],
            s1.at[d - 1],
            r1.at[d - 1],
            others[d - 1],
        )
        for d in range(1, pairs)
    ]
    mine = part(core * half + pair * chunk, chunk)
    gather = [
        remote(all_ref.at[mine], all_ref.at[mine], s2.at[d - 1], r2.at[d - 1], others[d - 1])
        for d in range(1, pairs)
    ]
    whole = part(core * half, half)
    last = remote(all_ref.at[whole], all_ref.at[whole], s3.at[0], r3.at[0], sibling)

    def scatter_stage():
        swap.wait()
        acc_ref[...] = (x_ref[part(core * half, half), :] + half_in[...]).astype(wire)
        for copy in scatter:
            copy.start()

    def gather_stage():
        total = x_ref[mine, :] + half_in[part(pair * chunk, chunk), :]
        for d in range(1, pairs):
            scatter[d - 1].wait_recv()
            total = total + slots_in[d - 1].astype(F32)
        all_ref[mine, :] = total.astype(wire)
        for copy in gather:
            copy.start()

    def last_stage():
        for copy in gather:
            copy.wait()
        for copy in scatter:
            copy.wait_send()
        last.start()

    return swap.start, scatter_stage, gather_stage, last_stage, last.wait


def back_kernel(
    pairs,
    index_ref,
    cross_hbm,
    sib_hbm,
    relay_hbm,
    direct_hbm,
    own_hbm,
    grad_hbm,
    hidden_hbm,
    before_hbm,
    agg_hbm,
    tiles_hbm,
    upstream1_hbm,
    act1_hbm,
    hidden1_hbm,
    before1_hbm,
    agg1_hbm,
    feats_ref,
    wcat_ref,
    w_self_ref,
    w_agg_ref,
    w_out_ref,
    loss_ref,
    early_ref,
    all_ref,
    wcat_t_ref,
    cross_in,
    sib_in,
    relay_in,
    total_in,
    relay_send,
    direct_send,
    relay_ref,
    direct_ref,
    own_ref,
    grad_ref,
    hidden_ref,
    before_ref,
    agg_ref,
    upstream1_ref,
    act1_ref,
    hidden1_ref,
    before1_ref,
    agg1_ref,
    tiles_ref,
    slope_ref,
    block_feats_ref,
    x_ref,
    half_in,
    acc_ref,
    slots_in,
    early_x,
    early_half,
    early_acc,
    early_slots,
    local_sem,
    *sems,
):
    ys, yr, zs, zr, cs, cr, ss, sr = sems[:8]
    direct, sibling, onward, source, to_direct = peers()
    me = lax.axis_index("phi")
    pair, core = me // 2, me % 2
    others = [((pair + d) % pairs) * 2 + core for d in range(1, pairs)]
    blocks, slots, rows, _ = tiles_ref.shape
    depth, width = wcat_ref.shape
    window = feats_ref.shape[1] // rows
    size = grad_ref.shape[0] // CHUNKS
    group = blocks // CHUNKS
    loads = [
        pltpu.make_async_copy(src, dst, local_sem.at[k])
        for k, (src, dst) in enumerate(
            (
                (relay_hbm, relay_ref),
                (direct_hbm, direct_ref),
                (own_hbm, own_ref),
                (grad_hbm, grad_ref),
                (hidden_hbm, hidden_ref),
                (before_hbm, before_ref),
                (agg_hbm, agg_ref),
                (tiles_hbm, tiles_ref),
                (upstream1_hbm, upstream1_ref),
                (act1_hbm, act1_ref),
                (hidden1_hbm, hidden1_ref),
                (before1_hbm, before1_ref),
                (agg1_hbm, agg1_ref),
            )
        )
    ]
    for copy in loads:
        copy.start()
    greet([sibling] + others)

    def span(i):
        return pl.ds(pl.multiple_of(i * size, size), size)

    def crosses(i):
        return remote(cross_hbm.at[span(i)], cross_in.at[span(i)], cs.at[i], cr.at[i], sibling)

    def first(i):
        return remote(relay_send.at[span(i)], relay_in.at[span(i)], zs.at[i], zr.at[i], source)

    def second(i):
        return remote(direct_send.at[span(i)], total_in.at[span(i)], ys.at[i], yr.at[i], direct)

    near = remote(sib_hbm, sib_in, ss.at[0], sr.at[0], sibling)
    lax.fori_loop(0, CHUNKS, lambda i, c: (crosses(i).start(), c)[1], 0)
    near.start()

    early = summer(pairs, early_x, early_half, early_acc, early_slots, early_ref, sems[8:16])
    final = summer(pairs, x_ref, half_in, acc_ref, slots_in, all_ref, sems[16:24])
    early_x[...] = jnp.zeros(early_x.shape, F32)
    early_x[3 * width : 3 * width + 8, :] = loss_ref[...]
    per = window // CHUNKS

    def slopes(i):
        for u in range(0, per, 2):
            at = pl.multiple_of((i * per + u) * rows, 2 * rows)
            feats = feats_ref[:, pl.ds(at, 2 * rows)]
            squashed = jnp.tanh(dot(wcat_t_ref[...], feats, 1, 0))
            slope = 1.0 - squashed * squashed
            for v in range(2):
                slope_ref[i * per + u + v] = slope[:, v * rows : (v + 1) * rows]
                block_feats_ref[i * per + u + v] = feats[:, v * rows : (v + 1) * rows]

    wcat_t_ref[...] = (
        jnp.concatenate([wcat_ref[...].astype(F32), jnp.zeros((width - depth, width), F32)], axis=0)
        .T[:, :depth]
        .astype(BF16)
    )
    x_ref[...] = jnp.zeros(x_ref.shape, F32)
    base = 3 * width
    slope_ref[window] = jnp.zeros(slope_ref.shape[1:], F32)
    block_feats_ref[window] = jnp.zeros(block_feats_ref.shape[1:], BF16)
    loads[0].wait()

    lag = 4

    def relay_step(i, carry):
        here = span(i)

        @pl.when(to_direct)
        def _():
            relay_send[here, :] = relay_ref[here, :]

        @pl.when(jnp.logical_not(to_direct))
        def _():
            crosses(i).wait_recv()
            relay_send[here, :] = (
                relay_ref[here, :].astype(F32) + cross_in[here, :].astype(F32)
            ).astype(BF16)

        first(i).start()

        @pl.when(i < CHUNKS - 2 * lag)
        def _():
            slopes(i)

        return carry

    lax.fori_loop(0, CHUNKS, relay_step, 0)
    for copy in loads[1:]:
        copy.wait()
    near.wait()

    def direct_step(i):
        here = span(i)
        first(i).wait_recv()
        value = direct_ref[here, :].astype(F32) + relay_in[here, :].astype(F32)

        @pl.when(to_direct)
        def _():
            crosses(i).wait_recv()
            direct_send[here, :] = (value + cross_in[here, :].astype(F32)).astype(BF16)

        @pl.when(jnp.logical_not(to_direct))
        def _():
            direct_send[here, :] = value.astype(BF16)

        second(i).start()

    def upper_step(i):
        here = pl.ds(pl.multiple_of(i * 2 * size, 2 * size), 2 * size)
        act_grad = act1_ref[here, :]
        early_x[0:width, :] += dot(hidden1_ref[here, :], upstream1_ref[here, :], 0, 0)
        early_x[width : 2 * width, :] += dot(before1_ref[here, :], act_grad, 0, 0)
        early_x[2 * width : 3 * width, :] += dot(agg1_ref[here, :], act_grad, 0, 0)
        grad_ref[here, :] = grad_ref[here, :] + dot(act_grad, w_self_ref[1], 1, 1)

    def layer_step(i):
        here = span(i)
        second(i).wait_recv()
        returned = own_ref[here, :] + (
            total_in[here, :].astype(F32) + sib_in[here, :].astype(F32)
        )
        gradient = grad_ref[here, :] + jnp.concatenate(
            [returned[g * width : (g + 1) * width].T for g in range(group)], axis=0
        )
        upstream = gradient.astype(BF16)
        hidden = hidden_ref[here, :]
        hidden_grad = dot(upstream, w_out_ref[0], 1, 1)
        act_grad = jnp.where(hidden.astype(F32) > 0, hidden_grad, 0.0).astype(BF16)
        agg_grad_t = dot(w_agg_ref[0], act_grad, 1, 1).astype(BF16)
        x_ref[0:width, :] += dot(hidden, upstream, 0, 0)
        x_ref[width : 2 * width, :] += dot(before_ref[here, :], act_grad, 0, 0)
        x_ref[2 * width : 3 * width, :] += dot(agg_ref[here, :], act_grad, 0, 0)
        own_grad = gradient + dot(act_grad, w_self_ref[0], 1, 1)
        feats = feats_ref[:, pl.ds(pl.multiple_of((window // 5) * rows + i * size, size), size)]
        squashed = jnp.tanh(dot(feats, wcat_ref[...], 0, 0))
        genc = dot(feats, (own_grad * (1.0 - squashed * squashed)).astype(BF16), 1, 0)
        for g in range(group):
            block = i * group + g
            tile = jnp.concatenate([tiles_ref[block, s] for s in range(slots)], axis=1)
            contrib = dot(agg_grad_t[:, g * rows : (g + 1) * rows], tile, 1, 0)
            places = [index_ref[block * slots + s] for s in range(slots)]
            slope = jnp.concatenate([slope_ref[at] for at in places], axis=1)
            source_feats = jnp.concatenate([block_feats_ref[at] for at in places], axis=1)
            genc = genc + dot(source_feats, (contrib * slope).astype(BF16), 1, 1)
        x_ref[base : base + depth, :] += genc

    turn = CHUNKS // 2

    def opening(i, carry):
        direct_step(i)
        upper_step(i)

        @pl.when(i < lag)
        def _():
            slopes(CHUNKS - 2 * lag + 2 * i)
            slopes(CHUNKS - 2 * lag + 2 * i + 1)

        @pl.when(i >= lag)
        def _():
            layer_step(i - lag)

        return carry

    def middle(i, carry):
        direct_step(i)
        layer_step(i - lag)
        return carry

    def closing(i, carry):
        layer_step(i)
        return carry

    lax.fori_loop(0, turn, opening, 0)
    early[0]()
    lax.fori_loop(turn, turn + 4, middle, 0)
    early[1]()
    lax.fori_loop(turn + 4, CHUNKS, middle, 0)
    early[2]()
    lax.fori_loop(CHUNKS - lag, CHUNKS, closing, 0)
    final[0]()
    early[3]()

    def drain(i, carry):
        crosses(i).wait_send()
        first(i).wait_send()
        second(i).wait_send()
        return carry

    lax.fori_loop(0, CHUNKS, drain, 0)

    for stage in final[1:]:
        stage()
    early[4]()


def finish_kernel(
    triplet_total,
    early_ref,
    sum_ref,
    loss_out,
    genc_out,
    gtable_out,
    gself_out,
    gagg_out,
    gout_out,
):
    width = gself_out.shape[1]
    for k, out in enumerate((gout_out, gself_out, gagg_out)):
        for layer, source in enumerate((sum_ref, early_ref)):
            out[layer] = source[k * width : (k + 1) * width, :].astype(F32)
    base = 3 * width
    genc_out[...] = sum_ref[base : base + 16, :].astype(F32)[: genc_out.shape[0]]
    gtable_out[...] = sum_ref[base + 16 : base + 16 + gtable_out.shape[0], :].astype(F32)
    loss_out[...] = early_ref[base : base + 1, 0:1] / triplet_total


def body(
    hit_feats,
    layer_ids,
    edge_tiles,
    src_blocks,
    live_slots,
    anchor_hits,
    positive_hits,
    negative_hits,
    w_enc,
    layer_table,
    w_self,
    w_agg,
    w_out,
):
    blocks, slots, rows, _ = edge_tiles.shape
    width = w_enc.shape[1]
    features = hit_feats.shape[0]
    kinds = layer_table.shape[0]
    hits = blocks * rows
    layer_total = w_self.shape[0]
    triplets = anchor_hits.shape[0]
    group = 8
    steps = blocks // group
    span = group * rows
    me = lax.axis_index("phi")
    is_even = me % 2 == 0
    even_pair = (me // 2) % 2 == 0

    def place(part):
        spots = (
            jnp.where(even_pair, 2, 0),
            jnp.where(is_even, 4, 3),
            1,
            jnp.where(is_even, 3, 4),
            jnp.where(even_pair, 0, 2),
        )
        return sum(jnp.where(part == k, spot, 0) for k, spot in enumerate(spots))

    live = jnp.arange(slots, dtype=jnp.int32)[None, :] < live_slots[:, None]
    index = jnp.where(
        live, place(src_blocks // blocks) * blocks + src_blocks % blocks, 5 * blocks
    ).reshape(blocks * slots)
    depth = 16 + kinds
    listed = 2 * triplets // 128 + 1
    list_shape = (-(-(listed + 1) // 8) * 8, 128)

    row_spec = pl.BlockSpec((span, width), lambda i, *_: (i, 0))
    weight_spec = full((width, width))
    any_spec = pl.BlockSpec(memory_space=pl.ANY)
    row_shape = jax.ShapeDtypeStruct((hits, width), BF16)
    weight_shape = jax.ShapeDtypeStruct((width, width), F32)

    wide_shape = jax.ShapeDtypeStruct((hits, width), F32)
    vmem = pl.BlockSpec(memory_space=pltpu.VMEM)
    smem = pl.BlockSpec(memory_space=pltpu.SMEM)
    few = pltpu.SemaphoreType.DMA((FEAT_CHUNKS,))
    each = pltpu.SemaphoreType.DMA((CHUNKS,))
    one = pltpu.SemaphoreType.DMA((1,))
    four = pltpu.SemaphoreType.DMA((4,))
    block_shape = jax.ShapeDtypeStruct((blocks, rows, width), BF16)
    before0, agg0, hidden0, latents1, agg1, hidden1, latents2, lists, feats, wcat = pl.pallas_call(
        functools.partial(forward_kernel, features),
        in_specs=[smem] + [vmem] * 4 + [any_spec] + [vmem] * 5,
        out_specs=[any_spec] * 10,
        out_shape=[block_shape, row_shape, row_shape, block_shape, row_shape, row_shape]
        + [
            wide_shape,
            jax.ShapeDtypeStruct((5,) + list_shape, jnp.int32),
            jax.ShapeDtypeStruct((depth, 5 * hits), BF16),
            jax.ShapeDtypeStruct((depth, width), BF16),
        ],
        scratch_shapes=[
            pltpu.VMEM((16, hits), BF16),
            pltpu.VMEM((depth, width), BF16),
            pltpu.VMEM(list_shape, jnp.int32),
            pltpu.VMEM((listed - 1, 128, 128), jnp.int32),
            pltpu.VMEM((listed - 1, 128, 128), jnp.int32),
            pltpu.VMEM((listed - 1, 128, 128), jnp.int32),
            pltpu.VMEM((5, 16, hits), BF16),
            pltpu.VMEM((depth, 5 * hits), BF16),
            pltpu.VMEM((5 * blocks + 1, rows, width), BF16),
            pltpu.VMEM((5 * blocks + 1, rows, width), BF16),
        ]
        + [pltpu.VMEM((hits, width), BF16)] * 4
        + [
            pltpu.VMEM((hits, width), F32),
            pltpu.VMEM(edge_tiles.shape, BF16),
            each,
            pltpu.SemaphoreType.DMA((6,)),
            pltpu.SemaphoreType.DMA((3 * LATER_STEPS,)),
            one,
        ]
        + [few] * 6
        + [four] * 2
        + [each] * 8
        + [one] * 2,
        compiler_params=pltpu.CompilerParams(
            collective_id=1, has_side_effects=True, vmem_limit_bytes=VMEM_BYTES
        ),
        name="forward",
    )(
        index,
        hit_feats,
        layer_ids.reshape(1, hits),
        positive_hits.reshape(triplets // 128, 128),
        negative_hits.reshape(triplets // 128, 128),
        edge_tiles,
        w_enc,
        layer_table,
        w_self,
        w_agg,
        w_out,
    )

    before0, latents1 = before0.reshape(hits, width), latents1.reshape(hits, width)
    lists = lists.reshape(-1)
    move_shape = jax.ShapeDtypeStruct((triplets, width), BF16)
    wide_move = jax.ShapeDtypeStruct((triplets, width), F32)
    move_spec = full((triplets, width))
    *found, anchors = pl.pallas_call(
        gather_kernel,
        grid_spec=pltpu.PrefetchScalarGridSpec(
            num_scalar_prefetch=2,
            grid=(1,),
            in_specs=[full((hits, width))],
            out_specs=[move_spec] * 6,
            scratch_shapes=[pltpu.VMEM((2 * triplets + 8, width), F32)],
        ),
        out_shape=[move_shape] * 6,
        compiler_params=params(),
        name="gather",
    )(lists, anchor_hits, latents2)
    coef_shape = (triplets // 128, 128)
    loss_part, ganchor, *moves, coef, coefs = pl.pallas_call(
        functools.partial(contrast_kernel, 1.0 / math.sqrt(width)),
        in_specs=[vmem] * 6,
        out_specs=[vmem] * 8,
        out_shape=[jax.ShapeDtypeStruct((8, width), F32), wide_move]
        + [move_shape] * 4
        + [jax.ShapeDtypeStruct(coef_shape, F32), jax.ShapeDtypeStruct((4,) + coef_shape, F32)],
        scratch_shapes=[pltpu.VMEM((triplets, width), F32)]
        + [pltpu.VMEM((triplets, width), BF16)] * 6
        + [pltpu.SemaphoreType.DMA((PARTS,))] * 16
        + [pltpu.SemaphoreType.DMA((4,))] * 2,
        compiler_params=pltpu.CompilerParams(
            collective_id=4, has_side_effects=True, vmem_limit_bytes=VMEM_BYTES
        ),
        name="contrast",
    )(*found, anchors)

    t_shape = jax.ShapeDtypeStruct((blocks, width, rows), F32)
    t_half = jax.ShapeDtypeStruct((blocks, width, rows), BF16)
    adj_shape = pltpu.VMEM((5 * blocks + 1, width, rows), F32)
    upstream1, act1, gradient2, obelow, own, oabove, osibling, ocross = pl.pallas_call(
        functools.partial(last_backward, group, steps),
        grid_spec=pltpu.PrefetchScalarGridSpec(
            num_scalar_prefetch=3,
            grid=(steps,),
            in_specs=[any_spec, move_spec, full(coef_shape), full((4,) + coef_shape)]
            + [move_spec] * 5
            + [row_spec]
            + [full((2, width, width))] * 2,
            out_specs=[row_spec] * 3 + [any_spec] * 5,
            scratch_shapes=[
                adj_shape,
                pltpu.VMEM((10 * triplets + 40, width), F32),
                pltpu.VMEM((4, blocks, width, rows), BF16),
                pltpu.VMEM(edge_tiles.shape, BF16),
                pltpu.SemaphoreType.DMA((steps,)),
                pltpu.SemaphoreType.DMA((5,)),
            ]
            + [pltpu.VMEM((hits, width), F32)] * 4,
        ),
        out_shape=[row_shape] * 2 + [wide_shape] + [t_half, t_shape] + [t_half] * 3,
        compiler_params=params(),
        name="last_backward",
    )(
        index, lists, anchor_hits, edge_tiles, ganchor, coef, coefs, anchors, *moves, hidden1, w_agg, w_out,
    )
    pairs = lax.axis_size("phi") // 2

    def sum_sizes(count, wire):
        chunk = -(-count // (32 * pairs)) * 16
        total = 2 * pairs * chunk
        return jax.ShapeDtypeStruct((total, width), wire), [
            pltpu.VMEM((total, width), F32),
            pltpu.VMEM((total // 2, width), F32),
            pltpu.VMEM((total // 2, width), wire),
            pltpu.VMEM((pairs - 1, chunk, width), wire),
        ]

    early_shape, early_scratch = sum_sizes(3 * width + 8, F32)
    final_shape, final_scratch = sum_sizes(3 * width + depth, F32)
    many = pltpu.SemaphoreType.DMA((pairs - 1,))
    flat = (hits, width)
    sums = pl.pallas_call(
        functools.partial(back_kernel, pairs),
        in_specs=[smem] + [any_spec] * 15 + [vmem] * 6,
        out_specs=[vmem] * 2,
        out_shape=[early_shape, final_shape],
        scratch_shapes=[pltpu.VMEM((width, depth), BF16)]
        + [pltpu.VMEM(flat, BF16)] * 8
        + [pltpu.VMEM(flat, F32)] * 2
        + [pltpu.VMEM(flat, BF16)] * 8
        + [
            pltpu.VMEM(edge_tiles.shape, BF16),
            pltpu.VMEM((5 * blocks + 1, width, rows), F32),
            pltpu.VMEM((5 * blocks + 1, depth, rows), BF16),
        ]
        + final_scratch
        + early_scratch
        + [pltpu.SemaphoreType.DMA((13,))]
        + [pltpu.SemaphoreType.DMA((CHUNKS,))] * 6
        + [one, one]
        + [one, one, many, many, many, many, one, one] * 2,
        compiler_params=pltpu.CompilerParams(
            collective_id=3, has_side_effects=True, vmem_limit_bytes=VMEM_BYTES
        ),
        name="back",
    )(
        index, ocross.reshape(flat), osibling.reshape(flat), oabove.reshape(flat),
        obelow.reshape(flat), own.reshape(flat), gradient2, hidden0, before0, agg0, edge_tiles,
        upstream1, act1, hidden1, latents1, agg1,
        feats, wcat, w_self, w_agg, w_out, loss_part,
    )
    stack = jax.ShapeDtypeStruct((2, width, width), F32)
    loss, genc, gtable, gself, gagg, gout = pl.pallas_call(
        functools.partial(finish_kernel, float(triplets * lax.axis_size("phi"))),
        in_specs=[vmem] * 2,
        out_specs=[vmem] * 6,
        out_shape=[
            jax.ShapeDtypeStruct((1, 1), F32),
            jax.ShapeDtypeStruct((features, width), F32),
            jax.ShapeDtypeStruct((kinds, width), F32),
            stack, stack, stack,
        ],
        name="finish",
    )(*sums)
    return (loss.reshape(1), genc, gtable, gself, gagg, gout)


def solution(mesh):
    both = ("event", "phi")
    in_specs = (
        P(None, both),
        P(both),
        P(both, None, None, None),
        P(both, None),
        P(both),
        P(both),
        P(both),
        P(both),
        P(),
        P(),
        P(),
        P(),
        P(),
    )
    out_specs = (
        P("event"),
        P("event", None),
        P("event", None),
        P("event", None, None),
        P("event", None, None),
        P("event", None, None),
    )
    return jax.shard_map(body, mesh=mesh, in_specs=in_specs, out_specs=out_specs, check_vma=False)
```

```python
import functools
import math

import jax
import jax.numpy as jnp
from jax import lax
from jax.experimental import pallas as pl
from jax.experimental.pallas import tpu as pltpu
from jax.sharding import PartitionSpec as P

loss_divisor = 64.0
F32 = jnp.float32
BF16 = jnp.bfloat16
VMEM_BYTES = 60 * 1024 * 1024


def dot(left, right, left_dim, right_dim):
    return lax.dot_general(
        left, right, (((left_dim,), (right_dim,)), ((), ())), preferred_element_type=F32
    )


def full(shape):
    return pl.BlockSpec(shape, lambda *_: (0,) * len(shape))


def params():
    return pltpu.CompilerParams(
        dimension_semantics=("arbitrary",), vmem_limit_bytes=VMEM_BYTES
    )


CHUNKS = 16
LATER_STEPS = 8


def peers():
    count = lax.axis_size("phi")
    me = lax.axis_index("phi")
    odd_pair = (me // 2) % 2
    odd_core = me % 2
    direct = me + 2 - 4 * odd_pair
    sibling = me + 1 - 2 * odd_core
    stride = 4 - 8 * odd_pair
    onward = (me + stride + count) % count
    source = (me - stride + count) % count
    return direct, sibling, onward, source, odd_pair == odd_core


def remote(src, dst, send, recv, target):
    return pltpu.make_async_remote_copy(
        src_ref=src,
        dst_ref=dst,
        send_sem=send,
        recv_sem=recv,
        device_id={"phi": target},
        device_id_type=pl.DeviceIdType.MESH,
    )


def announce(targets):
    barrier = pltpu.get_barrier_semaphore()
    for target in targets:
        pl.semaphore_signal(
            barrier, inc=1, device_id={"phi": target}, device_id_type=pl.DeviceIdType.MESH
        )


def greet(targets):
    announce(targets)
    pl.semaphore_wait(pltpu.get_barrier_semaphore(), len(targets))


def role_targets():
    count = lax.axis_size("phi")
    me = lax.axis_index("phi")
    odd_pair = (me // 2) % 2
    odd_core = me % 2
    sibling = me + 1 - 2 * odd_core
    across = (me - 1 + 2 * odd_core + count) % count
    direct = me + 2 - 4 * odd_pair
    far = (me - 2 + 4 * odd_pair + count) % count
    return sibling, across, direct, far


def aggregate_group(index_ref, tiles_ref, window_ref, step, group, slots, rows):
    results = []
    for g in range(group):
        tile = jnp.concatenate([tiles_ref[step * group + g, s] for s in range(slots)], axis=1)
        source = jnp.concatenate(
            [
                window_ref[index_ref[(step * group + g) * slots + s]] for s in range(slots)
            ],
            axis=0,
        )
        results.append(dot(tile, source, 1, 0).astype(BF16))
    return jnp.concatenate(results, axis=0)


def node_update(own, aggregated, w_self, w_agg, w_out):
    activation = dot(own, w_self, 1, 0) + dot(aggregated, w_agg, 1, 0)
    hidden = jnp.maximum(activation, 0.0).astype(BF16)
    updated = (own.astype(F32) + dot(hidden, w_out, 1, 0)).astype(BF16)
    return hidden, updated


FEAT_CHUNKS = 2


def forward_kernel(
    features,
    index_ref,
    hit_ref,
    id_ref,
    positive_ref,
    negative_ref,
    tiles_hbm,
    enc_ref,
    table_ref,
    w_self_ref,
    w_agg_ref,
    w_out_ref,
    before_out,
    agg0_out,
    hidden0_out,
    latents_out,
    agg1_out,
    hidden1_out,
    z_out,
    lists_out,
    feats_out,
    wcat_out,
    packed_ref,
    wcat_ref,
    keys_ref,
    key_cols,
    place_cols,
    entry_cols,
    packs_ref,
    feats_ref,
    window_ref,
    later_ref,
    agg0_ref,
    hidden0_ref,
    agg1_ref,
    hidden1_ref,
    z_ref,
    tiles_ref,
    tile_sem,
    out_sem,
    late_sem,
    list_sem,
    *sems,
):
    fys, fyr, fzs, fzr, fcs, fcr, ls, lr = sems[:8]
    ys, yr, zs, zr, cs, cr, ss, sr = sems[8:16]
    fss, fsr = sems[16:]
    direct, sibling, onward, source, direct_crosses = peers()
    roles = role_targets()
    blocks, slots, rows, _ = tiles_ref.shape
    hits = packed_ref.shape[1]
    group = blocks // CHUNKS
    span = group * rows

    def tile_load(i):
        part = pl.ds(i * group, group)
        return pltpu.make_async_copy(tiles_hbm.at[part], tiles_ref.at[part], tile_sem.at[i])

    lax.fori_loop(0, CHUNKS, lambda i, c: (tile_load(i).start(), c)[1], 0)
    beside = [t + 1 - 2 * lax.rem(t, 2) for t in (onward, source)]
    announce((direct, sibling, onward, source, beside[0], beside[1], roles[1], roles[3]))
    kinds, width = table_ref.shape
    filler = jnp.zeros((16 - features, width), F32)
    wcat_ref[...] = jnp.concatenate(
        [enc_ref[...].astype(F32), filler, table_ref[...].astype(F32)], axis=0
    ).astype(BF16)

    def gather_input(i, carry):
        at = pl.ds(pl.multiple_of(i * 512, 512), 512)
        packed_ref[:, at] = jnp.concatenate(
            [
                hit_ref[:, at].astype(F32),
                id_ref[:, at].astype(F32),
                jnp.zeros((15 - features, 512), F32),
            ],
            axis=0,
        ).astype(BF16)
        return carry

    lax.fori_loop(0, hits // 512, gather_input, 0)
    pl.semaphore_wait(pltpu.get_barrier_semaphore(), 8)
    columns = hits // FEAT_CHUNKS

    def pack(k, i):
        return packs_ref.at[k, :, pl.ds(i * columns, columns)]

    chunks = range(FEAT_CHUNKS)
    f_first = [
        remote(
            packed_ref.at[:, pl.ds(i * columns, columns)], pack(0, i), fys.at[i], fyr.at[i], direct
        )
        for i in chunks
    ]
    f_second = [remote(pack(0, i), pack(2, i), fzs.at[i], fzr.at[i], onward) for i in chunks]
    f_cross_a = [remote(pack(0, i), pack(4, i), fcs.at[i], fcr.at[i], sibling) for i in chunks]
    f_cross_b = [remote(pack(0, i), pack(4, i), fcs.at[i], fcr.at[i], beside[0]) for i in chunks]
    f_near = remote(packed_ref, packs_ref.at[3], fss.at[0], fsr.at[0], sibling)
    for copy in f_first:
        copy.start()
    f_near.start()

    def encode(k, ref):
        step = 512
        is_feature = lax.broadcasted_iota(jnp.int32, (16, step), 0) < features
        kind = lax.broadcasted_iota(jnp.int32, (16, step), 0).astype(F32)

        def run(i, carry):
            at = pl.multiple_of(i * step, step)
            data = ref[:, pl.ds(at, step)].astype(F32)
            onehot = jnp.where(kind == data[features : features + 1], 1.0, 0.0)
            feats = jnp.concatenate([jnp.where(is_feature, data, 0.0), onehot], axis=0).astype(BF16)
            feats_ref[:, pl.ds(pl.multiple_of(k * hits + i * step, step), step)] = feats
            encoded = dot(feats, wcat_ref[...], 0, 0)
            squashed = jnp.tanh(encoded).astype(BF16)
            for u in range(step // rows):
                window_ref[k * blocks + i * (step // rows) + u] = squashed[
                    u * rows : (u + 1) * rows
                ]
            return carry

        lax.fori_loop(0, hits // step, run, 0)

    encode(1, packed_ref)
    for i in chunks:
        f_first[i].wait_recv()
        f_second[i].start()

        @pl.when(direct_crosses)
        def _():
            f_cross_a[i].start()

        @pl.when(jnp.logical_not(direct_crosses))
        def _():
            f_cross_b[i].start()

    f_near.wait_recv()
    encode(3, packs_ref.at[3])
    encode(0, packs_ref.at[0])
    for i in chunks:
        f_second[i].wait_recv()
    encode(2, packs_ref.at[2])
    for i in chunks:
        f_cross_a[i].wait_recv()
    encode(4, packs_ref.at[4])
    window_ref[5 * blocks] = jnp.zeros((rows, width), BF16)
    later_ref[5 * blocks] = jnp.zeros((rows, width), BF16)

    def part(k, i):
        return pl.ds(k * blocks + i * group, group)

    def first(i):
        return remote(later_ref.at[part(1, i)], later_ref.at[part(0, i)], ys.at[i], yr.at[i], direct)

    def near(i):
        return remote(later_ref.at[part(1, i)], later_ref.at[part(3, i)], ss.at[i], sr.at[i], sibling)

    def second(i):
        return remote(later_ref.at[part(0, i)], later_ref.at[part(2, i)], zs.at[i], zr.at[i], onward)

    def cross_a(i):
        return remote(later_ref.at[part(0, i)], later_ref.at[part(4, i)], cs.at[i], cr.at[i], sibling)

    def cross_b(i):
        return remote(later_ref.at[part(2, i)], later_ref.at[part(4, i)], cs.at[i], cr.at[i], sibling)

    def cross_c(i):
        return remote(
            later_ref.at[part(0, i)], later_ref.at[part(4, i)], cs.at[i], cr.at[i], beside[0]
        )

    def relay(i):
        first(i).wait_recv()
        second(i).start()

        @pl.when(direct_crosses)
        def _():
            cross_a(i).start()

        if isinstance(i, int) and i == CHUNKS - 1:

            @pl.when(jnp.logical_not(direct_crosses))
            def _():
                cross_c(i).start()

    def land(i):
        second(i).wait_recv()

        if not (isinstance(i, int) and i == CHUNKS - 1):

            @pl.when(jnp.logical_not(direct_crosses))
            def _():
                cross_b(i).start()

    lead = 5
    relayed = (CHUNKS - lead + 1) // 2

    def layer0(i, carry):
        tile_load(i).wait()
        here = pl.ds(pl.multiple_of(i * span, span), span)
        aggregated = aggregate_group(index_ref, tiles_ref, window_ref, i, group, slots, rows)
        own = window_ref[part(1, i)].reshape(span, width)
        hidden, updated = node_update(own, aggregated, w_self_ref[0], w_agg_ref[0], w_out_ref[0])
        later_ref[part(1, i)] = updated.reshape(group, rows, width)
        first(i).start()
        near(i).start()
        agg0_ref[here, :] = aggregated
        hidden0_ref[here, :] = hidden

        @pl.when(jnp.logical_and(i >= lead, lax.rem(i, 2) == 1))
        def _():
            relay(lax.div(i - lead, 2))

        return carry

    lax.fori_loop(0, CHUNKS, layer0, 0)
    own = pl.ds(blocks, blocks)
    saves = [
        pltpu.make_async_copy(src, dst, out_sem.at[k])
        for k, (src, dst) in enumerate(
            (
                (window_ref.at[own], before_out),
                (agg0_ref, agg0_out),
                (hidden0_ref, hidden0_out),
                (later_ref.at[own], latents_out),
                (feats_ref, feats_out),
                (wcat_ref, wcat_out),
            )
        )
    ]
    for copy in saves:
        copy.start()

    wanted = jnp.concatenate([positive_ref[...], negative_ref[...]], axis=0)
    lines = wanted.shape[0]
    pairs_of = lines * 128
    line = lax.broadcasted_iota(jnp.int32, (lines, 128), 0)
    lane = lax.broadcasted_iota(jnp.int32, (lines, 128), 1)
    keys = wanted * pairs_of + (line * 128 + lane)
    tall = jnp.concatenate(
        [wanted.astype(F32), jnp.zeros((128 - lines, 128), F32)], axis=0
    ).T.astype(jnp.int32)
    down = lax.broadcasted_iota(jnp.int32, (128, 1), 0)
    counts = []
    for k in range(5):
        mine = jnp.logical_and(wanted >= k * hits, wanted < (k + 1) * hits)
        counted = jnp.sum(jnp.where(mine, 1.0, 0.0), axis=1, keepdims=True)
        counts.append(jnp.sum(counted, axis=0, keepdims=True).astype(jnp.int32))
    aligned, shift = [jnp.zeros((1, 1), jnp.int32)], [jnp.zeros((1, 1), jnp.int32)]
    for k in range(5):
        filled = lax.bitwise_and(counts[k] + 7, -8)
        aligned.append(aligned[k] + filled)
        shift.append(shift[k] + filled - counts[k])
    for c in range(lines):
        column = tall[:, c : c + 1]
        slot = down + c * 128
        moved = jnp.zeros((128, 1), jnp.int32)
        first_row = jnp.zeros((128, 1), jnp.int32)
        for k in range(5):
            mine = jnp.logical_and(column >= k * hits, column < (k + 1) * hits)
            moved = moved + jnp.where(mine, shift[k], 0)
            first_row = first_row + jnp.where(mine, k * hits, 0)
        entry = (column - first_row) * (1 << ENTRY_BITS) + slot - pairs_of
        key_cols[c] = jnp.broadcast_to(column * pairs_of + slot, (128, 128))
        place_cols[c] = jnp.broadcast_to(moved, (128, 128))
        entry_cols[c] = jnp.broadcast_to(entry, (128, 128))

    def rank(c, carry):
        column = key_cols[c]
        count = jnp.zeros((128, 128), F32)
        for r in range(lines):
            count = count + jnp.where(keys[r : r + 1] < column, 1.0, 0.0)
        total = jnp.sum(count, axis=1, keepdims=True).astype(jnp.int32)
        place_cols[c] = place_cols[c] + jnp.broadcast_to(total, (128, 128))
        return carry

    keys_ref[...] = jnp.zeros(keys_ref.shape, jnp.int32)

    def put(q, carry):
        target = lax.broadcasted_iota(jnp.int32, (128, 128), 1) + q * 128

        def match(c, total):
            return total + jnp.where(place_cols[c] == target, entry_cols[c], 0)

        total = lax.fori_loop(0, lines, match, jnp.zeros((128, 128), jnp.int32))
        found = jnp.sum(total.astype(F32), axis=0, keepdims=True).astype(jnp.int32)
        keys_ref[pl.ds(q, 1), :] = found + pairs_of
        return carry

    turns = 3
    for k in range(turns):
        relay(relayed + k)
        land(k)
        lax.fori_loop(lines * k // turns, lines * (k + 1) // turns, rank, 0)
    put_turns = CHUNKS - relayed - turns - 2
    for k in range(put_turns):
        relay(relayed + turns + k)
        land(turns + k)
        lax.fori_loop(
            (lines + 1) * k // put_turns, (lines + 1) * (k + 1) // put_turns, put, 0
        )
    lane = lax.broadcasted_iota(jnp.int32, (1, 128), 1)
    keys_ref[pl.ds(lines + 1, 1), :] = sum(
        jnp.where(lane == k, aligned[k] // 8, 0) for k in range(6)
    )
    lists = [
        remote(keys_ref, lists_out.at[j + 1], ls.at[j], lr.at[j], target)
        for j, target in enumerate(roles)
    ]
    for copy in lists:
        copy.start()
    own_list = pltpu.make_async_copy(keys_ref, lists_out.at[0], list_sem.at[0])
    own_list.start()

    for k in range(CHUNKS - 2, CHUNKS):
        relay(k)
    for k in range(turns + put_turns, CHUNKS):
        land(k)

    def settle(i, carry):
        near(i).wait()
        cross_a(i).wait_recv()
        return carry

    lax.fori_loop(0, CHUNKS, settle, 0)

    later_group = blocks // LATER_STEPS
    later_span = later_group * rows

    def late_saves(i):
        here = pl.ds(pl.multiple_of(i * later_span, later_span), later_span)
        return [
            pltpu.make_async_copy(src.at[here], dst.at[here], late_sem.at[k * LATER_STEPS + i])
            for k, (src, dst) in enumerate(
                ((agg1_ref, agg1_out), (hidden1_ref, hidden1_out), (z_ref, z_out))
            )
        ]

    def layer1(i, carry):
        here = pl.ds(pl.multiple_of(i * later_span, later_span), later_span)
        aggregated = aggregate_group(index_ref, tiles_ref, later_ref, i, later_group, slots, rows)
        own = later_ref[pl.ds(blocks + i * later_group, later_group)].reshape(later_span, width)
        hidden, updated = node_update(own, aggregated, w_self_ref[1], w_agg_ref[1], w_out_ref[1])
        agg1_ref[here, :] = aggregated
        hidden1_ref[here, :] = hidden
        z_ref[here, :] = updated.astype(F32)
        for copy in late_saves(i):
            copy.start()
        return carry

    lax.fori_loop(0, LATER_STEPS, layer1, 0)

    def drain(i, carry):
        first(i).wait_send()
        second(i).wait_send()
        cross_a(i).wait_send()
        return carry

    lax.fori_loop(0, CHUNKS, drain, 0)

    def saved(i, carry):
        for copy in late_saves(i):
            copy.wait()
        return carry

    lax.fori_loop(0, LATER_STEPS, saved, 0)
    for i in chunks:
        f_first[i].wait_send()
        f_second[i].wait_send()
        f_cross_a[i].wait_send()
    f_near.wait_send()
    own_list.wait()
    for copy in lists:
        copy.wait()
    for copy in saves:
        copy.wait()


def segments(list_ref, stride, listed):
    me = lax.axis_index("phi")
    odd_core, odd_pair = lax.rem(me, 2), lax.rem(lax.div(me, 2), 2)
    places = (2, 1 + 2 * odd_core, 3 - 2 * odd_core, 4 * odd_pair, 4 - 4 * odd_pair)
    starts = [j * stride + listed + k for j, k in enumerate(places)]
    return [(list_ref[at], list_ref[at + 1]) for at in starts]


def gather_kernel(list_ref, anchor_ref, z_ref, *refs):
    outs, (anchor_out, buf_ref) = refs[:5], refs[5:]
    triplets, width = anchor_out.shape
    stride = list_ref.shape[0] // 5
    bounds = segments(list_ref, stride, 2 * triplets + 128)

    def anchors(i, carry):
        at = pl.multiple_of(i * 16, 16)
        anchor_out[pl.ds(at, 16), :] = jnp.concatenate(
            [z_ref[pl.ds(anchor_ref[i * 16 + u], 1), :] for u in range(16)], axis=0
        ).astype(BF16)
        return carry

    lax.fori_loop(0, triplets // 16, anchors, 0)
    zeros = jnp.zeros((64, width), F32)

    def clear(i, carry):
        for u in range(4):
            buf_ref[pl.ds(pl.multiple_of(i * 256 + u * 64, 64), 64), :] = zeros
        return carry

    lax.fori_loop(0, 2 * triplets // 256, clear, 0)
    for j in range(5):

        def fetch(i, carry, j=j):
            for u in range(8):
                entry = list_ref[j * stride + i * 8 + u]
                row = z_ref[pl.ds(lax.shift_right_logical(entry, ENTRY_BITS), 1), :]
                buf_ref[pl.ds(lax.bitwise_and(entry, ENTRY_MASK), 1), :] = row
            return carry

        lax.fori_loop(bounds[j][0], bounds[j][1], fetch, 0)

        def subtract(i, carry, j=j):
            for u in range(8):
                at = pl.multiple_of(i * 256 + u * 32, 32)
                value = buf_ref[pl.ds(triplets + at, 32), :] - buf_ref[pl.ds(at, 32), :]
                outs[j][pl.ds(at, 32), :] = value.astype(BF16)
                if j < 4:
                    buf_ref[pl.ds(triplets + at, 32), :] = zeros[:32]
                    buf_ref[pl.ds(at, 32), :] = zeros[:32]
            return carry

        lax.fori_loop(0, triplets // 256, subtract, 0)


ENTRY_BITS = 12
ENTRY_MASK = (1 << ENTRY_BITS) - 1
PARTS = 8


def contrast_kernel(
    inv_root,
    self_ref,
    sib_ref,
    cross_ref,
    near_ref,
    far_ref,
    anchor_ref,
    loss_ref,
    ganchor_ref,
    asib_ref,
    across_ref,
    adirect_ref,
    afar_ref,
    coef_out,
    coefs_out,
    change_ref,
    sib_in,
    cross_in,
    far_send,
    far_in,
    near_send,
    near_in,
    *sems,
):
    s = [sems[2 * i : 2 * i + 2] for i in range(9)]
    direct, sibling, onward, source, near_adds = peers()
    roles = role_targets()
    size = anchor_ref.shape[0] // PARTS
    beside = [t + 1 - 2 * lax.rem(t, 2) for t in (onward, source)]
    greet((direct, sibling, onward, source, beside[0], beside[1], roles[1], roles[3]))

    def rows(i):
        return pl.ds(i * size, size)

    def copies(k, src, dst, target):
        return [
            remote(src.at[rows(i)], dst.at[rows(i)], s[k][0].at[i], s[k][1].at[i], target)
            for i in range(PARTS)
        ]

    crosses = copies(0, cross_ref, cross_in, sibling)
    sibs = copies(1, sib_ref, sib_in, sibling)
    hops = copies(2, far_send, far_in, source)
    nears = copies(3, near_send, near_in, direct)
    to_direct = copies(4, anchor_ref, adirect_ref, direct)
    to_sibling = copies(5, anchor_ref, asib_ref, sibling)
    relays = copies(6, adirect_ref, afar_ref, onward)
    cross_a = copies(7, adirect_ref, across_ref, sibling)
    cross_b = copies(7, afar_ref, across_ref, sibling)
    cross_b[-1] = copies(7, adirect_ref, across_ref, beside[0])[-1]
    coefs = [
        remote(coef_out, coefs_out.at[j], s[8][0].at[j], s[8][1].at[j], target)
        for j, target in enumerate(roles)
    ]
    for copy in crosses:
        copy.start()
    for copy in sibs:
        copy.start()
    for i in range(PARTS):
        @pl.when(near_adds)
        def _():
            far_send[rows(i), :] = far_ref[rows(i), :]

        @pl.when(jnp.logical_not(near_adds))
        def _():
            crosses[i].wait_recv()
            far_send[rows(i), :] = (
                far_ref[rows(i), :].astype(F32) + cross_in[rows(i), :].astype(F32)
            ).astype(BF16)

        hops[i].start()
        if i < PARTS // 2:
            to_direct[i].start()
    def relay(i):
        to_sibling[i].start()
        to_direct[i].wait_recv()
        relays[i].start()

        @pl.when(near_adds)
        def _():
            cross_a[i].start()

        if i == PARTS - 1:

            @pl.when(jnp.logical_not(near_adds))
            def _():
                cross_b[i].start()

    for i in range(PARTS):
        hops[i].wait_recv()
        value = near_ref[rows(i), :].astype(F32) + far_in[rows(i), :].astype(F32)

        @pl.when(near_adds)
        def _():
            crosses[i].wait_recv()
            near_send[rows(i), :] = (value + cross_in[rows(i), :].astype(F32)).astype(BF16)

        @pl.when(jnp.logical_not(near_adds))
        def _():
            near_send[rows(i), :] = value.astype(BF16)

        nears[i].start()
        if i >= PARTS // 2:
            relay(i - PARTS // 2)
    for i in range(PARTS // 2, PARTS):
        to_direct[i].start()
    gaps = []
    for i in range(PARTS):
        sibs[i].wait_recv()
        nears[i].wait_recv()
        change = (
            near_in[rows(i), :].astype(F32)
            + self_ref[rows(i), :].astype(F32)
            + sib_in[rows(i), :].astype(F32)
        )
        change_ref[rows(i), :] = change
        product = anchor_ref[rows(i), :].astype(F32) * change
        for u in range(size // 128):
            gaps.append(
                jnp.sum(product[u * 128 : (u + 1) * 128].T, axis=0, keepdims=True) * inv_root
            )
    gap = jnp.concatenate(gaps, axis=0)
    coef_out[...] = jax.nn.sigmoid(gap) * (inv_root / loss_divisor)
    for copy in coefs:
        copy.start()
    soft = jnp.maximum(gap, 0.0) + jnp.log1p(jnp.exp(-jnp.abs(gap)))
    loss_ref[...] = jnp.broadcast_to(jnp.sum(soft, keepdims=True), loss_ref.shape)
    for i in range(PARTS // 2, PARTS):
        relay(i)
    for i in range(PARTS):
        relays[i].wait_recv()

        if i < PARTS - 1:

            @pl.when(jnp.logical_not(near_adds))
            def _():
                cross_b[i].start()

    size = 128
    eye = lax.broadcasted_iota(jnp.int32, (size, size), 0) == lax.broadcasted_iota(
        jnp.int32, (size, size), 1
    )
    for i in range(coef_out.shape[0]):
        coef = coef_out[pl.ds(i, 1), :]
        column = jnp.sum(jnp.where(eye, coef, 0.0), axis=1, keepdims=True)
        here = pl.ds(i * size, size)
        ganchor_ref[here, :] = column * change_ref[here, :]
    for copy in coefs:
        copy.wait()
    for i in range(PARTS):
        crosses[i].wait_send()
        sibs[i].wait_send()
        hops[i].wait_send()
        nears[i].wait_send()
        to_direct[i].wait_send()
        to_sibling[i].wait()
        relays[i].wait_send()
        cross_a[i].wait()


def spread_group(index_ref, tiles_ref, adj_ref, agg_grad_t, step, group, slots, rows):
    for g in range(group):
        block = step * group + g
        tile = jnp.concatenate([tiles_ref[block, s] for s in range(slots)], axis=1)
        contrib = dot(agg_grad_t[:, g * rows : (g + 1) * rows], tile, 1, 0)
        for s in range(slots):
            at = index_ref[(step * group + g) * slots + s]
            adj_ref[at] = adj_ref[at] + contrib[:, s * rows : (s + 1) * rows]


def clear_blocks(adj_ref):
    def clear(i, carry):
        adj_ref[i] = jnp.zeros(adj_ref.shape[1:], F32)
        return carry

    lax.fori_loop(0, adj_ref.shape[0], clear, 0)


def scatter_rows(
    list_ref, anchor_ref, ganchor_ref, coef_ref, coefs_ref, rows_in, moved_ref, sums
):
    triplets, width = ganchor_ref.shape
    hits = sums[0].shape[0]
    stride = list_ref.shape[0] // 5
    span = 2 * triplets + 8
    bounds = segments(list_ref, stride, 2 * triplets + 128)
    zeros = jnp.zeros((64, width), F32)

    def clear(i, carry):
        for target in sums:
            target[pl.ds(pl.multiple_of(i * 64, 64), 64), :] = zeros
        return carry

    lax.fori_loop(0, hits // 64, clear, 0)
    eye = lax.broadcasted_iota(jnp.int32, (128, 128), 0) == lax.broadcasted_iota(
        jnp.int32, (128, 128), 1
    )
    for j, source in enumerate(rows_in):
        for i in range(triplets // 128):
            coef = coef_ref[pl.ds(i, 1), :] if j == 0 else coefs_ref[j - 1, pl.ds(i, 1), :]
            spread = jnp.where(eye, coef, 0.0)
            high = spread.astype(BF16)
            low = (spread - high.astype(F32)).astype(BF16)
            part = source[pl.ds(i * 128, 128), :]
            value = dot(high, part, 1, 0) + dot(low, part, 1, 0)
            moved_ref[pl.ds(j * span + i * 128, 128), :] = -value
            moved_ref[pl.ds(j * span + triplets + i * 128, 128), :] = value
        moved_ref[pl.ds(j * span + 2 * triplets, 8), :] = zeros[:8]

    def anchors(i, carry):
        for u in range(8):
            t = i * 8 + u
            here = pl.ds(anchor_ref[t], 1)
            target = sums[u % 4]
            target[here, :] = target[here, :] + ganchor_ref[pl.ds(t, 1), :]
        return carry

    lax.fori_loop(0, triplets // 8, anchors, 0)
    for j in range(5):

        def add(i, carry, j=j):
            for u in range(8):
                entry = list_ref[j * stride + i * 8 + u]
                here = pl.ds(lax.shift_right_logical(entry, ENTRY_BITS), 1)
                target = sums[u % 4]
                moved = moved_ref[pl.ds(j * span + lax.bitwise_and(entry, ENTRY_MASK), 1), :]
                target[here, :] = target[here, :] + moved
            return carry

        lax.fori_loop(bounds[j][0], bounds[j][1], add, 0)


def last_backward(
    group,
    steps,
    index_ref,
    list_ref,
    anchor_ref,
    tiles_hbm,
    ganchor_ref,
    coef_ref,
    coefs_ref,
    aself_ref,
    asib_ref,
    across_ref,
    adirect_ref,
    afar_ref,
    hidden_ref,
    w_agg_ref,
    w_out_ref,
    upstream_ref,
    act_ref,
    gradient_ref,
    obelow_ref,
    oown_ref,
    oabove_ref,
    osibling_ref,
    ocross_ref,
    adj_ref,
    moved_ref,
    stage_ref,
    tiles_ref,
    tile_sem,
    piece_sem,
    *sums,
):
    step = pl.program_id(0)
    slots, rows = tiles_ref.shape[1], tiles_ref.shape[2]
    span = group * rows

    def tile_load(i):
        part = pl.ds(i * group, group)
        return pltpu.make_async_copy(tiles_hbm.at[part], tiles_ref.at[part], tile_sem.at[i])

    @pl.when(step == 0)
    def _():
        for i in range(steps):
            tile_load(i).start()
        clear_blocks(adj_ref)
        scatter_rows(
            list_ref, anchor_ref, ganchor_ref, coef_ref, coefs_ref,
            (aself_ref, asib_ref, across_ref, adirect_ref, afar_ref), moved_ref, sums,
        )

    here = pl.ds(pl.multiple_of(step * span, span), span)
    gradient = (sums[0][here, :] + sums[1][here, :]) + (sums[2][here, :] + sums[3][here, :])
    upstream = gradient.astype(BF16)
    hidden_grad = dot(upstream, w_out_ref[1], 1, 1)
    act_grad = jnp.where(hidden_ref[...].astype(F32) > 0, hidden_grad, 0.0).astype(BF16)
    upstream_ref[...] = upstream
    act_ref[...] = act_grad
    gradient_ref[...] = gradient
    tile_load(step).wait()
    agg_grad_t = dot(w_agg_ref[1], act_grad, 1, 1).astype(BF16)
    spread_group(index_ref, tiles_ref, adj_ref, agg_grad_t, step, group, slots, rows)

    @pl.when(step == steps - 1)
    def _():
        blocks = oown_ref.shape[0]
        copies = [
            pltpu.make_async_copy(
                adj_ref.at[pl.ds(blocks, blocks)], oown_ref, piece_sem.at[4]
            )
        ]
        copies[0].start()
        for j, (k, target) in enumerate(
            ((4, ocross_ref), (3, osibling_ref), (2, oabove_ref), (0, obelow_ref))
        ):

            def store(i, carry, k=k, j=j):
                for u in range(2):
                    stage_ref[j, 2 * i + u] = adj_ref[k * blocks + 2 * i + u].astype(BF16)
                return carry

            lax.fori_loop(0, blocks // 2, store, 0)
            copies.append(pltpu.make_async_copy(stage_ref.at[j], target, piece_sem.at[j]))
            copies[-1].start()
        for copy in copies:
            copy.wait()


def summer(pairs, x_ref, half_in, acc_ref, slots_in, all_ref, sems):
    s0, r0, s1, r1, s2, r2, s3, r3 = sems
    wire = acc_ref.dtype
    me = lax.axis_index("phi")
    pair, core = me // 2, me % 2
    sibling = me + 1 - 2 * core
    others = [((pair + d) % pairs) * 2 + core for d in range(1, pairs)]
    half = x_ref.shape[0] // 2
    chunk = half // pairs

    def part(start, length):
        return pl.ds(pl.multiple_of(start, 16 if wire == BF16 else 8), length)

    swap = remote(x_ref.at[part((1 - core) * half, half)], half_in, s0.at[0], r0.at[0], sibling)
    scatter = [
        remote(
            acc_ref.at[part(((pair + d) % pairs) * chunk, chunk)],
            slots_in.at[d - 1],
            s1.at[d - 1],
            r1.at[d - 1],
            others[d - 1],
        )
        for d in range(1, pairs)
    ]
    mine = part(core * half + pair * chunk, chunk)
    gather = [
        remote(all_ref.at[mine], all_ref.at[mine], s2.at[d - 1], r2.at[d - 1], others[d - 1])
        for d in range(1, pairs)
    ]
    whole = part(core * half, half)
    last = remote(all_ref.at[whole], all_ref.at[whole], s3.at[0], r3.at[0], sibling)

    def scatter_stage():
        swap.wait()
        acc_ref[...] = (x_ref[part(core * half, half), :] + half_in[...]).astype(wire)
        for copy in scatter:
            copy.start()

    def gather_stage():
        total = x_ref[mine, :] + half_in[part(pair * chunk, chunk), :]
        for d in range(1, pairs):
            scatter[d - 1].wait_recv()
            total = total + slots_in[d - 1].astype(F32)
        all_ref[mine, :] = total.astype(wire)
        for copy in gather:
            copy.start()

    def last_stage():
        for copy in gather:
            copy.wait()
        for copy in scatter:
            copy.wait_send()
        last.start()

    return swap.start, scatter_stage, gather_stage, last_stage, last.wait


def back_kernel(
    pairs,
    index_ref,
    cross_hbm,
    sib_hbm,
    relay_hbm,
    direct_hbm,
    own_hbm,
    grad_hbm,
    hidden_hbm,
    before_hbm,
    agg_hbm,
    tiles_hbm,
    upstream1_hbm,
    act1_hbm,
    hidden1_hbm,
    before1_hbm,
    agg1_hbm,
    feats_ref,
    wcat_ref,
    w_self_ref,
    w_agg_ref,
    w_out_ref,
    loss_ref,
    early_ref,
    all_ref,
    wcat_t_ref,
    cross_in,
    sib_in,
    relay_in,
    total_in,
    relay_send,
    direct_send,
    relay_ref,
    direct_ref,
    own_ref,
    grad_ref,
    hidden_ref,
    before_ref,
    agg_ref,
    upstream1_ref,
    act1_ref,
    hidden1_ref,
    before1_ref,
    agg1_ref,
    tiles_ref,
    slope_ref,
    block_feats_ref,
    x_ref,
    half_in,
    acc_ref,
    slots_in,
    early_x,
    early_half,
    early_acc,
    early_slots,
    local_sem,
    *sems,
):
    ys, yr, zs, zr, cs, cr, ss, sr = sems[:8]
    direct, sibling, onward, source, to_direct = peers()
    me = lax.axis_index("phi")
    pair, core = me // 2, me % 2
    others = [((pair + d) % pairs) * 2 + core for d in range(1, pairs)]
    blocks, slots, rows, _ = tiles_ref.shape
    depth, width = wcat_ref.shape
    window = feats_ref.shape[1] // rows
    size = grad_ref.shape[0] // CHUNKS
    group = blocks // CHUNKS
    loads = [
        pltpu.make_async_copy(src, dst, local_sem.at[k])
        for k, (src, dst) in enumerate(
            (
                (relay_hbm, relay_ref),
                (direct_hbm, direct_ref),
                (own_hbm, own_ref),
                (grad_hbm, grad_ref),
                (hidden_hbm, hidden_ref),
                (before_hbm, before_ref),
                (agg_hbm, agg_ref),
                (tiles_hbm, tiles_ref),
                (upstream1_hbm, upstream1_ref),
                (act1_hbm, act1_ref),
                (hidden1_hbm, hidden1_ref),
                (before1_hbm, before1_ref),
                (agg1_hbm, agg1_ref),
            )
        )
    ]
    for copy in loads:
        copy.start()
    greet([sibling] + others)

    def span(i):
        return pl.ds(pl.multiple_of(i * size, size), size)

    def crosses(i):
        return remote(cross_hbm.at[span(i)], cross_in.at[span(i)], cs.at[i], cr.at[i], sibling)

    def first(i):
        return remote(relay_send.at[span(i)], relay_in.at[span(i)], zs.at[i], zr.at[i], source)

    def second(i):
        return remote(direct_send.at[span(i)], total_in.at[span(i)], ys.at[i], yr.at[i], direct)

    near = remote(sib_hbm, sib_in, ss.at[0], sr.at[0], sibling)
    lax.fori_loop(0, CHUNKS, lambda i, c: (crosses(i).start(), c)[1], 0)
    near.start()

    early = summer(pairs, early_x, early_half, early_acc, early_slots, early_ref, sems[8:16])
    final = summer(pairs, x_ref, half_in, acc_ref, slots_in, all_ref, sems[16:24])
    early_x[...] = jnp.zeros(early_x.shape, F32)
    early_x[3 * width : 3 * width + 8, :] = loss_ref[...]
    per = window // CHUNKS

    def slopes(i):
        for u in range(0, per, 2):
            at = pl.multiple_of((i * per + u) * rows, 2 * rows)
            feats = feats_ref[:, pl.ds(at, 2 * rows)]
            squashed = jnp.tanh(dot(wcat_t_ref[...], feats, 1, 0))
            slope = 1.0 - squashed * squashed
            for v in range(2):
                slope_ref[i * per + u + v] = slope[:, v * rows : (v + 1) * rows]
                block_feats_ref[i * per + u + v] = feats[:, v * rows : (v + 1) * rows]

    wcat_t_ref[...] = (
        jnp.concatenate([wcat_ref[...].astype(F32), jnp.zeros((width - depth, width), F32)], axis=0)
        .T[:, :depth]
        .astype(BF16)
    )
    x_ref[...] = jnp.zeros(x_ref.shape, F32)
    base = 3 * width
    slope_ref[window] = jnp.zeros(slope_ref.shape[1:], F32)
    block_feats_ref[window] = jnp.zeros(block_feats_ref.shape[1:], BF16)
    loads[0].wait()

    lag = 4

    def relay_step(i, carry):
        here = span(i)

        @pl.when(to_direct)
        def _():
            relay_send[here, :] = relay_ref[here, :]

        @pl.when(jnp.logical_not(to_direct))
        def _():
            crosses(i).wait_recv()
            relay_send[here, :] = (
                relay_ref[here, :].astype(F32) + cross_in[here, :].astype(F32)
            ).astype(BF16)

        first(i).start()

        @pl.when(i < CHUNKS - 2 * lag)
        def _():
            slopes(i)

        return carry

    lax.fori_loop(0, CHUNKS, relay_step, 0)
    for copy in loads[1:]:
        copy.wait()
    near.wait()

    def direct_step(i):
        here = span(i)
        first(i).wait_recv()
        value = direct_ref[here, :].astype(F32) + relay_in[here, :].astype(F32)

        @pl.when(to_direct)
        def _():
            crosses(i).wait_recv()
            direct_send[here, :] = (value + cross_in[here, :].astype(F32)).astype(BF16)

        @pl.when(jnp.logical_not(to_direct))
        def _():
            direct_send[here, :] = value.astype(BF16)

        second(i).start()

    def upper_step(i):
        here = pl.ds(pl.multiple_of(i * 2 * size, 2 * size), 2 * size)
        act_grad = act1_ref[here, :]
        early_x[0:width, :] += dot(hidden1_ref[here, :], upstream1_ref[here, :], 0, 0)
        early_x[width : 2 * width, :] += dot(before1_ref[here, :], act_grad, 0, 0)
        early_x[2 * width : 3 * width, :] += dot(agg1_ref[here, :], act_grad, 0, 0)
        grad_ref[here, :] = grad_ref[here, :] + dot(act_grad, w_self_ref[1], 1, 1)

    def layer_step(i):
        here = span(i)
        second(i).wait_recv()
        returned = own_ref[here, :] + (
            total_in[here, :].astype(F32) + sib_in[here, :].astype(F32)
        )
        gradient = grad_ref[here, :] + jnp.concatenate(
            [returned[g * width : (g + 1) * width].T for g in range(group)], axis=0
        )
        upstream = gradient.astype(BF16)
        hidden = hidden_ref[here, :]
        hidden_grad = dot(upstream, w_out_ref[0], 1, 1)
        act_grad = jnp.where(hidden.astype(F32) > 0, hidden_grad, 0.0).astype(BF16)
        agg_grad_t = dot(w_agg_ref[0], act_grad, 1, 1).astype(BF16)
        x_ref[0:width, :] += dot(hidden, upstream, 0, 0)
        x_ref[width : 2 * width, :] += dot(before_ref[here, :], act_grad, 0, 0)
        x_ref[2 * width : 3 * width, :] += dot(agg_ref[here, :], act_grad, 0, 0)
        own_grad = gradient + dot(act_grad, w_self_ref[0], 1, 1)
        feats = feats_ref[:, pl.ds(pl.multiple_of((window // 5) * rows + i * size, size), size)]
        squashed = jnp.tanh(dot(feats, wcat_ref[...], 0, 0))
        genc = dot(feats, (own_grad * (1.0 - squashed * squashed)).astype(BF16), 1, 0)
        for g in range(group):
            block = i * group + g
            tile = jnp.concatenate([tiles_ref[block, s] for s in range(slots)], axis=1)
            contrib = dot(agg_grad_t[:, g * rows : (g + 1) * rows], tile, 1, 0)
            places = [index_ref[block * slots + s] for s in range(slots)]
            slope = jnp.concatenate([slope_ref[at] for at in places], axis=1)
            source_feats = jnp.concatenate([block_feats_ref[at] for at in places], axis=1)
            genc = genc + dot(source_feats, (contrib * slope).astype(BF16), 1, 1)
        x_ref[base : base + depth, :] += genc

    turn = CHUNKS // 2

    def opening(i, carry):
        direct_step(i)
        upper_step(i)

        @pl.when(i < lag)
        def _():
            slopes(CHUNKS - 2 * lag + 2 * i)
            slopes(CHUNKS - 2 * lag + 2 * i + 1)

        @pl.when(i >= lag)
        def _():
            layer_step(i - lag)

        return carry

    def middle(i, carry):
        direct_step(i)
        layer_step(i - lag)
        return carry

    def closing(i, carry):
        layer_step(i)
        return carry

    lax.fori_loop(0, turn, opening, 0)
    early[0]()
    lax.fori_loop(turn, turn + 4, middle, 0)
    early[1]()
    lax.fori_loop(turn + 4, CHUNKS, middle, 0)
    early[2]()
    lax.fori_loop(CHUNKS - lag, CHUNKS, closing, 0)
    final[0]()
    early[3]()

    def drain(i, carry):
        crosses(i).wait_send()
        first(i).wait_send()
        second(i).wait_send()
        return carry

    lax.fori_loop(0, CHUNKS, drain, 0)

    for stage in final[1:]:
        stage()
    early[4]()


def finish_kernel(
    triplet_total,
    early_ref,
    sum_ref,
    loss_out,
    genc_out,
    gtable_out,
    gself_out,
    gagg_out,
    gout_out,
):
    width = gself_out.shape[1]
    for k, out in enumerate((gout_out, gself_out, gagg_out)):
        for layer, source in enumerate((sum_ref, early_ref)):
            out[layer] = source[k * width : (k + 1) * width, :].astype(F32)
    base = 3 * width
    genc_out[...] = sum_ref[base : base + 16, :].astype(F32)[: genc_out.shape[0]]
    gtable_out[...] = sum_ref[base + 16 : base + 16 + gtable_out.shape[0], :].astype(F32)
    loss_out[...] = early_ref[base : base + 1, 0:1] / triplet_total


def body(
    hit_feats,
    layer_ids,
    edge_tiles,
    src_blocks,
    live_slots,
    anchor_hits,
    positive_hits,
    negative_hits,
    w_enc,
    layer_table,
    w_self,
    w_agg,
    w_out,
):
    blocks, slots, rows, _ = edge_tiles.shape
    width = w_enc.shape[1]
    features = hit_feats.shape[0]
    kinds = layer_table.shape[0]
    hits = blocks * rows
    layer_total = w_self.shape[0]
    triplets = anchor_hits.shape[0]
    group = 8
    steps = blocks // group
    span = group * rows
    me = lax.axis_index("phi")
    is_even = me % 2 == 0
    even_pair = (me // 2) % 2 == 0

    def place(part):
        spots = (
            jnp.where(even_pair, 2, 0),
            jnp.where(is_even, 4, 3),
            1,
            jnp.where(is_even, 3, 4),
            jnp.where(even_pair, 0, 2),
        )
        return sum(jnp.where(part == k, spot, 0) for k, spot in enumerate(spots))

    live = jnp.arange(slots, dtype=jnp.int32)[None, :] < live_slots[:, None]
    index = jnp.where(
        live, place(src_blocks // blocks) * blocks + src_blocks % blocks, 5 * blocks
    ).reshape(blocks * slots)
    depth = 16 + kinds
    listed = 2 * triplets // 128 + 1
    list_shape = (-(-(listed + 1) // 8) * 8, 128)

    row_spec = pl.BlockSpec((span, width), lambda i, *_: (i, 0))
    weight_spec = full((width, width))
    any_spec = pl.BlockSpec(memory_space=pl.ANY)
    row_shape = jax.ShapeDtypeStruct((hits, width), BF16)
    weight_shape = jax.ShapeDtypeStruct((width, width), F32)

    wide_shape = jax.ShapeDtypeStruct((hits, width), F32)
    vmem = pl.BlockSpec(memory_space=pltpu.VMEM)
    smem = pl.BlockSpec(memory_space=pltpu.SMEM)
    few = pltpu.SemaphoreType.DMA((FEAT_CHUNKS,))
    each = pltpu.SemaphoreType.DMA((CHUNKS,))
    one = pltpu.SemaphoreType.DMA((1,))
    four = pltpu.SemaphoreType.DMA((4,))
    block_shape = jax.ShapeDtypeStruct((blocks, rows, width), BF16)
    before0, agg0, hidden0, latents1, agg1, hidden1, latents2, lists, feats, wcat = pl.pallas_call(
        functools.partial(forward_kernel, features),
        in_specs=[smem] + [vmem] * 4 + [any_spec] + [vmem] * 5,
        out_specs=[any_spec] * 10,
        out_shape=[block_shape, row_shape, row_shape, block_shape, row_shape, row_shape]
        + [
            wide_shape,
            jax.ShapeDtypeStruct((5,) + list_shape, jnp.int32),
            jax.ShapeDtypeStruct((depth, 5 * hits), BF16),
            jax.ShapeDtypeStruct((depth, width), BF16),
        ],
        scratch_shapes=[
            pltpu.VMEM((16, hits), BF16),
            pltpu.VMEM((depth, width), BF16),
            pltpu.VMEM(list_shape, jnp.int32),
            pltpu.VMEM((listed - 1, 128, 128), jnp.int32),
            pltpu.VMEM((listed - 1, 128, 128), jnp.int32),
            pltpu.VMEM((listed - 1, 128, 128), jnp.int32),
            pltpu.VMEM((5, 16, hits), BF16),
            pltpu.VMEM((depth, 5 * hits), BF16),
            pltpu.VMEM((5 * blocks + 1, rows, width), BF16),
            pltpu.VMEM((5 * blocks + 1, rows, width), BF16),
        ]
        + [pltpu.VMEM((hits, width), BF16)] * 4
        + [
            pltpu.VMEM((hits, width), F32),
            pltpu.VMEM(edge_tiles.shape, BF16),
            each,
            pltpu.SemaphoreType.DMA((6,)),
            pltpu.SemaphoreType.DMA((3 * LATER_STEPS,)),
            one,
        ]
        + [few] * 6
        + [four] * 2
        + [each] * 8
        + [one] * 2,
        compiler_params=pltpu.CompilerParams(
            collective_id=1, has_side_effects=True, vmem_limit_bytes=VMEM_BYTES
        ),
        name="forward",
    )(
        index,
        hit_feats,
        layer_ids.reshape(1, hits),
        positive_hits.reshape(triplets // 128, 128),
        negative_hits.reshape(triplets // 128, 128),
        edge_tiles,
        w_enc,
        layer_table,
        w_self,
        w_agg,
        w_out,
    )

    before0, latents1 = before0.reshape(hits, width), latents1.reshape(hits, width)
    lists = lists.reshape(-1)
    move_shape = jax.ShapeDtypeStruct((triplets, width), BF16)
    wide_move = jax.ShapeDtypeStruct((triplets, width), F32)
    move_spec = full((triplets, width))
    *found, anchors = pl.pallas_call(
        gather_kernel,
        grid_spec=pltpu.PrefetchScalarGridSpec(
            num_scalar_prefetch=2,
            grid=(1,),
            in_specs=[full((hits, width))],
            out_specs=[move_spec] * 6,
            scratch_shapes=[pltpu.VMEM((2 * triplets + 8, width), F32)],
        ),
        out_shape=[move_shape] * 6,
        compiler_params=params(),
        name="gather",
    )(lists, anchor_hits, latents2)
    coef_shape = (triplets // 128, 128)
    loss_part, ganchor, *moves, coef, coefs = pl.pallas_call(
        functools.partial(contrast_kernel, 1.0 / math.sqrt(width)),
        in_specs=[vmem] * 6,
        out_specs=[vmem] * 8,
        out_shape=[jax.ShapeDtypeStruct((8, width), F32), wide_move]
        + [move_shape] * 4
        + [jax.ShapeDtypeStruct(coef_shape, F32), jax.ShapeDtypeStruct((4,) + coef_shape, F32)],
        scratch_shapes=[pltpu.VMEM((triplets, width), F32)]
        + [pltpu.VMEM((triplets, width), BF16)] * 6
        + [pltpu.SemaphoreType.DMA((PARTS,))] * 16
        + [pltpu.SemaphoreType.DMA((4,))] * 2,
        compiler_params=pltpu.CompilerParams(
            collective_id=4, has_side_effects=True, vmem_limit_bytes=VMEM_BYTES
        ),
        name="contrast",
    )(*found, anchors)

    t_shape = jax.ShapeDtypeStruct((blocks, width, rows), F32)
    t_half = jax.ShapeDtypeStruct((blocks, width, rows), BF16)
    adj_shape = pltpu.VMEM((5 * blocks + 1, width, rows), F32)
    upstream1, act1, gradient2, obelow, own, oabove, osibling, ocross = pl.pallas_call(
        functools.partial(last_backward, group, steps),
        grid_spec=pltpu.PrefetchScalarGridSpec(
            num_scalar_prefetch=3,
            grid=(steps,),
            in_specs=[any_spec, move_spec, full(coef_shape), full((4,) + coef_shape)]
            + [move_spec] * 5
            + [row_spec]
            + [full((2, width, width))] * 2,
            out_specs=[row_spec] * 3 + [any_spec] * 5,
            scratch_shapes=[
                adj_shape,
                pltpu.VMEM((10 * triplets + 40, width), F32),
                pltpu.VMEM((4, blocks, width, rows), BF16),
                pltpu.VMEM(edge_tiles.shape, BF16),
                pltpu.SemaphoreType.DMA((steps,)),
                pltpu.SemaphoreType.DMA((5,)),
            ]
            + [pltpu.VMEM((hits, width), F32)] * 4,
        ),
        out_shape=[row_shape] * 2 + [wide_shape] + [t_half, t_shape] + [t_half] * 3,
        compiler_params=params(),
        name="last_backward",
    )(
        index, lists, anchor_hits, edge_tiles, ganchor, coef, coefs, anchors, *moves, hidden1, w_agg, w_out,
    )
    pairs = lax.axis_size("phi") // 2

    def sum_sizes(count, wire):
        chunk = -(-count // (32 * pairs)) * 16
        total = 2 * pairs * chunk
        return jax.ShapeDtypeStruct((total, width), wire), [
            pltpu.VMEM((total, width), F32),
            pltpu.VMEM((total // 2, width), F32),
            pltpu.VMEM((total // 2, width), wire),
            pltpu.VMEM((pairs - 1, chunk, width), wire),
        ]

    early_shape, early_scratch = sum_sizes(3 * width + 8, F32)
    final_shape, final_scratch = sum_sizes(3 * width + depth, F32)
    many = pltpu.SemaphoreType.DMA((pairs - 1,))
    flat = (hits, width)
    sums = pl.pallas_call(
        functools.partial(back_kernel, pairs),
        in_specs=[smem] + [any_spec] * 15 + [vmem] * 6,
        out_specs=[vmem] * 2,
        out_shape=[early_shape, final_shape],
        scratch_shapes=[pltpu.VMEM((width, depth), BF16)]
        + [pltpu.VMEM(flat, BF16)] * 8
        + [pltpu.VMEM(flat, F32)] * 2
        + [pltpu.VMEM(flat, BF16)] * 8
        + [
            pltpu.VMEM(edge_tiles.shape, BF16),
            pltpu.VMEM((5 * blocks + 1, width, rows), F32),
            pltpu.VMEM((5 * blocks + 1, depth, rows), BF16),
        ]
        + final_scratch
        + early_scratch
        + [pltpu.SemaphoreType.DMA((13,))]
        + [pltpu.SemaphoreType.DMA((CHUNKS,))] * 6
        + [one, one]
        + [one, one, many, many, many, many, one, one] * 2,
        compiler_params=pltpu.CompilerParams(
            collective_id=3, has_side_effects=True, vmem_limit_bytes=VMEM_BYTES
        ),
        name="back",
    )(
        index, ocross.reshape(flat), osibling.reshape(flat), oabove.reshape(flat),
        obelow.reshape(flat), own.reshape(flat), gradient2, hidden0, before0, agg0, edge_tiles,
        upstream1, act1, hidden1, latents1, agg1,
        feats, wcat, w_self, w_agg, w_out, loss_part,
    )
    stack = jax.ShapeDtypeStruct((2, width, width), F32)
    loss, genc, gtable, gself, gagg, gout = pl.pallas_call(
        functools.partial(finish_kernel, float(triplets * lax.axis_size("phi"))),
        in_specs=[vmem] * 2,
        out_specs=[vmem] * 6,
        out_shape=[
            jax.ShapeDtypeStruct((1, 1), F32),
            jax.ShapeDtypeStruct((features, width), F32),
            jax.ShapeDtypeStruct((kinds, width), F32),
            stack, stack, stack,
        ],
        name="finish",
    )(*sums)
    return (loss.reshape(1), genc, gtable, gself, gagg, gout)


def solution(mesh):
    both = ("event", "phi")
    in_specs = (
        P(None, both),
        P(both),
        P(both, None, None, None),
        P(both, None),
        P(both),
        P(both),
        P(both),
        P(both),
        P(),
        P(),
        P(),
        P(),
        P(),
    )
    out_specs = (
        P("event"),
        P("event", None),
        P("event", None),
        P("event", None, None),
        P("event", None, None),
        P("event", None, None),
    )
    return jax.shard_map(body, mesh=mesh, in_specs=in_specs, out_specs=out_specs, check_vma=False)
```

```python
import functools
import math

import jax
import jax.numpy as jnp
from jax import lax
from jax.experimental import pallas as pl
from jax.experimental.pallas import tpu as pltpu
from jax.sharding import PartitionSpec as P

loss_divisor = 64.0
F32 = jnp.float32
BF16 = jnp.bfloat16
VMEM_BYTES = 60 * 1024 * 1024


def dot(left, right, left_dim, right_dim):
    return lax.dot_general(
        left, right, (((left_dim,), (right_dim,)), ((), ())), preferred_element_type=F32
    )


def full(shape):
    return pl.BlockSpec(shape, lambda *_: (0,) * len(shape))


def params():
    return pltpu.CompilerParams(
        dimension_semantics=("arbitrary",), vmem_limit_bytes=VMEM_BYTES
    )


CHUNKS = 16
LATER_STEPS = 4


def peers():
    count = lax.axis_size("phi")
    me = lax.axis_index("phi")
    odd_pair = (me // 2) % 2
    odd_core = me % 2
    direct = me + 2 - 4 * odd_pair
    sibling = me + 1 - 2 * odd_core
    stride = 4 - 8 * odd_pair
    onward = (me + stride + count) % count
    source = (me - stride + count) % count
    return direct, sibling, onward, source, odd_pair == odd_core


def remote(src, dst, send, recv, target):
    return pltpu.make_async_remote_copy(
        src_ref=src,
        dst_ref=dst,
        send_sem=send,
        recv_sem=recv,
        device_id={"phi": target},
        device_id_type=pl.DeviceIdType.MESH,
    )


def announce(targets):
    barrier = pltpu.get_barrier_semaphore()
    for target in targets:
        pl.semaphore_signal(
            barrier, inc=1, device_id={"phi": target}, device_id_type=pl.DeviceIdType.MESH
        )


def greet(targets):
    announce(targets)
    pl.semaphore_wait(pltpu.get_barrier_semaphore(), len(targets))


def role_targets():
    count = lax.axis_size("phi")
    me = lax.axis_index("phi")
    odd_pair = (me // 2) % 2
    odd_core = me % 2
    sibling = me + 1 - 2 * odd_core
    across = (me - 1 + 2 * odd_core + count) % count
    direct = me + 2 - 4 * odd_pair
    far = (me - 2 + 4 * odd_pair + count) % count
    return sibling, across, direct, far


def aggregate_group(index_ref, tiles_ref, window_ref, step, group, slots, rows):
    results = []
    for g in range(group):
        tile = jnp.concatenate([tiles_ref[step * group + g, s] for s in range(slots)], axis=1)
        source = jnp.concatenate(
            [
                window_ref[index_ref[(step * group + g) * slots + s]] for s in range(slots)
            ],
            axis=0,
        )
        results.append(dot(tile, source, 1, 0).astype(BF16))
    return jnp.concatenate(results, axis=0)


def node_update(own, aggregated, w_self, w_agg, w_out):
    activation = dot(own, w_self, 1, 0) + dot(aggregated, w_agg, 1, 0)
    hidden = jnp.maximum(activation, 0.0).astype(BF16)
    updated = (own.astype(F32) + dot(hidden, w_out, 1, 0)).astype(BF16)
    return hidden, updated


FEAT_CHUNKS = 4


def forward_kernel(
    features,
    index_ref,
    hit_ref,
    id_ref,
    positive_ref,
    negative_ref,
    tiles_hbm,
    enc_ref,
    table_ref,
    w_self_ref,
    w_agg_ref,
    w_out_ref,
    before_out,
    agg0_out,
    hidden0_out,
    latents_out,
    agg1_out,
    hidden1_out,
    z_out,
    lists_out,
    feats_out,
    wcat_out,
    packed_ref,
    wcat_ref,
    keys_ref,
    key_cols,
    place_cols,
    entry_cols,
    packs_ref,
    feats_ref,
    window_ref,
    later_ref,
    agg0_ref,
    hidden0_ref,
    agg1_ref,
    hidden1_ref,
    z_ref,
    tiles_ref,
    tile_sem,
    out_sem,
    late_sem,
    list_sem,
    *sems,
):
    fys, fyr, fzs, fzr, fcs, fcr, ls, lr = sems[:8]
    ys, yr, zs, zr, cs, cr, ss, sr = sems[8:16]
    fss, fsr = sems[16:]
    direct, sibling, onward, source, direct_crosses = peers()
    roles = role_targets()
    blocks, slots, rows, _ = tiles_ref.shape
    hits = packed_ref.shape[1]
    group = blocks // CHUNKS
    span = group * rows

    def tile_load(i):
        part = pl.ds(i * group, group)
        return pltpu.make_async_copy(tiles_hbm.at[part], tiles_ref.at[part], tile_sem.at[i])

    lax.fori_loop(0, CHUNKS, lambda i, c: (tile_load(i).start(), c)[1], 0)
    beside = [t + 1 - 2 * lax.rem(t, 2) for t in (onward, source)]
    announce((direct, sibling, onward, source, beside[0], beside[1], roles[1], roles[3]))
    kinds, width = table_ref.shape
    filler = jnp.zeros((16 - features, width), F32)
    wcat_ref[...] = jnp.concatenate(
        [enc_ref[...].astype(F32), filler, table_ref[...].astype(F32)], axis=0
    ).astype(BF16)

    def gather_input(i, carry):
        at = pl.ds(pl.multiple_of(i * 512, 512), 512)
        packed_ref[:, at] = jnp.concatenate(
            [
                hit_ref[:, at].astype(F32),
                id_ref[:, at].astype(F32),
                jnp.zeros((15 - features, 512), F32),
            ],
            axis=0,
        ).astype(BF16)
        return carry

    lax.fori_loop(0, hits // 512, gather_input, 0)
    pl.semaphore_wait(pltpu.get_barrier_semaphore(), 8)
    columns = hits // FEAT_CHUNKS

    def pack(k, i):
        return packs_ref.at[k, :, pl.ds(i * columns, columns)]

    chunks = range(FEAT_CHUNKS)
    f_first = [
        remote(
            packed_ref.at[:, pl.ds(i * columns, columns)], pack(0, i), fys.at[i], fyr.at[i], direct
        )
        for i in chunks
    ]
    f_second = [remote(pack(0, i), pack(2, i), fzs.at[i], fzr.at[i], onward) for i in chunks]
    f_cross_a = [remote(pack(0, i), pack(4, i), fcs.at[i], fcr.at[i], sibling) for i in chunks]
    f_cross_b = [remote(pack(0, i), pack(4, i), fcs.at[i], fcr.at[i], beside[0]) for i in chunks]
    f_near = remote(packed_ref, packs_ref.at[3], fss.at[0], fsr.at[0], sibling)
    for copy in f_first:
        copy.start()
    f_near.start()

    def encode(k, ref):
        step = 512
        is_feature = lax.broadcasted_iota(jnp.int32, (16, step), 0) < features
        kind = lax.broadcasted_iota(jnp.int32, (16, step), 0).astype(F32)

        def run(i, carry):
            at = pl.multiple_of(i * step, step)
            data = ref[:, pl.ds(at, step)].astype(F32)
            onehot = jnp.where(kind == data[features : features + 1], 1.0, 0.0)
            feats = jnp.concatenate([jnp.where(is_feature, data, 0.0), onehot], axis=0).astype(BF16)
            feats_ref[:, pl.ds(pl.multiple_of(k * hits + i * step, step), step)] = feats
            encoded = dot(feats, wcat_ref[...], 0, 0)
            squashed = jnp.tanh(encoded).astype(BF16)
            for u in range(step // rows):
                window_ref[k * blocks + i * (step // rows) + u] = squashed[
                    u * rows : (u + 1) * rows
                ]
            return carry

        lax.fori_loop(0, hits // step, run, 0)

    encode(1, packed_ref)
    for i in chunks:
        f_first[i].wait_recv()
        f_second[i].start()

        @pl.when(direct_crosses)
        def _():
            f_cross_a[i].start()

        @pl.when(jnp.logical_not(direct_crosses))
        def _():
            f_cross_b[i].start()

    f_near.wait_recv()
    encode(3, packs_ref.at[3])
    encode(0, packs_ref.at[0])
    for i in chunks:
        f_second[i].wait_recv()
    encode(2, packs_ref.at[2])
    for i in chunks:
        f_cross_a[i].wait_recv()
    encode(4, packs_ref.at[4])
    window_ref[5 * blocks] = jnp.zeros((rows, width), BF16)
    later_ref[5 * blocks] = jnp.zeros((rows, width), BF16)

    def part(k, i):
        return pl.ds(k * blocks + i * group, group)

    def first(i):
        return remote(later_ref.at[part(1, i)], later_ref.at[part(0, i)], ys.at[i], yr.at[i], direct)

    def near(i):
        return remote(later_ref.at[part(1, i)], later_ref.at[part(3, i)], ss.at[i], sr.at[i], sibling)

    def second(i):
        return remote(later_ref.at[part(0, i)], later_ref.at[part(2, i)], zs.at[i], zr.at[i], onward)

    def cross_a(i):
        return remote(later_ref.at[part(0, i)], later_ref.at[part(4, i)], cs.at[i], cr.at[i], sibling)

    def cross_b(i):
        return remote(later_ref.at[part(2, i)], later_ref.at[part(4, i)], cs.at[i], cr.at[i], sibling)

    def cross_c(i):
        return remote(
            later_ref.at[part(0, i)], later_ref.at[part(4, i)], cs.at[i], cr.at[i], beside[0]
        )

    def relay(i):
        first(i).wait_recv()
        second(i).start()

        @pl.when(direct_crosses)
        def _():
            cross_a(i).start()

        if isinstance(i, int) and i == CHUNKS - 1:

            @pl.when(jnp.logical_not(direct_crosses))
            def _():
                cross_c(i).start()

    def land(i):
        second(i).wait_recv()

        if not (isinstance(i, int) and i == CHUNKS - 1):

            @pl.when(jnp.logical_not(direct_crosses))
            def _():
                cross_b(i).start()

    lead = 5
    relayed = (CHUNKS - lead + 1) // 2

    def layer0(i, carry):
        tile_load(i).wait()
        here = pl.ds(pl.multiple_of(i * span, span), span)
        aggregated = aggregate_group(index_ref, tiles_ref, window_ref, i, group, slots, rows)
        own = window_ref[part(1, i)].reshape(span, width)
        hidden, updated = node_update(own, aggregated, w_self_ref[0], w_agg_ref[0], w_out_ref[0])
        later_ref[part(1, i)] = updated.reshape(group, rows, width)
        first(i).start()
        near(i).start()
        agg0_ref[here, :] = aggregated
        hidden0_ref[here, :] = hidden

        @pl.when(jnp.logical_and(i >= lead, lax.rem(i, 2) == 1))
        def _():
            relay(lax.div(i - lead, 2))

        return carry

    lax.fori_loop(0, CHUNKS, layer0, 0)
    own = pl.ds(blocks, blocks)
    saves = [
        pltpu.make_async_copy(src, dst, out_sem.at[k])
        for k, (src, dst) in enumerate(
            (
                (window_ref.at[own], before_out),
                (agg0_ref, agg0_out),
                (hidden0_ref, hidden0_out),
                (later_ref.at[own], latents_out),
                (feats_ref, feats_out),
                (wcat_ref, wcat_out),
            )
        )
    ]
    for copy in saves:
        copy.start()

    wanted = jnp.concatenate([positive_ref[...], negative_ref[...]], axis=0)
    lines = wanted.shape[0]
    pairs_of = lines * 128
    line = lax.broadcasted_iota(jnp.int32, (lines, 128), 0)
    lane = lax.broadcasted_iota(jnp.int32, (lines, 128), 1)
    keys = wanted * pairs_of + (line * 128 + lane)
    tall = jnp.concatenate(
        [wanted.astype(F32), jnp.zeros((128 - lines, 128), F32)], axis=0
    ).T.astype(jnp.int32)
    down = lax.broadcasted_iota(jnp.int32, (128, 1), 0)
    counts = []
    for k in range(5):
        mine = jnp.logical_and(wanted >= k * hits, wanted < (k + 1) * hits)
        counted = jnp.sum(jnp.where(mine, 1.0, 0.0), axis=1, keepdims=True)
        counts.append(jnp.sum(counted, axis=0, keepdims=True).astype(jnp.int32))
    aligned, shift = [jnp.zeros((1, 1), jnp.int32)], [jnp.zeros((1, 1), jnp.int32)]
    for k in range(5):
        filled = lax.bitwise_and(counts[k] + 7, -8)
        aligned.append(aligned[k] + filled)
        shift.append(shift[k] + filled - counts[k])
    for c in range(lines):
        column = tall[:, c : c + 1]
        slot = down + c * 128
        moved = jnp.zeros((128, 1), jnp.int32)
        first_row = jnp.zeros((128, 1), jnp.int32)
        for k in range(5):
            mine = jnp.logical_and(column >= k * hits, column < (k + 1) * hits)
            moved = moved + jnp.where(mine, shift[k], 0)
            first_row = first_row + jnp.where(mine, k * hits, 0)
        entry = (column - first_row) * (1 << ENTRY_BITS) + slot - pairs_of
        key_cols[c] = jnp.broadcast_to(column * pairs_of + slot, (128, 128))
        place_cols[c] = jnp.broadcast_to(moved, (128, 128))
        entry_cols[c] = jnp.broadcast_to(entry, (128, 128))

    def rank(c, carry):
        column = key_cols[c]
        count = jnp.zeros((128, 128), F32)
        for r in range(lines):
            count = count + jnp.where(keys[r : r + 1] < column, 1.0, 0.0)
        total = jnp.sum(count, axis=1, keepdims=True).astype(jnp.int32)
        place_cols[c] = place_cols[c] + jnp.broadcast_to(total, (128, 128))
        return carry

    keys_ref[...] = jnp.zeros(keys_ref.shape, jnp.int32)

    def put(q, carry):
        target = lax.broadcasted_iota(jnp.int32, (128, 128), 1) + q * 128

        def match(c, total):
            return total + jnp.where(place_cols[c] == target, entry_cols[c], 0)

        total = lax.fori_loop(0, lines, match, jnp.zeros((128, 128), jnp.int32))
        found = jnp.sum(total.astype(F32), axis=0, keepdims=True).astype(jnp.int32)
        keys_ref[pl.ds(q, 1), :] = found + pairs_of
        return carry

    turns = 3
    for k in range(turns):
        relay(relayed + k)
        land(k)
        lax.fori_loop(lines * k // turns, lines * (k + 1) // turns, rank, 0)
    put_turns = CHUNKS - relayed - turns - 2
    for k in range(put_turns):
        relay(relayed + turns + k)
        land(turns + k)
        lax.fori_loop(
            (lines + 1) * k // put_turns, (lines + 1) * (k + 1) // put_turns, put, 0
        )
    lane = lax.broadcasted_iota(jnp.int32, (1, 128), 1)
    keys_ref[pl.ds(lines + 1, 1), :] = sum(
        jnp.where(lane == k, aligned[k] // 8, 0) for k in range(6)
    )
    lists = [
        remote(keys_ref, lists_out.at[j + 1], ls.at[j], lr.at[j], target)
        for j, target in enumerate(roles)
    ]
    for copy in lists:
        copy.start()
    own_list = pltpu.make_async_copy(keys_ref, lists_out.at[0], list_sem.at[0])
    own_list.start()

    for k in range(CHUNKS - 2, CHUNKS):
        relay(k)
    for k in range(turns + put_turns, CHUNKS):
        land(k)

    def settle(i, carry):
        near(i).wait()
        cross_a(i).wait_recv()
        return carry

    lax.fori_loop(0, CHUNKS, settle, 0)

    later_group = blocks // LATER_STEPS
    later_span = later_group * rows

    def late_saves(i):
        here = pl.ds(pl.multiple_of(i * later_span, later_span), later_span)
        return [
            pltpu.make_async_copy(src.at[here], dst.at[here], late_sem.at[k * LATER_STEPS + i])
            for k, (src, dst) in enumerate(
                ((agg1_ref, agg1_out), (hidden1_ref, hidden1_out), (z_ref, z_out))
            )
        ]

    def layer1(i, carry):
        here = pl.ds(pl.multiple_of(i * later_span, later_span), later_span)
        aggregated = aggregate_group(index_ref, tiles_ref, later_ref, i, later_group, slots, rows)
        own = later_ref[pl.ds(blocks + i * later_group, later_group)].reshape(later_span, width)
        hidden, updated = node_update(own, aggregated, w_self_ref[1], w_agg_ref[1], w_out_ref[1])
        agg1_ref[here, :] = aggregated
        hidden1_ref[here, :] = hidden
        z_ref[here, :] = updated.astype(F32)
        for copy in late_saves(i):
            copy.start()
        return carry

    lax.fori_loop(0, LATER_STEPS, layer1, 0)

    def drain(i, carry):
        first(i).wait_send()
        second(i).wait_send()
        cross_a(i).wait_send()
        return carry

    lax.fori_loop(0, CHUNKS, drain, 0)

    def saved(i, carry):
        for copy in late_saves(i):
            copy.wait()
        return carry

    lax.fori_loop(0, LATER_STEPS, saved, 0)
    for i in chunks:
        f_first[i].wait_send()
        f_second[i].wait_send()
        f_cross_a[i].wait_send()
    f_near.wait_send()
    own_list.wait()
    for copy in lists:
        copy.wait()
    for copy in saves:
        copy.wait()


def segments(list_ref, stride, listed):
    me = lax.axis_index("phi")
    odd_core, odd_pair = lax.rem(me, 2), lax.rem(lax.div(me, 2), 2)
    places = (2, 1 + 2 * odd_core, 3 - 2 * odd_core, 4 * odd_pair, 4 - 4 * odd_pair)
    starts = [j * stride + listed + k for j, k in enumerate(places)]
    return [(list_ref[at], list_ref[at + 1]) for at in starts]


def gather_kernel(list_ref, anchor_ref, z_ref, *refs):
    outs, (anchor_out, buf_ref) = refs[:5], refs[5:]
    triplets, width = anchor_out.shape
    stride = list_ref.shape[0] // 5
    bounds = segments(list_ref, stride, 2 * triplets + 128)

    def anchors(i, carry):
        at = pl.multiple_of(i * 16, 16)
        anchor_out[pl.ds(at, 16), :] = jnp.concatenate(
            [z_ref[pl.ds(anchor_ref[i * 16 + u], 1), :] for u in range(16)], axis=0
        ).astype(BF16)
        return carry

    lax.fori_loop(0, triplets // 16, anchors, 0)
    zeros = jnp.zeros((64, width), F32)

    def clear(i, carry):
        for u in range(4):
            buf_ref[pl.ds(pl.multiple_of(i * 256 + u * 64, 64), 64), :] = zeros
        return carry

    lax.fori_loop(0, 2 * triplets // 256, clear, 0)
    for j in range(5):

        def fetch(i, carry, j=j):
            for u in range(8):
                entry = list_ref[j * stride + i * 8 + u]
                row = z_ref[pl.ds(lax.shift_right_logical(entry, ENTRY_BITS), 1), :]
                buf_ref[pl.ds(lax.bitwise_and(entry, ENTRY_MASK), 1), :] = row
            return carry

        lax.fori_loop(bounds[j][0], bounds[j][1], fetch, 0)

        def subtract(i, carry, j=j):
            for u in range(8):
                at = pl.multiple_of(i * 256 + u * 32, 32)
                value = buf_ref[pl.ds(triplets + at, 32), :] - buf_ref[pl.ds(at, 32), :]
                outs[j][pl.ds(at, 32), :] = value.astype(BF16)
                if j < 4:
                    buf_ref[pl.ds(triplets + at, 32), :] = zeros[:32]
                    buf_ref[pl.ds(at, 32), :] = zeros[:32]
            return carry

        lax.fori_loop(0, triplets // 256, subtract, 0)


ENTRY_BITS = 12
ENTRY_MASK = (1 << ENTRY_BITS) - 1
PARTS = 8


def contrast_kernel(
    inv_root,
    self_ref,
    sib_ref,
    cross_ref,
    near_ref,
    far_ref,
    anchor_ref,
    loss_ref,
    ganchor_ref,
    asib_ref,
    across_ref,
    adirect_ref,
    afar_ref,
    coef_out,
    coefs_out,
    change_ref,
    sib_in,
    cross_in,
    far_send,
    far_in,
    near_send,
    near_in,
    *sems,
):
    s = [sems[2 * i : 2 * i + 2] for i in range(9)]
    direct, sibling, onward, source, near_adds = peers()
    roles = role_targets()
    size = anchor_ref.shape[0] // PARTS
    beside = [t + 1 - 2 * lax.rem(t, 2) for t in (onward, source)]
    greet((direct, sibling, onward, source, beside[0], beside[1], roles[1], roles[3]))

    def rows(i):
        return pl.ds(i * size, size)

    def copies(k, src, dst, target):
        return [
            remote(src.at[rows(i)], dst.at[rows(i)], s[k][0].at[i], s[k][1].at[i], target)
            for i in range(PARTS)
        ]

    crosses = copies(0, cross_ref, cross_in, sibling)
    sibs = copies(1, sib_ref, sib_in, sibling)
    hops = copies(2, far_send, far_in, source)
    nears = copies(3, near_send, near_in, direct)
    to_direct = copies(4, anchor_ref, adirect_ref, direct)
    to_sibling = copies(5, anchor_ref, asib_ref, sibling)
    relays = copies(6, adirect_ref, afar_ref, onward)
    cross_a = copies(7, adirect_ref, across_ref, sibling)
    cross_b = copies(7, afar_ref, across_ref, sibling)
    cross_b[-1] = copies(7, adirect_ref, across_ref, beside[0])[-1]
    coefs = [
        remote(coef_out, coefs_out.at[j], s[8][0].at[j], s[8][1].at[j], target)
        for j, target in enumerate(roles)
    ]
    for copy in crosses:
        copy.start()
    for copy in sibs:
        copy.start()
    for i in range(PARTS):
        @pl.when(near_adds)
        def _():
            far_send[rows(i), :] = far_ref[rows(i), :]

        @pl.when(jnp.logical_not(near_adds))
        def _():
            crosses[i].wait_recv()
            far_send[rows(i), :] = (
                far_ref[rows(i), :].astype(F32) + cross_in[rows(i), :].astype(F32)
            ).astype(BF16)

        hops[i].start()
        if i < PARTS // 2:
            to_direct[i].start()
    def relay(i):
        to_sibling[i].start()
        to_direct[i].wait_recv()
        relays[i].start()

        @pl.when(near_adds)
        def _():
            cross_a[i].start()

        if i == PARTS - 1:

            @pl.when(jnp.logical_not(near_adds))
            def _():
                cross_b[i].start()

    for i in range(PARTS):
        hops[i].wait_recv()
        value = near_ref[rows(i), :].astype(F32) + far_in[rows(i), :].astype(F32)

        @pl.when(near_adds)
        def _():
            crosses[i].wait_recv()
            near_send[rows(i), :] = (value + cross_in[rows(i), :].astype(F32)).astype(BF16)

        @pl.when(jnp.logical_not(near_adds))
        def _():
            near_send[rows(i), :] = value.astype(BF16)

        nears[i].start()
        if i >= PARTS // 2:
            relay(i - PARTS // 2)
    for i in range(PARTS // 2, PARTS):
        to_direct[i].start()
    gaps = []
    for i in range(PARTS):
        sibs[i].wait_recv()
        nears[i].wait_recv()
        change = (
            near_in[rows(i), :].astype(F32)
            + self_ref[rows(i), :].astype(F32)
            + sib_in[rows(i), :].astype(F32)
        )
        change_ref[rows(i), :] = change
        product = anchor_ref[rows(i), :].astype(F32) * change
        for u in range(size // 128):
            gaps.append(
                jnp.sum(product[u * 128 : (u + 1) * 128].T, axis=0, keepdims=True) * inv_root
            )
    gap = jnp.concatenate(gaps, axis=0)
    coef_out[...] = jax.nn.sigmoid(gap) * (inv_root / loss_divisor)
    for copy in coefs:
        copy.start()
    soft = jnp.maximum(gap, 0.0) + jnp.log1p(jnp.exp(-jnp.abs(gap)))
    loss_ref[...] = jnp.broadcast_to(jnp.sum(soft, keepdims=True), loss_ref.shape)
    for i in range(PARTS // 2, PARTS):
        relay(i)
    for i in range(PARTS):
        relays[i].wait_recv()

        if i < PARTS - 1:

            @pl.when(jnp.logical_not(near_adds))
            def _():
                cross_b[i].start()

    size = 128
    eye = lax.broadcasted_iota(jnp.int32, (size, size), 0) == lax.broadcasted_iota(
        jnp.int32, (size, size), 1
    )
    for i in range(coef_out.shape[0]):
        coef = coef_out[pl.ds(i, 1), :]
        column = jnp.sum(jnp.where(eye, coef, 0.0), axis=1, keepdims=True)
        here = pl.ds(i * size, size)
        ganchor_ref[here, :] = column * change_ref[here, :]
    for copy in coefs:
        copy.wait()
    for i in range(PARTS):
        crosses[i].wait_send()
        sibs[i].wait_send()
        hops[i].wait_send()
        nears[i].wait_send()
        to_direct[i].wait_send()
        to_sibling[i].wait()
        relays[i].wait_send()
        cross_a[i].wait()


def spread_group(index_ref, tiles_ref, adj_ref, agg_grad_t, step, group, slots, rows):
    for g in range(group):
        block = step * group + g
        tile = jnp.concatenate([tiles_ref[block, s] for s in range(slots)], axis=1)
        contrib = dot(agg_grad_t[:, g * rows : (g + 1) * rows], tile, 1, 0)
        for s in range(slots):
            at = index_ref[(step * group + g) * slots + s]
            adj_ref[at] = adj_ref[at] + contrib[:, s * rows : (s + 1) * rows]


def clear_blocks(adj_ref):
    def clear(i, carry):
        adj_ref[i] = jnp.zeros(adj_ref.shape[1:], F32)
        return carry

    lax.fori_loop(0, adj_ref.shape[0], clear, 0)


def scatter_rows(
    list_ref, anchor_ref, ganchor_ref, coef_ref, coefs_ref, rows_in, moved_ref, sums
):
    triplets, width = ganchor_ref.shape
    hits = sums[0].shape[0]
    stride = list_ref.shape[0] // 5
    span = 2 * triplets + 8
    bounds = segments(list_ref, stride, 2 * triplets + 128)
    zeros = jnp.zeros((64, width), F32)

    def clear(i, carry):
        for target in sums:
            target[pl.ds(pl.multiple_of(i * 64, 64), 64), :] = zeros
        return carry

    lax.fori_loop(0, hits // 64, clear, 0)
    eye = lax.broadcasted_iota(jnp.int32, (128, 128), 0) == lax.broadcasted_iota(
        jnp.int32, (128, 128), 1
    )
    for j, source in enumerate(rows_in):
        for i in range(triplets // 128):
            coef = coef_ref[pl.ds(i, 1), :] if j == 0 else coefs_ref[j - 1, pl.ds(i, 1), :]
            spread = jnp.where(eye, coef, 0.0)
            high = spread.astype(BF16)
            low = (spread - high.astype(F32)).astype(BF16)
            part = source[pl.ds(i * 128, 128), :]
            value = dot(high, part, 1, 0) + dot(low, part, 1, 0)
            moved_ref[pl.ds(j * span + i * 128, 128), :] = -value
            moved_ref[pl.ds(j * span + triplets + i * 128, 128), :] = value
        moved_ref[pl.ds(j * span + 2 * triplets, 8), :] = zeros[:8]

    def anchors(i, carry):
        for u in range(8):
            t = i * 8 + u
            here = pl.ds(anchor_ref[t], 1)
            target = sums[u % 4]
            target[here, :] = target[here, :] + ganchor_ref[pl.ds(t, 1), :]
        return carry

    lax.fori_loop(0, triplets // 8, anchors, 0)
    for j in range(5):

        def add(i, carry, j=j):
            for u in range(8):
                entry = list_ref[j * stride + i * 8 + u]
                here = pl.ds(lax.shift_right_logical(entry, ENTRY_BITS), 1)
                target = sums[u % 4]
                moved = moved_ref[pl.ds(j * span + lax.bitwise_and(entry, ENTRY_MASK), 1), :]
                target[here, :] = target[here, :] + moved
            return carry

        lax.fori_loop(bounds[j][0], bounds[j][1], add, 0)


def last_backward(
    group,
    steps,
    index_ref,
    list_ref,
    anchor_ref,
    tiles_hbm,
    ganchor_ref,
    coef_ref,
    coefs_ref,
    aself_ref,
    asib_ref,
    across_ref,
    adirect_ref,
    afar_ref,
    hidden_ref,
    w_agg_ref,
    w_out_ref,
    upstream_ref,
    act_ref,
    gradient_ref,
    obelow_ref,
    oown_ref,
    oabove_ref,
    osibling_ref,
    ocross_ref,
    adj_ref,
    moved_ref,
    stage_ref,
    tiles_ref,
    tile_sem,
    piece_sem,
    *sums,
):
    step = pl.program_id(0)
    slots, rows = tiles_ref.shape[1], tiles_ref.shape[2]
    span = group * rows

    def tile_load(i):
        part = pl.ds(i * group, group)
        return pltpu.make_async_copy(tiles_hbm.at[part], tiles_ref.at[part], tile_sem.at[i])

    @pl.when(step == 0)
    def _():
        for i in range(steps):
            tile_load(i).start()
        clear_blocks(adj_ref)
        scatter_rows(
            list_ref, anchor_ref, ganchor_ref, coef_ref, coefs_ref,
            (aself_ref, asib_ref, across_ref, adirect_ref, afar_ref), moved_ref, sums,
        )

    here = pl.ds(pl.multiple_of(step * span, span), span)
    gradient = (sums[0][here, :] + sums[1][here, :]) + (sums[2][here, :] + sums[3][here, :])
    upstream = gradient.astype(BF16)
    hidden_grad = dot(upstream, w_out_ref[1], 1, 1)
    act_grad = jnp.where(hidden_ref[...].astype(F32) > 0, hidden_grad, 0.0).astype(BF16)
    upstream_ref[...] = upstream
    act_ref[...] = act_grad
    gradient_ref[...] = gradient
    tile_load(step).wait()
    agg_grad_t = dot(w_agg_ref[1], act_grad, 1, 1).astype(BF16)
    spread_group(index_ref, tiles_ref, adj_ref, agg_grad_t, step, group, slots, rows)

    @pl.when(step == steps - 1)
    def _():
        blocks = oown_ref.shape[0]
        copies = [
            pltpu.make_async_copy(
                adj_ref.at[pl.ds(blocks, blocks)], oown_ref, piece_sem.at[4]
            )
        ]
        copies[0].start()
        for j, (k, target) in enumerate(
            ((4, ocross_ref), (3, osibling_ref), (2, oabove_ref), (0, obelow_ref))
        ):

            def store(i, carry, k=k, j=j):
                for u in range(2):
                    stage_ref[j, 2 * i + u] = adj_ref[k * blocks + 2 * i + u].astype(BF16)
                return carry

            lax.fori_loop(0, blocks // 2, store, 0)
            copies.append(pltpu.make_async_copy(stage_ref.at[j], target, piece_sem.at[j]))
            copies[-1].start()
        for copy in copies:
            copy.wait()


def summer(pairs, x_ref, half_in, acc_ref, slots_in, all_ref, sems):
    s0, r0, s1, r1, s2, r2, s3, r3 = sems
    wire = acc_ref.dtype
    me = lax.axis_index("phi")
    pair, core = me // 2, me % 2
    sibling = me + 1 - 2 * core
    others = [((pair + d) % pairs) * 2 + core for d in range(1, pairs)]
    half = x_ref.shape[0] // 2
    chunk = half // pairs

    def part(start, length):
        return pl.ds(pl.multiple_of(start, 16 if wire == BF16 else 8), length)

    swap = remote(x_ref.at[part((1 - core) * half, half)], half_in, s0.at[0], r0.at[0], sibling)
    scatter = [
        remote(
            acc_ref.at[part(((pair + d) % pairs) * chunk, chunk)],
            slots_in.at[d - 1],
            s1.at[d - 1],
            r1.at[d - 1],
            others[d - 1],
        )
        for d in range(1, pairs)
    ]
    mine = part(core * half + pair * chunk, chunk)
    gather = [
        remote(all_ref.at[mine], all_ref.at[mine], s2.at[d - 1], r2.at[d - 1], others[d - 1])
        for d in range(1, pairs)
    ]
    whole = part(core * half, half)
    last = remote(all_ref.at[whole], all_ref.at[whole], s3.at[0], r3.at[0], sibling)

    def scatter_stage():
        swap.wait()
        acc_ref[...] = (x_ref[part(core * half, half), :] + half_in[...]).astype(wire)
        for copy in scatter:
            copy.start()

    def gather_stage():
        total = x_ref[mine, :] + half_in[part(pair * chunk, chunk), :]
        for d in range(1, pairs):
            scatter[d - 1].wait_recv()
            total = total + slots_in[d - 1].astype(F32)
        all_ref[mine, :] = total.astype(wire)
        for copy in gather:
            copy.start()

    def last_stage():
        for copy in gather:
            copy.wait()
        for copy in scatter:
            copy.wait_send()
        last.start()

    return swap.start, scatter_stage, gather_stage, last_stage, last.wait


def back_kernel(
    pairs,
    index_ref,
    cross_hbm,
    sib_hbm,
    relay_hbm,
    direct_hbm,
    own_hbm,
    grad_hbm,
    hidden_hbm,
    before_hbm,
    agg_hbm,
    tiles_hbm,
    upstream1_hbm,
    act1_hbm,
    hidden1_hbm,
    before1_hbm,
    agg1_hbm,
    feats_ref,
    wcat_ref,
    w_self_ref,
    w_agg_ref,
    w_out_ref,
    loss_ref,
    early_ref,
    all_ref,
    wcat_t_ref,
    cross_in,
    sib_in,
    relay_in,
    total_in,
    relay_send,
    direct_send,
    relay_ref,
    direct_ref,
    own_ref,
    grad_ref,
    hidden_ref,
    before_ref,
    agg_ref,
    upstream1_ref,
    act1_ref,
    hidden1_ref,
    before1_ref,
    agg1_ref,
    tiles_ref,
    slope_ref,
    block_feats_ref,
    x_ref,
    half_in,
    acc_ref,
    slots_in,
    early_x,
    early_half,
    early_acc,
    early_slots,
    local_sem,
    *sems,
):
    ys, yr, zs, zr, cs, cr, ss, sr = sems[:8]
    direct, sibling, onward, source, to_direct = peers()
    me = lax.axis_index("phi")
    pair, core = me // 2, me % 2
    others = [((pair + d) % pairs) * 2 + core for d in range(1, pairs)]
    blocks, slots, rows, _ = tiles_ref.shape
    depth, width = wcat_ref.shape
    window = feats_ref.shape[1] // rows
    size = grad_ref.shape[0] // CHUNKS
    group = blocks // CHUNKS
    loads = [
        pltpu.make_async_copy(src, dst, local_sem.at[k])
        for k, (src, dst) in enumerate(
            (
                (relay_hbm, relay_ref),
                (direct_hbm, direct_ref),
                (own_hbm, own_ref),
                (grad_hbm, grad_ref),
                (hidden_hbm, hidden_ref),
                (before_hbm, before_ref),
                (agg_hbm, agg_ref),
                (tiles_hbm, tiles_ref),
                (upstream1_hbm, upstream1_ref),
                (act1_hbm, act1_ref),
                (hidden1_hbm, hidden1_ref),
                (before1_hbm, before1_ref),
                (agg1_hbm, agg1_ref),
            )
        )
    ]
    for copy in loads:
        copy.start()
    greet([sibling] + others)

    def span(i):
        return pl.ds(pl.multiple_of(i * size, size), size)

    def crosses(i):
        return remote(cross_hbm.at[span(i)], cross_in.at[span(i)], cs.at[i], cr.at[i], sibling)

    def first(i):
        return remote(relay_send.at[span(i)], relay_in.at[span(i)], zs.at[i], zr.at[i], source)

    def second(i):
        return remote(direct_send.at[span(i)], total_in.at[span(i)], ys.at[i], yr.at[i], direct)

    near = remote(sib_hbm, sib_in, ss.at[0], sr.at[0], sibling)
    lax.fori_loop(0, CHUNKS, lambda i, c: (crosses(i).start(), c)[1], 0)
    near.start()

    early = summer(pairs, early_x, early_half, early_acc, early_slots, early_ref, sems[8:16])
    final = summer(pairs, x_ref, half_in, acc_ref, slots_in, all_ref, sems[16:24])
    early_x[...] = jnp.zeros(early_x.shape, F32)
    early_x[3 * width : 3 * width + 8, :] = loss_ref[...]
    per = window // CHUNKS

    def slopes(i):
        for u in range(0, per, 2):
            at = pl.multiple_of((i * per + u) * rows, 2 * rows)
            feats = feats_ref[:, pl.ds(at, 2 * rows)]
            squashed = jnp.tanh(dot(wcat_t_ref[...], feats, 1, 0))
            slope = 1.0 - squashed * squashed
            for v in range(2):
                slope_ref[i * per + u + v] = slope[:, v * rows : (v + 1) * rows]
                block_feats_ref[i * per + u + v] = feats[:, v * rows : (v + 1) * rows]

    wcat_t_ref[...] = (
        jnp.concatenate([wcat_ref[...].astype(F32), jnp.zeros((width - depth, width), F32)], axis=0)
        .T[:, :depth]
        .astype(BF16)
    )
    x_ref[...] = jnp.zeros(x_ref.shape, F32)
    base = 3 * width
    slope_ref[window] = jnp.zeros(slope_ref.shape[1:], F32)
    block_feats_ref[window] = jnp.zeros(block_feats_ref.shape[1:], BF16)
    loads[0].wait()

    lag = 4

    def relay_step(i, carry):
        here = span(i)

        @pl.when(to_direct)
        def _():
            relay_send[here, :] = relay_ref[here, :]

        @pl.when(jnp.logical_not(to_direct))
        def _():
            crosses(i).wait_recv()
            relay_send[here, :] = (
                relay_ref[here, :].astype(F32) + cross_in[here, :].astype(F32)
            ).astype(BF16)

        first(i).start()

        @pl.when(i < CHUNKS - 2 * lag)
        def _():
            slopes(i)

        return carry

    lax.fori_loop(0, CHUNKS, relay_step, 0)
    for copy in loads[1:]:
        copy.wait()
    near.wait()

    def direct_step(i):
        here = span(i)
        first(i).wait_recv()
        value = direct_ref[here, :].astype(F32) + relay_in[here, :].astype(F32)

        @pl.when(to_direct)
        def _():
            crosses(i).wait_recv()
            direct_send[here, :] = (value + cross_in[here, :].astype(F32)).astype(BF16)

        @pl.when(jnp.logical_not(to_direct))
        def _():
            direct_send[here, :] = value.astype(BF16)

        second(i).start()

    def upper_step(i):
        here = pl.ds(pl.multiple_of(i * 2 * size, 2 * size), 2 * size)
        act_grad = act1_ref[here, :]
        early_x[0:width, :] += dot(hidden1_ref[here, :], upstream1_ref[here, :], 0, 0)
        early_x[width : 2 * width, :] += dot(before1_ref[here, :], act_grad, 0, 0)
        early_x[2 * width : 3 * width, :] += dot(agg1_ref[here, :], act_grad, 0, 0)
        grad_ref[here, :] = grad_ref[here, :] + dot(act_grad, w_self_ref[1], 1, 1)

    def layer_step(i):
        here = span(i)
        second(i).wait_recv()
        returned = own_ref[here, :] + (
            total_in[here, :].astype(F32) + sib_in[here, :].astype(F32)
        )
        gradient = grad_ref[here, :] + jnp.concatenate(
            [returned[g * width : (g + 1) * width].T for g in range(group)], axis=0
        )
        upstream = gradient.astype(BF16)
        hidden = hidden_ref[here, :]
        hidden_grad = dot(upstream, w_out_ref[0], 1, 1)
        act_grad = jnp.where(hidden.astype(F32) > 0, hidden_grad, 0.0).astype(BF16)
        agg_grad_t = dot(w_agg_ref[0], act_grad, 1, 1).astype(BF16)
        x_ref[0:width, :] += dot(hidden, upstream, 0, 0)
        x_ref[width : 2 * width, :] += dot(before_ref[here, :], act_grad, 0, 0)
        x_ref[2 * width : 3 * width, :] += dot(agg_ref[here, :], act_grad, 0, 0)
        own_grad = gradient + dot(act_grad, w_self_ref[0], 1, 1)
        feats = feats_ref[:, pl.ds(pl.multiple_of((window // 5) * rows + i * size, size), size)]
        squashed = jnp.tanh(dot(feats, wcat_ref[...], 0, 0))
        genc = dot(feats, (own_grad * (1.0 - squashed * squashed)).astype(BF16), 1, 0)
        for g in range(group):
            block = i * group + g
            tile = jnp.concatenate([tiles_ref[block, s] for s in range(slots)], axis=1)
            contrib = dot(agg_grad_t[:, g * rows : (g + 1) * rows], tile, 1, 0)
            places = [index_ref[block * slots + s] for s in range(slots)]
            slope = jnp.concatenate([slope_ref[at] for at in places], axis=1)
            source_feats = jnp.concatenate([block_feats_ref[at] for at in places], axis=1)
            genc = genc + dot(source_feats, (contrib * slope).astype(BF16), 1, 1)
        x_ref[base : base + depth, :] += genc

    turn = CHUNKS // 2

    def opening(i, carry):
        direct_step(i)
        upper_step(i)

        @pl.when(i < lag)
        def _():
            slopes(CHUNKS - 2 * lag + 2 * i)
            slopes(CHUNKS - 2 * lag + 2 * i + 1)

        @pl.when(i >= lag)
        def _():
            layer_step(i - lag)

        return carry

    def middle(i, carry):
        direct_step(i)
        layer_step(i - lag)
        return carry

    def closing(i, carry):
        layer_step(i)
        return carry

    lax.fori_loop(0, turn, opening, 0)
    early[0]()
    lax.fori_loop(turn, turn + 4, middle, 0)
    early[1]()
    lax.fori_loop(turn + 4, CHUNKS, middle, 0)
    early[2]()
    lax.fori_loop(CHUNKS - lag, CHUNKS, closing, 0)
    final[0]()
    early[3]()

    def drain(i, carry):
        crosses(i).wait_send()
        first(i).wait_send()
        second(i).wait_send()
        return carry

    lax.fori_loop(0, CHUNKS, drain, 0)

    for stage in final[1:]:
        stage()
    early[4]()


def finish_kernel(
    triplet_total,
    early_ref,
    sum_ref,
    loss_out,
    genc_out,
    gtable_out,
    gself_out,
    gagg_out,
    gout_out,
):
    width = gself_out.shape[1]
    for k, out in enumerate((gout_out, gself_out, gagg_out)):
        for layer, source in enumerate((sum_ref, early_ref)):
            out[layer] = source[k * width : (k + 1) * width, :].astype(F32)
    base = 3 * width
    genc_out[...] = sum_ref[base : base + 16, :].astype(F32)[: genc_out.shape[0]]
    gtable_out[...] = sum_ref[base + 16 : base + 16 + gtable_out.shape[0], :].astype(F32)
    loss_out[...] = early_ref[base : base + 1, 0:1] / triplet_total


def body(
    hit_feats,
    layer_ids,
    edge_tiles,
    src_blocks,
    live_slots,
    anchor_hits,
    positive_hits,
    negative_hits,
    w_enc,
    layer_table,
    w_self,
    w_agg,
    w_out,
):
    blocks, slots, rows, _ = edge_tiles.shape
    width = w_enc.shape[1]
    features = hit_feats.shape[0]
    kinds = layer_table.shape[0]
    hits = blocks * rows
    layer_total = w_self.shape[0]
    triplets = anchor_hits.shape[0]
    group = 8
    steps = blocks // group
    span = group * rows
    me = lax.axis_index("phi")
    is_even = me % 2 == 0
    even_pair = (me // 2) % 2 == 0

    def place(part):
        spots = (
            jnp.where(even_pair, 2, 0),
            jnp.where(is_even, 4, 3),
            1,
            jnp.where(is_even, 3, 4),
            jnp.where(even_pair, 0, 2),
        )
        return sum(jnp.where(part == k, spot, 0) for k, spot in enumerate(spots))

    live = jnp.arange(slots, dtype=jnp.int32)[None, :] < live_slots[:, None]
    index = jnp.where(
        live, place(src_blocks // blocks) * blocks + src_blocks % blocks, 5 * blocks
    ).reshape(blocks * slots)
    depth = 16 + kinds
    listed = 2 * triplets // 128 + 1
    list_shape = (-(-(listed + 1) // 8) * 8, 128)

    row_spec = pl.BlockSpec((span, width), lambda i, *_: (i, 0))
    weight_spec = full((width, width))
    any_spec = pl.BlockSpec(memory_space=pl.ANY)
    row_shape = jax.ShapeDtypeStruct((hits, width), BF16)
    weight_shape = jax.ShapeDtypeStruct((width, width), F32)

    wide_shape = jax.ShapeDtypeStruct((hits, width), F32)
    vmem = pl.BlockSpec(memory_space=pltpu.VMEM)
    smem = pl.BlockSpec(memory_space=pltpu.SMEM)
    few = pltpu.SemaphoreType.DMA((FEAT_CHUNKS,))
    each = pltpu.SemaphoreType.DMA((CHUNKS,))
    one = pltpu.SemaphoreType.DMA((1,))
    four = pltpu.SemaphoreType.DMA((4,))
    block_shape = jax.ShapeDtypeStruct((blocks, rows, width), BF16)
    before0, agg0, hidden0, latents1, agg1, hidden1, latents2, lists, feats, wcat = pl.pallas_call(
        functools.partial(forward_kernel, features),
        in_specs=[smem] + [vmem] * 4 + [any_spec] + [vmem] * 5,
        out_specs=[any_spec] * 10,
        out_shape=[block_shape, row_shape, row_shape, block_shape, row_shape, row_shape]
        + [
            wide_shape,
            jax.ShapeDtypeStruct((5,) + list_shape, jnp.int32),
            jax.ShapeDtypeStruct((depth, 5 * hits), BF16),
            jax.ShapeDtypeStruct((depth, width), BF16),
        ],
        scratch_shapes=[
            pltpu.VMEM((16, hits), BF16),
            pltpu.VMEM((depth, width), BF16),
            pltpu.VMEM(list_shape, jnp.int32),
            pltpu.VMEM((listed - 1, 128, 128), jnp.int32),
            pltpu.VMEM((listed - 1, 128, 128), jnp.int32),
            pltpu.VMEM((listed - 1, 128, 128), jnp.int32),
            pltpu.VMEM((5, 16, hits), BF16),
            pltpu.VMEM((depth, 5 * hits), BF16),
            pltpu.VMEM((5 * blocks + 1, rows, width), BF16),
            pltpu.VMEM((5 * blocks + 1, rows, width), BF16),
        ]
        + [pltpu.VMEM((hits, width), BF16)] * 4
        + [
            pltpu.VMEM((hits, width), F32),
            pltpu.VMEM(edge_tiles.shape, BF16),
            each,
            pltpu.SemaphoreType.DMA((6,)),
            pltpu.SemaphoreType.DMA((3 * LATER_STEPS,)),
            one,
        ]
        + [few] * 6
        + [four] * 2
        + [each] * 8
        + [one] * 2,
        compiler_params=pltpu.CompilerParams(
            collective_id=1, has_side_effects=True, vmem_limit_bytes=VMEM_BYTES
        ),
        name="forward",
    )(
        index,
        hit_feats,
        layer_ids.reshape(1, hits),
        positive_hits.reshape(triplets // 128, 128),
        negative_hits.reshape(triplets // 128, 128),
        edge_tiles,
        w_enc,
        layer_table,
        w_self,
        w_agg,
        w_out,
    )

    before0, latents1 = before0.reshape(hits, width), latents1.reshape(hits, width)
    lists = lists.reshape(-1)
    move_shape = jax.ShapeDtypeStruct((triplets, width), BF16)
    wide_move = jax.ShapeDtypeStruct((triplets, width), F32)
    move_spec = full((triplets, width))
    *found, anchors = pl.pallas_call(
        gather_kernel,
        grid_spec=pltpu.PrefetchScalarGridSpec(
            num_scalar_prefetch=2,
            grid=(1,),
            in_specs=[full((hits, width))],
            out_specs=[move_spec] * 6,
            scratch_shapes=[pltpu.VMEM((2 * triplets + 8, width), F32)],
        ),
        out_shape=[move_shape] * 6,
        compiler_params=params(),
        name="gather",
    )(lists, anchor_hits, latents2)
    coef_shape = (triplets // 128, 128)
    loss_part, ganchor, *moves, coef, coefs = pl.pallas_call(
        functools.partial(contrast_kernel, 1.0 / math.sqrt(width)),
        in_specs=[vmem] * 6,
        out_specs=[vmem] * 8,
        out_shape=[jax.ShapeDtypeStruct((8, width), F32), wide_move]
        + [move_shape] * 4
        + [jax.ShapeDtypeStruct(coef_shape, F32), jax.ShapeDtypeStruct((4,) + coef_shape, F32)],
        scratch_shapes=[pltpu.VMEM((triplets, width), F32)]
        + [pltpu.VMEM((triplets, width), BF16)] * 6
        + [pltpu.SemaphoreType.DMA((PARTS,))] * 16
        + [pltpu.SemaphoreType.DMA((4,))] * 2,
        compiler_params=pltpu.CompilerParams(
            collective_id=4, has_side_effects=True, vmem_limit_bytes=VMEM_BYTES
        ),
        name="contrast",
    )(*found, anchors)

    t_shape = jax.ShapeDtypeStruct((blocks, width, rows), F32)
    t_half = jax.ShapeDtypeStruct((blocks, width, rows), BF16)
    adj_shape = pltpu.VMEM((5 * blocks + 1, width, rows), F32)
    upstream1, act1, gradient2, obelow, own, oabove, osibling, ocross = pl.pallas_call(
        functools.partial(last_backward, group, steps),
        grid_spec=pltpu.PrefetchScalarGridSpec(
            num_scalar_prefetch=3,
            grid=(steps,),
            in_specs=[any_spec, move_spec, full(coef_shape), full((4,) + coef_shape)]
            + [move_spec] * 5
            + [row_spec]
            + [full((2, width, width))] * 2,
            out_specs=[row_spec] * 3 + [any_spec] * 5,
            scratch_shapes=[
                adj_shape,
                pltpu.VMEM((10 * triplets + 40, width), F32),
                pltpu.VMEM((4, blocks, width, rows), BF16),
                pltpu.VMEM(edge_tiles.shape, BF16),
                pltpu.SemaphoreType.DMA((steps,)),
                pltpu.SemaphoreType.DMA((5,)),
            ]
            + [pltpu.VMEM((hits, width), F32)] * 4,
        ),
        out_shape=[row_shape] * 2 + [wide_shape] + [t_half, t_shape] + [t_half] * 3,
        compiler_params=params(),
        name="last_backward",
    )(
        index, lists, anchor_hits, edge_tiles, ganchor, coef, coefs, anchors, *moves, hidden1, w_agg, w_out,
    )
    pairs = lax.axis_size("phi") // 2

    def sum_sizes(count, wire):
        chunk = -(-count // (32 * pairs)) * 16
        total = 2 * pairs * chunk
        return jax.ShapeDtypeStruct((total, width), wire), [
            pltpu.VMEM((total, width), F32),
            pltpu.VMEM((total // 2, width), F32),
            pltpu.VMEM((total // 2, width), wire),
            pltpu.VMEM((pairs - 1, chunk, width), wire),
        ]

    early_shape, early_scratch = sum_sizes(3 * width + 8, F32)
    final_shape, final_scratch = sum_sizes(3 * width + depth, F32)
    many = pltpu.SemaphoreType.DMA((pairs - 1,))
    flat = (hits, width)
    sums = pl.pallas_call(
        functools.partial(back_kernel, pairs),
        in_specs=[smem] + [any_spec] * 15 + [vmem] * 6,
        out_specs=[vmem] * 2,
        out_shape=[early_shape, final_shape],
        scratch_shapes=[pltpu.VMEM((width, depth), BF16)]
        + [pltpu.VMEM(flat, BF16)] * 8
        + [pltpu.VMEM(flat, F32)] * 2
        + [pltpu.VMEM(flat, BF16)] * 8
        + [
            pltpu.VMEM(edge_tiles.shape, BF16),
            pltpu.VMEM((5 * blocks + 1, width, rows), F32),
            pltpu.VMEM((5 * blocks + 1, depth, rows), BF16),
        ]
        + final_scratch
        + early_scratch
        + [pltpu.SemaphoreType.DMA((13,))]
        + [pltpu.SemaphoreType.DMA((CHUNKS,))] * 6
        + [one, one]
        + [one, one, many, many, many, many, one, one] * 2,
        compiler_params=pltpu.CompilerParams(
            collective_id=3, has_side_effects=True, vmem_limit_bytes=VMEM_BYTES
        ),
        name="back",
    )(
        index, ocross.reshape(flat), osibling.reshape(flat), oabove.reshape(flat),
        obelow.reshape(flat), own.reshape(flat), gradient2, hidden0, before0, agg0, edge_tiles,
        upstream1, act1, hidden1, latents1, agg1,
        feats, wcat, w_self, w_agg, w_out, loss_part,
    )
    stack = jax.ShapeDtypeStruct((2, width, width), F32)
    loss, genc, gtable, gself, gagg, gout = pl.pallas_call(
        functools.partial(finish_kernel, float(triplets * lax.axis_size("phi"))),
        in_specs=[vmem] * 2,
        out_specs=[vmem] * 6,
        out_shape=[
            jax.ShapeDtypeStruct((1, 1), F32),
            jax.ShapeDtypeStruct((features, width), F32),
            jax.ShapeDtypeStruct((kinds, width), F32),
            stack, stack, stack,
        ],
        name="finish",
    )(*sums)
    return (loss.reshape(1), genc, gtable, gself, gagg, gout)


def solution(mesh):
    both = ("event", "phi")
    in_specs = (
        P(None, both),
        P(both),
        P(both, None, None, None),
        P(both, None),
        P(both),
        P(both),
        P(both),
        P(both),
        P(),
        P(),
        P(),
        P(),
        P(),
    )
    out_specs = (
        P("event"),
        P("event", None),
        P("event", None),
        P("event", None, None),
        P("event", None, None),
        P("event", None, None),
    )
    return jax.shard_map(body, mesh=mesh, in_specs=in_specs, out_specs=out_specs, check_vma=False)
```

```python
import functools
import math

import jax
import jax.numpy as jnp
from jax import lax
from jax.experimental import pallas as pl
from jax.experimental.pallas import tpu as pltpu
from jax.sharding import PartitionSpec as P

loss_divisor = 64.0
F32 = jnp.float32
BF16 = jnp.bfloat16
VMEM_BYTES = 60 * 1024 * 1024


def dot(left, right, left_dim, right_dim):
    return lax.dot_general(
        left, right, (((left_dim,), (right_dim,)), ((), ())), preferred_element_type=F32
    )


def full(shape):
    return pl.BlockSpec(shape, lambda *_: (0,) * len(shape))


def params():
    return pltpu.CompilerParams(
        dimension_semantics=("arbitrary",), vmem_limit_bytes=VMEM_BYTES
    )


CHUNKS = 16
LATER_STEPS = 4


def peers():
    count = lax.axis_size("phi")
    me = lax.axis_index("phi")
    odd_pair = (me // 2) % 2
    odd_core = me % 2
    direct = me + 2 - 4 * odd_pair
    sibling = me + 1 - 2 * odd_core
    stride = 4 - 8 * odd_pair
    onward = (me + stride + count) % count
    source = (me - stride + count) % count
    return direct, sibling, onward, source, odd_pair == odd_core


def remote(src, dst, send, recv, target):
    return pltpu.make_async_remote_copy(
        src_ref=src,
        dst_ref=dst,
        send_sem=send,
        recv_sem=recv,
        device_id={"phi": target},
        device_id_type=pl.DeviceIdType.MESH,
    )


def announce(targets):
    barrier = pltpu.get_barrier_semaphore()
    for target in targets:
        pl.semaphore_signal(
            barrier, inc=1, device_id={"phi": target}, device_id_type=pl.DeviceIdType.MESH
        )


def greet(targets):
    announce(targets)
    pl.semaphore_wait(pltpu.get_barrier_semaphore(), len(targets))


def role_targets():
    count = lax.axis_size("phi")
    me = lax.axis_index("phi")
    odd_pair = (me // 2) % 2
    odd_core = me % 2
    sibling = me + 1 - 2 * odd_core
    across = (me - 1 + 2 * odd_core + count) % count
    direct = me + 2 - 4 * odd_pair
    far = (me - 2 + 4 * odd_pair + count) % count
    return sibling, across, direct, far


def aggregate_group(index_ref, tiles_ref, window_ref, step, group, slots, rows):
    results = []
    for g in range(group):
        tile = jnp.concatenate([tiles_ref[step * group + g, s] for s in range(slots)], axis=1)
        source = jnp.concatenate(
            [
                window_ref[index_ref[(step * group + g) * slots + s]] for s in range(slots)
            ],
            axis=0,
        )
        results.append(dot(tile, source, 1, 0).astype(BF16))
    return jnp.concatenate(results, axis=0)


def node_update(own, aggregated, w_self, w_agg, w_out):
    activation = dot(own, w_self, 1, 0) + dot(aggregated, w_agg, 1, 0)
    hidden = jnp.maximum(activation, 0.0).astype(BF16)
    updated = (own.astype(F32) + dot(hidden, w_out, 1, 0)).astype(BF16)
    return hidden, updated


FEAT_CHUNKS = 8


def forward_kernel(
    features,
    index_ref,
    hit_ref,
    id_ref,
    positive_ref,
    negative_ref,
    tiles_hbm,
    enc_ref,
    table_ref,
    w_self_ref,
    w_agg_ref,
    w_out_ref,
    before_out,
    agg0_out,
    hidden0_out,
    latents_out,
    agg1_out,
    hidden1_out,
    z_out,
    lists_out,
    feats_out,
    wcat_out,
    packed_ref,
    wcat_ref,
    keys_ref,
    key_cols,
    place_cols,
    entry_cols,
    packs_ref,
    feats_ref,
    window_ref,
    later_ref,
    agg0_ref,
    hidden0_ref,
    agg1_ref,
    hidden1_ref,
    z_ref,
    tiles_ref,
    tile_sem,
    out_sem,
    late_sem,
    list_sem,
    *sems,
):
    fys, fyr, fzs, fzr, fcs, fcr, ls, lr = sems[:8]
    ys, yr, zs, zr, cs, cr, ss, sr = sems[8:16]
    fss, fsr = sems[16:]
    direct, sibling, onward, source, direct_crosses = peers()
    roles = role_targets()
    blocks, slots, rows, _ = tiles_ref.shape
    hits = packed_ref.shape[1]
    group = blocks // CHUNKS
    span = group * rows

    def tile_load(i):
        part = pl.ds(i * group, group)
        return pltpu.make_async_copy(tiles_hbm.at[part], tiles_ref.at[part], tile_sem.at[i])

    lax.fori_loop(0, CHUNKS, lambda i, c: (tile_load(i).start(), c)[1], 0)
    beside = [t + 1 - 2 * lax.rem(t, 2) for t in (onward, source)]
    announce((direct, sibling, onward, source, beside[0], beside[1], roles[1], roles[3]))
    kinds, width = table_ref.shape
    filler = jnp.zeros((16 - features, width), F32)
    wcat_ref[...] = jnp.concatenate(
        [enc_ref[...].astype(F32), filler, table_ref[...].astype(F32)], axis=0
    ).astype(BF16)

    def gather_input(i, carry):
        at = pl.ds(pl.multiple_of(i * 512, 512), 512)
        packed_ref[:, at] = jnp.concatenate(
            [
                hit_ref[:, at].astype(F32),
                id_ref[:, at].astype(F32),
                jnp.zeros((15 - features, 512), F32),
            ],
            axis=0,
        ).astype(BF16)
        return carry

    lax.fori_loop(0, hits // 512, gather_input, 0)
    pl.semaphore_wait(pltpu.get_barrier_semaphore(), 8)
    columns = hits // FEAT_CHUNKS

    def pack(k, i):
        return packs_ref.at[k, :, pl.ds(i * columns, columns)]

    chunks = range(FEAT_CHUNKS)
    f_first = [
        remote(
            packed_ref.at[:, pl.ds(i * columns, columns)], pack(0, i), fys.at[i], fyr.at[i], direct
        )
        for i in chunks
    ]
    f_second = [remote(pack(0, i), pack(2, i), fzs.at[i], fzr.at[i], onward) for i in chunks]
    f_cross_a = [remote(pack(0, i), pack(4, i), fcs.at[i], fcr.at[i], sibling) for i in chunks]
    f_cross_b = [remote(pack(0, i), pack(4, i), fcs.at[i], fcr.at[i], beside[0]) for i in chunks]
    f_near = remote(packed_ref, packs_ref.at[3], fss.at[0], fsr.at[0], sibling)
    for copy in f_first:
        copy.start()
    f_near.start()

    def encode(k, ref):
        step = 512
        is_feature = lax.broadcasted_iota(jnp.int32, (16, step), 0) < features
        kind = lax.broadcasted_iota(jnp.int32, (16, step), 0).astype(F32)

        def run(i, carry):
            at = pl.multiple_of(i * step, step)
            data = ref[:, pl.ds(at, step)].astype(F32)
            onehot = jnp.where(kind == data[features : features + 1], 1.0, 0.0)
            feats = jnp.concatenate([jnp.where(is_feature, data, 0.0), onehot], axis=0).astype(BF16)
            feats_ref[:, pl.ds(pl.multiple_of(k * hits + i * step, step), step)] = feats
            encoded = dot(feats, wcat_ref[...], 0, 0)
            squashed = jnp.tanh(encoded).astype(BF16)
            for u in range(step // rows):
                window_ref[k * blocks + i * (step // rows) + u] = squashed[
                    u * rows : (u + 1) * rows
                ]
            return carry

        lax.fori_loop(0, hits // step, run, 0)

    encode(1, packed_ref)
    for i in chunks:
        f_first[i].wait_recv()
        f_second[i].start()

        @pl.when(direct_crosses)
        def _():
            f_cross_a[i].start()

        @pl.when(jnp.logical_not(direct_crosses))
        def _():
            f_cross_b[i].start()

    f_near.wait_recv()
    encode(3, packs_ref.at[3])
    encode(0, packs_ref.at[0])
    for i in chunks:
        f_second[i].wait_recv()
    encode(2, packs_ref.at[2])
    for i in chunks:
        f_cross_a[i].wait_recv()
    encode(4, packs_ref.at[4])
    window_ref[5 * blocks] = jnp.zeros((rows, width), BF16)
    later_ref[5 * blocks] = jnp.zeros((rows, width), BF16)

    def part(k, i):
        return pl.ds(k * blocks + i * group, group)

    def first(i):
        return remote(later_ref.at[part(1, i)], later_ref.at[part(0, i)], ys.at[i], yr.at[i], direct)

    def near(i):
        return remote(later_ref.at[part(1, i)], later_ref.at[part(3, i)], ss.at[i], sr.at[i], sibling)

    def second(i):
        return remote(later_ref.at[part(0, i)], later_ref.at[part(2, i)], zs.at[i], zr.at[i], onward)

    def cross_a(i):
        return remote(later_ref.at[part(0, i)], later_ref.at[part(4, i)], cs.at[i], cr.at[i], sibling)

    def cross_b(i):
        return remote(later_ref.at[part(2, i)], later_ref.at[part(4, i)], cs.at[i], cr.at[i], sibling)

    def cross_c(i):
        return remote(
            later_ref.at[part(0, i)], later_ref.at[part(4, i)], cs.at[i], cr.at[i], beside[0]
        )

    def relay(i):
        first(i).wait_recv()
        second(i).start()

        @pl.when(direct_crosses)
        def _():
            cross_a(i).start()

        if isinstance(i, int) and i == CHUNKS - 1:

            @pl.when(jnp.logical_not(direct_crosses))
            def _():
                cross_c(i).start()

    def land(i):
        second(i).wait_recv()

        if not (isinstance(i, int) and i == CHUNKS - 1):

            @pl.when(jnp.logical_not(direct_crosses))
            def _():
                cross_b(i).start()

    lead = 5
    relayed = (CHUNKS - lead + 1) // 2

    def layer0(i, carry):
        tile_load(i).wait()
        here = pl.ds(pl.multiple_of(i * span, span), span)
        aggregated = aggregate_group(index_ref, tiles_ref, window_ref, i, group, slots, rows)
        own = window_ref[part(1, i)].reshape(span, width)
        hidden, updated = node_update(own, aggregated, w_self_ref[0], w_agg_ref[0], w_out_ref[0])
        later_ref[part(1, i)] = updated.reshape(group, rows, width)
        first(i).start()
        near(i).start()
        agg0_ref[here, :] = aggregated
        hidden0_ref[here, :] = hidden

        @pl.when(jnp.logical_and(i >= lead, lax.rem(i, 2) == 1))
        def _():
            relay(lax.div(i - lead, 2))

        return carry

    lax.fori_loop(0, CHUNKS, layer0, 0)
    own = pl.ds(blocks, blocks)
    saves = [
        pltpu.make_async_copy(src, dst, out_sem.at[k])
        for k, (src, dst) in enumerate(
            (
                (window_ref.at[own], before_out),
                (agg0_ref, agg0_out),
                (hidden0_ref, hidden0_out),
                (later_ref.at[own], latents_out),
                (feats_ref, feats_out),
                (wcat_ref, wcat_out),
            )
        )
    ]
    for copy in saves:
        copy.start()

    wanted = jnp.concatenate([positive_ref[...], negative_ref[...]], axis=0)
    lines = wanted.shape[0]
    pairs_of = lines * 128
    line = lax.broadcasted_iota(jnp.int32, (lines, 128), 0)
    lane = lax.broadcasted_iota(jnp.int32, (lines, 128), 1)
    keys = wanted * pairs_of + (line * 128 + lane)
    tall = jnp.concatenate(
        [wanted.astype(F32), jnp.zeros((128 - lines, 128), F32)], axis=0
    ).T.astype(jnp.int32)
    down = lax.broadcasted_iota(jnp.int32, (128, 1), 0)
    counts = []
    for k in range(5):
        mine = jnp.logical_and(wanted >= k * hits, wanted < (k + 1) * hits)
        counted = jnp.sum(jnp.where(mine, 1.0, 0.0), axis=1, keepdims=True)
        counts.append(jnp.sum(counted, axis=0, keepdims=True).astype(jnp.int32))
    aligned, shift = [jnp.zeros((1, 1), jnp.int32)], [jnp.zeros((1, 1), jnp.int32)]
    for k in range(5):
        filled = lax.bitwise_and(counts[k] + 7, -8)
        aligned.append(aligned[k] + filled)
        shift.append(shift[k] + filled - counts[k])
    for c in range(lines):
        column = tall[:, c : c + 1]
        slot = down + c * 128
        moved = jnp.zeros((128, 1), jnp.int32)
        first_row = jnp.zeros((128, 1), jnp.int32)
        for k in range(5):
            mine = jnp.logical_and(column >= k * hits, column < (k + 1) * hits)
            moved = moved + jnp.where(mine, shift[k], 0)
            first_row = first_row + jnp.where(mine, k * hits, 0)
        entry = (column - first_row) * (1 << ENTRY_BITS) + slot - pairs_of
        key_cols[c] = jnp.broadcast_to(column * pairs_of + slot, (128, 128))
        place_cols[c] = jnp.broadcast_to(moved, (128, 128))
        entry_cols[c] = jnp.broadcast_to(entry, (128, 128))

    def rank(c, carry):
        column = key_cols[c]
        count = jnp.zeros((128, 128), F32)
        for r in range(lines):
            count = count + jnp.where(keys[r : r + 1] < column, 1.0, 0.0)
        total = jnp.sum(count, axis=1, keepdims=True).astype(jnp.int32)
        place_cols[c] = place_cols[c] + jnp.broadcast_to(total, (128, 128))
        return carry

    keys_ref[...] = jnp.zeros(keys_ref.shape, jnp.int32)

    def put(q, carry):
        target = lax.broadcasted_iota(jnp.int32, (128, 128), 1) + q * 128

        def match(c, total):
            return total + jnp.where(place_cols[c] == target, entry_cols[c], 0)

        total = lax.fori_loop(0, lines, match, jnp.zeros((128, 128), jnp.int32))
        found = jnp.sum(total.astype(F32), axis=0, keepdims=True).astype(jnp.int32)
        keys_ref[pl.ds(q, 1), :] = found + pairs_of
        return carry

    turns = 3
    for k in range(turns):
        relay(relayed + k)
        land(k)
        lax.fori_loop(lines * k // turns, lines * (k + 1) // turns, rank, 0)
    put_turns = CHUNKS - relayed - turns - 2
    for k in range(put_turns):
        relay(relayed + turns + k)
        land(turns + k)
        lax.fori_loop(
            (lines + 1) * k // put_turns, (lines + 1) * (k + 1) // put_turns, put, 0
        )
    lane = lax.broadcasted_iota(jnp.int32, (1, 128), 1)
    keys_ref[pl.ds(lines + 1, 1), :] = sum(
        jnp.where(lane == k, aligned[k] // 8, 0) for k in range(6)
    )
    lists = [
        remote(keys_ref, lists_out.at[j + 1], ls.at[j], lr.at[j], target)
        for j, target in enumerate(roles)
    ]
    for copy in lists:
        copy.start()
    own_list = pltpu.make_async_copy(keys_ref, lists_out.at[0], list_sem.at[0])
    own_list.start()

    for k in range(CHUNKS - 2, CHUNKS):
        relay(k)
    for k in range(turns + put_turns, CHUNKS):
        land(k)

    def settle(i, carry):
        near(i).wait()
        cross_a(i).wait_recv()
        return carry

    lax.fori_loop(0, CHUNKS, settle, 0)

    later_group = blocks // LATER_STEPS
    later_span = later_group * rows

    def late_saves(i):
        here = pl.ds(pl.multiple_of(i * later_span, later_span), later_span)
        return [
            pltpu.make_async_copy(src.at[here], dst.at[here], late_sem.at[k * LATER_STEPS + i])
            for k, (src, dst) in enumerate(
                ((agg1_ref, agg1_out), (hidden1_ref, hidden1_out), (z_ref, z_out))
            )
        ]

    def layer1(i, carry):
        here = pl.ds(pl.multiple_of(i * later_span, later_span), later_span)
        aggregated = aggregate_group(index_ref, tiles_ref, later_ref, i, later_group, slots, rows)
        own = later_ref[pl.ds(blocks + i * later_group, later_group)].reshape(later_span, width)
        hidden, updated = node_update(own, aggregated, w_self_ref[1], w_agg_ref[1], w_out_ref[1])
        agg1_ref[here, :] = aggregated
        hidden1_ref[here, :] = hidden
        z_ref[here, :] = updated.astype(F32)
        for copy in late_saves(i):
            copy.start()
        return carry

    lax.fori_loop(0, LATER_STEPS, layer1, 0)

    def drain(i, carry):
        first(i).wait_send()
        second(i).wait_send()
        cross_a(i).wait_send()
        return carry

    lax.fori_loop(0, CHUNKS, drain, 0)

    def saved(i, carry):
        for copy in late_saves(i):
            copy.wait()
        return carry

    lax.fori_loop(0, LATER_STEPS, saved, 0)
    for i in chunks:
        f_first[i].wait_send()
        f_second[i].wait_send()
        f_cross_a[i].wait_send()
    f_near.wait_send()
    own_list.wait()
    for copy in lists:
        copy.wait()
    for copy in saves:
        copy.wait()


def segments(list_ref, stride, listed):
    me = lax.axis_index("phi")
    odd_core, odd_pair = lax.rem(me, 2), lax.rem(lax.div(me, 2), 2)
    places = (2, 1 + 2 * odd_core, 3 - 2 * odd_core, 4 * odd_pair, 4 - 4 * odd_pair)
    starts = [j * stride + listed + k for j, k in enumerate(places)]
    return [(list_ref[at], list_ref[at + 1]) for at in starts]


def gather_kernel(list_ref, anchor_ref, z_ref, *refs):
    outs, (anchor_out, buf_ref) = refs[:5], refs[5:]
    triplets, width = anchor_out.shape
    stride = list_ref.shape[0] // 5
    bounds = segments(list_ref, stride, 2 * triplets + 128)

    def anchors(i, carry):
        at = pl.multiple_of(i * 16, 16)
        anchor_out[pl.ds(at, 16), :] = jnp.concatenate(
            [z_ref[pl.ds(anchor_ref[i * 16 + u], 1), :] for u in range(16)], axis=0
        ).astype(BF16)
        return carry

    lax.fori_loop(0, triplets // 16, anchors, 0)
    zeros = jnp.zeros((64, width), F32)

    def clear(i, carry):
        for u in range(4):
            buf_ref[pl.ds(pl.multiple_of(i * 256 + u * 64, 64), 64), :] = zeros
        return carry

    lax.fori_loop(0, 2 * triplets // 256, clear, 0)
    for j in range(5):

        def fetch(i, carry, j=j):
            for u in range(8):
                entry = list_ref[j * stride + i * 8 + u]
                row = z_ref[pl.ds(lax.shift_right_logical(entry, ENTRY_BITS), 1), :]
                buf_ref[pl.ds(lax.bitwise_and(entry, ENTRY_MASK), 1), :] = row
            return carry

        lax.fori_loop(bounds[j][0], bounds[j][1], fetch, 0)

        def subtract(i, carry, j=j):
            for u in range(8):
                at = pl.multiple_of(i * 256 + u * 32, 32)
                value = buf_ref[pl.ds(triplets + at, 32), :] - buf_ref[pl.ds(at, 32), :]
                outs[j][pl.ds(at, 32), :] = value.astype(BF16)
                if j < 4:
                    buf_ref[pl.ds(triplets + at, 32), :] = zeros[:32]
                    buf_ref[pl.ds(at, 32), :] = zeros[:32]
            return carry

        lax.fori_loop(0, triplets // 256, subtract, 0)


ENTRY_BITS = 12
ENTRY_MASK = (1 << ENTRY_BITS) - 1
PARTS = 8


def contrast_kernel(
    inv_root,
    self_ref,
    sib_ref,
    cross_ref,
    near_ref,
    far_ref,
    anchor_ref,
    loss_ref,
    ganchor_ref,
    asib_ref,
    across_ref,
    adirect_ref,
    afar_ref,
    coef_out,
    coefs_out,
    change_ref,
    sib_in,
    cross_in,
    far_send,
    far_in,
    near_send,
    near_in,
    *sems,
):
    s = [sems[2 * i : 2 * i + 2] for i in range(9)]
    direct, sibling, onward, source, near_adds = peers()
    roles = role_targets()
    size = anchor_ref.shape[0] // PARTS
    beside = [t + 1 - 2 * lax.rem(t, 2) for t in (onward, source)]
    greet((direct, sibling, onward, source, beside[0], beside[1], roles[1], roles[3]))

    def rows(i):
        return pl.ds(i * size, size)

    def copies(k, src, dst, target):
        return [
            remote(src.at[rows(i)], dst.at[rows(i)], s[k][0].at[i], s[k][1].at[i], target)
            for i in range(PARTS)
        ]

    crosses = copies(0, cross_ref, cross_in, sibling)
    sibs = copies(1, sib_ref, sib_in, sibling)
    hops = copies(2, far_send, far_in, source)
    nears = copies(3, near_send, near_in, direct)
    to_direct = copies(4, anchor_ref, adirect_ref, direct)
    to_sibling = copies(5, anchor_ref, asib_ref, sibling)
    relays = copies(6, adirect_ref, afar_ref, onward)
    cross_a = copies(7, adirect_ref, across_ref, sibling)
    cross_b = copies(7, afar_ref, across_ref, sibling)
    cross_b[-1] = copies(7, adirect_ref, across_ref, beside[0])[-1]
    coefs = [
        remote(coef_out, coefs_out.at[j], s[8][0].at[j], s[8][1].at[j], target)
        for j, target in enumerate(roles)
    ]
    for copy in crosses:
        copy.start()
    for copy in sibs:
        copy.start()
    for i in range(PARTS):
        @pl.when(near_adds)
        def _():
            far_send[rows(i), :] = far_ref[rows(i), :]

        @pl.when(jnp.logical_not(near_adds))
        def _():
            crosses[i].wait_recv()
            far_send[rows(i), :] = (
                far_ref[rows(i), :].astype(F32) + cross_in[rows(i), :].astype(F32)
            ).astype(BF16)

        hops[i].start()
        if i < PARTS // 2:
            to_direct[i].start()
    def relay(i):
        to_sibling[i].start()
        to_direct[i].wait_recv()
        relays[i].start()

        @pl.when(near_adds)
        def _():
            cross_a[i].start()

        if i == PARTS - 1:

            @pl.when(jnp.logical_not(near_adds))
            def _():
                cross_b[i].start()

    for i in range(PARTS):
        hops[i].wait_recv()
        value = near_ref[rows(i), :].astype(F32) + far_in[rows(i), :].astype(F32)

        @pl.when(near_adds)
        def _():
            crosses[i].wait_recv()
            near_send[rows(i), :] = (value + cross_in[rows(i), :].astype(F32)).astype(BF16)

        @pl.when(jnp.logical_not(near_adds))
        def _():
            near_send[rows(i), :] = value.astype(BF16)

        nears[i].start()
        if i >= PARTS // 2:
            relay(i - PARTS // 2)
    for i in range(PARTS // 2, PARTS):
        to_direct[i].start()
    gaps = []
    for i in range(PARTS):
        sibs[i].wait_recv()
        nears[i].wait_recv()
        change = (
            near_in[rows(i), :].astype(F32)
            + self_ref[rows(i), :].astype(F32)
            + sib_in[rows(i), :].astype(F32)
        )
        change_ref[rows(i), :] = change
        product = anchor_ref[rows(i), :].astype(F32) * change
        for u in range(size // 128):
            gaps.append(
                jnp.sum(product[u * 128 : (u + 1) * 128].T, axis=0, keepdims=True) * inv_root
            )
    gap = jnp.concatenate(gaps, axis=0)
    coef_out[...] = jax.nn.sigmoid(gap) * (inv_root / loss_divisor)
    for copy in coefs:
        copy.start()
    soft = jnp.maximum(gap, 0.0) + jnp.log1p(jnp.exp(-jnp.abs(gap)))
    loss_ref[...] = jnp.broadcast_to(jnp.sum(soft, keepdims=True), loss_ref.shape)
    for i in range(PARTS // 2, PARTS):
        relay(i)
    for i in range(PARTS):
        relays[i].wait_recv()

        if i < PARTS - 1:

            @pl.when(jnp.logical_not(near_adds))
            def _():
                cross_b[i].start()

    size = 128
    eye = lax.broadcasted_iota(jnp.int32, (size, size), 0) == lax.broadcasted_iota(
        jnp.int32, (size, size), 1
    )
    for i in range(coef_out.shape[0]):
        coef = coef_out[pl.ds(i, 1), :]
        column = jnp.sum(jnp.where(eye, coef, 0.0), axis=1, keepdims=True)
        here = pl.ds(i * size, size)
        ganchor_ref[here, :] = column * change_ref[here, :]
    for copy in coefs:
        copy.wait()
    for i in range(PARTS):
        crosses[i].wait_send()
        sibs[i].wait_send()
        hops[i].wait_send()
        nears[i].wait_send()
        to_direct[i].wait_send()
        to_sibling[i].wait()
        relays[i].wait_send()
        cross_a[i].wait()


def spread_group(index_ref, tiles_ref, adj_ref, agg_grad_t, step, group, slots, rows):
    for g in range(group):
        block = step * group + g
        tile = jnp.concatenate([tiles_ref[block, s] for s in range(slots)], axis=1)
        contrib = dot(agg_grad_t[:, g * rows : (g + 1) * rows], tile, 1, 0)
        for s in range(slots):
            at = index_ref[(step * group + g) * slots + s]
            adj_ref[at] = adj_ref[at] + contrib[:, s * rows : (s + 1) * rows]


def clear_blocks(adj_ref):
    def clear(i, carry):
        adj_ref[i] = jnp.zeros(adj_ref.shape[1:], F32)
        return carry

    lax.fori_loop(0, adj_ref.shape[0], clear, 0)


def scatter_rows(
    list_ref, anchor_ref, ganchor_ref, coef_ref, coefs_ref, rows_in, moved_ref, sums
):
    triplets, width = ganchor_ref.shape
    hits = sums[0].shape[0]
    stride = list_ref.shape[0] // 5
    span = 2 * triplets + 8
    bounds = segments(list_ref, stride, 2 * triplets + 128)
    zeros = jnp.zeros((64, width), F32)

    def clear(i, carry):
        for target in sums:
            target[pl.ds(pl.multiple_of(i * 64, 64), 64), :] = zeros
        return carry

    lax.fori_loop(0, hits // 64, clear, 0)
    eye = lax.broadcasted_iota(jnp.int32, (128, 128), 0) == lax.broadcasted_iota(
        jnp.int32, (128, 128), 1
    )
    for j, source in enumerate(rows_in):
        for i in range(triplets // 128):
            coef = coef_ref[pl.ds(i, 1), :] if j == 0 else coefs_ref[j - 1, pl.ds(i, 1), :]
            spread = jnp.where(eye, coef, 0.0)
            high = spread.astype(BF16)
            low = (spread - high.astype(F32)).astype(BF16)
            part = source[pl.ds(i * 128, 128), :]
            value = dot(high, part, 1, 0) + dot(low, part, 1, 0)
            moved_ref[pl.ds(j * span + i * 128, 128), :] = -value
            moved_ref[pl.ds(j * span + triplets + i * 128, 128), :] = value
        moved_ref[pl.ds(j * span + 2 * triplets, 8), :] = zeros[:8]

    def anchors(i, carry):
        for u in range(8):
            t = i * 8 + u
            here = pl.ds(anchor_ref[t], 1)
            target = sums[u % 4]
            target[here, :] = target[here, :] + ganchor_ref[pl.ds(t, 1), :]
        return carry

    lax.fori_loop(0, triplets // 8, anchors, 0)
    for j in range(5):

        def add(i, carry, j=j):
            for u in range(8):
                entry = list_ref[j * stride + i * 8 + u]
                here = pl.ds(lax.shift_right_logical(entry, ENTRY_BITS), 1)
                target = sums[u % 4]
                moved = moved_ref[pl.ds(j * span + lax.bitwise_and(entry, ENTRY_MASK), 1), :]
                target[here, :] = target[here, :] + moved
            return carry

        lax.fori_loop(bounds[j][0], bounds[j][1], add, 0)


def last_backward(
    group,
    steps,
    index_ref,
    list_ref,
    anchor_ref,
    tiles_hbm,
    ganchor_ref,
    coef_ref,
    coefs_ref,
    aself_ref,
    asib_ref,
    across_ref,
    adirect_ref,
    afar_ref,
    hidden_ref,
    w_agg_ref,
    w_out_ref,
    upstream_ref,
    act_ref,
    gradient_ref,
    obelow_ref,
    oown_ref,
    oabove_ref,
    osibling_ref,
    ocross_ref,
    adj_ref,
    moved_ref,
    stage_ref,
    tiles_ref,
    tile_sem,
    piece_sem,
    *sums,
):
    step = pl.program_id(0)
    slots, rows = tiles_ref.shape[1], tiles_ref.shape[2]
    span = group * rows

    def tile_load(i):
        part = pl.ds(i * group, group)
        return pltpu.make_async_copy(tiles_hbm.at[part], tiles_ref.at[part], tile_sem.at[i])

    @pl.when(step == 0)
    def _():
        for i in range(steps):
            tile_load(i).start()
        clear_blocks(adj_ref)
        scatter_rows(
            list_ref, anchor_ref, ganchor_ref, coef_ref, coefs_ref,
            (aself_ref, asib_ref, across_ref, adirect_ref, afar_ref), moved_ref, sums,
        )

    here = pl.ds(pl.multiple_of(step * span, span), span)
    gradient = (sums[0][here, :] + sums[1][here, :]) + (sums[2][here, :] + sums[3][here, :])
    upstream = gradient.astype(BF16)
    hidden_grad = dot(upstream, w_out_ref[1], 1, 1)
    act_grad = jnp.where(hidden_ref[...].astype(F32) > 0, hidden_grad, 0.0).astype(BF16)
    upstream_ref[...] = upstream
    act_ref[...] = act_grad
    gradient_ref[...] = gradient
    tile_load(step).wait()
    agg_grad_t = dot(w_agg_ref[1], act_grad, 1, 1).astype(BF16)
    spread_group(index_ref, tiles_ref, adj_ref, agg_grad_t, step, group, slots, rows)

    @pl.when(step == steps - 1)
    def _():
        blocks = oown_ref.shape[0]
        copies = [
            pltpu.make_async_copy(
                adj_ref.at[pl.ds(blocks, blocks)], oown_ref, piece_sem.at[4]
            )
        ]
        copies[0].start()
        for j, (k, target) in enumerate(
            ((4, ocross_ref), (3, osibling_ref), (2, oabove_ref), (0, obelow_ref))
        ):

            def store(i, carry, k=k, j=j):
                for u in range(2):
                    stage_ref[j, 2 * i + u] = adj_ref[k * blocks + 2 * i + u].astype(BF16)
                return carry

            lax.fori_loop(0, blocks // 2, store, 0)
            copies.append(pltpu.make_async_copy(stage_ref.at[j], target, piece_sem.at[j]))
            copies[-1].start()
        for copy in copies:
            copy.wait()


def summer(pairs, x_ref, half_in, acc_ref, slots_in, all_ref, sems):
    s0, r0, s1, r1, s2, r2, s3, r3 = sems
    wire = acc_ref.dtype
    me = lax.axis_index("phi")
    pair, core = me // 2, me % 2
    sibling = me + 1 - 2 * core
    others = [((pair + d) % pairs) * 2 + core for d in range(1, pairs)]
    half = x_ref.shape[0] // 2
    chunk = half // pairs

    def part(start, length):
        return pl.ds(pl.multiple_of(start, 16 if wire == BF16 else 8), length)

    swap = remote(x_ref.at[part((1 - core) * half, half)], half_in, s0.at[0], r0.at[0], sibling)
    scatter = [
        remote(
            acc_ref.at[part(((pair + d) % pairs) * chunk, chunk)],
            slots_in.at[d - 1],
            s1.at[d - 1],
            r1.at[d - 1],
            others[d - 1],
        )
        for d in range(1, pairs)
    ]
    mine = part(core * half + pair * chunk, chunk)
    gather = [
        remote(all_ref.at[mine], all_ref.at[mine], s2.at[d - 1], r2.at[d - 1], others[d - 1])
        for d in range(1, pairs)
    ]
    whole = part(core * half, half)
    last = remote(all_ref.at[whole], all_ref.at[whole], s3.at[0], r3.at[0], sibling)

    def scatter_stage():
        swap.wait()
        acc_ref[...] = (x_ref[part(core * half, half), :] + half_in[...]).astype(wire)
        for copy in scatter:
            copy.start()

    def gather_stage():
        total = x_ref[mine, :] + half_in[part(pair * chunk, chunk), :]
        for d in range(1, pairs):
            scatter[d - 1].wait_recv()
            total = total + slots_in[d - 1].astype(F32)
        all_ref[mine, :] = total.astype(wire)
        for copy in gather:
            copy.start()

    def last_stage():
        for copy in gather:
            copy.wait()
        for copy in scatter:
            copy.wait_send()
        last.start()

    return swap.start, scatter_stage, gather_stage, last_stage, last.wait


def back_kernel(
    pairs,
    index_ref,
    cross_hbm,
    sib_hbm,
    relay_hbm,
    direct_hbm,
    own_hbm,
    grad_hbm,
    hidden_hbm,
    before_hbm,
    agg_hbm,
    tiles_hbm,
    upstream1_hbm,
    act1_hbm,
    hidden1_hbm,
    before1_hbm,
    agg1_hbm,
    feats_ref,
    wcat_ref,
    w_self_ref,
    w_agg_ref,
    w_out_ref,
    loss_ref,
    early_ref,
    all_ref,
    wcat_t_ref,
    cross_in,
    sib_in,
    relay_in,
    total_in,
    relay_send,
    direct_send,
    relay_ref,
    direct_ref,
    own_ref,
    grad_ref,
    hidden_ref,
    before_ref,
    agg_ref,
    upstream1_ref,
    act1_ref,
    hidden1_ref,
    before1_ref,
    agg1_ref,
    tiles_ref,
    slope_ref,
    block_feats_ref,
    x_ref,
    half_in,
    acc_ref,
    slots_in,
    early_x,
    early_half,
    early_acc,
    early_slots,
    local_sem,
    *sems,
):
    ys, yr, zs, zr, cs, cr, ss, sr = sems[:8]
    direct, sibling, onward, source, to_direct = peers()
    me = lax.axis_index("phi")
    pair, core = me // 2, me % 2
    others = [((pair + d) % pairs) * 2 + core for d in range(1, pairs)]
    blocks, slots, rows, _ = tiles_ref.shape
    depth, width = wcat_ref.shape
    window = feats_ref.shape[1] // rows
    size = grad_ref.shape[0] // CHUNKS
    group = blocks // CHUNKS
    loads = [
        pltpu.make_async_copy(src, dst, local_sem.at[k])
        for k, (src, dst) in enumerate(
            (
                (relay_hbm, relay_ref),
                (direct_hbm, direct_ref),
                (own_hbm, own_ref),
                (grad_hbm, grad_ref),
                (hidden_hbm, hidden_ref),
                (before_hbm, before_ref),
                (agg_hbm, agg_ref),
                (tiles_hbm, tiles_ref),
                (upstream1_hbm, upstream1_ref),
                (act1_hbm, act1_ref),
                (hidden1_hbm, hidden1_ref),
                (before1_hbm, before1_ref),
                (agg1_hbm, agg1_ref),
            )
        )
    ]
    for copy in loads:
        copy.start()
    greet([sibling] + others)

    def span(i):
        return pl.ds(pl.multiple_of(i * size, size), size)

    def crosses(i):
        return remote(cross_hbm.at[span(i)], cross_in.at[span(i)], cs.at[i], cr.at[i], sibling)

    def first(i):
        return remote(relay_send.at[span(i)], relay_in.at[span(i)], zs.at[i], zr.at[i], source)

    def second(i):
        return remote(direct_send.at[span(i)], total_in.at[span(i)], ys.at[i], yr.at[i], direct)

    near = remote(sib_hbm, sib_in, ss.at[0], sr.at[0], sibling)
    lax.fori_loop(0, CHUNKS, lambda i, c: (crosses(i).start(), c)[1], 0)
    near.start()

    early = summer(pairs, early_x, early_half, early_acc, early_slots, early_ref, sems[8:16])
    final = summer(pairs, x_ref, half_in, acc_ref, slots_in, all_ref, sems[16:24])
    early_x[...] = jnp.zeros(early_x.shape, F32)
    early_x[3 * width : 3 * width + 8, :] = loss_ref[...]
    per = window // CHUNKS

    def slopes(i):
        for u in range(0, per, 2):
            at = pl.multiple_of((i * per + u) * rows, 2 * rows)
            feats = feats_ref[:, pl.ds(at, 2 * rows)]
            squashed = jnp.tanh(dot(wcat_t_ref[...], feats, 1, 0))
            slope = 1.0 - squashed * squashed
            for v in range(2):
                slope_ref[i * per + u + v] = slope[:, v * rows : (v + 1) * rows]
                block_feats_ref[i * per + u + v] = feats[:, v * rows : (v + 1) * rows]

    wcat_t_ref[...] = (
        jnp.concatenate([wcat_ref[...].astype(F32), jnp.zeros((width - depth, width), F32)], axis=0)
        .T[:, :depth]
        .astype(BF16)
    )
    x_ref[...] = jnp.zeros(x_ref.shape, F32)
    base = 3 * width
    slope_ref[window] = jnp.zeros(slope_ref.shape[1:], F32)
    block_feats_ref[window] = jnp.zeros(block_feats_ref.shape[1:], BF16)
    loads[0].wait()

    lag = 3

    def relay_step(i, carry):
        here = span(i)

        @pl.when(to_direct)
        def _():
            relay_send[here, :] = relay_ref[here, :]

        @pl.when(jnp.logical_not(to_direct))
        def _():
            crosses(i).wait_recv()
            relay_send[here, :] = (
                relay_ref[here, :].astype(F32) + cross_in[here, :].astype(F32)
            ).astype(BF16)

        first(i).start()

        @pl.when(i < CHUNKS - 2 * lag)
        def _():
            slopes(i)

        return carry

    lax.fori_loop(0, CHUNKS, relay_step, 0)
    for copy in loads[1:]:
        copy.wait()
    near.wait()

    def direct_step(i):
        here = span(i)
        first(i).wait_recv()
        value = direct_ref[here, :].astype(F32) + relay_in[here, :].astype(F32)

        @pl.when(to_direct)
        def _():
            crosses(i).wait_recv()
            direct_send[here, :] = (value + cross_in[here, :].astype(F32)).astype(BF16)

        @pl.when(jnp.logical_not(to_direct))
        def _():
            direct_send[here, :] = value.astype(BF16)

        second(i).start()

    def upper_step(i):
        here = pl.ds(pl.multiple_of(i * 2 * size, 2 * size), 2 * size)
        act_grad = act1_ref[here, :]
        early_x[0:width, :] += dot(hidden1_ref[here, :], upstream1_ref[here, :], 0, 0)
        early_x[width : 2 * width, :] += dot(before1_ref[here, :], act_grad, 0, 0)
        early_x[2 * width : 3 * width, :] += dot(agg1_ref[here, :], act_grad, 0, 0)
        grad_ref[here, :] = grad_ref[here, :] + dot(act_grad, w_self_ref[1], 1, 1)

    def layer_step(i):
        here = span(i)
        second(i).wait_recv()
        returned = own_ref[here, :] + (
            total_in[here, :].astype(F32) + sib_in[here, :].astype(F32)
        )
        gradient = grad_ref[here, :] + jnp.concatenate(
            [returned[g * width : (g + 1) * width].T for g in range(group)], axis=0
        )
        upstream = gradient.astype(BF16)
        hidden = hidden_ref[here, :]
        hidden_grad = dot(upstream, w_out_ref[0], 1, 1)
        act_grad = jnp.where(hidden.astype(F32) > 0, hidden_grad, 0.0).astype(BF16)
        agg_grad_t = dot(w_agg_ref[0], act_grad, 1, 1).astype(BF16)
        x_ref[0:width, :] += dot(hidden, upstream, 0, 0)
        x_ref[width : 2 * width, :] += dot(before_ref[here, :], act_grad, 0, 0)
        x_ref[2 * width : 3 * width, :] += dot(agg_ref[here, :], act_grad, 0, 0)
        own_grad = gradient + dot(act_grad, w_self_ref[0], 1, 1)
        feats = feats_ref[:, pl.ds(pl.multiple_of((window // 5) * rows + i * size, size), size)]
        squashed = jnp.tanh(dot(feats, wcat_ref[...], 0, 0))
        genc = dot(feats, (own_grad * (1.0 - squashed * squashed)).astype(BF16), 1, 0)
        for g in range(group):
            block = i * group + g
            tile = jnp.concatenate([tiles_ref[block, s] for s in range(slots)], axis=1)
            contrib = dot(agg_grad_t[:, g * rows : (g + 1) * rows], tile, 1, 0)
            places = [index_ref[block * slots + s] for s in range(slots)]
            slope = jnp.concatenate([slope_ref[at] for at in places], axis=1)
            source_feats = jnp.concatenate([block_feats_ref[at] for at in places], axis=1)
            genc = genc + dot(source_feats, (contrib * slope).astype(BF16), 1, 1)
        x_ref[base : base + depth, :] += genc

    turn = CHUNKS // 2

    def opening(i, carry):
        direct_step(i)
        upper_step(i)

        @pl.when(i < lag)
        def _():
            slopes(CHUNKS - 2 * lag + 2 * i)
            slopes(CHUNKS - 2 * lag + 2 * i + 1)

        @pl.when(i >= lag)
        def _():
            layer_step(i - lag)

        return carry

    def middle(i, carry):
        direct_step(i)
        layer_step(i - lag)
        return carry

    def closing(i, carry):
        layer_step(i)
        return carry

    lax.fori_loop(0, turn, opening, 0)
    early[0]()
    lax.fori_loop(turn, turn + 4, middle, 0)
    early[1]()
    lax.fori_loop(turn + 4, CHUNKS, middle, 0)
    early[2]()
    lax.fori_loop(CHUNKS - lag, CHUNKS, closing, 0)
    final[0]()
    early[3]()

    def drain(i, carry):
        crosses(i).wait_send()
        first(i).wait_send()
        second(i).wait_send()
        return carry

    lax.fori_loop(0, CHUNKS, drain, 0)

    for stage in final[1:]:
        stage()
    early[4]()


def finish_kernel(
    triplet_total,
    early_ref,
    sum_ref,
    loss_out,
    genc_out,
    gtable_out,
    gself_out,
    gagg_out,
    gout_out,
):
    width = gself_out.shape[1]
    for k, out in enumerate((gout_out, gself_out, gagg_out)):
        for layer, source in enumerate((sum_ref, early_ref)):
            out[layer] = source[k * width : (k + 1) * width, :].astype(F32)
    base = 3 * width
    genc_out[...] = sum_ref[base : base + 16, :].astype(F32)[: genc_out.shape[0]]
    gtable_out[...] = sum_ref[base + 16 : base + 16 + gtable_out.shape[0], :].astype(F32)
    loss_out[...] = early_ref[base : base + 1, 0:1] / triplet_total


def body(
    hit_feats,
    layer_ids,
    edge_tiles,
    src_blocks,
    live_slots,
    anchor_hits,
    positive_hits,
    negative_hits,
    w_enc,
    layer_table,
    w_self,
    w_agg,
    w_out,
):
    blocks, slots, rows, _ = edge_tiles.shape
    width = w_enc.shape[1]
    features = hit_feats.shape[0]
    kinds = layer_table.shape[0]
    hits = blocks * rows
    layer_total = w_self.shape[0]
    triplets = anchor_hits.shape[0]
    group = 8
    steps = blocks // group
    span = group * rows
    me = lax.axis_index("phi")
    is_even = me % 2 == 0
    even_pair = (me // 2) % 2 == 0

    def place(part):
        spots = (
            jnp.where(even_pair, 2, 0),
            jnp.where(is_even, 4, 3),
            1,
            jnp.where(is_even, 3, 4),
            jnp.where(even_pair, 0, 2),
        )
        return sum(jnp.where(part == k, spot, 0) for k, spot in enumerate(spots))

    live = jnp.arange(slots, dtype=jnp.int32)[None, :] < live_slots[:, None]
    index = jnp.where(
        live, place(src_blocks // blocks) * blocks + src_blocks % blocks, 5 * blocks
    ).reshape(blocks * slots)
    depth = 16 + kinds
    listed = 2 * triplets // 128 + 1
    list_shape = (-(-(listed + 1) // 8) * 8, 128)

    row_spec = pl.BlockSpec((span, width), lambda i, *_: (i, 0))
    weight_spec = full((width, width))
    any_spec = pl.BlockSpec(memory_space=pl.ANY)
    row_shape = jax.ShapeDtypeStruct((hits, width), BF16)
    weight_shape = jax.ShapeDtypeStruct((width, width), F32)

    wide_shape = jax.ShapeDtypeStruct((hits, width), F32)
    vmem = pl.BlockSpec(memory_space=pltpu.VMEM)
    smem = pl.BlockSpec(memory_space=pltpu.SMEM)
    few = pltpu.SemaphoreType.DMA((FEAT_CHUNKS,))
    each = pltpu.SemaphoreType.DMA((CHUNKS,))
    one = pltpu.SemaphoreType.DMA((1,))
    four = pltpu.SemaphoreType.DMA((4,))
    block_shape = jax.ShapeDtypeStruct((blocks, rows, width), BF16)
    before0, agg0, hidden0, latents1, agg1, hidden1, latents2, lists, feats, wcat = pl.pallas_call(
        functools.partial(forward_kernel, features),
        in_specs=[smem] + [vmem] * 4 + [any_spec] + [vmem] * 5,
        out_specs=[any_spec] * 10,
        out_shape=[block_shape, row_shape, row_shape, block_shape, row_shape, row_shape]
        + [
            wide_shape,
            jax.ShapeDtypeStruct((5,) + list_shape, jnp.int32),
            jax.ShapeDtypeStruct((depth, 5 * hits), BF16),
            jax.ShapeDtypeStruct((depth, width), BF16),
        ],
        scratch_shapes=[
            pltpu.VMEM((16, hits), BF16),
            pltpu.VMEM((depth, width), BF16),
            pltpu.VMEM(list_shape, jnp.int32),
            pltpu.VMEM((listed - 1, 128, 128), jnp.int32),
            pltpu.VMEM((listed - 1, 128, 128), jnp.int32),
            pltpu.VMEM((listed - 1, 128, 128), jnp.int32),
            pltpu.VMEM((5, 16, hits), BF16),
            pltpu.VMEM((depth, 5 * hits), BF16),
            pltpu.VMEM((5 * blocks + 1, rows, width), BF16),
            pltpu.VMEM((5 * blocks + 1, rows, width), BF16),
        ]
        + [pltpu.VMEM((hits, width), BF16)] * 4
        + [
            pltpu.VMEM((hits, width), F32),
            pltpu.VMEM(edge_tiles.shape, BF16),
            each,
            pltpu.SemaphoreType.DMA((6,)),
            pltpu.SemaphoreType.DMA((3 * LATER_STEPS,)),
            one,
        ]
        + [few] * 6
        + [four] * 2
        + [each] * 8
        + [one] * 2,
        compiler_params=pltpu.CompilerParams(
            collective_id=1, has_side_effects=True, vmem_limit_bytes=VMEM_BYTES
        ),
        name="forward",
    )(
        index,
        hit_feats,
        layer_ids.reshape(1, hits),
        positive_hits.reshape(triplets // 128, 128),
        negative_hits.reshape(triplets // 128, 128),
        edge_tiles,
        w_enc,
        layer_table,
        w_self,
        w_agg,
        w_out,
    )

    before0, latents1 = before0.reshape(hits, width), latents1.reshape(hits, width)
    lists = lists.reshape(-1)
    move_shape = jax.ShapeDtypeStruct((triplets, width), BF16)
    wide_move = jax.ShapeDtypeStruct((triplets, width), F32)
    move_spec = full((triplets, width))
    *found, anchors = pl.pallas_call(
        gather_kernel,
        grid_spec=pltpu.PrefetchScalarGridSpec(
            num_scalar_prefetch=2,
            grid=(1,),
            in_specs=[full((hits, width))],
            out_specs=[move_spec] * 6,
            scratch_shapes=[pltpu.VMEM((2 * triplets + 8, width), F32)],
        ),
        out_shape=[move_shape] * 6,
        compiler_params=params(),
        name="gather",
    )(lists, anchor_hits, latents2)
    coef_shape = (triplets // 128, 128)
    loss_part, ganchor, *moves, coef, coefs = pl.pallas_call(
        functools.partial(contrast_kernel, 1.0 / math.sqrt(width)),
        in_specs=[vmem] * 6,
        out_specs=[vmem] * 8,
        out_shape=[jax.ShapeDtypeStruct((8, width), F32), wide_move]
        + [move_shape] * 4
        + [jax.ShapeDtypeStruct(coef_shape, F32), jax.ShapeDtypeStruct((4,) + coef_shape, F32)],
        scratch_shapes=[pltpu.VMEM((triplets, width), F32)]
        + [pltpu.VMEM((triplets, width), BF16)] * 6
        + [pltpu.SemaphoreType.DMA((PARTS,))] * 16
        + [pltpu.SemaphoreType.DMA((4,))] * 2,
        compiler_params=pltpu.CompilerParams(
            collective_id=4, has_side_effects=True, vmem_limit_bytes=VMEM_BYTES
        ),
        name="contrast",
    )(*found, anchors)

    t_shape = jax.ShapeDtypeStruct((blocks, width, rows), F32)
    t_half = jax.ShapeDtypeStruct((blocks, width, rows), BF16)
    adj_shape = pltpu.VMEM((5 * blocks + 1, width, rows), F32)
    upstream1, act1, gradient2, obelow, own, oabove, osibling, ocross = pl.pallas_call(
        functools.partial(last_backward, group, steps),
        grid_spec=pltpu.PrefetchScalarGridSpec(
            num_scalar_prefetch=3,
            grid=(steps,),
            in_specs=[any_spec, move_spec, full(coef_shape), full((4,) + coef_shape)]
            + [move_spec] * 5
            + [row_spec]
            + [full((2, width, width))] * 2,
            out_specs=[row_spec] * 3 + [any_spec] * 5,
            scratch_shapes=[
                adj_shape,
                pltpu.VMEM((10 * triplets + 40, width), F32),
                pltpu.VMEM((4, blocks, width, rows), BF16),
                pltpu.VMEM(edge_tiles.shape, BF16),
                pltpu.SemaphoreType.DMA((steps,)),
                pltpu.SemaphoreType.DMA((5,)),
            ]
            + [pltpu.VMEM((hits, width), F32)] * 4,
        ),
        out_shape=[row_shape] * 2 + [wide_shape] + [t_half, t_shape] + [t_half] * 3,
        compiler_params=params(),
        name="last_backward",
    )(
        index, lists, anchor_hits, edge_tiles, ganchor, coef, coefs, anchors, *moves, hidden1, w_agg, w_out,
    )
    pairs = lax.axis_size("phi") // 2

    def sum_sizes(count, wire):
        chunk = -(-count // (32 * pairs)) * 16
        total = 2 * pairs * chunk
        return jax.ShapeDtypeStruct((total, width), wire), [
            pltpu.VMEM((total, width), F32),
            pltpu.VMEM((total // 2, width), F32),
            pltpu.VMEM((total // 2, width), wire),
            pltpu.VMEM((pairs - 1, chunk, width), wire),
        ]

    early_shape, early_scratch = sum_sizes(3 * width + 8, F32)
    final_shape, final_scratch = sum_sizes(3 * width + depth, F32)
    many = pltpu.SemaphoreType.DMA((pairs - 1,))
    flat = (hits, width)
    sums = pl.pallas_call(
        functools.partial(back_kernel, pairs),
        in_specs=[smem] + [any_spec] * 15 + [vmem] * 6,
        out_specs=[vmem] * 2,
        out_shape=[early_shape, final_shape],
        scratch_shapes=[pltpu.VMEM((width, depth), BF16)]
        + [pltpu.VMEM(flat, BF16)] * 8
        + [pltpu.VMEM(flat, F32)] * 2
        + [pltpu.VMEM(flat, BF16)] * 8
        + [
            pltpu.VMEM(edge_tiles.shape, BF16),
            pltpu.VMEM((5 * blocks + 1, width, rows), F32),
            pltpu.VMEM((5 * blocks + 1, depth, rows), BF16),
        ]
        + final_scratch
        + early_scratch
        + [pltpu.SemaphoreType.DMA((13,))]
        + [pltpu.SemaphoreType.DMA((CHUNKS,))] * 6
        + [one, one]
        + [one, one, many, many, many, many, one, one] * 2,
        compiler_params=pltpu.CompilerParams(
            collective_id=3, has_side_effects=True, vmem_limit_bytes=VMEM_BYTES
        ),
        name="back",
    )(
        index, ocross.reshape(flat), osibling.reshape(flat), oabove.reshape(flat),
        obelow.reshape(flat), own.reshape(flat), gradient2, hidden0, before0, agg0, edge_tiles,
        upstream1, act1, hidden1, latents1, agg1,
        feats, wcat, w_self, w_agg, w_out, loss_part,
    )
    stack = jax.ShapeDtypeStruct((2, width, width), F32)
    loss, genc, gtable, gself, gagg, gout = pl.pallas_call(
        functools.partial(finish_kernel, float(triplets * lax.axis_size("phi"))),
        in_specs=[vmem] * 2,
        out_specs=[vmem] * 6,
        out_shape=[
            jax.ShapeDtypeStruct((1, 1), F32),
            jax.ShapeDtypeStruct((features, width), F32),
            jax.ShapeDtypeStruct((kinds, width), F32),
            stack, stack, stack,
        ],
        name="finish",
    )(*sums)
    return (loss.reshape(1), genc, gtable, gself, gagg, gout)


def solution(mesh):
    both = ("event", "phi")
    in_specs = (
        P(None, both),
        P(both),
        P(both, None, None, None),
        P(both, None),
        P(both),
        P(both),
        P(both),
        P(both),
        P(),
        P(),
        P(),
        P(),
        P(),
    )
    out_specs = (
        P("event"),
        P("event", None),
        P("event", None),
        P("event", None, None),
        P("event", None, None),
        P("event", None, None),
    )
    return jax.shard_map(body, mesh=mesh, in_specs=in_specs, out_specs=out_specs, check_vma=False)
```

```python
import functools
import math

import jax
import jax.numpy as jnp
from jax import lax
from jax.experimental import pallas as pl
from jax.experimental.pallas import tpu as pltpu
from jax.sharding import PartitionSpec as P

loss_divisor = 64.0
F32 = jnp.float32
BF16 = jnp.bfloat16
VMEM_BYTES = 60 * 1024 * 1024


def dot(left, right, left_dim, right_dim):
    return lax.dot_general(
        left, right, (((left_dim,), (right_dim,)), ((), ())), preferred_element_type=F32
    )


def full(shape):
    return pl.BlockSpec(shape, lambda *_: (0,) * len(shape))


def params():
    return pltpu.CompilerParams(
        dimension_semantics=("arbitrary",), vmem_limit_bytes=VMEM_BYTES
    )


CHUNKS = 16
LATER_STEPS = 2


def peers():
    count = lax.axis_size("phi")
    me = lax.axis_index("phi")
    odd_pair = (me // 2) % 2
    odd_core = me % 2
    direct = me + 2 - 4 * odd_pair
    sibling = me + 1 - 2 * odd_core
    stride = 4 - 8 * odd_pair
    onward = (me + stride + count) % count
    source = (me - stride + count) % count
    return direct, sibling, onward, source, odd_pair == odd_core


def remote(src, dst, send, recv, target):
    return pltpu.make_async_remote_copy(
        src_ref=src,
        dst_ref=dst,
        send_sem=send,
        recv_sem=recv,
        device_id={"phi": target},
        device_id_type=pl.DeviceIdType.MESH,
    )


def announce(targets):
    barrier = pltpu.get_barrier_semaphore()
    for target in targets:
        pl.semaphore_signal(
            barrier, inc=1, device_id={"phi": target}, device_id_type=pl.DeviceIdType.MESH
        )


def greet(targets):
    announce(targets)
    pl.semaphore_wait(pltpu.get_barrier_semaphore(), len(targets))


def role_targets():
    count = lax.axis_size("phi")
    me = lax.axis_index("phi")
    odd_pair = (me // 2) % 2
    odd_core = me % 2
    sibling = me + 1 - 2 * odd_core
    across = (me - 1 + 2 * odd_core + count) % count
    direct = me + 2 - 4 * odd_pair
    far = (me - 2 + 4 * odd_pair + count) % count
    return sibling, across, direct, far


def aggregate_group(index_ref, tiles_ref, window_ref, step, group, slots, rows):
    results = []
    for g in range(group):
        tile = jnp.concatenate([tiles_ref[step * group + g, s] for s in range(slots)], axis=1)
        source = jnp.concatenate(
            [
                window_ref[index_ref[(step * group + g) * slots + s]] for s in range(slots)
            ],
            axis=0,
        )
        results.append(dot(tile, source, 1, 0).astype(BF16))
    return jnp.concatenate(results, axis=0)


def node_update(own, aggregated, w_self, w_agg, w_out):
    activation = dot(own, w_self, 1, 0) + dot(aggregated, w_agg, 1, 0)
    hidden = jnp.maximum(activation, 0.0).astype(BF16)
    updated = (own.astype(F32) + dot(hidden, w_out, 1, 0)).astype(BF16)
    return hidden, updated


FEAT_CHUNKS = 8


def forward_kernel(
    features,
    index_ref,
    hit_ref,
    id_ref,
    positive_ref,
    negative_ref,
    tiles_hbm,
    enc_ref,
    table_ref,
    w_self_ref,
    w_agg_ref,
    w_out_ref,
    before_out,
    agg0_out,
    hidden0_out,
    latents_out,
    agg1_out,
    hidden1_out,
    z_out,
    lists_out,
    feats_out,
    wcat_out,
    packed_ref,
    wcat_ref,
    keys_ref,
    key_cols,
    place_cols,
    entry_cols,
    packs_ref,
    feats_ref,
    window_ref,
    later_ref,
    agg0_ref,
    hidden0_ref,
    agg1_ref,
    hidden1_ref,
    z_ref,
    tiles_ref,
    tile_sem,
    out_sem,
    late_sem,
    list_sem,
    *sems,
):
    fys, fyr, fzs, fzr, fcs, fcr, ls, lr = sems[:8]
    ys, yr, zs, zr, cs, cr, ss, sr = sems[8:16]
    fss, fsr = sems[16:]
    direct, sibling, onward, source, direct_crosses = peers()
    roles = role_targets()
    blocks, slots, rows, _ = tiles_ref.shape
    hits = packed_ref.shape[1]
    group = blocks // CHUNKS
    span = group * rows

    def tile_load(i):
        part = pl.ds(i * group, group)
        return pltpu.make_async_copy(tiles_hbm.at[part], tiles_ref.at[part], tile_sem.at[i])

    lax.fori_loop(0, CHUNKS, lambda i, c: (tile_load(i).start(), c)[1], 0)
    beside = [t + 1 - 2 * lax.rem(t, 2) for t in (onward, source)]
    announce((direct, sibling, onward, source, beside[0], beside[1], roles[1], roles[3]))
    kinds, width = table_ref.shape
    filler = jnp.zeros((16 - features, width), F32)
    wcat_ref[...] = jnp.concatenate(
        [enc_ref[...].astype(F32), filler, table_ref[...].astype(F32)], axis=0
    ).astype(BF16)

    def gather_input(i, carry):
        at = pl.ds(pl.multiple_of(i * 512, 512), 512)
        packed_ref[:, at] = jnp.concatenate(
            [
                hit_ref[:, at].astype(F32),
                id_ref[:, at].astype(F32),
                jnp.zeros((15 - features, 512), F32),
            ],
            axis=0,
        ).astype(BF16)
        return carry

    lax.fori_loop(0, hits // 512, gather_input, 0)
    pl.semaphore_wait(pltpu.get_barrier_semaphore(), 8)
    columns = hits // FEAT_CHUNKS

    def pack(k, i):
        return packs_ref.at[k, :, pl.ds(i * columns, columns)]

    chunks = range(FEAT_CHUNKS)
    f_first = [
        remote(
            packed_ref.at[:, pl.ds(i * columns, columns)], pack(0, i), fys.at[i], fyr.at[i], direct
        )
        for i in chunks
    ]
    f_second = [remote(pack(0, i), pack(2, i), fzs.at[i], fzr.at[i], onward) for i in chunks]
    f_cross_a = [remote(pack(0, i), pack(4, i), fcs.at[i], fcr.at[i], sibling) for i in chunks]
    f_cross_b = [remote(pack(0, i), pack(4, i), fcs.at[i], fcr.at[i], beside[0]) for i in chunks]
    f_near = remote(packed_ref, packs_ref.at[3], fss.at[0], fsr.at[0], sibling)
    for copy in f_first:
        copy.start()
    f_near.start()

    def encode(k, ref):
        step = 512
        is_feature = lax.broadcasted_iota(jnp.int32, (16, step), 0) < features
        kind = lax.broadcasted_iota(jnp.int32, (16, step), 0).astype(F32)

        def run(i, carry):
            at = pl.multiple_of(i * step, step)
            data = ref[:, pl.ds(at, step)].astype(F32)
            onehot = jnp.where(kind == data[features : features + 1], 1.0, 0.0)
            feats = jnp.concatenate([jnp.where(is_feature, data, 0.0), onehot], axis=0).astype(BF16)
            feats_ref[:, pl.ds(pl.multiple_of(k * hits + i * step, step), step)] = feats
            encoded = dot(feats, wcat_ref[...], 0, 0)
            squashed = jnp.tanh(encoded).astype(BF16)
            for u in range(step // rows):
                window_ref[k * blocks + i * (step // rows) + u] = squashed[
                    u * rows : (u + 1) * rows
                ]
            return carry

        lax.fori_loop(0, hits // step, run, 0)

    encode(1, packed_ref)
    for i in chunks:
        f_first[i].wait_recv()
        f_second[i].start()

        @pl.when(direct_crosses)
        def _():
            f_cross_a[i].start()

        @pl.when(jnp.logical_not(direct_crosses))
        def _():
            f_cross_b[i].start()

    f_near.wait_recv()
    encode(3, packs_ref.at[3])
    encode(0, packs_ref.at[0])
    for i in chunks:
        f_second[i].wait_recv()
    encode(2, packs_ref.at[2])
    for i in chunks:
        f_cross_a[i].wait_recv()
    encode(4, packs_ref.at[4])
    window_ref[5 * blocks] = jnp.zeros((rows, width), BF16)
    later_ref[5 * blocks] = jnp.zeros((rows, width), BF16)

    def part(k, i):
        return pl.ds(k * blocks + i * group, group)

    def first(i):
        return remote(later_ref.at[part(1, i)], later_ref.at[part(0, i)], ys.at[i], yr.at[i], direct)

    def near(i):
        return remote(later_ref.at[part(1, i)], later_ref.at[part(3, i)], ss.at[i], sr.at[i], sibling)

    def second(i):
        return remote(later_ref.at[part(0, i)], later_ref.at[part(2, i)], zs.at[i], zr.at[i], onward)

    def cross_a(i):
        return remote(later_ref.at[part(0, i)], later_ref.at[part(4, i)], cs.at[i], cr.at[i], sibling)

    def cross_b(i):
        return remote(later_ref.at[part(2, i)], later_ref.at[part(4, i)], cs.at[i], cr.at[i], sibling)

    def cross_c(i):
        return remote(
            later_ref.at[part(0, i)], later_ref.at[part(4, i)], cs.at[i], cr.at[i], beside[0]
        )

    def relay(i):
        first(i).wait_recv()
        second(i).start()

        @pl.when(direct_crosses)
        def _():
            cross_a(i).start()

        if isinstance(i, int) and i == CHUNKS - 1:

            @pl.when(jnp.logical_not(direct_crosses))
            def _():
                cross_c(i).start()

    def land(i):
        second(i).wait_recv()

        if not (isinstance(i, int) and i == CHUNKS - 1):

            @pl.when(jnp.logical_not(direct_crosses))
            def _():
                cross_b(i).start()

    lead = 5
    relayed = (CHUNKS - lead + 1) // 2

    def layer0(i, carry):
        tile_load(i).wait()
        here = pl.ds(pl.multiple_of(i * span, span), span)
        aggregated = aggregate_group(index_ref, tiles_ref, window_ref, i, group, slots, rows)
        own = window_ref[part(1, i)].reshape(span, width)
        hidden, updated = node_update(own, aggregated, w_self_ref[0], w_agg_ref[0], w_out_ref[0])
        later_ref[part(1, i)] = updated.reshape(group, rows, width)
        first(i).start()
        near(i).start()
        agg0_ref[here, :] = aggregated
        hidden0_ref[here, :] = hidden

        @pl.when(jnp.logical_and(i >= lead, lax.rem(i, 2) == 1))
        def _():
            relay(lax.div(i - lead, 2))

        return carry

    lax.fori_loop(0, CHUNKS, layer0, 0)
    own = pl.ds(blocks, blocks)
    saves = [
        pltpu.make_async_copy(src, dst, out_sem.at[k])
        for k, (src, dst) in enumerate(
            (
                (window_ref.at[own], before_out),
                (agg0_ref, agg0_out),
                (hidden0_ref, hidden0_out),
                (later_ref.at[own], latents_out),
                (feats_ref, feats_out),
                (wcat_ref, wcat_out),
            )
        )
    ]
    for copy in saves:
        copy.start()

    wanted = jnp.concatenate([positive_ref[...], negative_ref[...]], axis=0)
    lines = wanted.shape[0]
    pairs_of = lines * 128
    line = lax.broadcasted_iota(jnp.int32, (lines, 128), 0)
    lane = lax.broadcasted_iota(jnp.int32, (lines, 128), 1)
    keys = wanted * pairs_of + (line * 128 + lane)
    tall = jnp.concatenate(
        [wanted.astype(F32), jnp.zeros((128 - lines, 128), F32)], axis=0
    ).T.astype(jnp.int32)
    down = lax.broadcasted_iota(jnp.int32, (128, 1), 0)
    counts = []
    for k in range(5):
        mine = jnp.logical_and(wanted >= k * hits, wanted < (k + 1) * hits)
        counted = jnp.sum(jnp.where(mine, 1.0, 0.0), axis=1, keepdims=True)
        counts.append(jnp.sum(counted, axis=0, keepdims=True).astype(jnp.int32))
    aligned, shift = [jnp.zeros((1, 1), jnp.int32)], [jnp.zeros((1, 1), jnp.int32)]
    for k in range(5):
        filled = lax.bitwise_and(counts[k] + 7, -8)
        aligned.append(aligned[k] + filled)
        shift.append(shift[k] + filled - counts[k])
    for c in range(lines):
        column = tall[:, c : c + 1]
        slot = down + c * 128
        moved = jnp.zeros((128, 1), jnp.int32)
        first_row = jnp.zeros((128, 1), jnp.int32)
        for k in range(5):
            mine = jnp.logical_and(column >= k * hits, column < (k + 1) * hits)
            moved = moved + jnp.where(mine, shift[k], 0)
            first_row = first_row + jnp.where(mine, k * hits, 0)
        entry = (column - first_row) * (1 << ENTRY_BITS) + slot - pairs_of
        key_cols[c] = jnp.broadcast_to(column * pairs_of + slot, (128, 128))
        place_cols[c] = jnp.broadcast_to(moved, (128, 128))
        entry_cols[c] = jnp.broadcast_to(entry, (128, 128))

    def rank(c, carry):
        column = key_cols[c]
        count = jnp.zeros((128, 128), F32)
        for r in range(lines):
            count = count + jnp.where(keys[r : r + 1] < column, 1.0, 0.0)
        total = jnp.sum(count, axis=1, keepdims=True).astype(jnp.int32)
        place_cols[c] = place_cols[c] + jnp.broadcast_to(total, (128, 128))
        return carry

    keys_ref[...] = jnp.zeros(keys_ref.shape, jnp.int32)

    def put(q, carry):
        target = lax.broadcasted_iota(jnp.int32, (128, 128), 1) + q * 128

        def match(c, total):
            return total + jnp.where(place_cols[c] == target, entry_cols[c], 0)

        total = lax.fori_loop(0, lines, match, jnp.zeros((128, 128), jnp.int32))
        found = jnp.sum(total.astype(F32), axis=0, keepdims=True).astype(jnp.int32)
        keys_ref[pl.ds(q, 1), :] = found + pairs_of
        return carry

    turns = 3
    for k in range(turns):
        relay(relayed + k)
        land(k)
        lax.fori_loop(lines * k // turns, lines * (k + 1) // turns, rank, 0)
    put_turns = CHUNKS - relayed - turns - 2
    for k in range(put_turns):
        relay(relayed + turns + k)
        land(turns + k)
        lax.fori_loop(
            (lines + 1) * k // put_turns, (lines + 1) * (k + 1) // put_turns, put, 0
        )
    lane = lax.broadcasted_iota(jnp.int32, (1, 128), 1)
    keys_ref[pl.ds(lines + 1, 1), :] = sum(
        jnp.where(lane == k, aligned[k] // 8, 0) for k in range(6)
    )
    lists = [
        remote(keys_ref, lists_out.at[j + 1], ls.at[j], lr.at[j], target)
        for j, target in enumerate(roles)
    ]
    for copy in lists:
        copy.start()
    own_list = pltpu.make_async_copy(keys_ref, lists_out.at[0], list_sem.at[0])
    own_list.start()

    for k in range(CHUNKS - 2, CHUNKS):
        relay(k)
    for k in range(turns + put_turns, CHUNKS):
        land(k)

    def settle(i, carry):
        near(i).wait()
        cross_a(i).wait_recv()
        return carry

    lax.fori_loop(0, CHUNKS, settle, 0)

    later_group = blocks // LATER_STEPS
    later_span = later_group * rows

    def late_saves(i):
        here = pl.ds(pl.multiple_of(i * later_span, later_span), later_span)
        return [
            pltpu.make_async_copy(src.at[here], dst.at[here], late_sem.at[k * LATER_STEPS + i])
            for k, (src, dst) in enumerate(
                ((agg1_ref, agg1_out), (hidden1_ref, hidden1_out), (z_ref, z_out))
            )
        ]

    def layer1(i, carry):
        here = pl.ds(pl.multiple_of(i * later_span, later_span), later_span)
        aggregated = aggregate_group(index_ref, tiles_ref, later_ref, i, later_group, slots, rows)
        own = later_ref[pl.ds(blocks + i * later_group, later_group)].reshape(later_span, width)
        hidden, updated = node_update(own, aggregated, w_self_ref[1], w_agg_ref[1], w_out_ref[1])
        agg1_ref[here, :] = aggregated
        hidden1_ref[here, :] = hidden
        z_ref[here, :] = updated.astype(F32)
        for copy in late_saves(i):
            copy.start()
        return carry

    lax.fori_loop(0, LATER_STEPS, layer1, 0)

    def drain(i, carry):
        first(i).wait_send()
        second(i).wait_send()
        cross_a(i).wait_send()
        return carry

    lax.fori_loop(0, CHUNKS, drain, 0)

    def saved(i, carry):
        for copy in late_saves(i):
            copy.wait()
        return carry

    lax.fori_loop(0, LATER_STEPS, saved, 0)
    for i in chunks:
        f_first[i].wait_send()
        f_second[i].wait_send()
        f_cross_a[i].wait_send()
    f_near.wait_send()
    own_list.wait()
    for copy in lists:
        copy.wait()
    for copy in saves:
        copy.wait()


def segments(list_ref, stride, listed):
    me = lax.axis_index("phi")
    odd_core, odd_pair = lax.rem(me, 2), lax.rem(lax.div(me, 2), 2)
    places = (2, 1 + 2 * odd_core, 3 - 2 * odd_core, 4 * odd_pair, 4 - 4 * odd_pair)
    starts = [j * stride + listed + k for j, k in enumerate(places)]
    return [(list_ref[at], list_ref[at + 1]) for at in starts]


def gather_kernel(list_ref, anchor_ref, z_ref, *refs):
    outs, (anchor_out, buf_ref) = refs[:5], refs[5:]
    triplets, width = anchor_out.shape
    stride = list_ref.shape[0] // 5
    bounds = segments(list_ref, stride, 2 * triplets + 128)

    def anchors(i, carry):
        at = pl.multiple_of(i * 16, 16)
        anchor_out[pl.ds(at, 16), :] = jnp.concatenate(
            [z_ref[pl.ds(anchor_ref[i * 16 + u], 1), :] for u in range(16)], axis=0
        ).astype(BF16)
        return carry

    lax.fori_loop(0, triplets // 16, anchors, 0)
    zeros = jnp.zeros((64, width), F32)

    def clear(i, carry):
        for u in range(4):
            buf_ref[pl.ds(pl.multiple_of(i * 256 + u * 64, 64), 64), :] = zeros
        return carry

    lax.fori_loop(0, 2 * triplets // 256, clear, 0)
    for j in range(5):

        def fetch(i, carry, j=j):
            for u in range(8):
                entry = list_ref[j * stride + i * 8 + u]
                row = z_ref[pl.ds(lax.shift_right_logical(entry, ENTRY_BITS), 1), :]
                buf_ref[pl.ds(lax.bitwise_and(entry, ENTRY_MASK), 1), :] = row
            return carry

        lax.fori_loop(bounds[j][0], bounds[j][1], fetch, 0)

        def subtract(i, carry, j=j):
            for u in range(8):
                at = pl.multiple_of(i * 256 + u * 32, 32)
                value = buf_ref[pl.ds(triplets + at, 32), :] - buf_ref[pl.ds(at, 32), :]
                outs[j][pl.ds(at, 32), :] = value.astype(BF16)
                if j < 4:
                    buf_ref[pl.ds(triplets + at, 32), :] = zeros[:32]
                    buf_ref[pl.ds(at, 32), :] = zeros[:32]
            return carry

        lax.fori_loop(0, triplets // 256, subtract, 0)


ENTRY_BITS = 12
ENTRY_MASK = (1 << ENTRY_BITS) - 1
PARTS = 8


def contrast_kernel(
    inv_root,
    self_ref,
    sib_ref,
    cross_ref,
    near_ref,
    far_ref,
    anchor_ref,
    loss_ref,
    ganchor_ref,
    asib_ref,
    across_ref,
    adirect_ref,
    afar_ref,
    coef_out,
    coefs_out,
    change_ref,
    sib_in,
    cross_in,
    far_send,
    far_in,
    near_send,
    near_in,
    *sems,
):
    s = [sems[2 * i : 2 * i + 2] for i in range(9)]
    direct, sibling, onward, source, near_adds = peers()
    roles = role_targets()
    size = anchor_ref.shape[0] // PARTS
    beside = [t + 1 - 2 * lax.rem(t, 2) for t in (onward, source)]
    greet((direct, sibling, onward, source, beside[0], beside[1], roles[1], roles[3]))

    def rows(i):
        return pl.ds(i * size, size)

    def copies(k, src, dst, target):
        return [
            remote(src.at[rows(i)], dst.at[rows(i)], s[k][0].at[i], s[k][1].at[i], target)
            for i in range(PARTS)
        ]

    crosses = copies(0, cross_ref, cross_in, sibling)
    sibs = copies(1, sib_ref, sib_in, sibling)
    hops = copies(2, far_send, far_in, source)
    nears = copies(3, near_send, near_in, direct)
    to_direct = copies(4, anchor_ref, adirect_ref, direct)
    to_sibling = copies(5, anchor_ref, asib_ref, sibling)
    relays = copies(6, adirect_ref, afar_ref, onward)
    cross_a = copies(7, adirect_ref, across_ref, sibling)
    cross_b = copies(7, afar_ref, across_ref, sibling)
    cross_b[-1] = copies(7, adirect_ref, across_ref, beside[0])[-1]
    coefs = [
        remote(coef_out, coefs_out.at[j], s[8][0].at[j], s[8][1].at[j], target)
        for j, target in enumerate(roles)
    ]
    for copy in crosses:
        copy.start()
    for copy in sibs:
        copy.start()
    for i in range(PARTS):
        @pl.when(near_adds)
        def _():
            far_send[rows(i), :] = far_ref[rows(i), :]

        @pl.when(jnp.logical_not(near_adds))
        def _():
            crosses[i].wait_recv()
            far_send[rows(i), :] = (
                far_ref[rows(i), :].astype(F32) + cross_in[rows(i), :].astype(F32)
            ).astype(BF16)

        hops[i].start()
        if i < PARTS // 2:
            to_direct[i].start()
    def relay(i):
        to_sibling[i].start()
        to_direct[i].wait_recv()
        relays[i].start()

        @pl.when(near_adds)
        def _():
            cross_a[i].start()

        if i == PARTS - 1:

            @pl.when(jnp.logical_not(near_adds))
            def _():
                cross_b[i].start()

    for i in range(PARTS):
        hops[i].wait_recv()
        value = near_ref[rows(i), :].astype(F32) + far_in[rows(i), :].astype(F32)

        @pl.when(near_adds)
        def _():
            crosses[i].wait_recv()
            near_send[rows(i), :] = (value + cross_in[rows(i), :].astype(F32)).astype(BF16)

        @pl.when(jnp.logical_not(near_adds))
        def _():
            near_send[rows(i), :] = value.astype(BF16)

        nears[i].start()
        if i >= PARTS // 2:
            relay(i - PARTS // 2)
    for i in range(PARTS // 2, PARTS):
        to_direct[i].start()
    gaps = []
    for i in range(PARTS):
        sibs[i].wait_recv()
        nears[i].wait_recv()
        change = (
            near_in[rows(i), :].astype(F32)
            + self_ref[rows(i), :].astype(F32)
            + sib_in[rows(i), :].astype(F32)
        )
        change_ref[rows(i), :] = change
        product = anchor_ref[rows(i), :].astype(F32) * change
        for u in range(size // 128):
            gaps.append(
                jnp.sum(product[u * 128 : (u + 1) * 128].T, axis=0, keepdims=True) * inv_root
            )
    gap = jnp.concatenate(gaps, axis=0)
    coef_out[...] = jax.nn.sigmoid(gap) * (inv_root / loss_divisor)
    for copy in coefs:
        copy.start()
    soft = jnp.maximum(gap, 0.0) + jnp.log1p(jnp.exp(-jnp.abs(gap)))
    loss_ref[...] = jnp.broadcast_to(jnp.sum(soft, keepdims=True), loss_ref.shape)
    for i in range(PARTS // 2, PARTS):
        relay(i)
    for i in range(PARTS):
        relays[i].wait_recv()

        if i < PARTS - 1:

            @pl.when(jnp.logical_not(near_adds))
            def _():
                cross_b[i].start()

    size = 128
    eye = lax.broadcasted_iota(jnp.int32, (size, size), 0) == lax.broadcasted_iota(
        jnp.int32, (size, size), 1
    )
    for i in range(coef_out.shape[0]):
        coef = coef_out[pl.ds(i, 1), :]
        column = jnp.sum(jnp.where(eye, coef, 0.0), axis=1, keepdims=True)
        here = pl.ds(i * size, size)
        ganchor_ref[here, :] = column * change_ref[here, :]
    for copy in coefs:
        copy.wait()
    for i in range(PARTS):
        crosses[i].wait_send()
        sibs[i].wait_send()
        hops[i].wait_send()
        nears[i].wait_send()
        to_direct[i].wait_send()
        to_sibling[i].wait()
        relays[i].wait_send()
        cross_a[i].wait()


def spread_group(index_ref, tiles_ref, adj_ref, agg_grad_t, step, group, slots, rows):
    for g in range(group):
        block = step * group + g
        tile = jnp.concatenate([tiles_ref[block, s] for s in range(slots)], axis=1)
        contrib = dot(agg_grad_t[:, g * rows : (g + 1) * rows], tile, 1, 0)
        for s in range(slots):
            at = index_ref[(step * group + g) * slots + s]
            adj_ref[at] = adj_ref[at] + contrib[:, s * rows : (s + 1) * rows]


def clear_blocks(adj_ref):
    def clear(i, carry):
        adj_ref[i] = jnp.zeros(adj_ref.shape[1:], F32)
        return carry

    lax.fori_loop(0, adj_ref.shape[0], clear, 0)


def scatter_rows(
    list_ref, anchor_ref, ganchor_ref, coef_ref, coefs_ref, rows_in, moved_ref, sums
):
    triplets, width = ganchor_ref.shape
    hits = sums[0].shape[0]
    stride = list_ref.shape[0] // 5
    span = 2 * triplets + 8
    bounds = segments(list_ref, stride, 2 * triplets + 128)
    zeros = jnp.zeros((64, width), F32)

    def clear(i, carry):
        for target in sums:
            target[pl.ds(pl.multiple_of(i * 64, 64), 64), :] = zeros
        return carry

    lax.fori_loop(0, hits // 64, clear, 0)
    eye = lax.broadcasted_iota(jnp.int32, (128, 128), 0) == lax.broadcasted_iota(
        jnp.int32, (128, 128), 1
    )
    for j, source in enumerate(rows_in):
        for i in range(triplets // 128):
            coef = coef_ref[pl.ds(i, 1), :] if j == 0 else coefs_ref[j - 1, pl.ds(i, 1), :]
            spread = jnp.where(eye, coef, 0.0)
            high = spread.astype(BF16)
            low = (spread - high.astype(F32)).astype(BF16)
            part = source[pl.ds(i * 128, 128), :]
            value = dot(high, part, 1, 0) + dot(low, part, 1, 0)
            moved_ref[pl.ds(j * span + i * 128, 128), :] = -value
            moved_ref[pl.ds(j * span + triplets + i * 128, 128), :] = value
        moved_ref[pl.ds(j * span + 2 * triplets, 8), :] = zeros[:8]

    def anchors(i, carry):
        for u in range(8):
            t = i * 8 + u
            here = pl.ds(anchor_ref[t], 1)
            target = sums[u % 4]
            target[here, :] = target[here, :] + ganchor_ref[pl.ds(t, 1), :]
        return carry

    lax.fori_loop(0, triplets // 8, anchors, 0)
    for j in range(5):

        def add(i, carry, j=j):
            for u in range(8):
                entry = list_ref[j * stride + i * 8 + u]
                here = pl.ds(lax.shift_right_logical(entry, ENTRY_BITS), 1)
                target = sums[u % 4]
                moved = moved_ref[pl.ds(j * span + lax.bitwise_and(entry, ENTRY_MASK), 1), :]
                target[here, :] = target[here, :] + moved
            return carry

        lax.fori_loop(bounds[j][0], bounds[j][1], add, 0)


def last_backward(
    group,
    steps,
    index_ref,
    list_ref,
    anchor_ref,
    tiles_hbm,
    ganchor_ref,
    coef_ref,
    coefs_ref,
    aself_ref,
    asib_ref,
    across_ref,
    adirect_ref,
    afar_ref,
    hidden_ref,
    w_agg_ref,
    w_out_ref,
    upstream_ref,
    act_ref,
    gradient_ref,
    obelow_ref,
    oown_ref,
    oabove_ref,
    osibling_ref,
    ocross_ref,
    adj_ref,
    moved_ref,
    stage_ref,
    tiles_ref,
    tile_sem,
    piece_sem,
    *sums,
):
    step = pl.program_id(0)
    slots, rows = tiles_ref.shape[1], tiles_ref.shape[2]
    span = group * rows

    def tile_load(i):
        part = pl.ds(i * group, group)
        return pltpu.make_async_copy(tiles_hbm.at[part], tiles_ref.at[part], tile_sem.at[i])

    @pl.when(step == 0)
    def _():
        for i in range(steps):
            tile_load(i).start()
        clear_blocks(adj_ref)
        scatter_rows(
            list_ref, anchor_ref, ganchor_ref, coef_ref, coefs_ref,
            (aself_ref, asib_ref, across_ref, adirect_ref, afar_ref), moved_ref, sums,
        )

    here = pl.ds(pl.multiple_of(step * span, span), span)
    gradient = (sums[0][here, :] + sums[1][here, :]) + (sums[2][here, :] + sums[3][here, :])
    upstream = gradient.astype(BF16)
    hidden_grad = dot(upstream, w_out_ref[1], 1, 1)
    act_grad = jnp.where(hidden_ref[...].astype(F32) > 0, hidden_grad, 0.0).astype(BF16)
    upstream_ref[...] = upstream
    act_ref[...] = act_grad
    gradient_ref[...] = gradient
    tile_load(step).wait()
    agg_grad_t = dot(w_agg_ref[1], act_grad, 1, 1).astype(BF16)
    spread_group(index_ref, tiles_ref, adj_ref, agg_grad_t, step, group, slots, rows)

    @pl.when(step == steps - 1)
    def _():
        blocks = oown_ref.shape[0]
        copies = [
            pltpu.make_async_copy(
                adj_ref.at[pl.ds(blocks, blocks)], oown_ref, piece_sem.at[4]
            )
        ]
        copies[0].start()
        for j, (k, target) in enumerate(
            ((4, ocross_ref), (3, osibling_ref), (2, oabove_ref), (0, obelow_ref))
        ):

            def store(i, carry, k=k, j=j):
                for u in range(2):
                    stage_ref[j, 2 * i + u] = adj_ref[k * blocks + 2 * i + u].astype(BF16)
                return carry

            lax.fori_loop(0, blocks // 2, store, 0)
            copies.append(pltpu.make_async_copy(stage_ref.at[j], target, piece_sem.at[j]))
            copies[-1].start()
        for copy in copies:
            copy.wait()


def summer(pairs, x_ref, half_in, acc_ref, slots_in, all_ref, sems):
    s0, r0, s1, r1, s2, r2, s3, r3 = sems
    wire = acc_ref.dtype
    me = lax.axis_index("phi")
    pair, core = me // 2, me % 2
    sibling = me + 1 - 2 * core
    others = [((pair + d) % pairs) * 2 + core for d in range(1, pairs)]
    half = x_ref.shape[0] // 2
    chunk = half // pairs

    def part(start, length):
        return pl.ds(pl.multiple_of(start, 16 if wire == BF16 else 8), length)

    swap = remote(x_ref.at[part((1 - core) * half, half)], half_in, s0.at[0], r0.at[0], sibling)
    scatter = [
        remote(
            acc_ref.at[part(((pair + d) % pairs) * chunk, chunk)],
            slots_in.at[d - 1],
            s1.at[d - 1],
            r1.at[d - 1],
            others[d - 1],
        )
        for d in range(1, pairs)
    ]
    mine = part(core * half + pair * chunk, chunk)
    gather = [
        remote(all_ref.at[mine], all_ref.at[mine], s2.at[d - 1], r2.at[d - 1], others[d - 1])
        for d in range(1, pairs)
    ]
    whole = part(core * half, half)
    last = remote(all_ref.at[whole], all_ref.at[whole], s3.at[0], r3.at[0], sibling)

    def scatter_stage():
        swap.wait()
        acc_ref[...] = (x_ref[part(core * half, half), :] + half_in[...]).astype(wire)
        for copy in scatter:
            copy.start()

    def gather_stage():
        total = x_ref[mine, :] + half_in[part(pair * chunk, chunk), :]
        for d in range(1, pairs):
            scatter[d - 1].wait_recv()
            total = total + slots_in[d - 1].astype(F32)
        all_ref[mine, :] = total.astype(wire)
        for copy in gather:
            copy.start()

    def last_stage():
        for copy in gather:
            copy.wait()
        for copy in scatter:
            copy.wait_send()
        last.start()

    return swap.start, scatter_stage, gather_stage, last_stage, last.wait


def back_kernel(
    pairs,
    index_ref,
    cross_hbm,
    sib_hbm,
    relay_hbm,
    direct_hbm,
    own_hbm,
    grad_hbm,
    hidden_hbm,
    before_hbm,
    agg_hbm,
    tiles_hbm,
    upstream1_hbm,
    act1_hbm,
    hidden1_hbm,
    before1_hbm,
    agg1_hbm,
    feats_ref,
    wcat_ref,
    w_self_ref,
    w_agg_ref,
    w_out_ref,
    loss_ref,
    early_ref,
    all_ref,
    wcat_t_ref,
    cross_in,
    sib_in,
    relay_in,
    total_in,
    relay_send,
    direct_send,
    relay_ref,
    direct_ref,
    own_ref,
    grad_ref,
    hidden_ref,
    before_ref,
    agg_ref,
    upstream1_ref,
    act1_ref,
    hidden1_ref,
    before1_ref,
    agg1_ref,
    tiles_ref,
    slope_ref,
    block_feats_ref,
    x_ref,
    half_in,
    acc_ref,
    slots_in,
    early_x,
    early_half,
    early_acc,
    early_slots,
    local_sem,
    *sems,
):
    ys, yr, zs, zr, cs, cr, ss, sr = sems[:8]
    direct, sibling, onward, source, to_direct = peers()
    me = lax.axis_index("phi")
    pair, core = me // 2, me % 2
    others = [((pair + d) % pairs) * 2 + core for d in range(1, pairs)]
    blocks, slots, rows, _ = tiles_ref.shape
    depth, width = wcat_ref.shape
    window = feats_ref.shape[1] // rows
    size = grad_ref.shape[0] // CHUNKS
    group = blocks // CHUNKS
    loads = [
        pltpu.make_async_copy(src, dst, local_sem.at[k])
        for k, (src, dst) in enumerate(
            (
                (relay_hbm, relay_ref),
                (direct_hbm, direct_ref),
                (own_hbm, own_ref),
                (grad_hbm, grad_ref),
                (hidden_hbm, hidden_ref),
                (before_hbm, before_ref),
                (agg_hbm, agg_ref),
                (tiles_hbm, tiles_ref),
                (upstream1_hbm, upstream1_ref),
                (act1_hbm, act1_ref),
                (hidden1_hbm, hidden1_ref),
                (before1_hbm, before1_ref),
                (agg1_hbm, agg1_ref),
            )
        )
    ]
    for copy in loads:
        copy.start()
    greet([sibling] + others)

    def span(i):
        return pl.ds(pl.multiple_of(i * size, size), size)

    def crosses(i):
        return remote(cross_hbm.at[span(i)], cross_in.at[span(i)], cs.at[i], cr.at[i], sibling)

    def first(i):
        return remote(relay_send.at[span(i)], relay_in.at[span(i)], zs.at[i], zr.at[i], source)

    def second(i):
        return remote(direct_send.at[span(i)], total_in.at[span(i)], ys.at[i], yr.at[i], direct)

    near = remote(sib_hbm, sib_in, ss.at[0], sr.at[0], sibling)
    lax.fori_loop(0, CHUNKS, lambda i, c: (crosses(i).start(), c)[1], 0)
    near.start()

    early = summer(pairs, early_x, early_half, early_acc, early_slots, early_ref, sems[8:16])
    final = summer(pairs, x_ref, half_in, acc_ref, slots_in, all_ref, sems[16:24])
    early_x[...] = jnp.zeros(early_x.shape, F32)
    early_x[3 * width : 3 * width + 8, :] = loss_ref[...]
    per = window // CHUNKS

    def slopes(i):
        for u in range(0, per, 2):
            at = pl.multiple_of((i * per + u) * rows, 2 * rows)
            feats = feats_ref[:, pl.ds(at, 2 * rows)]
            squashed = jnp.tanh(dot(wcat_t_ref[...], feats, 1, 0))
            slope = 1.0 - squashed * squashed
            for v in range(2):
                slope_ref[i * per + u + v] = slope[:, v * rows : (v + 1) * rows]
                block_feats_ref[i * per + u + v] = feats[:, v * rows : (v + 1) * rows]

    wcat_t_ref[...] = (
        jnp.concatenate([wcat_ref[...].astype(F32), jnp.zeros((width - depth, width), F32)], axis=0)
        .T[:, :depth]
        .astype(BF16)
    )
    x_ref[...] = jnp.zeros(x_ref.shape, F32)
    base = 3 * width
    slope_ref[window] = jnp.zeros(slope_ref.shape[1:], F32)
    block_feats_ref[window] = jnp.zeros(block_feats_ref.shape[1:], BF16)
    loads[0].wait()

    lag = 3

    def relay_step(i, carry):
        here = span(i)

        @pl.when(to_direct)
        def _():
            relay_send[here, :] = relay_ref[here, :]

        @pl.when(jnp.logical_not(to_direct))
        def _():
            crosses(i).wait_recv()
            relay_send[here, :] = (
                relay_ref[here, :].astype(F32) + cross_in[here, :].astype(F32)
            ).astype(BF16)

        first(i).start()

        @pl.when(i < CHUNKS - 2 * lag)
        def _():
            slopes(i)

        return carry

    lax.fori_loop(0, CHUNKS, relay_step, 0)
    for copy in loads[1:]:
        copy.wait()
    near.wait()

    def direct_step(i):
        here = span(i)
        first(i).wait_recv()
        value = direct_ref[here, :].astype(F32) + relay_in[here, :].astype(F32)

        @pl.when(to_direct)
        def _():
            crosses(i).wait_recv()
            direct_send[here, :] = (value + cross_in[here, :].astype(F32)).astype(BF16)

        @pl.when(jnp.logical_not(to_direct))
        def _():
            direct_send[here, :] = value.astype(BF16)

        second(i).start()

    def upper_step(i):
        here = pl.ds(pl.multiple_of(i * 2 * size, 2 * size), 2 * size)
        act_grad = act1_ref[here, :]
        early_x[0:width, :] += dot(hidden1_ref[here, :], upstream1_ref[here, :], 0, 0)
        early_x[width : 2 * width, :] += dot(before1_ref[here, :], act_grad, 0, 0)
        early_x[2 * width : 3 * width, :] += dot(agg1_ref[here, :], act_grad, 0, 0)
        grad_ref[here, :] = grad_ref[here, :] + dot(act_grad, w_self_ref[1], 1, 1)

    def layer_step(i):
        here = span(i)
        second(i).wait_recv()
        returned = own_ref[here, :] + (
            total_in[here, :].astype(F32) + sib_in[here, :].astype(F32)
        )
        gradient = grad_ref[here, :] + jnp.concatenate(
            [returned[g * width : (g + 1) * width].T for g in range(group)], axis=0
        )
        upstream = gradient.astype(BF16)
        hidden = hidden_ref[here, :]
        hidden_grad = dot(upstream, w_out_ref[0], 1, 1)
        act_grad = jnp.where(hidden.astype(F32) > 0, hidden_grad, 0.0).astype(BF16)
        agg_grad_t = dot(w_agg_ref[0], act_grad, 1, 1).astype(BF16)
        x_ref[0:width, :] += dot(hidden, upstream, 0, 0)
        x_ref[width : 2 * width, :] += dot(before_ref[here, :], act_grad, 0, 0)
        x_ref[2 * width : 3 * width, :] += dot(agg_ref[here, :], act_grad, 0, 0)
        own_grad = gradient + dot(act_grad, w_self_ref[0], 1, 1)
        feats = feats_ref[:, pl.ds(pl.multiple_of((window // 5) * rows + i * size, size), size)]
        squashed = jnp.tanh(dot(feats, wcat_ref[...], 0, 0))
        genc = dot(feats, (own_grad * (1.0 - squashed * squashed)).astype(BF16), 1, 0)
        for g in range(group):
            block = i * group + g
            tile = jnp.concatenate([tiles_ref[block, s] for s in range(slots)], axis=1)
            contrib = dot(agg_grad_t[:, g * rows : (g + 1) * rows], tile, 1, 0)
            places = [index_ref[block * slots + s] for s in range(slots)]
            slope = jnp.concatenate([slope_ref[at] for at in places], axis=1)
            source_feats = jnp.concatenate([block_feats_ref[at] for at in places], axis=1)
            genc = genc + dot(source_feats, (contrib * slope).astype(BF16), 1, 1)
        x_ref[base : base + depth, :] += genc

    turn = CHUNKS // 2

    def opening(i, carry):
        direct_step(i)
        upper_step(i)

        @pl.when(i < lag)
        def _():
            slopes(CHUNKS - 2 * lag + 2 * i)
            slopes(CHUNKS - 2 * lag + 2 * i + 1)

        @pl.when(i >= lag)
        def _():
            layer_step(i - lag)

        return carry

    def middle(i, carry):
        direct_step(i)
        layer_step(i - lag)
        return carry

    def closing(i, carry):
        layer_step(i)
        return carry

    lax.fori_loop(0, turn, opening, 0)
    early[0]()
    lax.fori_loop(turn, turn + 4, middle, 0)
    early[1]()
    lax.fori_loop(turn + 4, CHUNKS, middle, 0)
    early[2]()
    lax.fori_loop(CHUNKS - lag, CHUNKS, closing, 0)
    final[0]()
    early[3]()

    def drain(i, carry):
        crosses(i).wait_send()
        first(i).wait_send()
        second(i).wait_send()
        return carry

    lax.fori_loop(0, CHUNKS, drain, 0)

    for stage in final[1:]:
        stage()
    early[4]()


def finish_kernel(
    triplet_total,
    early_ref,
    sum_ref,
    loss_out,
    genc_out,
    gtable_out,
    gself_out,
    gagg_out,
    gout_out,
):
    width = gself_out.shape[1]
    for k, out in enumerate((gout_out, gself_out, gagg_out)):
        for layer, source in enumerate((sum_ref, early_ref)):
            out[layer] = source[k * width : (k + 1) * width, :].astype(F32)
    base = 3 * width
    genc_out[...] = sum_ref[base : base + 16, :].astype(F32)[: genc_out.shape[0]]
    gtable_out[...] = sum_ref[base + 16 : base + 16 + gtable_out.shape[0], :].astype(F32)
    loss_out[...] = early_ref[base : base + 1, 0:1] / triplet_total


def body(
    hit_feats,
    layer_ids,
    edge_tiles,
    src_blocks,
    live_slots,
    anchor_hits,
    positive_hits,
    negative_hits,
    w_enc,
    layer_table,
    w_self,
    w_agg,
    w_out,
):
    blocks, slots, rows, _ = edge_tiles.shape
    width = w_enc.shape[1]
    features = hit_feats.shape[0]
    kinds = layer_table.shape[0]
    hits = blocks * rows
    layer_total = w_self.shape[0]
    triplets = anchor_hits.shape[0]
    group = 8
    steps = blocks // group
    span = group * rows
    me = lax.axis_index("phi")
    is_even = me % 2 == 0
    even_pair = (me // 2) % 2 == 0

    def place(part):
        spots = (
            jnp.where(even_pair, 2, 0),
            jnp.where(is_even, 4, 3),
            1,
            jnp.where(is_even, 3, 4),
            jnp.where(even_pair, 0, 2),
        )
        return sum(jnp.where(part == k, spot, 0) for k, spot in enumerate(spots))

    live = jnp.arange(slots, dtype=jnp.int32)[None, :] < live_slots[:, None]
    index = jnp.where(
        live, place(src_blocks // blocks) * blocks + src_blocks % blocks, 5 * blocks
    ).reshape(blocks * slots)
    depth = 16 + kinds
    listed = 2 * triplets // 128 + 1
    list_shape = (-(-(listed + 1) // 8) * 8, 128)

    row_spec = pl.BlockSpec((span, width), lambda i, *_: (i, 0))
    weight_spec = full((width, width))
    any_spec = pl.BlockSpec(memory_space=pl.ANY)
    row_shape = jax.ShapeDtypeStruct((hits, width), BF16)
    weight_shape = jax.ShapeDtypeStruct((width, width), F32)

    wide_shape = jax.ShapeDtypeStruct((hits, width), F32)
    vmem = pl.BlockSpec(memory_space=pltpu.VMEM)
    smem = pl.BlockSpec(memory_space=pltpu.SMEM)
    few = pltpu.SemaphoreType.DMA((FEAT_CHUNKS,))
    each = pltpu.SemaphoreType.DMA((CHUNKS,))
    one = pltpu.SemaphoreType.DMA((1,))
    four = pltpu.SemaphoreType.DMA((4,))
    block_shape = jax.ShapeDtypeStruct((blocks, rows, width), BF16)
    before0, agg0, hidden0, latents1, agg1, hidden1, latents2, lists, feats, wcat = pl.pallas_call(
        functools.partial(forward_kernel, features),
        in_specs=[smem] + [vmem] * 4 + [any_spec] + [vmem] * 5,
        out_specs=[any_spec] * 10,
        out_shape=[block_shape, row_shape, row_shape, block_shape, row_shape, row_shape]
        + [
            wide_shape,
            jax.ShapeDtypeStruct((5,) + list_shape, jnp.int32),
            jax.ShapeDtypeStruct((depth, 5 * hits), BF16),
            jax.ShapeDtypeStruct((depth, width), BF16),
        ],
        scratch_shapes=[
            pltpu.VMEM((16, hits), BF16),
            pltpu.VMEM((depth, width), BF16),
            pltpu.VMEM(list_shape, jnp.int32),
            pltpu.VMEM((listed - 1, 128, 128), jnp.int32),
            pltpu.VMEM((listed - 1, 128, 128), jnp.int32),
            pltpu.VMEM((listed - 1, 128, 128), jnp.int32),
            pltpu.VMEM((5, 16, hits), BF16),
            pltpu.VMEM((depth, 5 * hits), BF16),
            pltpu.VMEM((5 * blocks + 1, rows, width), BF16),
            pltpu.VMEM((5 * blocks + 1, rows, width), BF16),
        ]
        + [pltpu.VMEM((hits, width), BF16)] * 4
        + [
            pltpu.VMEM((hits, width), F32),
            pltpu.VMEM(edge_tiles.shape, BF16),
            each,
            pltpu.SemaphoreType.DMA((6,)),
            pltpu.SemaphoreType.DMA((3 * LATER_STEPS,)),
            one,
        ]
        + [few] * 6
        + [four] * 2
        + [each] * 8
        + [one] * 2,
        compiler_params=pltpu.CompilerParams(
            collective_id=1, has_side_effects=True, vmem_limit_bytes=VMEM_BYTES
        ),
        name="forward",
    )(
        index,
        hit_feats,
        layer_ids.reshape(1, hits),
        positive_hits.reshape(triplets // 128, 128),
        negative_hits.reshape(triplets // 128, 128),
        edge_tiles,
        w_enc,
        layer_table,
        w_self,
        w_agg,
        w_out,
    )

    before0, latents1 = before0.reshape(hits, width), latents1.reshape(hits, width)
    lists = lists.reshape(-1)
    move_shape = jax.ShapeDtypeStruct((triplets, width), BF16)
    wide_move = jax.ShapeDtypeStruct((triplets, width), F32)
    move_spec = full((triplets, width))
    *found, anchors = pl.pallas_call(
        gather_kernel,
        grid_spec=pltpu.PrefetchScalarGridSpec(
            num_scalar_prefetch=2,
            grid=(1,),
            in_specs=[full((hits, width))],
            out_specs=[move_spec] * 6,
            scratch_shapes=[pltpu.VMEM((2 * triplets + 8, width), F32)],
        ),
        out_shape=[move_shape] * 6,
        compiler_params=params(),
        name="gather",
    )(lists, anchor_hits, latents2)
    coef_shape = (triplets // 128, 128)
    loss_part, ganchor, *moves, coef, coefs = pl.pallas_call(
        functools.partial(contrast_kernel, 1.0 / math.sqrt(width)),
        in_specs=[vmem] * 6,
        out_specs=[vmem] * 8,
        out_shape=[jax.ShapeDtypeStruct((8, width), F32), wide_move]
        + [move_shape] * 4
        + [jax.ShapeDtypeStruct(coef_shape, F32), jax.ShapeDtypeStruct((4,) + coef_shape, F32)],
        scratch_shapes=[pltpu.VMEM((triplets, width), F32)]
        + [pltpu.VMEM((triplets, width), BF16)] * 6
        + [pltpu.SemaphoreType.DMA((PARTS,))] * 16
        + [pltpu.SemaphoreType.DMA((4,))] * 2,
        compiler_params=pltpu.CompilerParams(
            collective_id=4, has_side_effects=True, vmem_limit_bytes=VMEM_BYTES
        ),
        name="contrast",
    )(*found, anchors)

    t_shape = jax.ShapeDtypeStruct((blocks, width, rows), F32)
    t_half = jax.ShapeDtypeStruct((blocks, width, rows), BF16)
    adj_shape = pltpu.VMEM((5 * blocks + 1, width, rows), F32)
    upstream1, act1, gradient2, obelow, own, oabove, osibling, ocross = pl.pallas_call(
        functools.partial(last_backward, group, steps),
        grid_spec=pltpu.PrefetchScalarGridSpec(
            num_scalar_prefetch=3,
            grid=(steps,),
            in_specs=[any_spec, move_spec, full(coef_shape), full((4,) + coef_shape)]
            + [move_spec] * 5
            + [row_spec]
            + [full((2, width, width))] * 2,
            out_specs=[row_spec] * 3 + [any_spec] * 5,
            scratch_shapes=[
                adj_shape,
                pltpu.VMEM((10 * triplets + 40, width), F32),
                pltpu.VMEM((4, blocks, width, rows), BF16),
                pltpu.VMEM(edge_tiles.shape, BF16),
                pltpu.SemaphoreType.DMA((steps,)),
                pltpu.SemaphoreType.DMA((5,)),
            ]
            + [pltpu.VMEM((hits, width), F32)] * 4,
        ),
        out_shape=[row_shape] * 2 + [wide_shape] + [t_half, t_shape] + [t_half] * 3,
        compiler_params=params(),
        name="last_backward",
    )(
        index, lists, anchor_hits, edge_tiles, ganchor, coef, coefs, anchors, *moves, hidden1, w_agg, w_out,
    )
    pairs = lax.axis_size("phi") // 2

    def sum_sizes(count, wire):
        chunk = -(-count // (32 * pairs)) * 16
        total = 2 * pairs * chunk
        return jax.ShapeDtypeStruct((total, width), wire), [
            pltpu.VMEM((total, width), F32),
            pltpu.VMEM((total // 2, width), F32),
            pltpu.VMEM((total // 2, width), wire),
            pltpu.VMEM((pairs - 1, chunk, width), wire),
        ]

    early_shape, early_scratch = sum_sizes(3 * width + 8, F32)
    final_shape, final_scratch = sum_sizes(3 * width + depth, F32)
    many = pltpu.SemaphoreType.DMA((pairs - 1,))
    flat = (hits, width)
    sums = pl.pallas_call(
        functools.partial(back_kernel, pairs),
        in_specs=[smem] + [any_spec] * 15 + [vmem] * 6,
        out_specs=[vmem] * 2,
        out_shape=[early_shape, final_shape],
        scratch_shapes=[pltpu.VMEM((width, depth), BF16)]
        + [pltpu.VMEM(flat, BF16)] * 8
        + [pltpu.VMEM(flat, F32)] * 2
        + [pltpu.VMEM(flat, BF16)] * 8
        + [
            pltpu.VMEM(edge_tiles.shape, BF16),
            pltpu.VMEM((5 * blocks + 1, width, rows), F32),
            pltpu.VMEM((5 * blocks + 1, depth, rows), BF16),
        ]
        + final_scratch
        + early_scratch
        + [pltpu.SemaphoreType.DMA((13,))]
        + [pltpu.SemaphoreType.DMA((CHUNKS,))] * 6
        + [one, one]
        + [one, one, many, many, many, many, one, one] * 2,
        compiler_params=pltpu.CompilerParams(
            collective_id=3, has_side_effects=True, vmem_limit_bytes=VMEM_BYTES
        ),
        name="back",
    )(
        index, ocross.reshape(flat), osibling.reshape(flat), oabove.reshape(flat),
        obelow.reshape(flat), own.reshape(flat), gradient2, hidden0, before0, agg0, edge_tiles,
        upstream1, act1, hidden1, latents1, agg1,
        feats, wcat, w_self, w_agg, w_out, loss_part,
    )
    stack = jax.ShapeDtypeStruct((2, width, width), F32)
    loss, genc, gtable, gself, gagg, gout = pl.pallas_call(
        functools.partial(finish_kernel, float(triplets * lax.axis_size("phi"))),
        in_specs=[vmem] * 2,
        out_specs=[vmem] * 6,
        out_shape=[
            jax.ShapeDtypeStruct((1, 1), F32),
            jax.ShapeDtypeStruct((features, width), F32),
            jax.ShapeDtypeStruct((kinds, width), F32),
            stack, stack, stack,
        ],
        name="finish",
    )(*sums)
    return (loss.reshape(1), genc, gtable, gself, gagg, gout)


def solution(mesh):
    both = ("event", "phi")
    in_specs = (
        P(None, both),
        P(both),
        P(both, None, None, None),
        P(both, None),
        P(both),
        P(both),
        P(both),
        P(both),
        P(),
        P(),
        P(),
        P(),
        P(),
    )
    out_specs = (
        P("event"),
        P("event", None),
        P("event", None),
        P("event", None, None),
        P("event", None, None),
        P("event", None, None),
    )
    return jax.shard_map(body, mesh=mesh, in_specs=in_specs, out_specs=out_specs, check_vma=False)
```
